32 devices in a mesh: dp: 2 (over core), expert: 4 (over z), tensor: 4 (over y, x).
Axes of the slice: x: 2, y: 2, z: 4, core: 2. Of those that a mesh axis runs over, the one named last changes fastest.
Arguments:
- tokens: bfloat16 [24, 197, 768], P(('dp', 'expert'))
- cotangent: bfloat16 [24, 197, 768], P(('dp', 'expert')), may hold values from -6 to 6
- expert_ids: int32 [24, 197, 2], P(('dp', 'expert')), may hold values from 0 to 3, as said below
- slot_rank: int32 [24, 197, 2], P(('dp', 'expert')), may hold values from -1 to 368, as said below
- qkv_weight: bfloat16 [3, 768, 768], P(None, None, 'tensor'), may hold values from -0.3125 to 0.3125
- out_weight: bfloat16 [768, 768], P('tensor'), may hold values from -0.625 to 0.625
- router_weight: bfloat16 [768, 4], replicated, may hold values from -0.15625 to 0.15625
- expert_in: bfloat16 [4, 768, 3072], P('expert', None, 'tensor'), may hold values from -0.21875 to 0.21875
- expert_out: bfloat16 [4, 3072, 768], P('expert', 'tensor'), may hold values from -0.875 to 0.875
- gain_attention: float32 [768], replicated, may hold values from 0.25 to 1.75
- gain_experts: float32 [768], replicated, may hold values from 0.25 to 1.75
Outputs:
- block_out: bfloat16 [24, 197, 768], P(('dp', 'expert'))
- grad_tokens: float32 [24, 197, 768], P(('dp', 'expert'))
- grad_qkv: float32 [3, 768, 768], P(None, None, 'tensor')
- grad_out: float32 [768, 768], P('tensor')
- grad_router: float32 [768, 4], replicated
- grad_expert_in: float32 [4, 768, 3072], P('expert', None, 'tensor')
- grad_expert_out: float32 [4, 3072, 768], P('expert', 'tensor')
- grad_gain_attention: float32 [768], replicated
- grad_gain_experts: float32 [768], replicated
- balance_loss: float32 [], replicated
The draws below stay inside these ranges and needn't reach their ends.
Inputs may be any that keep to these rules, and one draw needn't show every extreme that they name: `expert_ids`: the two experts of a token differ. Within each aligned block of 591 tokens, the pairs that name one expert are ranked: first choices of all the block's tokens in token order, then second choices in token order. A pair's slot_rank is its rank if that is below 369, else -1. In every block some expert has its slot 368 filled and a pair dropped.
All inputs are finite; a program needn't handle non-finite values.
Results may differ from the reference program's by a relative error of at most 0.017.
The reference program's roundings to bfloat16 on the way count: a program that leaves them out, or rounds other values in their place, can miss the bound.
Values may be sent and summed in bfloat16 or wider, within the bound.
No kernel may reach another device: no remote copies, remote signals or barrier semaphores. Data moves between devices by JAX's collectives and lax.ppermute only.
A program may use at most 192 MiB of HBM per device.

```python
import jax
import jax.numpy as jnp
from jax import lax

D = 768
HEADS = 12
HD = 64
FF = 3072
SEQ = 197
IMG_DEV = 3
EXPERTS = 4
IMAGES = 24
TOK_DEV = 591
CAP = 369


def routing(key):
    blocks = IMAGES // IMG_DEV
    count = TOK_DEV
    k_perm, k_low, k_step, k_roll = jax.random.split(jax.random.fold_in(key, 11), 4)
    order = jax.random.permutation(k_perm, EXPERTS)
    draws = jax.random.randint(k_low, (3, blocks, count), 0, EXPERTS)
    low_pick = jnp.min(draws, axis=0)
    roll = jax.random.randint(k_roll, (blocks, count), 0, 1000)
    level = (jnp.arange(blocks) * 500 // max(blocks - 1, 1))[:, None]
    first_rank = jnp.where(roll < level, 0, low_pick)
    stride = jax.random.randint(k_step, (blocks, count), 1, EXPERTS)
    place = jnp.arange(count)[None, :]
    first_rank = jnp.where(place < CAP, 0, first_rank)
    forced = (place >= CAP) & (place < CAP + 4)
    first_rank = jnp.where(forced, 1, first_rank)
    stride = jnp.where(forced, EXPERTS - 1, stride)
    second_rank = (first_rank + stride) % EXPERTS
    first = order[first_rank]
    second = order[second_rank]
    pairs = jnp.concatenate([first, second], axis=1)
    onehot = (pairs[:, :, None] == jnp.arange(EXPERTS)[None, None, :]).astype(jnp.int32)
    rank = jnp.sum(jnp.cumsum(onehot, axis=1) * onehot, axis=2) - 1
    slot = jnp.where(rank < CAP, rank, -1)
    ids = jnp.stack([first, second], axis=-1).reshape(IMAGES, SEQ, 2).astype(jnp.int32)
    slots = jnp.stack([slot[:, :count], slot[:, count:]], axis=-1).reshape(IMAGES, SEQ, 2).astype(jnp.int32)
    return (ids, slots)


def draw_expert_ids(key, part):
    return routing(key)[0]


def draw_slot_rank(key, part):
    return routing(key)[1]


def draw_tokens(key, part):
    k_base, k_common = jax.random.split(jax.random.fold_in(key, 5))
    base = jax.random.normal(k_base, (IMAGES, SEQ, D), jnp.float32)
    common = jax.random.normal(k_common, (D,), jnp.float32)
    amplitude = jnp.arange(IMAGES).astype(jnp.float32) / max(IMAGES - 1, 1)
    return (base + amplitude[:, None, None] * common[None, None, :]).astype(jnp.bfloat16)


def levels(stream_key, extent, cuts, smallest, largest):
    factor_of = 1.0
    for axis_at, parts in cuts:
        steps = jax.random.uniform(jax.random.fold_in(jax.random.fold_in(stream_key, 6), axis_at), (parts,), jnp.float32, smallest / len(cuts), largest / len(cuts))
        factor_of = factor_of * jnp.repeat(jnp.exp(steps), extent[axis_at] // parts).reshape((-1,) + (1,) * (len(extent) - 1 - axis_at))
    return factor_of


def normal_values(rng, shape, deviation, limit, cuts=(), held_as=jnp.bfloat16):
    values = deviation * jax.random.normal(rng, shape, jnp.float32)
    if cuts:
        values = values * levels(rng, shape, cuts, -0.22, 0.18)
    return jnp.clip(values, -limit, limit).astype(held_as)


def setup_inputs(seed: int = 0) -> dict:
    key_of = jax.random.split(jax.random.key(seed), 12)
    tokens = draw_tokens(jax.random.fold_in(key_of[11], 71), 0)
    cotangent = normal_values(key_of[1], (IMAGES, SEQ, D), 1.0, 6.0, ((0, 8),))
    expert_ids = draw_expert_ids(jax.random.fold_in(key_of[11], 71), 0)
    slot_rank = draw_slot_rank(jax.random.fold_in(key_of[11], 71), 0)
    qkv_weight = normal_values(key_of[4], (3, D, D), (D // 2) ** -0.5, 0.3125, ((2, 4),))
    out_weight = normal_values(key_of[5], (D, D), (D // 8) ** -0.5, 0.625, ((0, 4),))
    router_weight = normal_values(key_of[6], (D, EXPERTS), (2 * D) ** -0.5, 0.15625)
    expert_in = normal_values(key_of[7], (EXPERTS, D, FF), D ** -0.5, 0.21875, ((0, 4), (2, 4)))
    expert_out = normal_values(key_of[8], (EXPERTS, FF, D), (0.8 * EXPERTS * FF ** -0.5), 0.875, ((0, 4), (1, 4)))
    gain_attention = jnp.clip(1.0 + 0.15 * jax.random.normal(key_of[9], (D,), jnp.float32), 0.25, 1.75)
    gain_experts = jnp.clip(1.0 + 0.15 * jax.random.normal(key_of[10], (D,), jnp.float32), 0.25, 1.75)
    return {"tokens": tokens, "cotangent": cotangent, "expert_ids": expert_ids, "slot_rank": slot_rank, "qkv_weight": qkv_weight, "out_weight": out_weight, "router_weight": router_weight, "expert_in": expert_in, "expert_out": expert_out, "gain_attention": gain_attention, "gain_experts": gain_experts}


@jax.custom_vjp
def low(v):
    return lax.optimization_barrier(v.astype(jnp.bfloat16)).astype(jnp.float32)

@jax.custom_vjp
def low_back(v):
    return v

def low_keep(v):
    return (low(v), None)

def low_pass(kept, grad):
    return (grad,)

def back_keep(v):
    return (v, None)

def back_low(kept, grad):
    return (low(grad),)
low.defvjp(low_keep, low_pass)
low_back.defvjp(back_keep, back_low)
highest = lax.Precision.HIGHEST
epsilon = 1e-06

def both_round(value):
    return low(low_back(value))

def layer_norm(values, gain_row):
    center = values - lax.optimization_barrier(jnp.mean(values, axis=-1, keepdims=True))
    return center * lax.rsqrt(lax.optimization_barrier(jnp.mean(center * center, axis=-1, keepdims=True)) + epsilon) * gain_row

def block_forward(weights, block_data):
    qkv_weight, out_weight, router_weight, expert_in, expert_out, gain_attention, gain_experts = weights
    inputs, chosen, ranked = block_data
    images = inputs.shape[0]
    token_count = images * SEQ
    entered = low(layer_norm(inputs, gain_attention))
    project = both_round(jnp.einsum('isd,cdf->cisf', entered, qkv_weight, precision=highest))
    project = project.reshape(3, images, SEQ, HEADS, HD)
    scores = low_back(jnp.einsum('ishe,ithe->ihst', project[0], project[1], precision=highest) * HD ** (-0.5))
    attn_probs = low(jax.nn.softmax(scores, axis=-1))
    attended = both_round(jnp.einsum('ihst,ithe->ishe', attn_probs, project[2], precision=highest)).reshape(images, SEQ, D)
    residual = inputs + low_back(jnp.einsum('isf,fd->isd', attended, out_weight, precision=highest))
    routed = low(layer_norm(residual, gain_experts)).reshape(token_count, D)
    logits = low_back(jnp.dot(routed, router_weight, precision=highest))
    route_prob = jax.nn.softmax(logits, axis=-1)
    chosen = chosen.reshape(token_count, 2)
    ranked = ranked.reshape(token_count, 2)
    slot_total = EXPERTS * CAP
    position = jnp.where(ranked >= 0, chosen * CAP + ranked, slot_total).reshape(-1)
    buffer = jnp.zeros((slot_total, D), jnp.float32).at[position].set(jnp.repeat(routed, 2, axis=0), mode='drop')
    dispatched = low_back(buffer.reshape(EXPERTS, CAP, D))
    before = low_back(jnp.einsum('ecd,edf->ecf', dispatched, expert_in, precision=highest))
    hidden = low(jax.nn.gelu(before, approximate=False))
    produced = both_round(jnp.einsum('ecf,efd->ecd', hidden, expert_out, precision=highest)).reshape(slot_total, D)
    picked = produced[jnp.minimum(position, slot_total - 1)].reshape(token_count, 2, D)
    gate_values = jnp.take_along_axis(route_prob, chosen, axis=1) * (ranked >= 0).astype(jnp.float32)
    combined = lax.optimization_barrier(jnp.sum(gate_values[:, :, None] * picked, axis=1))
    return (residual + combined.reshape(images, SEQ, D), lax.optimization_barrier(jnp.sum(route_prob, axis=0)))

def reference(tokens, cotangent, expert_ids, slot_rank, qkv_weight, out_weight, router_weight, expert_in, expert_out, gain_attention, gain_experts):
    blocks = IMAGES // IMG_DEV
    weights = tuple((weight.astype(jnp.float32) for weight in (qkv_weight, out_weight, router_weight, expert_in, expert_out, gain_attention, gain_experts)))
    inputs = tokens.astype(jnp.float32).reshape(blocks, IMG_DEV, SEQ, D)
    chosen = expert_ids.reshape(blocks, IMG_DEV, SEQ, 2)
    ranked = slot_rank.reshape(blocks, IMG_DEV, SEQ, 2)
    checked = jax.checkpoint(block_forward)

    def forward(inputs, weights):

        def scan_step(running, block_data):
            output, prob_sum = checked(weights, block_data)
            return (running + prob_sum, output)
        prob_total, outputs = lax.scan(scan_step, jnp.zeros((EXPERTS,), jnp.float32), (inputs, chosen, ranked))
        return (outputs, prob_total)
    outputs, pullback, prob_total = jax.vjp(forward, inputs, weights, has_aux=True)
    grad_inputs, grad_weights = pullback(cotangent.astype(jnp.float32).reshape(blocks, IMG_DEV, SEQ, D))
    counts = lax.optimization_barrier(jnp.sum((expert_ids[..., None] == jnp.arange(EXPERTS)).astype(jnp.float32), axis=(0, 1, 2)))
    token_total = IMAGES * SEQ
    balance_loss = EXPERTS * jnp.sum(counts / (2.0 * token_total) * prob_total / token_total)
    return (outputs.reshape(IMAGES, SEQ, D).astype(jnp.bfloat16), grad_inputs.reshape(IMAGES, SEQ, D), grad_weights[0], grad_weights[1], grad_weights[2], grad_weights[3], grad_weights[4], grad_weights[5], grad_weights[6], balance_loss)
```

```python
import jax
import jax.numpy as jnp
from jax import lax
from jax.sharding import PartitionSpec as P

HD = 64


epsilon = 1e-06


def normalize(values, gain_row):
    center = values - jnp.mean(values, axis=-1, keepdims=True)
    inverse = lax.rsqrt(jnp.mean(center * center, axis=-1, keepdims=True) + epsilon)
    normed = center * inverse
    return (normed, inverse, normed * gain_row)


def normalize_back(upstream, normed, inverse, gain_row):
    scaled = upstream * gain_row
    result = inverse * (
        scaled
        - jnp.mean(scaled, axis=-1, keepdims=True)
        - normed * jnp.mean(scaled * normed, axis=-1, keepdims=True)
    )
    return (result, jnp.sum(upstream * normed, axis=0))


def exact_gelu(values):
    return jax.nn.gelu(values, approximate=False)


def body(
    tokens,
    cotangent,
    expert_ids,
    slot_rank,
    qkv_weight,
    out_weight,
    router_weight,
    expert_in,
    expert_out,
    gain_attention,
    gain_experts,
):
    images, seq_len, model_width = tokens.shape
    token_rows = images * seq_len
    local_width = qkv_weight.shape[2]
    local_heads = local_width // HD
    slice_width = model_width // lax.axis_size("tensor")
    experts = router_weight.shape[1]
    capacity = 5 * token_rows // (2 * experts)
    owners = lax.axis_size("expert")
    per_owner = experts // owners
    slot_total = experts * capacity
    score_scale = HD ** (-0.5)
    inputs = tokens.reshape(token_rows, model_width).astype(jnp.float32)
    normed_one, inverse_one, mixed_one = normalize(inputs, gain_attention)
    entered = mixed_one.astype(jnp.bfloat16)
    project = jnp.einsum(
        "td,cdf->ctf", entered, qkv_weight, preferred_element_type=jnp.float32
    ).astype(jnp.bfloat16)
    projected_heads = project.reshape(3, images, seq_len, local_heads, HD)
    queries, key_rows, value_rows = (projected_heads[0], projected_heads[1], projected_heads[2])
    scores = (
        jnp.einsum("ishe,ithe->ihst", queries, key_rows, preferred_element_type=jnp.float32)
        * score_scale
    )
    log_total = jax.nn.logsumexp(scores, axis=-1, keepdims=True)
    attn_probs = jnp.exp(scores - log_total).astype(jnp.bfloat16)
    attended = jnp.einsum(
        "ihst,ithe->ishe", attn_probs, value_rows, preferred_element_type=jnp.float32
    )
    attended = attended.astype(jnp.bfloat16).reshape(token_rows, local_width)
    attn_part = jnp.dot(attended, out_weight, preferred_element_type=jnp.float32)
    residual = inputs + lax.psum(attn_part, "tensor")
    normed_two, inverse_two, mixed_two = normalize(residual, gain_experts)
    routed = mixed_two.astype(jnp.bfloat16)
    route_prob = jax.nn.softmax(
        jnp.dot(routed, router_weight, preferred_element_type=jnp.float32), axis=-1
    )
    chosen = expert_ids.reshape(token_rows, 2)
    ranked = slot_rank.reshape(token_rows, 2)
    kept_mask = (ranked >= 0).astype(jnp.float32)
    position = jnp.where(ranked >= 0, chosen * capacity + ranked, slot_total).reshape(-1)
    send_rows = (
        jnp.zeros((slot_total, model_width), jnp.bfloat16)
        .at[position]
        .set(jnp.repeat(routed, 2, axis=0), mode="drop")
        .reshape(experts, capacity, model_width)
    )
    fragment = lax.all_to_all(send_rows, "expert", split_axis=0, concat_axis=0, tiled=True)
    grouped = fragment.reshape(owners, per_owner, fragment.shape[1], model_width)
    before = jnp.einsum("sjcd,jdf->sjcf", grouped, expert_in, preferred_element_type=jnp.float32)
    hidden = exact_gelu(before).astype(jnp.bfloat16)
    expert_part = jnp.einsum(
        "sjcf,jfd->sjcd", hidden, expert_out, preferred_element_type=jnp.float32
    )
    produced = lax.psum_scatter(expert_part, "tensor", scatter_dimension=3, tiled=True).astype(
        jnp.bfloat16
    )
    returned = lax.all_to_all(
        produced.reshape(experts, capacity, slice_width),
        "expert",
        split_axis=0,
        concat_axis=0,
        tiled=True,
    )
    returned = lax.all_gather(returned, "tensor", axis=2, tiled=True).reshape(
        slot_total, model_width
    )
    safe_index = jnp.minimum(position, slot_total - 1)
    picked = returned[safe_index].reshape(token_rows, 2, model_width).astype(jnp.float32)
    gate_values = jnp.take_along_axis(route_prob, chosen, axis=1) * kept_mask
    output = residual + jnp.sum(gate_values[:, :, None] * picked, axis=1)
    block_out = output.astype(jnp.bfloat16).reshape(images, seq_len, model_width)
    upstream = cotangent.reshape(token_rows, model_width).astype(jnp.float32)
    gate_grad = jnp.sum(upstream[:, None, :] * picked, axis=-1) * kept_mask
    member = (chosen[:, :, None] == jnp.arange(experts)[None, None, :]).astype(jnp.float32)
    route_grad = jnp.sum(member * gate_grad[:, :, None], axis=1)
    logit_grad = (
        route_prob * (route_grad - jnp.sum(route_grad * route_prob, axis=-1, keepdims=True))
    ).astype(jnp.bfloat16)
    row_grad = (
        (gate_values[:, :, None] * upstream[:, None, :])
        .astype(jnp.bfloat16)
        .reshape(2 * token_rows, model_width)
    )
    grad_send = (
        jnp.zeros((slot_total, model_width), jnp.bfloat16)
        .at[position]
        .set(row_grad, mode="drop")
        .reshape(experts, capacity, model_width)
    )
    grad_arrived = lax.all_to_all(grad_send, "expert", split_axis=0, concat_axis=0, tiled=True)
    grad_arrived = grad_arrived.reshape(owners, per_owner, capacity, model_width)
    hidden_grad = jnp.einsum(
        "sjcd,jfd->sjcf", grad_arrived, expert_out, preferred_element_type=jnp.float32
    )
    grad_expert_out = jnp.einsum(
        "sjcf,sjcd->jfd", hidden, grad_arrived, preferred_element_type=jnp.float32
    )
    pre_grad = jax.vjp(exact_gelu, before)[1](hidden_grad)[0].astype(jnp.bfloat16)
    grad_expert_in = jnp.einsum(
        "sjcd,sjcf->jdf", grouped, pre_grad, preferred_element_type=jnp.float32
    )
    buffer_part = jnp.einsum(
        "sjcf,jdf->sjcd", pre_grad, expert_in, preferred_element_type=jnp.float32
    )
    buffer_share = lax.psum_scatter(buffer_part, "tensor", scatter_dimension=3, tiled=True).astype(
        jnp.bfloat16
    )
    buffer_back = lax.all_to_all(
        buffer_share.reshape(experts, capacity, slice_width),
        "expert",
        split_axis=0,
        concat_axis=0,
        tiled=True,
    )
    buffer_grad = lax.all_gather(buffer_back, "tensor", axis=2, tiled=True).reshape(
        slot_total, model_width
    )
    routed_grad = jnp.sum(
        buffer_grad[safe_index].reshape(token_rows, 2, model_width).astype(jnp.float32)
        * kept_mask[:, :, None],
        axis=1,
    )
    routed_grad = routed_grad + jnp.dot(
        logit_grad, router_weight.T, preferred_element_type=jnp.float32
    )
    grad_router = jnp.einsum("td,te->de", routed, logit_grad, preferred_element_type=jnp.float32)
    from_norm_two, grad_gain_experts = normalize_back(
        routed_grad, normed_two, inverse_two, gain_experts
    )
    residual_grad = upstream + from_norm_two
    attn_grad = residual_grad.astype(jnp.bfloat16)
    grad_out = jnp.einsum("tf,td->fd", attended, attn_grad, preferred_element_type=jnp.float32)
    heads_grad = jnp.dot(attn_grad, out_weight.T, preferred_element_type=jnp.float32).astype(
        jnp.bfloat16
    )
    heads_grad = heads_grad.reshape(images, seq_len, local_heads, HD)
    again = (
        jnp.einsum("ishe,ithe->ihst", queries, key_rows, preferred_element_type=jnp.float32)
        * score_scale
    )
    probs_full = jnp.exp(again - log_total)
    prob_grad = jnp.einsum(
        "ishe,ithe->ihst", heads_grad, value_rows, preferred_element_type=jnp.float32
    )
    value_grad = jnp.einsum(
        "ihst,ishe->ithe",
        probs_full.astype(jnp.bfloat16),
        heads_grad,
        preferred_element_type=jnp.float32,
    )
    score_grad = (
        probs_full * (prob_grad - jnp.sum(prob_grad * probs_full, axis=-1, keepdims=True))
    ).astype(jnp.bfloat16)
    query_grad = (
        jnp.einsum("ihst,ithe->ishe", score_grad, key_rows, preferred_element_type=jnp.float32)
        * score_scale
    )
    key_grad = (
        jnp.einsum("ihst,ishe->ithe", score_grad, queries, preferred_element_type=jnp.float32)
        * score_scale
    )
    project_grad = (
        jnp.stack([query_grad, key_grad, value_grad])
        .astype(jnp.bfloat16)
        .reshape(3, token_rows, local_width)
    )
    grad_qkv = jnp.einsum("td,ctf->cdf", entered, project_grad, preferred_element_type=jnp.float32)
    entered_part = jnp.einsum(
        "ctf,cdf->td", project_grad, qkv_weight, preferred_element_type=jnp.float32
    )
    entered_grad = lax.psum(entered_part.astype(jnp.bfloat16), "tensor").astype(jnp.float32)
    from_norm_one, grad_gain_attention = normalize_back(
        entered_grad, normed_one, inverse_one, gain_attention
    )
    grad_tokens = (residual_grad + from_norm_one).reshape(images, seq_len, model_width)
    counts = jnp.sum(member, axis=(0, 1))
    prob_sum = jnp.sum(route_prob, axis=0)
    grad_qkv, grad_out, grad_router, grad_gain_attention, grad_gain_experts, counts, prob_sum = (
        lax.psum(
            (
                grad_qkv,
                grad_out,
                grad_router,
                grad_gain_attention,
                grad_gain_experts,
                counts,
                prob_sum,
            ),
            ("dp", "expert"),
        )
    )
    grad_expert_in, grad_expert_out = (
        lax.psum(grad_expert_in.astype(jnp.bfloat16), "dp").astype(jnp.float32),
        lax.psum(grad_expert_out.astype(jnp.bfloat16), "dp").astype(jnp.float32),
    )
    token_total = token_rows * lax.axis_size("dp") * lax.axis_size("expert")
    balance_loss = experts * jnp.sum(counts / (2.0 * token_total) * prob_sum / token_total)
    return (
        block_out,
        grad_tokens,
        grad_qkv,
        grad_out,
        grad_router,
        grad_expert_in,
        grad_expert_out,
        grad_gain_attention,
        grad_gain_experts,
        balance_loss,
    )


def round_up(value, step):
    return -(-value // step) * step


def swap_core(value):
    return lax.ppermute(value, "dp", [(0, 1), (1, 0)])


def ring(value, shift):
    size = lax.axis_size("expert")
    return lax.ppermute(value, "expert", [(i, (i + shift) % size) for i in range(size)])


def cross(value, bit):
    size = lax.axis_size("tensor")
    return lax.ppermute(value, "tensor", [(i, i ^ bit) for i in range(size)])


def rows_at(value, start, count):
    return lax.dynamic_slice_in_dim(value, start, count, axis=0)


def dense_body(
    tokens,
    cotangent,
    expert_ids,
    slot_rank,
    qkv_weight,
    out_weight,
    router_weight,
    expert_in,
    expert_out,
    gain_attention,
    gain_experts,
):
    f32, b16 = jnp.float32, jnp.bfloat16
    images, seq_len, width = tokens.shape
    token_rows = images * seq_len
    local_width = qkv_weight.shape[2]
    local_heads = local_width // HD
    experts = router_weight.shape[1]
    owners = lax.axis_size("expert")
    tensors = lax.axis_size("tensor")
    cores = lax.axis_size("dp")
    chunk = round_up(-(-token_rows // tensors), 16)
    padded = chunk * tensors
    half = expert_in.shape[2] // cores
    my_core, my_owner, my_tensor = (
        lax.axis_index("dp"),
        lax.axis_index("expert"),
        lax.axis_index("tensor"),
    )
    score_scale = HD ** (-0.5)

    def flat(value):
        value = value.reshape(token_rows, value.shape[-1])
        return jnp.pad(value, ((0, padded - token_rows), (0, 0)))

    in_half = lax.dynamic_slice_in_dim(expert_in[0], my_core * half, half, axis=1)
    out_half = lax.dynamic_slice_in_dim(expert_out[0], my_core * half, half, axis=0)
    in_all = jnp.concatenate(
        [in_half] + [cross(in_half, j) for j in range(1, tensors)], axis=1
    )
    out_all = jnp.concatenate(
        [out_half] + [cross(out_half, j) for j in range(1, tensors)], axis=0
    )
    wo_all = lax.all_gather(out_weight, "tensor", axis=0, tiled=True)

    chosen = jnp.pad(
        expert_ids.reshape(token_rows, 2), ((0, padded - token_rows), (0, 0)), constant_values=-1
    )
    ranked = jnp.pad(
        slot_rank.reshape(token_rows, 2), ((0, padded - token_rows), (0, 0)), constant_values=-1
    )
    member = (chosen[:, :, None] == jnp.arange(experts)[None, None, :]).astype(f32)
    kept = jnp.sum(member * (ranked >= 0).astype(f32)[:, :, None], axis=1)
    upstream = flat(cotangent)
    payload = jnp.concatenate(
        [upstream, jnp.pad(kept.astype(b16), ((0, 0), (0, 128 - experts)))], axis=1
    )
    payload = rows_at(payload, my_tensor * chunk, chunk)
    my_kept = rows_at(kept, my_tensor * chunk, chunk)
    my_upstream = payload[:, :width].astype(f32)

    def to_owners(value):
        own = jnp.stack([value] + [ring(value, k) for k in range(1, owners)])
        return jnp.stack([own, swap_core(own)])

    payload_all = to_owners(payload)

    inputs = tokens.reshape(token_rows, width).astype(f32)
    normed_one, inverse_one, mixed_one = normalize(inputs, gain_attention)
    entered = mixed_one.astype(b16)
    project = jnp.einsum("td,cdf->ctf", entered, qkv_weight, preferred_element_type=f32).astype(b16)
    heads = project.reshape(3, images, seq_len, local_heads, HD)
    queries, keys, values = heads[0], heads[1], heads[2]
    scores = (
        jnp.einsum("ishe,ithe->ihst", queries, keys, preferred_element_type=f32) * score_scale
    )
    log_total = jax.nn.logsumexp(scores, axis=-1, keepdims=True)
    probs_full = jnp.exp(scores - log_total)
    attn_probs = probs_full.astype(b16)
    attended = jnp.einsum("ihst,ithe->ishe", attn_probs, values, preferred_element_type=f32)
    attended = flat(attended.astype(b16).reshape(token_rows, local_width))
    gathered = lax.all_to_all(
        attended.reshape(tensors, chunk, local_width), "tensor", 0, 0, tiled=True
    )
    my_inputs = rows_at(flat(tokens), my_tensor * chunk, chunk).astype(f32)
    residual = my_inputs + jnp.einsum(
        "htf,hfd->td",
        gathered,
        wo_all.reshape(tensors, local_width, width),
        preferred_element_type=f32,
    )
    normed_two, inverse_two, mixed_two = normalize(residual, gain_experts)
    routed = mixed_two.astype(b16)
    route_prob = jax.nn.softmax(
        jnp.dot(routed, router_weight, preferred_element_type=f32), axis=-1
    )

    rows = to_owners(routed).reshape(-1, width)
    payload_rows = payload_all.reshape(-1, payload.shape[1])
    mine = (jnp.arange(experts) == my_owner).astype(f32)
    prob = jax.nn.softmax(jnp.dot(rows, router_weight, preferred_element_type=f32), axis=-1)
    keep = jnp.sum(payload_rows[:, width : width + experts].astype(f32) * mine, -1, keepdims=True)
    gate = jnp.sum(prob * mine, axis=-1, keepdims=True) * keep
    dy_rows = payload_rows[:, :width].astype(f32)
    before = jnp.dot(rows, in_all, preferred_element_type=f32)
    hidden = exact_gelu(before).astype(b16)
    part = jnp.dot(hidden, out_all, preferred_element_type=f32)
    gate_grad = jnp.sum(part * dy_rows, axis=-1, keepdims=True) * keep
    row_grad = (gate * dy_rows).astype(b16)
    hidden_grad = jnp.einsum("td,fd->tf", row_grad, out_all, preferred_element_type=f32)
    pre_grad = jax.vjp(exact_gelu, before)[1](hidden_grad)[0].astype(b16)
    buffer_part = jnp.einsum("tf,df->td", pre_grad, in_all, preferred_element_type=f32)
    grad_in_part = jnp.einsum("td,tf->df", rows, pre_grad, preferred_element_type=f32).astype(b16)
    grad_out_part = jnp.einsum("tf,td->fd", hidden, row_grad, preferred_element_type=f32).astype(
        b16
    )

    def from_owners(value):
        value = value.reshape(2, owners, chunk, value.shape[-1])
        both = (value[0] + swap_core(value[1])).astype(b16)
        return [both[0]] + [ring(both[k], -k) for k in range(1, owners)]

    wide = jnp.concatenate([buffer_part, jnp.pad(gate_grad, ((0, 0), (0, 127)))], axis=1)
    wide = wide.reshape(2, owners, chunk, width + 128)
    wide = wide[0] + swap_core(wide[1])
    upper = wide[..., width:].astype(b16)
    lower = (wide[..., width:] - upper.astype(f32)).astype(b16)
    wide = jnp.concatenate([wide[..., :width].astype(b16), upper, lower], axis=-1)
    back = [wide[0]] + [ring(wide[k], -k) for k in range(1, owners)]
    place = [(my_owner + k) % owners for k in range(owners)]
    route_grad = sum(
        (b[:, width : width + 1].astype(f32) + b[:, width + 128 : width + 129].astype(f32))
        * (jnp.arange(experts) == p).astype(f32)
        for b, p in zip(back, place)
    )
    routed_grad = sum(b[:, :width].astype(f32) for b in back)

    combined = sum(b.astype(f32) for b in from_owners(part * gate))
    block_chunk = (residual + combined).astype(b16)
    block_out = lax.all_gather(block_chunk, "tensor", axis=0, tiled=True)[:token_rows]

    logit_grad = (
        route_prob * (route_grad - jnp.sum(route_grad * route_prob, axis=-1, keepdims=True))
    ).astype(b16)
    routed_grad = routed_grad + jnp.dot(logit_grad, router_weight.T, preferred_element_type=f32)
    grad_router = jnp.einsum("td,te->ed", routed, logit_grad, preferred_element_type=f32)
    from_norm_two, grad_gain_experts = normalize_back(
        routed_grad, normed_two, inverse_two, gain_experts
    )
    residual_grad = my_upstream + from_norm_two
    attn_grad = lax.all_gather(residual_grad.astype(b16), "tensor", axis=0, tiled=True)

    grad_out = jnp.einsum("tf,td->fd", attended, attn_grad, preferred_element_type=f32)
    heads_grad = jnp.einsum("td,fd->tf", attn_grad[:token_rows], out_weight, preferred_element_type=f32)
    heads_grad = heads_grad.astype(b16).reshape(images, seq_len, local_heads, HD)
    prob_grad = jnp.einsum("ishe,ithe->ihst", heads_grad, values, preferred_element_type=f32)
    value_grad = jnp.einsum("ihst,ishe->ithe", attn_probs, heads_grad, preferred_element_type=f32)
    score_grad = (
        probs_full * (prob_grad - jnp.sum(prob_grad * probs_full, axis=-1, keepdims=True))
    ).astype(b16)
    query_grad = (
        jnp.einsum("ihst,ithe->ishe", score_grad, keys, preferred_element_type=f32) * score_scale
    )
    key_grad = (
        jnp.einsum("ihst,ishe->ithe", score_grad, queries, preferred_element_type=f32)
        * score_scale
    )
    project_grad = (
        jnp.stack([query_grad, key_grad, value_grad]).astype(b16).reshape(3, token_rows, local_width)
    )
    grad_qkv = jnp.einsum("td,ctf->cfd", entered, project_grad, preferred_element_type=f32)
    entered_part = jnp.einsum("ctf,cdf->td", project_grad, qkv_weight, preferred_element_type=f32)
    grad_gain_attention = jnp.sum(entered_part * normed_one, axis=0)
    arrived = lax.all_to_all(
        flat(entered_part).astype(b16).reshape(tensors, chunk, width), "tensor", 0, 0, tiled=True
    )
    entered_grad = jnp.sum(arrived.astype(f32), axis=0)
    my_normed, my_inverse, _ = normalize(my_inputs, gain_attention)
    from_norm_one, _ = normalize_back(entered_grad, my_normed, my_inverse, gain_attention)
    grad_chunk = (residual_grad + from_norm_one).astype(b16)
    grad_tokens = lax.all_gather(grad_chunk, "tensor", axis=0, tiled=True)[:token_rows].astype(f32)

    def in_order(parts, index, size):
        stacked = jnp.zeros((size,) + parts[0].shape, parts[0].dtype)
        for i, part_value in zip(index, parts):
            stacked = lax.dynamic_update_index_in_dim(stacked, part_value, i, 0)
        return stacked

    small = jnp.concatenate(
        [
            grad_router,
            grad_gain_attention[None],
            grad_gain_experts[None],
            jnp.pad(jnp.sum(route_prob * (my_tensor * chunk + jnp.arange(chunk) < token_rows)[:, None], axis=0), (0, width - experts))[None],
            jnp.pad(
                jnp.sum(rows_at(member, my_tensor * chunk, chunk), axis=(0, 1)),
                (0, width - experts),
            )[None],
        ]
    )
    small = small + swap_core(small)
    small = jnp.sum(
        in_order(
            [small] + [ring(small, k) for k in range(1, owners)],
            [(my_owner - k) % owners for k in range(owners)],
            owners,
        ),
        axis=0,
    )
    small = jnp.sum(
        in_order(
            [small] + [cross(small, j) for j in range(1, tensors)],
            [my_tensor ^ j for j in range(tensors)],
            tensors,
        ),
        axis=0,
    )
    grad_router = small[:experts].T
    token_total = token_rows * cores * owners
    balance_loss = experts * jnp.sum(
        small[experts + 3, :experts]
        / (2.0 * token_total)
        * small[experts + 2, :experts]
        / token_total
    )

    big = jnp.concatenate([grad_qkv.reshape(-1, width), grad_out])
    span = big.shape[0] // cores
    piece = span // owners
    kept_part = rows_at(big, my_core * span, span)
    sent_part = rows_at(big, (1 - my_core) * span, span)
    shared = kept_part + swap_core(sent_part)
    shared16 = shared.astype(b16)
    gathered_parts = [
        ring(rows_at(shared16, ((my_owner + k) % owners) * piece, piece), k).astype(f32)
        for k in range(1, owners)
    ]
    summed = rows_at(shared, my_owner * piece, piece) + sum(gathered_parts)
    summed = summed.astype(b16)
    whole = in_order(
        [summed] + [ring(summed, k) for k in range(1, owners)],
        [(my_owner - k) % owners for k in range(owners)],
        owners,
    ).reshape(span, width)
    other = swap_core(whole)
    big = in_order([whole, other], [my_core, 1 - my_core], 2).reshape(-1, width).astype(f32)
    grad_qkv = big[: 3 * local_width].reshape(3, local_width, width).transpose(0, 2, 1)
    grad_out = big[3 * local_width :]

    in_parts = grad_in_part.reshape(width, tensors, half)
    out_parts = grad_out_part.reshape(tensors, half, width)
    grad_in_half = in_parts[:, 0].astype(f32) + sum(
        cross(in_parts[:, j], j).astype(f32) for j in range(1, tensors)
    )
    grad_out_half = out_parts[0].astype(f32) + sum(
        cross(out_parts[j], j).astype(f32) for j in range(1, tensors)
    )
    grad_in_half, grad_out_half = grad_in_half.astype(b16), grad_out_half.astype(b16)
    order = [my_core, 1 - my_core]
    grad_expert_in = in_order([grad_in_half, swap_core(grad_in_half)], order, 2)
    grad_expert_in = grad_expert_in.transpose(1, 0, 2).reshape(1, width, -1).astype(f32)
    grad_expert_out = in_order([grad_out_half, swap_core(grad_out_half)], order, 2)
    grad_expert_out = grad_expert_out.reshape(1, -1, width).astype(f32)
    return (
        block_out.reshape(images, seq_len, width),
        grad_tokens.reshape(images, seq_len, width),
        grad_qkv,
        grad_out,
        grad_router,
        grad_expert_in,
        grad_expert_out,
        small[experts],
        small[experts + 1],
        balance_loss,
    )


def solution(mesh):
    placed = (
        P(("dp", "expert"), None, None),
        P(("dp", "expert"), None, None),
        P(("dp", "expert"), None, None),
        P(("dp", "expert"), None, None),
        P(None, None, "tensor"),
        P("tensor", None),
        P(),
        P("expert", None, "tensor"),
        P("expert", "tensor", None),
        P(),
        P(),
    )
    shape = mesh.shape
    dense = shape["dp"] == 2 and shape["expert"] == 4 and shape["tensor"] == 4
    return jax.shard_map(
        dense_body if dense else body,
        mesh=mesh,
        in_specs=placed,
        out_specs=(
            P(("dp", "expert"), None, None),
            P(("dp", "expert"), None, None),
            P(None, None, "tensor"),
            P("tensor", None),
            P(),
            P("expert", None, "tensor"),
            P("expert", "tensor", None),
            P(),
            P(),
            P(),
        ),
        check_vma=False,
    )
```

```python
import functools
import math

import jax
import jax.numpy as jnp
from jax import lax
from jax.experimental import pallas as pl
from jax.experimental.pallas import tpu as pltpu
from jax.sharding import PartitionSpec as P

HD = 64


epsilon = 1e-06


def normalize(values, gain_row):
    center = values - jnp.mean(values, axis=-1, keepdims=True)
    inverse = lax.rsqrt(jnp.mean(center * center, axis=-1, keepdims=True) + epsilon)
    normed = center * inverse
    return (normed, inverse, normed * gain_row)


def normalize_back(upstream, normed, inverse, gain_row):
    scaled = upstream * gain_row
    result = inverse * (
        scaled
        - jnp.mean(scaled, axis=-1, keepdims=True)
        - normed * jnp.mean(scaled * normed, axis=-1, keepdims=True)
    )
    return (result, jnp.sum(upstream * normed, axis=0))


def exact_gelu(values):
    return jax.nn.gelu(values, approximate=False)


def body(
    tokens,
    cotangent,
    expert_ids,
    slot_rank,
    qkv_weight,
    out_weight,
    router_weight,
    expert_in,
    expert_out,
    gain_attention,
    gain_experts,
):
    images, seq_len, model_width = tokens.shape
    token_rows = images * seq_len
    local_width = qkv_weight.shape[2]
    local_heads = local_width // HD
    slice_width = model_width // lax.axis_size("tensor")
    experts = router_weight.shape[1]
    capacity = 5 * token_rows // (2 * experts)
    owners = lax.axis_size("expert")
    per_owner = experts // owners
    slot_total = experts * capacity
    score_scale = HD ** (-0.5)
    inputs = tokens.reshape(token_rows, model_width).astype(jnp.float32)
    normed_one, inverse_one, mixed_one = normalize(inputs, gain_attention)
    entered = mixed_one.astype(jnp.bfloat16)
    project = jnp.einsum(
        "td,cdf->ctf", entered, qkv_weight, preferred_element_type=jnp.float32
    ).astype(jnp.bfloat16)
    projected_heads = project.reshape(3, images, seq_len, local_heads, HD)
    queries, key_rows, value_rows = (projected_heads[0], projected_heads[1], projected_heads[2])
    scores = (
        jnp.einsum("ishe,ithe->ihst", queries, key_rows, preferred_element_type=jnp.float32)
        * score_scale
    )
    log_total = jax.nn.logsumexp(scores, axis=-1, keepdims=True)
    attn_probs = jnp.exp(scores - log_total).astype(jnp.bfloat16)
    attended = jnp.einsum(
        "ihst,ithe->ishe", attn_probs, value_rows, preferred_element_type=jnp.float32
    )
    attended = attended.astype(jnp.bfloat16).reshape(token_rows, local_width)
    attn_part = jnp.dot(attended, out_weight, preferred_element_type=jnp.float32)
    residual = inputs + lax.psum(attn_part, "tensor")
    normed_two, inverse_two, mixed_two = normalize(residual, gain_experts)
    routed = mixed_two.astype(jnp.bfloat16)
    route_prob = jax.nn.softmax(
        jnp.dot(routed, router_weight, preferred_element_type=jnp.float32), axis=-1
    )
    chosen = expert_ids.reshape(token_rows, 2)
    ranked = slot_rank.reshape(token_rows, 2)
    kept_mask = (ranked >= 0).astype(jnp.float32)
    position = jnp.where(ranked >= 0, chosen * capacity + ranked, slot_total).reshape(-1)
    send_rows = (
        jnp.zeros((slot_total, model_width), jnp.bfloat16)
        .at[position]
        .set(jnp.repeat(routed, 2, axis=0), mode="drop")
        .reshape(experts, capacity, model_width)
    )
    fragment = lax.all_to_all(send_rows, "expert", split_axis=0, concat_axis=0, tiled=True)
    grouped = fragment.reshape(owners, per_owner, fragment.shape[1], model_width)
    before = jnp.einsum("sjcd,jdf->sjcf", grouped, expert_in, preferred_element_type=jnp.float32)
    hidden = exact_gelu(before).astype(jnp.bfloat16)
    expert_part = jnp.einsum(
        "sjcf,jfd->sjcd", hidden, expert_out, preferred_element_type=jnp.float32
    )
    produced = lax.psum_scatter(expert_part, "tensor", scatter_dimension=3, tiled=True).astype(
        jnp.bfloat16
    )
    returned = lax.all_to_all(
        produced.reshape(experts, capacity, slice_width),
        "expert",
        split_axis=0,
        concat_axis=0,
        tiled=True,
    )
    returned = lax.all_gather(returned, "tensor", axis=2, tiled=True).reshape(
        slot_total, model_width
    )
    safe_index = jnp.minimum(position, slot_total - 1)
    picked = returned[safe_index].reshape(token_rows, 2, model_width).astype(jnp.float32)
    gate_values = jnp.take_along_axis(route_prob, chosen, axis=1) * kept_mask
    output = residual + jnp.sum(gate_values[:, :, None] * picked, axis=1)
    block_out = output.astype(jnp.bfloat16).reshape(images, seq_len, model_width)
    upstream = cotangent.reshape(token_rows, model_width).astype(jnp.float32)
    gate_grad = jnp.sum(upstream[:, None, :] * picked, axis=-1) * kept_mask
    member = (chosen[:, :, None] == jnp.arange(experts)[None, None, :]).astype(jnp.float32)
    route_grad = jnp.sum(member * gate_grad[:, :, None], axis=1)
    logit_grad = (
        route_prob * (route_grad - jnp.sum(route_grad * route_prob, axis=-1, keepdims=True))
    ).astype(jnp.bfloat16)
    row_grad = (
        (gate_values[:, :, None] * upstream[:, None, :])
        .astype(jnp.bfloat16)
        .reshape(2 * token_rows, model_width)
    )
    grad_send = (
        jnp.zeros((slot_total, model_width), jnp.bfloat16)
        .at[position]
        .set(row_grad, mode="drop")
        .reshape(experts, capacity, model_width)
    )
    grad_arrived = lax.all_to_all(grad_send, "expert", split_axis=0, concat_axis=0, tiled=True)
    grad_arrived = grad_arrived.reshape(owners, per_owner, capacity, model_width)
    hidden_grad = jnp.einsum(
        "sjcd,jfd->sjcf", grad_arrived, expert_out, preferred_element_type=jnp.float32
    )
    grad_expert_out = jnp.einsum(
        "sjcf,sjcd->jfd", hidden, grad_arrived, preferred_element_type=jnp.float32
    )
    pre_grad = jax.vjp(exact_gelu, before)[1](hidden_grad)[0].astype(jnp.bfloat16)
    grad_expert_in = jnp.einsum(
        "sjcd,sjcf->jdf", grouped, pre_grad, preferred_element_type=jnp.float32
    )
    buffer_part = jnp.einsum(
        "sjcf,jdf->sjcd", pre_grad, expert_in, preferred_element_type=jnp.float32
    )
    buffer_share = lax.psum_scatter(buffer_part, "tensor", scatter_dimension=3, tiled=True).astype(
        jnp.bfloat16
    )
    buffer_back = lax.all_to_all(
        buffer_share.reshape(experts, capacity, slice_width),
        "expert",
        split_axis=0,
        concat_axis=0,
        tiled=True,
    )
    buffer_grad = lax.all_gather(buffer_back, "tensor", axis=2, tiled=True).reshape(
        slot_total, model_width
    )
    routed_grad = jnp.sum(
        buffer_grad[safe_index].reshape(token_rows, 2, model_width).astype(jnp.float32)
        * kept_mask[:, :, None],
        axis=1,
    )
    routed_grad = routed_grad + jnp.dot(
        logit_grad, router_weight.T, preferred_element_type=jnp.float32
    )
    grad_router = jnp.einsum("td,te->de", routed, logit_grad, preferred_element_type=jnp.float32)
    from_norm_two, grad_gain_experts = normalize_back(
        routed_grad, normed_two, inverse_two, gain_experts
    )
    residual_grad = upstream + from_norm_two
    attn_grad = residual_grad.astype(jnp.bfloat16)
    grad_out = jnp.einsum("tf,td->fd", attended, attn_grad, preferred_element_type=jnp.float32)
    heads_grad = jnp.dot(attn_grad, out_weight.T, preferred_element_type=jnp.float32).astype(
        jnp.bfloat16
    )
    heads_grad = heads_grad.reshape(images, seq_len, local_heads, HD)
    again = (
        jnp.einsum("ishe,ithe->ihst", queries, key_rows, preferred_element_type=jnp.float32)
        * score_scale
    )
    probs_full = jnp.exp(again - log_total)
    prob_grad = jnp.einsum(
        "ishe,ithe->ihst", heads_grad, value_rows, preferred_element_type=jnp.float32
    )
    value_grad = jnp.einsum(
        "ihst,ishe->ithe",
        probs_full.astype(jnp.bfloat16),
        heads_grad,
        preferred_element_type=jnp.float32,
    )
    score_grad = (
        probs_full * (prob_grad - jnp.sum(prob_grad * probs_full, axis=-1, keepdims=True))
    ).astype(jnp.bfloat16)
    query_grad = (
        jnp.einsum("ihst,ithe->ishe", score_grad, key_rows, preferred_element_type=jnp.float32)
        * score_scale
    )
    key_grad = (
        jnp.einsum("ihst,ishe->ithe", score_grad, queries, preferred_element_type=jnp.float32)
        * score_scale
    )
    project_grad = (
        jnp.stack([query_grad, key_grad, value_grad])
        .astype(jnp.bfloat16)
        .reshape(3, token_rows, local_width)
    )
    grad_qkv = jnp.einsum("td,ctf->cdf", entered, project_grad, preferred_element_type=jnp.float32)
    entered_part = jnp.einsum(
        "ctf,cdf->td", project_grad, qkv_weight, preferred_element_type=jnp.float32
    )
    entered_grad = lax.psum(entered_part.astype(jnp.bfloat16), "tensor").astype(jnp.float32)
    from_norm_one, grad_gain_attention = normalize_back(
        entered_grad, normed_one, inverse_one, gain_attention
    )
    grad_tokens = (residual_grad + from_norm_one).reshape(images, seq_len, model_width)
    counts = jnp.sum(member, axis=(0, 1))
    prob_sum = jnp.sum(route_prob, axis=0)
    grad_qkv, grad_out, grad_router, grad_gain_attention, grad_gain_experts, counts, prob_sum = (
        lax.psum(
            (
                grad_qkv,
                grad_out,
                grad_router,
                grad_gain_attention,
                grad_gain_experts,
                counts,
                prob_sum,
            ),
            ("dp", "expert"),
        )
    )
    grad_expert_in, grad_expert_out = (
        lax.psum(grad_expert_in.astype(jnp.bfloat16), "dp").astype(jnp.float32),
        lax.psum(grad_expert_out.astype(jnp.bfloat16), "dp").astype(jnp.float32),
    )
    token_total = token_rows * lax.axis_size("dp") * lax.axis_size("expert")
    balance_loss = experts * jnp.sum(counts / (2.0 * token_total) * prob_sum / token_total)
    return (
        block_out,
        grad_tokens,
        grad_qkv,
        grad_out,
        grad_router,
        grad_expert_in,
        grad_expert_out,
        grad_gain_attention,
        grad_gain_experts,
        balance_loss,
    )


NN = ((1,), (0,))
NT = ((1,), (1,))
TN = ((0,), (0,))
LANES = 128
SMALL = 8
VMEM_BYTES = 56 << 20


def round_up(value, step):
    return -(-value // step) * step


def contract(a, b, dims):
    return lax.dot_general(a, b, (dims, ((), ())), preferred_element_type=jnp.float32)


def fixed(shape):
    return pl.BlockSpec(shape, lambda *_: (0,) * len(shape))


def kernel_call(kernel, name, position, args, outs, scratch=(), blocks=None, grid=(1,), flops=0):
    bytes_moved = sum(a.size * a.dtype.itemsize for a in args)
    bytes_moved += sum(o.size * o.dtype.itemsize for o in outs)
    return pl.pallas_call(
        kernel,
        grid_spec=pltpu.PrefetchScalarGridSpec(
            num_scalar_prefetch=1,
            grid=grid,
            in_specs=[fixed((blocks or {}).get(i, a.shape)) for i, a in enumerate(args)],
            out_specs=[fixed(o.shape) for o in outs],
            scratch_shapes=list(scratch),
        ),
        out_shape=list(outs),
        compiler_params=pltpu.CompilerParams(vmem_limit_bytes=VMEM_BYTES),
        cost_estimate=pl.CostEstimate(flops=flops, bytes_accessed=bytes_moved, transcendentals=0),
        name=name,
    )(position, *args)


def like(shape, dtype):
    return jax.ShapeDtypeStruct(shape, dtype)


def live_rows(shape, limit, offset=0):
    return lax.broadcasted_iota(jnp.int32, shape, 0) + offset < limit


def head_masks(rows, heads):
    lane = lax.broadcasted_iota(jnp.int32, (rows, heads * HD), 1)
    return [(lane >= h * HD) & (lane < (h + 1) * HD) for h in range(heads)]


def keep_lanes(value, mask):
    return jnp.where(mask, value, jnp.zeros_like(value))


def split_high_low(value):
    high = value.astype(jnp.bfloat16)
    return high, (value - high.astype(jnp.float32)).astype(jnp.bfloat16)


def image_rows(ref, i, seq_len):
    values = ref[i].astype(jnp.float32)
    return jnp.where(live_rows(values.shape, seq_len), values, 0.0)


def chunk_kernel(seq_len, pos_ref, tok_ref, cot_ref, kept_ref, x_ref, pay_ref, flat_ref):
    images, rows, width = tok_ref.shape
    chunk = x_ref.shape[0]
    start = pl.multiple_of(pos_ref[2] * chunk, 16)
    for source, target in ((tok_ref, x_ref), (cot_ref, pay_ref)):
        flat_ref[images * seq_len :, :] = jnp.zeros(
            (flat_ref.shape[0] - images * seq_len, width), jnp.float32
        )
        for i in range(images):
            flat_ref[pl.ds(i * seq_len, rows), :] = image_rows(source, i, seq_len)
        target[:, :width] = flat_ref[pl.ds(start, chunk), :].astype(jnp.bfloat16)
    pay_ref[:, width:] = kept_ref[pl.ds(start, chunk), :]


def attention_kernel(
    seq_len, heads, pos_ref, tok_ref, gain_ref, w_ref, wo_ref, qkv_ref, lse_ref, att_ref, part_ref, flat_ref
):
    images, rows, width = qkv_ref.shape[1], qkv_ref.shape[2], heads * HD
    masks = head_masks(rows, heads)
    keys_live = lax.broadcasted_iota(jnp.int32, (rows, rows), 1) < seq_len
    lane = lax.broadcasted_iota(jnp.int32, (rows, LANES), 1)
    flat_ref[images * seq_len :, :] = jnp.zeros(
        (flat_ref.shape[0] - images * seq_len, width), jnp.float32
    )
    for i in range(images):
        entered = normalize(image_rows(tok_ref, i, seq_len), gain_ref[...])[2].astype(jnp.bfloat16)
        q, k, v = (
            contract(entered, w_ref[c * width : (c + 1) * width, :], NT).astype(jnp.bfloat16)
            for c in range(3)
        )
        qkv_ref[0, i], qkv_ref[1, i], qkv_ref[2, i] = q, k, v
        attended = jnp.zeros((rows, width), jnp.float32)
        lse_all = jnp.zeros((rows, LANES), jnp.float32)
        for h in range(heads):
            scores = contract(keep_lanes(q, masks[h]), k, NT) * (HD ** (-0.5))
            scores = jnp.where(keys_live, scores, -1e30)
            top = jnp.max(scores, axis=-1, keepdims=True)
            lse = top + jnp.log(jnp.sum(jnp.exp(scores - top), axis=-1, keepdims=True))
            probs = jnp.exp(scores - lse).astype(jnp.bfloat16)
            attended = attended + contract(probs, keep_lanes(v, masks[h]), NN)
            lse_all = jnp.where(lane == h, lse, lse_all)
        lse_ref[i] = lse_all
        flat_ref[pl.ds(i * seq_len, rows), :] = jnp.where(
            live_rows(attended.shape, seq_len), attended, 0.0
        )
    att = flat_ref[...].astype(jnp.bfloat16)
    att_ref[...] = att
    part_ref[...] = contract(att, wo_ref[...], NN).astype(jnp.bfloat16)


def route_kernel(experts, pos_ref, got_ref, x_ref, gain_ref, router_ref, res_ref, routed_ref, prob_ref):
    residual = x_ref[...].astype(jnp.float32)
    for j in range(got_ref.shape[0]):
        residual = residual + got_ref[j].astype(jnp.float32)
    res_ref[...] = residual
    routed = normalize(residual, gain_ref[...])[2].astype(jnp.bfloat16)
    routed_ref[...] = routed
    prob_ref[...] = route_probs(routed, router_ref[...], experts)


def route_probs(rows, router, experts):
    logits = contract(rows, router, NT)
    lane = lax.broadcasted_iota(jnp.int32, logits.shape, 1)
    logits = jnp.where(lane < experts, logits, -1e30)
    weight = jnp.exp(logits - jnp.max(logits, axis=-1, keepdims=True))
    return weight / jnp.sum(weight, axis=-1, keepdims=True)


def gelu_parts(x):
    square = jnp.exp(-0.5 * x * x)
    t = 1.0 / (1.0 + (0.3275911 * 0.5**0.5) * jnp.abs(x))
    poly = 0.5 * 1.061405429
    for coefficient in (-1.453152027, 1.421413741, -0.284496736, 0.254829592):
        poly = poly * t + 0.5 * coefficient
    tail = poly * t * square
    share = jnp.where(x < 0, tail, 1.0 - tail)
    return x * share, share + x * square * (0.5 / math.pi) ** 0.5


def expert_kernel(experts, owners, *refs):
    pos_ref, *blocks = refs[: 1 + owners]
    pay_ref, router_ref, w0_ref, w1a_ref, w1b_ref, w2_ref, w3_ref = refs[1 + owners : 8 + owners]
    hidden_ref, pre_ref, x_ref, rg_ref, gated_ref, back_ref = refs[8 + owners : 14 + owners]
    w_ref, gate_ref, acc_ref, back_acc = refs[14 + owners :]
    chunk, width = blocks[0].shape
    part_rows = w_ref.shape[1] // 2
    step = pl.program_id(0)

    def load_halves(first, second):
        w_ref[:, :part_rows, :] = first
        w_ref[:, part_rows:, :] = second

    @pl.when(step == 0)
    def _():
        w_ref[...] = w0_ref[...]
        me = pos_ref[1]
        for k in range(owners):
            here = pl.ds(k * chunk, chunk)
            rows = blocks[k][...]
            x_ref[here, :] = rows
            source = pl.ds(pl.multiple_of(lax.rem(me - k + owners, owners) * chunk, 16), chunk)
            prob = route_probs(rows, router_ref[...], experts)
            lane = lax.broadcasted_iota(jnp.int32, prob.shape, 1)
            kept = pay_ref[source, width:].astype(jnp.float32)
            kept = jnp.sum(jnp.where(lane == me, kept, 0.0), axis=-1, keepdims=True)
            gate = jnp.sum(jnp.where(lane == me, prob, 0.0), axis=-1, keepdims=True) * kept
            gate_ref[here, :LANES] = jnp.broadcast_to(gate, (chunk, LANES))
            gate_ref[here, LANES:] = jnp.broadcast_to(kept, (chunk, LANES))
            rg_ref[here, :] = (gate * pay_ref[source, :width].astype(jnp.float32)).astype(
                jnp.bfloat16
            )
        acc_ref[...] = jnp.zeros_like(acc_ref)
        back_acc[...] = jnp.zeros_like(back_acc)

    @pl.when(step == 1)
    def _():
        load_halves(w1a_ref[...], w1b_ref[...])

    @pl.when(step == 2)
    def _():
        load_halves(w2_ref[0], w2_ref[1])

    @pl.when(step == 3)
    def _():
        load_halves(w3_ref[0], w3_ref[1])

    before = contract(x_ref[...], w_ref[0], NT)
    value, slope = gelu_parts(before)
    hidden = value.astype(jnp.bfloat16)
    hidden_ref[...] = hidden
    acc_ref[...] += contract(hidden, w_ref[1], NN)
    pre = (contract(rg_ref[...], w_ref[1], NT) * slope).astype(jnp.bfloat16)
    pre_ref[...] = pre
    back_acc[...] += contract(pre, w_ref[0], NN)

    @pl.when(step == pl.num_programs(0) - 1)
    def _():
        me = pos_ref[1]
        for k in range(owners):
            here = pl.ds(k * chunk, chunk)
            source = pl.ds(pl.multiple_of(lax.rem(me - k + owners, owners) * chunk, 16), chunk)
            part = acc_ref[here, :]
            gated_ref[here, :] = (gate_ref[here, 0:1] * part).astype(jnp.bfloat16)
            back_ref[here, :width] = back_acc[here, :]
            inner = jnp.sum(
                part * pay_ref[source, :width].astype(jnp.float32), axis=-1, keepdims=True
            )
            back_ref[here, width:] = gate_ref[here, LANES:] * inner


def expert_pass(position, blocks, payload, router, weights, experts):
    chunk, width = blocks[0].shape
    owners = len(blocks)
    count, tile = owners * chunk, weights[0].shape[1]
    args = [*blocks, payload, router, *weights]
    outs = [
        like((count, 4 * tile), jnp.bfloat16),
        like((count, 4 * tile), jnp.bfloat16),
        like((count, width), jnp.bfloat16),
        like((count, width), jnp.bfloat16),
        like((count, width), jnp.bfloat16),
        like((count, width + LANES), jnp.float32),
    ]
    column = pl.BlockSpec((count, tile), lambda j, *_: (0, j))
    return pl.pallas_call(
        functools.partial(expert_kernel, experts, owners),
        grid_spec=pltpu.PrefetchScalarGridSpec(
            num_scalar_prefetch=1,
            grid=(4,),
            in_specs=[fixed(a.shape) for a in args],
            out_specs=[column, column] + [fixed(o.shape) for o in outs[2:]],
            scratch_shapes=[
                pltpu.VMEM((2, tile, width), jnp.bfloat16),
                pltpu.VMEM((count, 2 * LANES), jnp.float32),
                pltpu.VMEM((count, width), jnp.float32),
                pltpu.VMEM((count, width), jnp.float32),
            ],
        ),
        out_shape=outs,
        compiler_params=pltpu.CompilerParams(vmem_limit_bytes=VMEM_BYTES),
        cost_estimate=pl.CostEstimate(
            flops=8 * count * width * 4 * tile,
            bytes_accessed=16 * width * tile + 12 * count * width + 16 * count * tile,
            transcendentals=2 * count * 4 * tile,
        ),
        name="experts",
    )(position, *args)


def join_kernel(pos_ref, back_ref, other_ref, gated_ref, gated_other_ref, *outs):
    owners = len(outs) // 2
    chunk, width = outs[owners].shape
    for k in range(owners):
        here = pl.ds(k * chunk, chunk)
        total = back_ref[here, :] + other_ref[here, :]
        outs[k][:, :width] = total[:, :width].astype(jnp.bfloat16)
        outs[k][:, width : width + LANES], outs[k][:, width + LANES :] = split_high_low(
            total[:, width:]
        )
        outs[owners + k][...] = (
            gated_ref[here, :].astype(jnp.float32) + gated_other_ref[here, :].astype(jnp.float32)
        ).astype(jnp.bfloat16)


def expert_grad_kernel(pos_ref, xa, xb, pa, pb, ha, hb, ra, rb, *outs):
    step = pl.program_id(0)
    part_rows = outs[0].shape[2]
    grad_in = contract(pa[...], xa[...], TN) + contract(pb[...], xb[...], TN)
    grad_in = grad_in.astype(jnp.bfloat16)
    grad_out = contract(ha[...], ra[...], TN) + contract(hb[...], rb[...], TN)
    grad_out = grad_out.astype(jnp.bfloat16)
    for j, out in enumerate(outs):

        @pl.when(step == j)
        def _(out=out):
            for s in range(2):
                here = slice(s * part_rows, (s + 1) * part_rows)
                out[s, 0] = grad_in[here]
                out[s, 1] = grad_out[here]


def expert_grads(position, rows, pre, hidden, row_grad):
    count, width = rows[0].shape
    tile = pre[0].shape[1] // 4
    column = pl.BlockSpec((count, tile), lambda j, *_: (0, j))
    outs = [like((2, 2, tile // 2, width), jnp.bfloat16)] * 4
    return pl.pallas_call(
        expert_grad_kernel,
        grid_spec=pltpu.PrefetchScalarGridSpec(
            num_scalar_prefetch=1,
            grid=(4,),
            in_specs=[fixed((count, width))] * 2 + [column] * 4 + [fixed((count, width))] * 2,
            out_specs=[fixed(o.shape) for o in outs],
        ),
        out_shape=outs,
        compiler_params=pltpu.CompilerParams(vmem_limit_bytes=VMEM_BYTES),
        cost_estimate=pl.CostEstimate(
            flops=8 * count * width * 4 * tile,
            bytes_accessed=16 * width * tile + 8 * count * width + 32 * count * tile,
            transcendentals=0,
        ),
        name="expert_grads",
    )(position, *rows, *pre, *hidden, *row_grad)


def route_back_kernel(
    experts, token_rows, owners, pos_ref, *refs
):
    backs = refs[:owners]
    prob_ref, res_ref, pay_ref, router_ref, gain_ref, count_ref = refs[owners : owners + 6]
    grad_ref, up_ref, small_ref = refs[owners + 6 :]
    chunk, width = res_ref.shape
    prob = prob_ref[...]
    lane = lax.broadcasted_iota(jnp.int32, prob.shape, 1)
    route_grad = jnp.zeros_like(prob)
    routed_grad = jnp.zeros((chunk, width), jnp.float32)
    for k, back in enumerate(backs):
        owner = lax.rem(pos_ref[1] + k, owners)
        inner = back[:, width : width + LANES].astype(jnp.float32)
        inner = inner + back[:, width + LANES :].astype(jnp.float32)
        route_grad = jnp.where(lane == owner, inner, route_grad)
        routed_grad = routed_grad + back[:, :width].astype(jnp.float32)
    mean = jnp.sum(route_grad * prob, axis=-1, keepdims=True)
    logit_grad = (prob * (route_grad - mean)).astype(jnp.bfloat16)
    routed_grad = routed_grad + contract(logit_grad, router_ref[...], NN)
    normed, inverse, mixed = normalize(res_ref[...], gain_ref[...])
    from_norm, gain_grad = normalize_back(routed_grad, normed, inverse, gain_ref[...])
    total = pay_ref[:, :width].astype(jnp.float32) + from_norm
    grad_ref[...] = total
    up_ref[...] = total.astype(jnp.bfloat16)
    live = live_rows(prob.shape, token_rows, pos_ref[2] * chunk)
    prob_sum = jnp.sum(jnp.where(live, prob, 0.0), axis=0, keepdims=True)
    grad_router = contract(logit_grad, mixed.astype(jnp.bfloat16), TN)
    small_ref[0:SMALL, :] = grad_router[0:SMALL]
    small_ref[experts : experts + 1, :] = gain_grad[None]
    small_ref[experts + 1 : experts + 2, :] = jnp.zeros((1, width), jnp.float32)
    small_ref[experts + 1 : experts + 2, :LANES] = prob_sum
    small_ref[experts + 2 : experts + 3, :] = count_ref[...]


def attention_back_kernel(
    seq_len, heads, owners, pos_ref, tok_ref, gain_ref, w_ref, wo_ref, qkv_ref, lse_ref, att_ref,
    up_ref, small_ref, keep_ref, send_ref, part_ref, hg_ref, flat_ref, big_ref,
):
    images, rows, width = qkv_ref.shape[1], qkv_ref.shape[2], heads * HD
    scale = HD ** (-0.5)
    padded, model = up_ref.shape
    tensors = part_ref.shape[0]
    chunk = padded // tensors
    masks = head_masks(rows, heads)
    keys_live = lax.broadcasted_iota(jnp.int32, (rows, rows), 1) < seq_len
    lane = lax.broadcasted_iota(jnp.int32, (rows, LANES), 1)
    up = up_ref[...]
    hg_ref[0:padded, :] = contract(up, wo_ref[...], NT)
    hg_ref[padded:, :] = jnp.zeros((hg_ref.shape[0] - padded, width), jnp.float32)
    big_ref[3 * width :, :] = contract(att_ref[...], up, TN)
    flat_ref[images * seq_len :, :] = jnp.zeros(
        (flat_ref.shape[0] - images * seq_len, model), jnp.float32
    )
    gain_grad = jnp.zeros((1, model), jnp.float32)
    for i in range(images):
        normed, _, mixed = normalize(image_rows(tok_ref, i, seq_len), gain_ref[...])
        entered = mixed.astype(jnp.bfloat16)
        q, k, v = qkv_ref[0, i], qkv_ref[1, i], qkv_ref[2, i]
        heads_grad = hg_ref[pl.ds(i * seq_len, rows), :]
        heads_grad = jnp.where(live_rows(heads_grad.shape, seq_len), heads_grad, 0.0)
        heads_grad = heads_grad.astype(jnp.bfloat16)
        dq = jnp.zeros((rows, width), jnp.float32)
        dk, dv = dq, dq
        for h in range(heads):
            q_h, k_h = keep_lanes(q, masks[h]), keep_lanes(k, masks[h])
            up_h = keep_lanes(heads_grad, masks[h])
            scores = contract(q_h, k, NT) * scale
            lse = jnp.sum(jnp.where(lane == h, lse_ref[i], 0.0), axis=-1, keepdims=True)
            probs = jnp.where(keys_live, jnp.exp(scores - lse), 0.0)
            prob_grad = contract(up_h, v, NT)
            total = jnp.sum(prob_grad * probs, axis=-1, keepdims=True)
            score_grad = (probs * (prob_grad - total)).astype(jnp.bfloat16)
            dv = dv + contract(probs.astype(jnp.bfloat16), up_h, TN)
            dq = dq + contract(score_grad, k_h, NN)
            dk = dk + contract(score_grad, q_h, TN)
        grads = [g.astype(jnp.bfloat16) for g in (dq * scale, dk * scale, dv)]
        part = jnp.zeros((rows, model), jnp.float32)
        for c in range(3):
            here = slice(c * width, (c + 1) * width)
            part = part + contract(grads[c], w_ref[here, :], NN)
            if i == 0:
                big_ref[here, :] = contract(grads[c], entered, TN)
            else:
                big_ref[here, :] += contract(grads[c], entered, TN)
        gain_grad = gain_grad + jnp.sum(part * normed, axis=0, keepdims=True)
        flat_ref[pl.ds(i * seq_len, rows), :] = part
    high, low = split_high_low(
        jnp.concatenate([small_ref[0 : SMALL - 1, :], gain_grad], axis=0)
    )
    for j in range(tensors):
        part_ref[j, 0:chunk, :] = flat_ref[j * chunk : (j + 1) * chunk, :].astype(jnp.bfloat16)
        part_ref[j, chunk : chunk + 2 * SMALL, :] = jnp.concatenate([high, low], axis=0)
    me, core = pos_ref[1], pos_ref[0]
    piece = keep_ref.shape[1]
    for k in range(owners):
        place = lax.rem(me + k, owners) * piece
        mine = pl.ds(pl.multiple_of(core * owners * piece + place, 8), piece)
        other = pl.ds(pl.multiple_of((1 - core) * owners * piece + place, 8), piece)
        keep_ref[k] = big_ref[mine, :]
        send_ref[k] = big_ref[other, :].astype(jnp.bfloat16)


def norm_back_kernel(pos_ref, got_ref, x_ref, res_ref, gain_ref, grad_ref, small_ref):
    tensors = got_ref.shape[0]
    chunk = x_ref.shape[0]
    upstream = jnp.zeros(x_ref.shape, jnp.float32)
    small = jnp.zeros(small_ref.shape, jnp.float32)
    for j in range(tensors):
        upstream = upstream + got_ref[j, 0:chunk, :].astype(jnp.float32)
        small = small + got_ref[j, chunk : chunk + SMALL, :].astype(jnp.float32)
        small = small + got_ref[j, chunk + SMALL :, :].astype(jnp.float32)
    small_ref[...] = small
    normed, inverse, _ = normalize(x_ref[...].astype(jnp.float32), gain_ref[...])
    from_norm = normalize_back(upstream, normed, inverse, gain_ref[...])[0]
    grad_ref[...] = (res_ref[...] + from_norm).astype(jnp.bfloat16)


def add_core_kernel(pos_ref, keep_ref, other_ref, own_ref, *outs):
    total = keep_ref[...] + other_ref[...].astype(jnp.float32)
    own_ref[...] = total[0]
    for k, out in enumerate(outs):
        out[...] = total[k + 1].astype(jnp.bfloat16)


def sum_owner_kernel(pos_ref, own_ref, *refs):
    *parts, small_ref, out_ref = refs
    piece = own_ref.shape[0]
    total = own_ref[...]
    for part in parts:
        total = total + part[...].astype(jnp.float32)
    high, low = split_high_low(small_ref[...])
    out_ref[0:piece, :] = total.astype(jnp.bfloat16)
    out_ref[piece:, :] = jnp.concatenate([high, low], axis=0)


def spread_kernel(owners, experts, token_total, pos_ref, *refs):
    blocks = refs[: 2 * owners]
    qkv_ref, wo_ref, small_ref, loss_ref, big_ref, parts_ref = refs[2 * owners :]
    piece = blocks[0].shape[0] - 2 * SMALL
    core, me = pos_ref[0], pos_ref[1]
    for c in range(2):
        side = core if c == 0 else 1 - core
        for k in range(owners):
            block = blocks[c * owners + k]
            place = side * owners + lax.rem(me - k + owners, owners)
            here = pl.ds(pl.multiple_of(place * piece, 8), piece)
            big_ref[here, :] = block[0:piece, :].astype(jnp.float32)
            parts_ref[place] = block[piece : piece + SMALL, :].astype(jnp.float32) + block[
                piece + SMALL :, :
            ].astype(jnp.float32)
    rows = qkv_ref.shape[0]
    qkv_ref[...] = big_ref[0:rows, :]
    wo_ref[...] = big_ref[rows:, :]
    small = parts_ref[0]
    for p in range(1, 2 * owners):
        small = small + parts_ref[p]
    small_ref[...] = small
    product = small[experts + 1 : experts + 2, :LANES] * small[experts + 2 : experts + 3, :LANES]
    lane = lax.broadcasted_iota(jnp.int32, product.shape, 1)
    product = jnp.where(lane < experts, product, 0.0)
    loss = jnp.sum(product, axis=-1, keepdims=True)
    loss_ref[...] = jnp.broadcast_to(
        loss * (experts / (2.0 * token_total * token_total)), loss_ref.shape
    )


def images_kernel(seq_len, pos_ref, rows_ref, out_ref, flat_ref):
    flat_ref[...] = rows_ref[...].astype(jnp.float32)
    for i in range(out_ref.shape[0]):
        out_ref[i] = flat_ref[pl.ds(i * seq_len, seq_len), :].astype(out_ref.dtype)


def gather_images_kernel(seq_len, pos_ref, *refs):
    *chunks, out_ref, flat_ref = refs
    chunk = chunks[0].shape[0]
    for j, part in enumerate(chunks):
        here = pl.ds(pl.multiple_of(lax.bitwise_xor(pos_ref[2], j) * chunk, 16), chunk)
        flat_ref[here, :] = part[...].astype(jnp.float32)
    for i in range(out_ref.shape[0]):
        out_ref[i] = flat_ref[pl.ds(i * seq_len, seq_len), :].astype(out_ref.dtype)


def weight_out_kernel(pos_ref, mine_ref, other_ref, in_ref, out_ref):
    first_is_mine = pos_ref[0] == 0
    half = mine_ref.shape[1]
    for c in range(2):
        here = slice(c * half, (c + 1) * half)
        take = first_is_mine if c == 0 else jnp.logical_not(first_is_mine)
        grad_in = jnp.where(take, mine_ref[0], other_ref[0]).astype(jnp.float32)
        in_ref[0, :, here] = grad_in.T
        out_ref[0, here, :] = jnp.where(take, mine_ref[1], other_ref[1]).astype(jnp.float32)


def swap_core(value):
    return lax.ppermute(value, "dp", [(0, 1), (1, 0)])


def ring(value, shift):
    size = lax.axis_size("expert")
    return lax.ppermute(value, "expert", [(i, (i + shift) % size) for i in range(size)])


def cross(value, bit):
    size = lax.axis_size("tensor")
    return lax.ppermute(value, "tensor", [(i, i ^ bit) for i in range(size)])


def after(value, *others):
    return lax.optimization_barrier((value, *others))[0]


def dense_body(
    tokens,
    cotangent,
    expert_ids,
    slot_rank,
    qkv_weight,
    out_weight,
    router_weight,
    expert_in,
    expert_out,
    gain_attention,
    gain_experts,
):
    f32, b16 = jnp.float32, jnp.bfloat16
    images, seq_len, width = tokens.shape
    token_rows = images * seq_len
    local = qkv_weight.shape[2]
    heads = local // HD
    experts = router_weight.shape[1]
    owners = lax.axis_size("expert")
    tensors = lax.axis_size("tensor")
    cores = lax.axis_size("dp")
    chunk = round_up(-(-token_rows // tensors), 16)
    padded = chunk * tensors
    rows = round_up(seq_len, 16)
    flat_rows = padded + 32
    half = expert_in.shape[2] // cores
    quarter = half // 2
    position = jnp.stack(
        [lax.axis_index("dp"), lax.axis_index("expert"), lax.axis_index("tensor")]
    ).astype(jnp.int32)
    my_core = position[0]
    weight_rows = qkv_weight.transpose(0, 2, 1).reshape(3 * local, width)
    router_rows = jnp.pad(router_weight.T, ((0, LANES - experts), (0, 0)))
    gain_one, gain_two = gain_attention[None], gain_experts[None]
    image_block = (images, rows, width)

    qkv, lse, attended, part = kernel_call(
        functools.partial(attention_kernel, seq_len, heads),
        "attention",
        position,
        [tokens, gain_one, weight_rows, out_weight],
        [
            like((3, images, rows, local), b16),
            like((images, rows, LANES), f32),
            like((padded, local), b16),
            like((padded, width), b16),
        ],
        [pltpu.VMEM((padded, local), f32)],
        {0: image_block},
        flops=2 * images * rows * (4 * local * width + 8 * rows * local),
    )
    arrived = lax.all_to_all(part.reshape(tensors, chunk, width), "tensor", 0, 0, tiled=True)

    expert_in, expert_out = after((expert_in, expert_out), part)
    in_rows = lax.dynamic_slice_in_dim(expert_in[0], my_core * half, half, axis=1).T
    out_rows = lax.dynamic_slice_in_dim(expert_out[0], my_core * half, half, axis=0)
    mine = jnp.stack([in_rows, out_rows])
    first, second = mine[:, :quarter], mine[:, quarter:]
    first_x = cross(first, 1)
    second_y = cross(second, 2)
    pair_y = cross(jnp.stack([first, first_x]), 2)
    pair_x = cross(jnp.stack([second, second_y]), 1)

    member = (expert_ids[..., None] == jnp.arange(experts)).astype(f32)
    kept = jnp.sum(member * (slot_rank >= 0).astype(f32)[..., None], axis=2)
    kept = jnp.pad(
        kept.reshape(token_rows, experts).astype(b16),
        ((0, padded - token_rows), (0, LANES - experts)),
    )
    counts = jnp.pad(
        jnp.sum(member, axis=(0, 1, 2)) / tensors, (0, width - experts)
    )[None]
    x_chunk, payload = kernel_call(
        functools.partial(chunk_kernel, seq_len),
        "chunk",
        position,
        [tokens, cotangent, kept],
        [like((chunk, width), b16), like((chunk, width + LANES), b16)],
        [pltpu.VMEM((flat_rows, width), f32)],
        {0: image_block, 1: image_block},
    )
    payload_mine = lax.all_gather(payload, "expert", axis=0, tiled=True)
    payload_other = swap_core(payload_mine)

    residual, routed, prob = kernel_call(
        functools.partial(route_kernel, experts),
        "route",
        position,
        [arrived, x_chunk, gain_two, router_rows],
        [like((chunk, width), f32), like((chunk, width), b16), like((chunk, LANES), f32)],
    )
    blocks = [routed] + [ring(routed, k) for k in range(1, owners)]
    other_blocks = [swap_core(b) for b in blocks]

    weights = (mine, first_x, second_y, pair_y, pair_x)
    hidden_b, pre_b, rows_b, row_grad_b, gated_b, back_b = expert_pass(
        position, other_blocks, payload_other, router_rows, weights, experts
    )
    back_other, gated_other = swap_core(back_b), swap_core(gated_b)
    hidden_a, pre_a, rows_a, row_grad_a, gated_a, back_a = expert_pass(
        position, blocks, payload_mine, router_rows, weights, experts
    )
    joined = kernel_call(
        join_kernel,
        "join",
        position,
        [back_a, back_other, gated_a, gated_other],
        [like((chunk, width + 2 * LANES), b16)] * owners + [like((chunk, width), b16)] * owners,
    )
    backs = [joined[0]] + [ring(joined[k], -k) for k in range(1, owners)]

    (rows_a, rows_b), _ = lax.optimization_barrier(((rows_a, rows_b), joined[:owners]))
    own_grad, near_grad, pair_y_grad, pair_x_grad = expert_grads(
        position,
        (rows_a, rows_b),
        (pre_a, pre_b),
        (hidden_a, hidden_b),
        (row_grad_a, row_grad_b),
    )
    from_y = cross(pair_y_grad, 2)
    from_x = cross(pair_x_grad, 1)
    up_first = (near_grad[0].astype(f32) + from_y[1].astype(f32)).astype(b16)
    up_second = (near_grad[1].astype(f32) + from_x[1].astype(f32)).astype(b16)
    last_x = cross(up_first, 1)
    last_y = cross(up_second, 2)
    grad_first = own_grad[0].astype(f32) + from_y[0].astype(f32) + last_x.astype(f32)
    grad_second = own_grad[1].astype(f32) + from_x[0].astype(f32) + last_y.astype(f32)
    grad_half = jnp.concatenate([grad_first, grad_second], axis=1).astype(b16)
    grad_expert_in, grad_expert_out = kernel_call(
        weight_out_kernel,
        "weight_out",
        position,
        [grad_half, swap_core(grad_half)],
        [like((1, width, 2 * half), f32), like((1, 2 * half, width), f32)],
    )

    residual_grad, attn_grad, small = kernel_call(
        functools.partial(route_back_kernel, experts, token_rows, owners),
        "route_back",
        position,
        [*backs, prob, residual, payload, router_rows, gain_two, counts],
        [like((chunk, width), f32), like((chunk, width), b16), like((SMALL, width), f32)],
    )
    attn_grad = lax.all_gather(attn_grad, "tensor", axis=0, tiled=True)

    gated_back = after(joined[owners:], attn_grad)
    combined = residual + gated_back[0].astype(f32)
    for k in range(1, owners):
        combined = combined + ring(gated_back[k], -k).astype(f32)
    combined = combined.astype(b16)
    block_out = kernel_call(
        functools.partial(gather_images_kernel, seq_len),
        "block_out",
        position,
        [combined] + [cross(combined, j) for j in range(1, tensors)],
        [like(tokens.shape, b16)],
        [pltpu.VMEM((padded, width), f32)],
    )[0]

    piece = 4 * local // (2 * owners)
    keep, send, part_grad = kernel_call(
        functools.partial(attention_back_kernel, seq_len, heads, owners),
        "attention_back",
        position,
        [tokens, gain_one, weight_rows, out_weight, qkv, lse, attended, attn_grad, small],
        [
            like((owners, piece, width), f32),
            like((owners, piece, width), b16),
            like((tensors, chunk + 2 * SMALL, width), b16),
        ],
        [
            pltpu.VMEM((flat_rows, local), f32),
            pltpu.VMEM((flat_rows, width), f32),
            pltpu.VMEM((4 * local, width), f32),
        ],
        {0: image_block},
        flops=2 * images * rows * (8 * local * width + 20 * rows * local),
    )
    got = lax.all_to_all(part_grad, "tensor", 0, 0, tiled=True)
    own_piece, *pieces = kernel_call(
        add_core_kernel,
        "add_core",
        position,
        [keep, swap_core(send)],
        [like((piece, width), f32)] + [like((piece, width), b16)] * (owners - 1),
    )
    reduced = [ring(p, k + 1) for k, p in enumerate(pieces)]
    grad_chunk, small = kernel_call(
        norm_back_kernel,
        "norm_back",
        position,
        [got, x_chunk, residual_grad, gain_one],
        [like((chunk, width), b16), like((SMALL, width), f32)],
    )
    summed = kernel_call(
        sum_owner_kernel,
        "sum_owner",
        position,
        [own_piece, *reduced, small],
        [like((piece + 2 * SMALL, width), b16)],
    )[0]
    around = [summed] + [ring(summed, k) for k in range(1, owners)]
    grad_rows = lax.all_gather(grad_chunk, "tensor", axis=0, tiled=True)
    grad_tokens = kernel_call(
        functools.partial(images_kernel, seq_len),
        "grad_tokens",
        position,
        [grad_rows],
        [like(tokens.shape, f32)],
        [pltpu.VMEM((padded, width), f32)],
    )[0]
    token_total = token_rows * cores * owners
    grad_qkv, grad_out, small, loss = kernel_call(
        functools.partial(spread_kernel, owners, experts, token_total),
        "spread",
        position,
        around + [swap_core(a) for a in around],
        [
            like((3 * local, width), f32),
            like((local, width), f32),
            like((SMALL, width), f32),
            like((SMALL, LANES), f32),
        ],
        [
            pltpu.VMEM((4 * local, width), f32),
            pltpu.VMEM((2 * owners, SMALL, width), f32),
        ],
    )
    return (
        block_out,
        grad_tokens,
        grad_qkv.reshape(3, local, width).transpose(0, 2, 1),
        grad_out,
        small[:experts].T,
        grad_expert_in,
        grad_expert_out,
        small[SMALL - 1],
        small[experts],
        loss[0, 0],
    )


def solution(mesh):
    placed = (
        P(("dp", "expert"), None, None),
        P(("dp", "expert"), None, None),
        P(("dp", "expert"), None, None),
        P(("dp", "expert"), None, None),
        P(None, None, "tensor"),
        P("tensor", None),
        P(),
        P("expert", None, "tensor"),
        P("expert", "tensor", None),
        P(),
        P(),
    )
    shape = mesh.shape
    dense = shape["dp"] == 2 and shape["expert"] == 4 and shape["tensor"] == 4
    return jax.shard_map(
        dense_body if dense else body,
        mesh=mesh,
        in_specs=placed,
        out_specs=(
            P(("dp", "expert"), None, None),
            P(("dp", "expert"), None, None),
            P(None, None, "tensor"),
            P("tensor", None),
            P(),
            P("expert", None, "tensor"),
            P("expert", "tensor", None),
            P(),
            P(),
            P(),
        ),
        check_vma=False,
    )
```

```python
import functools
import math

import jax
import jax.numpy as jnp
from jax import lax
from jax.experimental import pallas as pl
from jax.experimental.pallas import tpu as pltpu
from jax.sharding import PartitionSpec as P

HD = 64


epsilon = 1e-06


def normalize(values, gain_row):
    center = values - jnp.mean(values, axis=-1, keepdims=True)
    inverse = lax.rsqrt(jnp.mean(center * center, axis=-1, keepdims=True) + epsilon)
    normed = center * inverse
    return (normed, inverse, normed * gain_row)


def normalize_back(upstream, normed, inverse, gain_row):
    scaled = upstream * gain_row
    result = inverse * (
        scaled
        - jnp.mean(scaled, axis=-1, keepdims=True)
        - normed * jnp.mean(scaled * normed, axis=-1, keepdims=True)
    )
    return (result, jnp.sum(upstream * normed, axis=0))


def exact_gelu(values):
    return jax.nn.gelu(values, approximate=False)


def body(
    tokens,
    cotangent,
    expert_ids,
    slot_rank,
    qkv_weight,
    out_weight,
    router_weight,
    expert_in,
    expert_out,
    gain_attention,
    gain_experts,
):
    images, seq_len, model_width = tokens.shape
    token_rows = images * seq_len
    local_width = qkv_weight.shape[2]
    local_heads = local_width // HD
    slice_width = model_width // lax.axis_size("tensor")
    experts = router_weight.shape[1]
    capacity = 5 * token_rows // (2 * experts)
    owners = lax.axis_size("expert")
    per_owner = experts // owners
    slot_total = experts * capacity
    score_scale = HD ** (-0.5)
    inputs = tokens.reshape(token_rows, model_width).astype(jnp.float32)
    normed_one, inverse_one, mixed_one = normalize(inputs, gain_attention)
    entered = mixed_one.astype(jnp.bfloat16)
    project = jnp.einsum(
        "td,cdf->ctf", entered, qkv_weight, preferred_element_type=jnp.float32
    ).astype(jnp.bfloat16)
    projected_heads = project.reshape(3, images, seq_len, local_heads, HD)
    queries, key_rows, value_rows = (projected_heads[0], projected_heads[1], projected_heads[2])
    scores = (
        jnp.einsum("ishe,ithe->ihst", queries, key_rows, preferred_element_type=jnp.float32)
        * score_scale
    )
    log_total = jax.nn.logsumexp(scores, axis=-1, keepdims=True)
    attn_probs = jnp.exp(scores - log_total).astype(jnp.bfloat16)
    attended = jnp.einsum(
        "ihst,ithe->ishe", attn_probs, value_rows, preferred_element_type=jnp.float32
    )
    attended = attended.astype(jnp.bfloat16).reshape(token_rows, local_width)
    attn_part = jnp.dot(attended, out_weight, preferred_element_type=jnp.float32)
    residual = inputs + lax.psum(attn_part, "tensor")
    normed_two, inverse_two, mixed_two = normalize(residual, gain_experts)
    routed = mixed_two.astype(jnp.bfloat16)
    route_prob = jax.nn.softmax(
        jnp.dot(routed, router_weight, preferred_element_type=jnp.float32), axis=-1
    )
    chosen = expert_ids.reshape(token_rows, 2)
    ranked = slot_rank.reshape(token_rows, 2)
    kept_mask = (ranked >= 0).astype(jnp.float32)
    position = jnp.where(ranked >= 0, chosen * capacity + ranked, slot_total).reshape(-1)
    send_rows = (
        jnp.zeros((slot_total, model_width), jnp.bfloat16)
        .at[position]
        .set(jnp.repeat(routed, 2, axis=0), mode="drop")
        .reshape(experts, capacity, model_width)
    )
    fragment = lax.all_to_all(send_rows, "expert", split_axis=0, concat_axis=0, tiled=True)
    grouped = fragment.reshape(owners, per_owner, fragment.shape[1], model_width)
    before = jnp.einsum("sjcd,jdf->sjcf", grouped, expert_in, preferred_element_type=jnp.float32)
    hidden = exact_gelu(before).astype(jnp.bfloat16)
    expert_part = jnp.einsum(
        "sjcf,jfd->sjcd", hidden, expert_out, preferred_element_type=jnp.float32
    )
    produced = lax.psum_scatter(expert_part, "tensor", scatter_dimension=3, tiled=True).astype(
        jnp.bfloat16
    )
    returned = lax.all_to_all(
        produced.reshape(experts, capacity, slice_width),
        "expert",
        split_axis=0,
        concat_axis=0,
        tiled=True,
    )
    returned = lax.all_gather(returned, "tensor", axis=2, tiled=True).reshape(
        slot_total, model_width
    )
    safe_index = jnp.minimum(position, slot_total - 1)
    picked = returned[safe_index].reshape(token_rows, 2, model_width).astype(jnp.float32)
    gate_values = jnp.take_along_axis(route_prob, chosen, axis=1) * kept_mask
    output = residual + jnp.sum(gate_values[:, :, None] * picked, axis=1)
    block_out = output.astype(jnp.bfloat16).reshape(images, seq_len, model_width)
    upstream = cotangent.reshape(token_rows, model_width).astype(jnp.float32)
    gate_grad = jnp.sum(upstream[:, None, :] * picked, axis=-1) * kept_mask
    member = (chosen[:, :, None] == jnp.arange(experts)[None, None, :]).astype(jnp.float32)
    route_grad = jnp.sum(member * gate_grad[:, :, None], axis=1)
    logit_grad = (
        route_prob * (route_grad - jnp.sum(route_grad * route_prob, axis=-1, keepdims=True))
    ).astype(jnp.bfloat16)
    row_grad = (
        (gate_values[:, :, None] * upstream[:, None, :])
        .astype(jnp.bfloat16)
        .reshape(2 * token_rows, model_width)
    )
    grad_send = (
        jnp.zeros((slot_total, model_width), jnp.bfloat16)
        .at[position]
        .set(row_grad, mode="drop")
        .reshape(experts, capacity, model_width)
    )
    grad_arrived = lax.all_to_all(grad_send, "expert", split_axis=0, concat_axis=0, tiled=True)
    grad_arrived = grad_arrived.reshape(owners, per_owner, capacity, model_width)
    hidden_grad = jnp.einsum(
        "sjcd,jfd->sjcf", grad_arrived, expert_out, preferred_element_type=jnp.float32
    )
    grad_expert_out = jnp.einsum(
        "sjcf,sjcd->jfd", hidden, grad_arrived, preferred_element_type=jnp.float32
    )
    pre_grad = jax.vjp(exact_gelu, before)[1](hidden_grad)[0].astype(jnp.bfloat16)
    grad_expert_in = jnp.einsum(
        "sjcd,sjcf->jdf", grouped, pre_grad, preferred_element_type=jnp.float32
    )
    buffer_part = jnp.einsum(
        "sjcf,jdf->sjcd", pre_grad, expert_in, preferred_element_type=jnp.float32
    )
    buffer_share = lax.psum_scatter(buffer_part, "tensor", scatter_dimension=3, tiled=True).astype(
        jnp.bfloat16
    )
    buffer_back = lax.all_to_all(
        buffer_share.reshape(experts, capacity, slice_width),
        "expert",
        split_axis=0,
        concat_axis=0,
        tiled=True,
    )
    buffer_grad = lax.all_gather(buffer_back, "tensor", axis=2, tiled=True).reshape(
        slot_total, model_width
    )
    routed_grad = jnp.sum(
        buffer_grad[safe_index].reshape(token_rows, 2, model_width).astype(jnp.float32)
        * kept_mask[:, :, None],
        axis=1,
    )
    routed_grad = routed_grad + jnp.dot(
        logit_grad, router_weight.T, preferred_element_type=jnp.float32
    )
    grad_router = jnp.einsum("td,te->de", routed, logit_grad, preferred_element_type=jnp.float32)
    from_norm_two, grad_gain_experts = normalize_back(
        routed_grad, normed_two, inverse_two, gain_experts
    )
    residual_grad = upstream + from_norm_two
    attn_grad = residual_grad.astype(jnp.bfloat16)
    grad_out = jnp.einsum("tf,td->fd", attended, attn_grad, preferred_element_type=jnp.float32)
    heads_grad = jnp.dot(attn_grad, out_weight.T, preferred_element_type=jnp.float32).astype(
        jnp.bfloat16
    )
    heads_grad = heads_grad.reshape(images, seq_len, local_heads, HD)
    again = (
        jnp.einsum("ishe,ithe->ihst", queries, key_rows, preferred_element_type=jnp.float32)
        * score_scale
    )
    probs_full = jnp.exp(again - log_total)
    prob_grad = jnp.einsum(
        "ishe,ithe->ihst", heads_grad, value_rows, preferred_element_type=jnp.float32
    )
    value_grad = jnp.einsum(
        "ihst,ishe->ithe",
        probs_full.astype(jnp.bfloat16),
        heads_grad,
        preferred_element_type=jnp.float32,
    )
    score_grad = (
        probs_full * (prob_grad - jnp.sum(prob_grad * probs_full, axis=-1, keepdims=True))
    ).astype(jnp.bfloat16)
    query_grad = (
        jnp.einsum("ihst,ithe->ishe", score_grad, key_rows, preferred_element_type=jnp.float32)
        * score_scale
    )
    key_grad = (
        jnp.einsum("ihst,ishe->ithe", score_grad, queries, preferred_element_type=jnp.float32)
        * score_scale
    )
    project_grad = (
        jnp.stack([query_grad, key_grad, value_grad])
        .astype(jnp.bfloat16)
        .reshape(3, token_rows, local_width)
    )
    grad_qkv = jnp.einsum("td,ctf->cdf", entered, project_grad, preferred_element_type=jnp.float32)
    entered_part = jnp.einsum(
        "ctf,cdf->td", project_grad, qkv_weight, preferred_element_type=jnp.float32
    )
    entered_grad = lax.psum(entered_part.astype(jnp.bfloat16), "tensor").astype(jnp.float32)
    from_norm_one, grad_gain_attention = normalize_back(
        entered_grad, normed_one, inverse_one, gain_attention
    )
    grad_tokens = (residual_grad + from_norm_one).reshape(images, seq_len, model_width)
    counts = jnp.sum(member, axis=(0, 1))
    prob_sum = jnp.sum(route_prob, axis=0)
    grad_qkv, grad_out, grad_router, grad_gain_attention, grad_gain_experts, counts, prob_sum = (
        lax.psum(
            (
                grad_qkv,
                grad_out,
                grad_router,
                grad_gain_attention,
                grad_gain_experts,
                counts,
                prob_sum,
            ),
            ("dp", "expert"),
        )
    )
    grad_expert_in, grad_expert_out = (
        lax.psum(grad_expert_in.astype(jnp.bfloat16), "dp").astype(jnp.float32),
        lax.psum(grad_expert_out.astype(jnp.bfloat16), "dp").astype(jnp.float32),
    )
    token_total = token_rows * lax.axis_size("dp") * lax.axis_size("expert")
    balance_loss = experts * jnp.sum(counts / (2.0 * token_total) * prob_sum / token_total)
    return (
        block_out,
        grad_tokens,
        grad_qkv,
        grad_out,
        grad_router,
        grad_expert_in,
        grad_expert_out,
        grad_gain_attention,
        grad_gain_experts,
        balance_loss,
    )


NN = ((1,), (0,))
NT = ((1,), (1,))
TN = ((0,), (0,))
LANES = 128
SMALL = 8


def round_up(value, step):
    return -(-value // step) * step


def contract(a, b, dims):
    return lax.dot_general(a, b, (dims, ((), ())), preferred_element_type=jnp.float32)


def kernel_call(kernel, name, position, args, outs, scratch=(), flops=0, limit=24):
    return pl.pallas_call(
        kernel,
        in_specs=[pl.BlockSpec(memory_space=pltpu.SMEM)]
        + [pl.BlockSpec(memory_space=pltpu.VMEM)] * len(args),
        out_specs=[pl.BlockSpec(memory_space=pltpu.VMEM)] * len(outs),
        out_shape=list(outs),
        scratch_shapes=list(scratch),
        compiler_params=pltpu.CompilerParams(vmem_limit_bytes=limit << 20),
        cost_estimate=pl.CostEstimate(flops=flops, bytes_accessed=0, transcendentals=0),
        name=name,
    )(position, *args)


def like(shape, dtype):
    return jax.ShapeDtypeStruct(shape, dtype)


def live_rows(shape, limit, offset=0):
    return lax.broadcasted_iota(jnp.int32, shape, 0) + offset < limit


def chunk_of(pos_ref, j, size):
    return pl.ds(pl.multiple_of(lax.bitwise_xor(pos_ref[2], j) * size, 16), size)


def head_masks(rows, heads):
    lane = lax.broadcasted_iota(jnp.int32, (rows, heads * HD), 1)
    return [(lane >= h * HD) & (lane < (h + 1) * HD) for h in range(heads)]


def keep_lanes(value, mask):
    return jnp.where(mask, value, jnp.zeros_like(value))


def split_high_low(value):
    high = value.astype(jnp.bfloat16)
    return high, (value - high.astype(jnp.float32)).astype(jnp.bfloat16)


def image_rows(ref, i, scratch_ref):
    seq_len = ref.shape[1]
    scratch_ref[seq_len:, :] = jnp.zeros((scratch_ref.shape[0] - seq_len, ref.shape[2]), jnp.float32)
    scratch_ref[0:seq_len, :] = ref[i].astype(jnp.float32)
    return scratch_ref[...]


def router_matrix(param_ref, experts):
    rows = param_ref[0:SMALL, :]
    rows = jnp.where(live_rows(rows.shape, experts), rows, 0.0).astype(jnp.bfloat16)
    zeros = jnp.zeros((LANES - SMALL, rows.shape[1]), jnp.bfloat16)
    return jnp.concatenate([rows, zeros], axis=0)


def weights_kernel(pos_ref, in_ref, out_ref, mine_ref, first_ref, second_ref):
    half = mine_ref.shape[1]
    quarter = half // 2
    start = pl.multiple_of(pos_ref[0] * half, LANES)
    for s, rows in (
        (0, in_ref[0, :, pl.ds(start, half)].T),
        (1, out_ref[0, pl.ds(start, half), :]),
    ):
        mine_ref[s] = rows
        first_ref[s] = rows[0:quarter]
        second_ref[s] = rows[quarter:]


def chunk_kernel(
    tensors, pos_ref, tok_ref, cot_ref, ids_ref, rank_ref, router_ref, one_ref, two_ref, x_ref, pay_ref,
    param_ref, flat_ref, kept_ref,
):
    images, seq_len, width = tok_ref.shape
    chunk, experts = x_ref.shape[0], router_ref.shape[0]
    start = pl.multiple_of(pos_ref[2] * chunk, 16)
    for source, target in ((tok_ref, x_ref), (cot_ref, pay_ref)):
        flat_ref[images * seq_len :, :] = jnp.zeros(
            (flat_ref.shape[0] - images * seq_len, width), jnp.float32
        )
        for i in range(images):
            flat_ref[pl.ds(i * seq_len, seq_len), :] = source[i].astype(jnp.float32)
        target[:, :width] = flat_ref[pl.ds(start, chunk), :].astype(jnp.bfloat16)
    kept_ref[...] = jnp.zeros_like(kept_ref)
    counts = jnp.zeros((1, LANES), jnp.float32)
    for i in range(images):
        rows, all_rows = [], []
        for e in range(experts):
            named = (ids_ref[i] == e).astype(jnp.float32)
            kept = jnp.where(rank_ref[i] >= 0, named, 0.0)
            rows.append(jnp.sum(kept, axis=0, keepdims=True))
            all_rows.append(jnp.sum(named, axis=0, keepdims=True))
        for group, is_kept in ((rows, True), (all_rows, False)):
            table = jnp.concatenate(group, axis=0)
            table = jnp.concatenate(
                [table, jnp.zeros((LANES - experts, seq_len), jnp.float32)], axis=0
            )
            table = jnp.concatenate(
                [table, jnp.zeros((LANES, 2 * LANES - seq_len), jnp.float32)], axis=1
            ).T
            if is_kept:
                kept_ref[pl.ds(i * seq_len, 2 * LANES), :] = table
            else:
                counts = counts + jnp.sum(table, axis=0, keepdims=True)
    pay_ref[:, width:] = kept_ref[pl.ds(start, chunk), :].astype(jnp.bfloat16)
    param_ref[...] = jnp.zeros_like(param_ref)
    param_ref[0:experts, :] = router_ref[...].astype(jnp.float32)
    param_ref[experts : experts + 1, :] = one_ref[...].reshape(1, width)
    param_ref[experts + 1 : experts + 2, :] = two_ref[...].reshape(1, width)
    param_ref[SMALL - 1 : SMALL, :LANES] = counts * (1.0 / tensors)


def gain_row(param_ref, experts, which):
    return param_ref[experts + which : experts + which + 1, :]


def attention_kernel(
    heads, experts, pos_ref, tok_ref, param_ref, w_ref, wo_ref, qkv_ref, lse_ref, att_ref, *refs,
):
    *parts, flat_ref, image_ref = refs
    images, rows, width = qkv_ref.shape[1], qkv_ref.shape[2], heads * HD
    seq_len = tok_ref.shape[1]
    masks = head_masks(rows, heads)
    keys_live = lax.broadcasted_iota(jnp.int32, (rows, rows), 1) < seq_len
    lane = lax.broadcasted_iota(jnp.int32, (rows, LANES), 1)
    flat_ref[images * seq_len :, :] = jnp.zeros(
        (flat_ref.shape[0] - images * seq_len, width), jnp.float32
    )
    for i in range(images):
        entered = normalize(image_rows(tok_ref, i, image_ref), gain_row(param_ref, experts, 0))[2].astype(
            jnp.bfloat16
        )
        q, k, v = (
            contract(entered, w_ref[c * width : (c + 1) * width, :], NT).astype(jnp.bfloat16)
            for c in range(3)
        )
        qkv_ref[0, i], qkv_ref[1, i], qkv_ref[2, i] = q, k, v
        attended = jnp.zeros((rows, width), jnp.float32)
        lse_all = jnp.zeros((rows, LANES), jnp.float32)
        for h in range(heads):
            scores = contract(keep_lanes(q, masks[h]), k, NT) * (HD ** (-0.5))
            scores = jnp.where(keys_live, scores, -1e30)
            top = jnp.max(scores, axis=-1, keepdims=True)
            lse = top + jnp.log(jnp.sum(jnp.exp(scores - top), axis=-1, keepdims=True))
            probs = jnp.exp(scores - lse).astype(jnp.bfloat16)
            attended = attended + contract(probs, keep_lanes(v, masks[h]), NN)
            lse_all = jnp.where(lane == h, lse, lse_all)
        lse_ref[i] = lse_all
        flat_ref[pl.ds(i * seq_len, rows), :] = jnp.where(
            live_rows(attended.shape, seq_len), attended, 0.0
        )
    att_ref[...] = flat_ref[...].astype(jnp.bfloat16)
    for j, part in enumerate(parts):
        rows_j = flat_ref[chunk_of(pos_ref, j, part.shape[0]), :].astype(jnp.bfloat16)
        part[...] = contract(rows_j, wo_ref[...], NN).astype(jnp.bfloat16)


def route_kernel(experts, pos_ref, *refs):
    *got, x_ref, param_ref, res_ref, routed_ref, prob_ref = refs
    residual = x_ref[...].astype(jnp.float32)
    for part in got:
        residual = residual + part[...].astype(jnp.float32)
    res_ref[...] = residual
    routed = normalize(residual, gain_row(param_ref, experts, 1))[2].astype(jnp.bfloat16)
    routed_ref[...] = routed
    prob_ref[...] = route_probs(routed, router_matrix(param_ref, experts), experts)


def route_probs(rows, router, experts):
    logits = contract(rows, router, NT)
    lane = lax.broadcasted_iota(jnp.int32, logits.shape, 1)
    logits = jnp.where(lane < experts, logits, -1e30)
    weight = jnp.exp(logits - jnp.max(logits, axis=-1, keepdims=True))
    return weight / jnp.sum(weight, axis=-1, keepdims=True)


def gelu_parts(x):
    square = jnp.exp(-0.5 * x * x)
    share = 0.5 * (1.0 + lax.erf(x * (0.5**0.5)))
    return x * share, share + x * square * (0.5 / math.pi) ** 0.5


def expert_kernel(experts, owners, *refs):
    pos_ref, *blocks = refs[: 1 + owners]
    pay_ref, param_ref, w0_ref, xa_ref, yb_ref, pair_y_ref, pair_x_ref = refs[
        1 + owners : 8 + owners
    ]
    hidden_ref, pre_ref, x_ref, rg_ref, gated_ref, back_ref = refs[8 + owners :][:6]
    gate_ref, acc_ref = refs[14 + owners :]
    chunk, width = blocks[0].shape
    me = pos_ref[1]

    def places(k):
        start = lax.rem(me - k + owners, owners) * chunk
        return pl.ds(k * chunk, chunk), pl.ds(pl.multiple_of(start, 16), chunk)

    router = router_matrix(param_ref, experts)
    for k in range(owners):
        here, source = places(k)
        rows = blocks[k][...]
        x_ref[here, :] = rows
        prob = route_probs(rows, router, experts)
        lane = lax.broadcasted_iota(jnp.int32, prob.shape, 1)
        kept = pay_ref[source, width:].astype(jnp.float32)
        kept = jnp.sum(jnp.where(lane == me, kept, 0.0), axis=-1, keepdims=True)
        gate = jnp.sum(jnp.where(lane == me, prob, 0.0), axis=-1, keepdims=True) * kept
        gate_ref[here, :LANES] = jnp.broadcast_to(gate, (chunk, LANES))
        gate_ref[here, LANES:] = jnp.broadcast_to(kept, (chunk, LANES))
        rg_ref[here, :] = (gate * pay_ref[source, :width].astype(jnp.float32)).astype(jnp.bfloat16)
    tile = 2 * w0_ref.shape[1]
    for t, pieces in enumerate(
        (
            [(w0_ref[s], xa_ref[s], yb_ref[s]) for s in range(2)],
            [
                (pair_y_ref[0, s], pair_y_ref[1, s], pair_x_ref[0, s], pair_x_ref[1, s])
                for s in range(2)
            ],
        )
    ):
        w_in, w_out = (jnp.concatenate(p, axis=0) for p in pieces)
        columns = slice(t * tile, (t + 1) * tile)
        before = contract(x_ref[...], w_in, NT)
        value, slope = gelu_parts(before)
        hidden = value.astype(jnp.bfloat16)
        hidden_ref[:, columns] = hidden
        part = contract(hidden, w_out, NN)
        pre = (contract(rg_ref[...], w_out, NT) * slope).astype(jnp.bfloat16)
        pre_ref[:, columns] = pre
        back = contract(pre, w_in, NN)
        if t == 0:
            acc_ref[...] = part
            back_ref[:, :width] = back
        else:
            acc_ref[...] += part
            back_ref[:, :width] += back
    for k in range(owners):
        here, source = places(k)
        part = acc_ref[here, :]
        gated_ref[here, :] = (gate_ref[here, 0:1] * part).astype(jnp.bfloat16)
        inner = jnp.sum(part * pay_ref[source, :width].astype(jnp.float32), axis=-1, keepdims=True)
        back_ref[here, width:] = gate_ref[here, LANES:] * inner


def expert_pass(position, blocks, payload, params, weights, experts):
    chunk, width = blocks[0].shape
    owners = len(blocks)
    count, hidden = owners * chunk, 4 * weights[0].shape[1]
    return kernel_call(
        functools.partial(expert_kernel, experts, owners),
        "experts",
        position,
        [*blocks, payload, params, *weights],
        [
            like((count, hidden), jnp.bfloat16),
            like((count, hidden), jnp.bfloat16),
            like((count, width), jnp.bfloat16),
            like((count, width), jnp.bfloat16),
            like((count, width), jnp.bfloat16),
            like((count, width + LANES), jnp.float32),
        ],
        [pltpu.VMEM((count, 2 * LANES), jnp.float32), pltpu.VMEM((count, width), jnp.float32)],
        limit=22,
    )


def join_kernel(pos_ref, back_ref, other_ref, gated_ref, gated_other_ref, *outs):
    owners = len(outs) // 2
    chunk, width = outs[owners].shape
    for k in range(owners):
        here = pl.ds(k * chunk, chunk)
        total = back_ref[here, :] + other_ref[here, :]
        outs[k][0:chunk, :] = total[:, :width].astype(jnp.bfloat16)
        inner = jnp.concatenate(
            [total[:, width:], jnp.zeros((2 * LANES - chunk, LANES), jnp.float32)], axis=0
        ).T
        high, low = split_high_low(inner[0:SMALL, :])
        outs[k][chunk:, : 2 * LANES] = jnp.concatenate([high, low], axis=0)
        outs[k][chunk:, 2 * LANES :] = jnp.zeros((2 * SMALL, width - 2 * LANES), jnp.bfloat16)
        outs[owners + k][...] = (
            gated_ref[here, :].astype(jnp.float32) + gated_other_ref[here, :].astype(jnp.float32)
        ).astype(jnp.bfloat16)


def expert_grad_kernel(pos_ref, *refs):
    *sources, own_ref, near_ref, far_y_ref, far_x_ref = refs
    part_rows = own_ref.shape[2]
    for j, out in ((2, far_y_ref), (3, far_x_ref), (1, near_ref), (0, own_ref)):
        columns = slice(2 * j * part_rows, 2 * (j + 1) * part_rows)
        for s in range(2):
            left_a, right_a, left_b, right_b = sources[4 * s : 4 * s + 4]
            grad = contract(left_a[:, columns], right_a[...], TN)
            grad = grad + contract(left_b[:, columns], right_b[...], TN)
            grad = grad.astype(jnp.bfloat16)
            out[0, s] = grad[0:part_rows]
            out[1, s] = grad[part_rows:]


def route_back_kernel(
    experts, token_rows, owners, pos_ref, *refs
):
    backs = refs[:owners]
    prob_ref, res_ref, pay_ref, param_ref = refs[owners : owners + 4]
    grad_ref, up_ref, small_ref = refs[owners + 4 :]
    chunk, width = res_ref.shape
    prob = prob_ref[...]
    lane = lax.broadcasted_iota(jnp.int32, prob.shape, 1)
    route_grad = jnp.zeros_like(prob)
    routed_grad = jnp.zeros((chunk, width), jnp.float32)
    for k, back in enumerate(backs):
        owner = lax.rem(pos_ref[1] + k, owners)
        inner = back[chunk : chunk + SMALL, : 2 * LANES].astype(jnp.float32)
        inner = inner + back[chunk + SMALL :, : 2 * LANES].astype(jnp.float32)
        inner = jnp.concatenate([inner] * (LANES // SMALL), axis=0).T[0:chunk]
        route_grad = jnp.where(lane == owner, inner, route_grad)
        routed_grad = routed_grad + back[0:chunk, :].astype(jnp.float32)
    mean = jnp.sum(route_grad * prob, axis=-1, keepdims=True)
    logit_grad = (prob * (route_grad - mean)).astype(jnp.bfloat16)
    routed_grad = routed_grad + contract(
        logit_grad, router_matrix(param_ref, experts), NN
    )
    normed, inverse, mixed = normalize(res_ref[...], gain_row(param_ref, experts, 1))
    from_norm, gain_grad = normalize_back(
        routed_grad, normed, inverse, gain_row(param_ref, experts, 1)
    )
    total = pay_ref[:, :width].astype(jnp.float32) + from_norm
    grad_ref[...] = total
    up_ref[...] = total.astype(jnp.bfloat16)
    live = live_rows(prob.shape, token_rows, pos_ref[2] * chunk)
    prob_sum = jnp.sum(jnp.where(live, prob, 0.0), axis=0, keepdims=True)
    grad_router = contract(logit_grad, mixed.astype(jnp.bfloat16), TN)
    small_ref[0:SMALL, :] = grad_router[0:SMALL]
    small_ref[experts : experts + 1, :] = gain_grad[None]
    small_ref[experts + 1 : experts + 2, :] = jnp.zeros((1, width), jnp.float32)
    small_ref[experts + 1 : experts + 2, :LANES] = prob_sum
    small_ref[experts + 2 : experts + 3, :] = param_ref[SMALL - 1 : SMALL, :]


def attention_back_kernel(
    heads, experts, owners, pos_ref, tok_ref, param_ref, w_ref, wo_ref, qkv_ref, lse_ref, att_ref,
    up_ref, small_ref, keep_ref, send_ref, *refs,
):
    *parts, hg_ref, flat_ref, big_ref, image_ref = refs
    images, rows, width = qkv_ref.shape[1], qkv_ref.shape[2], heads * HD
    seq_len = tok_ref.shape[1]
    scale = HD ** (-0.5)
    padded, model = up_ref.shape
    chunk = padded // len(parts)
    masks = head_masks(rows, heads)
    keys_live = lax.broadcasted_iota(jnp.int32, (rows, rows), 1) < seq_len
    lane = lax.broadcasted_iota(jnp.int32, (rows, LANES), 1)
    up = up_ref[...]
    hg_ref[0:padded, :] = contract(up, wo_ref[...], NT)
    hg_ref[padded:, :] = jnp.zeros((hg_ref.shape[0] - padded, width), jnp.float32)
    big_ref[3 * width :, :] = contract(att_ref[...], up, TN)
    flat_ref[images * seq_len :, :] = jnp.zeros(
        (flat_ref.shape[0] - images * seq_len, model), jnp.float32
    )
    gain_grad = jnp.zeros((1, model), jnp.float32)
    for i in range(images):
        normed, _, mixed = normalize(
            image_rows(tok_ref, i, image_ref), gain_row(param_ref, experts, 0)
        )
        entered = mixed.astype(jnp.bfloat16)
        q, k, v = qkv_ref[0, i], qkv_ref[1, i], qkv_ref[2, i]
        heads_grad = hg_ref[pl.ds(i * seq_len, rows), :]
        heads_grad = jnp.where(live_rows(heads_grad.shape, seq_len), heads_grad, 0.0)
        heads_grad = heads_grad.astype(jnp.bfloat16)
        dq = jnp.zeros((rows, width), jnp.float32)
        dk, dv = dq, dq
        for h in range(heads):
            q_h, k_h = keep_lanes(q, masks[h]), keep_lanes(k, masks[h])
            up_h = keep_lanes(heads_grad, masks[h])
            scores = contract(q_h, k, NT) * scale
            lse = jnp.sum(jnp.where(lane == h, lse_ref[i], 0.0), axis=-1, keepdims=True)
            probs = jnp.where(keys_live, jnp.exp(scores - lse), 0.0)
            prob_grad = contract(up_h, v, NT)
            total = jnp.sum(prob_grad * probs, axis=-1, keepdims=True)
            score_grad = (probs * (prob_grad - total)).astype(jnp.bfloat16)
            dv = dv + contract(probs.astype(jnp.bfloat16), up_h, TN)
            dq = dq + contract(score_grad, k_h, NN)
            dk = dk + contract(score_grad, q_h, TN)
        grads = [g.astype(jnp.bfloat16) for g in (dq * scale, dk * scale, dv)]
        part = jnp.zeros((rows, model), jnp.float32)
        for c in range(3):
            here = slice(c * width, (c + 1) * width)
            part = part + contract(grads[c], w_ref[here, :], NN)
            if i == 0:
                big_ref[here, :] = contract(grads[c], entered, TN)
            else:
                big_ref[here, :] += contract(grads[c], entered, TN)
        gain_grad = gain_grad + jnp.sum(part * normed, axis=0, keepdims=True)
        flat_ref[pl.ds(i * seq_len, rows), :] = part
    high, low = split_high_low(
        jnp.concatenate([small_ref[0 : SMALL - 1, :], gain_grad], axis=0)
    )
    for j, part in enumerate(parts):
        part[0:chunk, :] = flat_ref[chunk_of(pos_ref, j, chunk), :].astype(jnp.bfloat16)
        part[chunk:, :] = jnp.concatenate([high, low], axis=0)
    me, core = pos_ref[1], pos_ref[0]
    piece = keep_ref.shape[1]
    for k in range(owners):
        place = lax.rem(me + k, owners) * piece
        mine = pl.ds(pl.multiple_of(core * owners * piece + place, 8), piece)
        other = pl.ds(pl.multiple_of((1 - core) * owners * piece + place, 8), piece)
        keep_ref[k] = big_ref[mine, :]
        send_ref[k] = big_ref[other, :].astype(jnp.bfloat16)


def norm_back_kernel(experts, tensors, pos_ref, *refs):
    got = refs[:tensors]
    x_ref, res_ref, param_ref, own_ref, *parts, grad_ref, out_ref, small_ref = refs[tensors:]
    chunk, width = x_ref.shape
    upstream = jnp.zeros((chunk, width), jnp.float32)
    for j, part in enumerate(got):
        upstream = upstream + part[0:chunk, :].astype(jnp.float32)
        small_ref[lax.bitwise_xor(pos_ref[2], j)] = part[chunk : chunk + SMALL, :].astype(
            jnp.float32
        ) + part[chunk + SMALL :, :].astype(jnp.float32)
    small = small_ref[0]
    for j in range(1, tensors):
        small = small + small_ref[j]
    gain = gain_row(param_ref, experts, 0)
    normed, inverse, _ = normalize(x_ref[...].astype(jnp.float32), gain)
    from_norm = normalize_back(upstream, normed, inverse, gain)[0]
    grad_ref[...] = (res_ref[...] + from_norm).astype(jnp.bfloat16)
    piece = own_ref.shape[0]
    total = own_ref[...]
    for part in parts:
        total = total + part[...].astype(jnp.float32)
    out_ref[0:piece, :] = total.astype(jnp.bfloat16)
    out_ref[piece:, :] = jnp.concatenate(split_high_low(small), axis=0)


def second_step_kernel(pos_ref, near_ref, from_y, from_x, x_ref, y_ref):
    for target, row, other in ((x_ref, 0, from_y), (y_ref, 1, from_x)):
        total = near_ref[row].astype(jnp.float32) + other[1].astype(jnp.float32)
        target[...] = total.astype(jnp.bfloat16)


def weight_sum_kernel(pos_ref, own_ref, from_y, from_x, last_x, last_y, out_ref):
    part_rows = last_x.shape[1]
    for row, other, last in ((0, from_y, last_x), (1, from_x, last_y)):
        total = own_ref[row].astype(jnp.float32) + other[0].astype(jnp.float32)
        total = total + last[...].astype(jnp.float32)
        out_ref[:, row * part_rows : (row + 1) * part_rows, :] = total.astype(jnp.bfloat16)


def add_core_kernel(pos_ref, keep_ref, other_ref, own_ref, *outs):
    total = keep_ref[...] + other_ref[...].astype(jnp.float32)
    own_ref[...] = total[0]
    for k, out in enumerate(outs):
        out[...] = total[k + 1].astype(jnp.bfloat16)


def spread_kernel(owners, experts, token_total, pos_ref, *refs):
    blocks = refs[: 2 * owners]
    qkv_ref, wo_ref, small_ref, loss_ref, big_ref, parts_ref = refs[2 * owners :]
    piece = blocks[0].shape[0] - 2 * SMALL
    core, me = pos_ref[0], pos_ref[1]
    for c in range(2):
        side = core if c == 0 else 1 - core
        for k in range(owners):
            block = blocks[c * owners + k]
            place = side * owners + lax.rem(me - k + owners, owners)
            here = pl.ds(pl.multiple_of(place * piece, 8), piece)
            big_ref[here, :] = block[0:piece, :].astype(jnp.float32)
            parts_ref[place] = block[piece : piece + SMALL, :].astype(jnp.float32) + block[
                piece + SMALL :, :
            ].astype(jnp.float32)
    rows = qkv_ref.shape[0]
    qkv_ref[...] = big_ref[0:rows, :]
    wo_ref[...] = big_ref[rows:, :]
    small = parts_ref[0]
    for p in range(1, 2 * owners):
        small = small + parts_ref[p]
    small_ref[...] = small
    product = small[experts + 1 : experts + 2, :LANES] * small[experts + 2 : experts + 3, :LANES]
    lane = lax.broadcasted_iota(jnp.int32, product.shape, 1)
    product = jnp.where(lane < experts, product, 0.0)
    loss = jnp.sum(product, axis=-1, keepdims=True)
    loss_ref[...] = jnp.broadcast_to(
        loss * (experts / (2.0 * token_total * token_total)), loss_ref.shape
    )


def images_kernel(pos_ref, *refs):
    *chunks, out_ref, flat_ref = refs
    images, seq_len, _ = out_ref.shape
    if len(chunks) == 1:
        flat_ref[...] = chunks[0][...].astype(jnp.float32)
    else:
        for j, part in enumerate(chunks):
            flat_ref[chunk_of(pos_ref, j, part.shape[0]), :] = part[...].astype(jnp.float32)
    for i in range(images):
        out_ref[i] = flat_ref[pl.ds(i * seq_len, seq_len), :].astype(out_ref.dtype)


def weight_out_kernel(pos_ref, mine_ref, other_ref, in_ref, out_ref):
    first_is_mine = pos_ref[0] == 0
    half = mine_ref.shape[1]
    for c in range(2):
        here = slice(c * half, (c + 1) * half)
        take = first_is_mine if c == 0 else jnp.logical_not(first_is_mine)
        grad_in = jnp.where(take, mine_ref[0], other_ref[0]).astype(jnp.float32)
        in_ref[0, :, here] = grad_in.T
        out_ref[0, here, :] = jnp.where(take, mine_ref[1], other_ref[1]).astype(jnp.float32)


def swap_core(value):
    return lax.ppermute(value, "dp", [(0, 1), (1, 0)])


def ring(value, shift):
    size = lax.axis_size("expert")
    return lax.ppermute(value, "expert", [(i, (i + shift) % size) for i in range(size)])


def cross(value, bit):
    size = lax.axis_size("tensor")
    return lax.ppermute(value, "tensor", [(i, i ^ bit) for i in range(size)])


def after(value, *others):
    return lax.optimization_barrier((value, *others))[0]


def dense_body(
    tokens,
    cotangent,
    expert_ids,
    slot_rank,
    qkv_weight,
    out_weight,
    router_weight,
    expert_in,
    expert_out,
    gain_attention,
    gain_experts,
):
    f32, b16 = jnp.float32, jnp.bfloat16
    images, seq_len, width = tokens.shape
    token_rows = images * seq_len
    local = qkv_weight.shape[2]
    heads = local // HD
    experts = router_weight.shape[1]
    owners = lax.axis_size("expert")
    tensors = lax.axis_size("tensor")
    cores = lax.axis_size("dp")
    chunk = round_up(-(-token_rows // tensors), 16)
    padded = chunk * tensors
    rows = round_up(seq_len, 16)
    flat_rows = padded + 32
    half = expert_in.shape[2] // cores
    quarter = half // 2
    position = jnp.stack(
        [lax.axis_index("dp"), lax.axis_index("expert"), lax.axis_index("tensor")]
    ).astype(jnp.int32)
    weight_rows = qkv_weight.transpose(0, 2, 1).reshape(3 * local, width)

    mine, first, second = kernel_call(
        weights_kernel,
        "weights",
        position,
        [expert_in, expert_out],
        [
            like((2, half, width), b16),
            like((2, quarter, width), b16),
            like((2, quarter, width), b16),
        ],
        limit=8,
    )
    first_x = cross(first, 1)
    second_y = cross(second, 2)

    x_chunk, payload, params = kernel_call(
        functools.partial(chunk_kernel, tensors),
        "chunk",
        after(position, mine),
        [
            tokens,
            cotangent,
            expert_ids.transpose(0, 2, 1),
            slot_rank.transpose(0, 2, 1),
            router_weight.T,
            gain_attention,
            gain_experts,
        ],
        [
            like((chunk, width), b16),
            like((chunk, width + LANES), b16),
            like((SMALL, width), f32),
        ],
        [
            pltpu.VMEM((flat_rows, width), f32),
            pltpu.VMEM((padded + 2 * LANES, LANES), f32),
        ],
        limit=12,
    )
    payload_mine = lax.all_gather(payload, "expert", axis=0, tiled=True)

    qkv, lse, attended, *parts = kernel_call(
        functools.partial(attention_kernel, heads, experts),
        "attention",
        position,
        [tokens, params, weight_rows, out_weight],
        [
            like((3, images, rows, local), b16),
            like((images, rows, LANES), f32),
            like((padded, local), b16),
        ]
        + [like((chunk, width), b16)] * tensors,
        [pltpu.VMEM((padded, local), f32), pltpu.VMEM((rows, width), f32)],
        limit=16,
    )
    arrived = [parts[0]] + [cross(parts[j], j) for j in range(1, tensors)]
    pair_first, pair_second = jnp.stack([first, first_x]), jnp.stack([second, second_y])

    residual, routed, prob = kernel_call(
        functools.partial(route_kernel, experts),
        "route",
        after(position, pair_first, pair_second),
        [*arrived, x_chunk, params],
        [like((chunk, width), f32), like((chunk, width), b16), like((chunk, LANES), f32)],
        limit=8,
    )
    blocks = [routed] + [ring(routed, k) for k in range(1, owners)]
    pair_first, pair_second = after((pair_first, pair_second), routed)
    pair_y = cross(pair_first, 2)
    pair_x = cross(pair_second, 1)
    other_blocks = [swap_core(b) for b in blocks]
    payload_other = swap_core(after(payload_mine, blocks))

    weights = (mine, first_x, second_y, pair_y, pair_x)
    hidden_b, pre_b, rows_b, row_grad_b, gated_b, back_b = expert_pass(
        position, other_blocks, payload_other, params, weights, experts
    )
    back_other, gated_other = swap_core(back_b), swap_core(gated_b)
    blocks[0] = after(blocks[0], gated_b)
    hidden_a, pre_a, rows_a, row_grad_a, gated_a, back_a = expert_pass(
        position, blocks, payload_mine, params, weights, experts
    )
    joined = kernel_call(
        join_kernel,
        "join",
        position,
        [back_a, back_other, gated_a, gated_other],
        [like((chunk + 2 * SMALL, width), b16)] * owners + [like((chunk, width), b16)] * owners,
        limit=8,
    )
    backs = [joined[0]] + [ring(joined[k], -k) for k in range(1, owners)]

    own_grad, near_grad, far_y, far_x = kernel_call(
        expert_grad_kernel,
        "expert_grads",
        after(position, joined[:owners]),
        [pre_a, rows_a, pre_b, rows_b, hidden_a, row_grad_a, hidden_b, row_grad_b],
        [like((2, 2, quarter, width), b16)] * 4,
        limit=14,
    )
    from_y, from_x = cross(far_y, 2), cross(far_x, 1)

    residual_grad, attn_grad, small = kernel_call(
        functools.partial(route_back_kernel, experts, token_rows, owners),
        "route_back",
        after(position, own_grad),
        [*backs, prob, residual, payload, params],
        [like((chunk, width), f32), like((chunk, width), b16), like((SMALL, width), f32)],
        flops=40_000_000_000,
        limit=8,
    )
    gated_back = [joined[owners]]
    for k in range(1, owners):
        gated_back.append(ring(after(joined[owners + k], backs[k]), -k))
    attn_grad = lax.all_gather(attn_grad, "tensor", axis=0, tiled=True)
    piece = 4 * local // (2 * owners)
    keep, send, *parts = kernel_call(
        functools.partial(attention_back_kernel, heads, experts, owners),
        "attention_back",
        after(position, from_y, from_x, gated_back[1:]),
        [tokens, params, weight_rows, out_weight, qkv, lse, attended, attn_grad, small],
        [
            like((owners, piece, width), f32),
            like((owners, piece, width), b16),
        ]
        + [like((chunk + 2 * SMALL, width), b16)] * tensors,
        [
            pltpu.VMEM((flat_rows, local), f32),
            pltpu.VMEM((flat_rows, width), f32),
            pltpu.VMEM((4 * local, width), f32),
            pltpu.VMEM((rows, width), f32),
        ],
        limit=20,
        flops=6_000_000_000,
    )
    combined = residual
    for part in gated_back:
        combined = combined + part.astype(f32)
    combined = combined.astype(b16)
    own_piece, *pieces = kernel_call(
        add_core_kernel,
        "add_core",
        position,
        [keep, swap_core(send)],
        [like((piece, width), f32)] + [like((piece, width), b16)] * (owners - 1),
        limit=8,
    )
    reduced = [ring(p, k + 1) for k, p in enumerate(pieces)]
    got = [parts[0]] + [cross(parts[j], j) for j in range(1, tensors)]
    grad_chunk, summed = kernel_call(
        functools.partial(norm_back_kernel, experts, tensors),
        "norm_back",
        position,
        [*got, x_chunk, residual_grad, params, own_piece, *reduced],
        [like((chunk, width), b16), like((piece + 2 * SMALL, width), b16)],
        [pltpu.VMEM((tensors, SMALL, width), f32)],
        limit=8,
    )
    up_x, up_y = kernel_call(
        second_step_kernel,
        "second_step",
        after(position, summed),
        [near_grad, from_y, from_x],
        [like((2, quarter, width), b16)] * 2,
        limit=8,
    )
    last_x, last_y = cross(up_x, 1), cross(up_y, 2)

    around = [summed] + [ring(summed, k) for k in range(1, owners)]
    grad_rows = lax.all_gather(grad_chunk, "tensor", axis=0, tiled=True)
    combined = after(combined, grad_rows)
    grad_tokens = kernel_call(
        images_kernel,
        "grad_tokens",
        after(position, around),
        [grad_rows],
        [like(tokens.shape, f32)],
        [pltpu.VMEM((padded, width), f32)],
        limit=8,
    )[0]
    block_out = kernel_call(
        images_kernel,
        "block_out",
        position,
        [combined] + [cross(combined, j) for j in range(1, tensors)],
        [like(tokens.shape, b16)],
        [pltpu.VMEM((padded, width), f32)],
        limit=8,
    )[0]
    grad_half = kernel_call(
        weight_sum_kernel,
        "weight_sum",
        after(position, grad_tokens),
        [own_grad, from_y, from_x, last_x, last_y],
        [like((2, half, width), b16)],
        limit=8,
    )[0]
    grad_expert_in, grad_expert_out = kernel_call(
        weight_out_kernel,
        "weight_out",
        position,
        [grad_half, swap_core(grad_half)],
        [like((1, width, 2 * half), f32), like((1, 2 * half, width), f32)],
        limit=10,
    )
    token_total = token_rows * cores * owners
    grad_qkv, grad_out, small, loss = kernel_call(
        functools.partial(spread_kernel, owners, experts, token_total),
        "spread",
        position,
        around + [swap_core(a) for a in around],
        [
            like((3 * local, width), f32),
            like((local, width), f32),
            like((SMALL, width), f32),
            like((SMALL, LANES), f32),
        ],
        [
            pltpu.VMEM((4 * local, width), f32),
            pltpu.VMEM((2 * owners, SMALL, width), f32),
        ],
        limit=8,
    )
    return (
        block_out,
        grad_tokens,
        grad_qkv.reshape(3, local, width).transpose(0, 2, 1),
        grad_out,
        small[:experts].T,
        grad_expert_in,
        grad_expert_out,
        small[SMALL - 1],
        small[experts],
        loss[0, 0],
    )


def solution(mesh):
    placed = (
        P(("dp", "expert"), None, None),
        P(("dp", "expert"), None, None),
        P(("dp", "expert"), None, None),
        P(("dp", "expert"), None, None),
        P(None, None, "tensor"),
        P("tensor", None),
        P(),
        P("expert", None, "tensor"),
        P("expert", "tensor", None),
        P(),
        P(),
    )
    shape = mesh.shape
    dense = shape["dp"] == 2 and shape["expert"] == 4 and shape["tensor"] == 4
    return jax.shard_map(
        dense_body if dense else body,
        mesh=mesh,
        in_specs=placed,
        out_specs=(
            P(("dp", "expert"), None, None),
            P(("dp", "expert"), None, None),
            P(None, None, "tensor"),
            P("tensor", None),
            P(),
            P("expert", None, "tensor"),
            P("expert", "tensor", None),
            P(),
            P(),
            P(),
        ),
        check_vma=False,
    )
```

```python
import functools
import math

import jax
import jax.numpy as jnp
from jax import lax
from jax.experimental import pallas as pl
from jax.experimental.pallas import tpu as pltpu
from jax.sharding import PartitionSpec as P

HD = 64


epsilon = 1e-06


def normalize(values, gain_row):
    center = values - jnp.mean(values, axis=-1, keepdims=True)
    inverse = lax.rsqrt(jnp.mean(center * center, axis=-1, keepdims=True) + epsilon)
    normed = center * inverse
    return (normed, inverse, normed * gain_row)


def normalize_back(upstream, normed, inverse, gain_row):
    scaled = upstream * gain_row
    result = inverse * (
        scaled
        - jnp.mean(scaled, axis=-1, keepdims=True)
        - normed * jnp.mean(scaled * normed, axis=-1, keepdims=True)
    )
    return (result, jnp.sum(upstream * normed, axis=0))


def exact_gelu(values):
    return jax.nn.gelu(values, approximate=False)


def body(
    tokens,
    cotangent,
    expert_ids,
    slot_rank,
    qkv_weight,
    out_weight,
    router_weight,
    expert_in,
    expert_out,
    gain_attention,
    gain_experts,
):
    images, seq_len, model_width = tokens.shape
    token_rows = images * seq_len
    local_width = qkv_weight.shape[2]
    local_heads = local_width // HD
    slice_width = model_width // lax.axis_size("tensor")
    experts = router_weight.shape[1]
    capacity = 5 * token_rows // (2 * experts)
    owners = lax.axis_size("expert")
    per_owner = experts // owners
    slot_total = experts * capacity
    score_scale = HD ** (-0.5)
    inputs = tokens.reshape(token_rows, model_width).astype(jnp.float32)
    normed_one, inverse_one, mixed_one = normalize(inputs, gain_attention)
    entered = mixed_one.astype(jnp.bfloat16)
    project = jnp.einsum(
        "td,cdf->ctf", entered, qkv_weight, preferred_element_type=jnp.float32
    ).astype(jnp.bfloat16)
    projected_heads = project.reshape(3, images, seq_len, local_heads, HD)
    queries, key_rows, value_rows = (projected_heads[0], projected_heads[1], projected_heads[2])
    scores = (
        jnp.einsum("ishe,ithe->ihst", queries, key_rows, preferred_element_type=jnp.float32)
        * score_scale
    )
    log_total = jax.nn.logsumexp(scores, axis=-1, keepdims=True)
    attn_probs = jnp.exp(scores - log_total).astype(jnp.bfloat16)
    attended = jnp.einsum(
        "ihst,ithe->ishe", attn_probs, value_rows, preferred_element_type=jnp.float32
    )
    attended = attended.astype(jnp.bfloat16).reshape(token_rows, local_width)
    attn_part = jnp.dot(attended, out_weight, preferred_element_type=jnp.float32)
    residual = inputs + lax.psum(attn_part, "tensor")
    normed_two, inverse_two, mixed_two = normalize(residual, gain_experts)
    routed = mixed_two.astype(jnp.bfloat16)
    route_prob = jax.nn.softmax(
        jnp.dot(routed, router_weight, preferred_element_type=jnp.float32), axis=-1
    )
    chosen = expert_ids.reshape(token_rows, 2)
    ranked = slot_rank.reshape(token_rows, 2)
    kept_mask = (ranked >= 0).astype(jnp.float32)
    position = jnp.where(ranked >= 0, chosen * capacity + ranked, slot_total).reshape(-1)
    send_rows = (
        jnp.zeros((slot_total, model_width), jnp.bfloat16)
        .at[position]
        .set(jnp.repeat(routed, 2, axis=0), mode="drop")
        .reshape(experts, capacity, model_width)
    )
    fragment = lax.all_to_all(send_rows, "expert", split_axis=0, concat_axis=0, tiled=True)
    grouped = fragment.reshape(owners, per_owner, fragment.shape[1], model_width)
    before = jnp.einsum("sjcd,jdf->sjcf", grouped, expert_in, preferred_element_type=jnp.float32)
    hidden = exact_gelu(before).astype(jnp.bfloat16)
    expert_part = jnp.einsum(
        "sjcf,jfd->sjcd", hidden, expert_out, preferred_element_type=jnp.float32
    )
    produced = lax.psum_scatter(expert_part, "tensor", scatter_dimension=3, tiled=True).astype(
        jnp.bfloat16
    )
    returned = lax.all_to_all(
        produced.reshape(experts, capacity, slice_width),
        "expert",
        split_axis=0,
        concat_axis=0,
        tiled=True,
    )
    returned = lax.all_gather(returned, "tensor", axis=2, tiled=True).reshape(
        slot_total, model_width
    )
    safe_index = jnp.minimum(position, slot_total - 1)
    picked = returned[safe_index].reshape(token_rows, 2, model_width).astype(jnp.float32)
    gate_values = jnp.take_along_axis(route_prob, chosen, axis=1) * kept_mask
    output = residual + jnp.sum(gate_values[:, :, None] * picked, axis=1)
    block_out = output.astype(jnp.bfloat16).reshape(images, seq_len, model_width)
    upstream = cotangent.reshape(token_rows, model_width).astype(jnp.float32)
    gate_grad = jnp.sum(upstream[:, None, :] * picked, axis=-1) * kept_mask
    member = (chosen[:, :, None] == jnp.arange(experts)[None, None, :]).astype(jnp.float32)
    route_grad = jnp.sum(member * gate_grad[:, :, None], axis=1)
    logit_grad = (
        route_prob * (route_grad - jnp.sum(route_grad * route_prob, axis=-1, keepdims=True))
    ).astype(jnp.bfloat16)
    row_grad = (
        (gate_values[:, :, None] * upstream[:, None, :])
        .astype(jnp.bfloat16)
        .reshape(2 * token_rows, model_width)
    )
    grad_send = (
        jnp.zeros((slot_total, model_width), jnp.bfloat16)
        .at[position]
        .set(row_grad, mode="drop")
        .reshape(experts, capacity, model_width)
    )
    grad_arrived = lax.all_to_all(grad_send, "expert", split_axis=0, concat_axis=0, tiled=True)
    grad_arrived = grad_arrived.reshape(owners, per_owner, capacity, model_width)
    hidden_grad = jnp.einsum(
        "sjcd,jfd->sjcf", grad_arrived, expert_out, preferred_element_type=jnp.float32
    )
    grad_expert_out = jnp.einsum(
        "sjcf,sjcd->jfd", hidden, grad_arrived, preferred_element_type=jnp.float32
    )
    pre_grad = jax.vjp(exact_gelu, before)[1](hidden_grad)[0].astype(jnp.bfloat16)
    grad_expert_in = jnp.einsum(
        "sjcd,sjcf->jdf", grouped, pre_grad, preferred_element_type=jnp.float32
    )
    buffer_part = jnp.einsum(
        "sjcf,jdf->sjcd", pre_grad, expert_in, preferred_element_type=jnp.float32
    )
    buffer_share = lax.psum_scatter(buffer_part, "tensor", scatter_dimension=3, tiled=True).astype(
        jnp.bfloat16
    )
    buffer_back = lax.all_to_all(
        buffer_share.reshape(experts, capacity, slice_width),
        "expert",
        split_axis=0,
        concat_axis=0,
        tiled=True,
    )
    buffer_grad = lax.all_gather(buffer_back, "tensor", axis=2, tiled=True).reshape(
        slot_total, model_width
    )
    routed_grad = jnp.sum(
        buffer_grad[safe_index].reshape(token_rows, 2, model_width).astype(jnp.float32)
        * kept_mask[:, :, None],
        axis=1,
    )
    routed_grad = routed_grad + jnp.dot(
        logit_grad, router_weight.T, preferred_element_type=jnp.float32
    )
    grad_router = jnp.einsum("td,te->de", routed, logit_grad, preferred_element_type=jnp.float32)
    from_norm_two, grad_gain_experts = normalize_back(
        routed_grad, normed_two, inverse_two, gain_experts
    )
    residual_grad = upstream + from_norm_two
    attn_grad = residual_grad.astype(jnp.bfloat16)
    grad_out = jnp.einsum("tf,td->fd", attended, attn_grad, preferred_element_type=jnp.float32)
    heads_grad = jnp.dot(attn_grad, out_weight.T, preferred_element_type=jnp.float32).astype(
        jnp.bfloat16
    )
    heads_grad = heads_grad.reshape(images, seq_len, local_heads, HD)
    again = (
        jnp.einsum("ishe,ithe->ihst", queries, key_rows, preferred_element_type=jnp.float32)
        * score_scale
    )
    probs_full = jnp.exp(again - log_total)
    prob_grad = jnp.einsum(
        "ishe,ithe->ihst", heads_grad, value_rows, preferred_element_type=jnp.float32
    )
    value_grad = jnp.einsum(
        "ihst,ishe->ithe",
        probs_full.astype(jnp.bfloat16),
        heads_grad,
        preferred_element_type=jnp.float32,
    )
    score_grad = (
        probs_full * (prob_grad - jnp.sum(prob_grad * probs_full, axis=-1, keepdims=True))
    ).astype(jnp.bfloat16)
    query_grad = (
        jnp.einsum("ihst,ithe->ishe", score_grad, key_rows, preferred_element_type=jnp.float32)
        * score_scale
    )
    key_grad = (
        jnp.einsum("ihst,ishe->ithe", score_grad, queries, preferred_element_type=jnp.float32)
        * score_scale
    )
    project_grad = (
        jnp.stack([query_grad, key_grad, value_grad])
        .astype(jnp.bfloat16)
        .reshape(3, token_rows, local_width)
    )
    grad_qkv = jnp.einsum("td,ctf->cdf", entered, project_grad, preferred_element_type=jnp.float32)
    entered_part = jnp.einsum(
        "ctf,cdf->td", project_grad, qkv_weight, preferred_element_type=jnp.float32
    )
    entered_grad = lax.psum(entered_part.astype(jnp.bfloat16), "tensor").astype(jnp.float32)
    from_norm_one, grad_gain_attention = normalize_back(
        entered_grad, normed_one, inverse_one, gain_attention
    )
    grad_tokens = (residual_grad + from_norm_one).reshape(images, seq_len, model_width)
    counts = jnp.sum(member, axis=(0, 1))
    prob_sum = jnp.sum(route_prob, axis=0)
    grad_qkv, grad_out, grad_router, grad_gain_attention, grad_gain_experts, counts, prob_sum = (
        lax.psum(
            (
                grad_qkv,
                grad_out,
                grad_router,
                grad_gain_attention,
                grad_gain_experts,
                counts,
                prob_sum,
            ),
            ("dp", "expert"),
        )
    )
    grad_expert_in, grad_expert_out = (
        lax.psum(grad_expert_in.astype(jnp.bfloat16), "dp").astype(jnp.float32),
        lax.psum(grad_expert_out.astype(jnp.bfloat16), "dp").astype(jnp.float32),
    )
    token_total = token_rows * lax.axis_size("dp") * lax.axis_size("expert")
    balance_loss = experts * jnp.sum(counts / (2.0 * token_total) * prob_sum / token_total)
    return (
        block_out,
        grad_tokens,
        grad_qkv,
        grad_out,
        grad_router,
        grad_expert_in,
        grad_expert_out,
        grad_gain_attention,
        grad_gain_experts,
        balance_loss,
    )


NN = ((1,), (0,))
NT = ((1,), (1,))
TN = ((0,), (0,))
LANES = 128
SMALL = 8


def round_up(value, step):
    return -(-value // step) * step


def contract(a, b, dims):
    return lax.dot_general(a, b, (dims, ((), ())), preferred_element_type=jnp.float32)


def load_then(kernel, loads, count, *refs):
    pos_ref, *refs = refs
    *refs, sem = refs
    buffers = refs[len(refs) - len(loads) :]
    refs = refs[: len(refs) - len(loads)]
    copies = [
        pltpu.make_async_copy(refs[index], buffer, sem.at[i])
        for i, (index, buffer) in enumerate(zip(loads, buffers))
    ]
    for copy in copies:
        copy.start()
    for copy in copies:
        copy.wait()
    for index, buffer in zip(loads, buffers):
        refs[index] = buffer
    kernel(pos_ref, *refs)


def kernel_call(kernel, name, position, args, outs, scratch=(), flops=0, limit=24, loads=()):
    if loads:
        kernel = functools.partial(load_then, kernel, loads, len(args))
        scratch = [
            *scratch,
            *(pltpu.VMEM(args[i].shape, args[i].dtype) for i in loads),
            pltpu.SemaphoreType.DMA((len(loads),)),
        ]
    places = [pltpu.HBM if i in loads else pltpu.VMEM for i in range(len(args))]
    return pl.pallas_call(
        kernel,
        in_specs=[pl.BlockSpec(memory_space=pltpu.SMEM)]
        + [pl.BlockSpec(memory_space=place) for place in places],
        out_specs=[pl.BlockSpec(memory_space=pltpu.VMEM)] * len(outs),
        out_shape=list(outs),
        scratch_shapes=list(scratch),
        compiler_params=pltpu.CompilerParams(vmem_limit_bytes=limit << 20),
        cost_estimate=pl.CostEstimate(flops=flops, bytes_accessed=0, transcendentals=0),
        name=name,
    )(position, *args)


def like(shape, dtype):
    return jax.ShapeDtypeStruct(shape, dtype)


def live_rows(shape, limit, offset=0):
    return lax.broadcasted_iota(jnp.int32, shape, 0) + offset < limit


def chunk_of(pos_ref, j, size):
    return pl.ds(pl.multiple_of(lax.bitwise_xor(pos_ref[2], j) * size, 16), size)


def head_masks(rows, heads):
    lane = lax.broadcasted_iota(jnp.int32, (rows, heads * HD), 1)
    return [(lane >= h * HD) & (lane < (h + 1) * HD) for h in range(heads)]


def keep_lanes(value, mask):
    return jnp.where(mask, value, jnp.zeros_like(value))


def split_high_low(value):
    high = value.astype(jnp.bfloat16)
    return high, (value - high.astype(jnp.float32)).astype(jnp.bfloat16)


def image_rows(ref, i, scratch_ref):
    seq_len = ref.shape[1]
    scratch_ref[seq_len:, :] = jnp.zeros((scratch_ref.shape[0] - seq_len, ref.shape[2]), jnp.float32)
    scratch_ref[0:seq_len, :] = ref[i].astype(jnp.float32)
    return scratch_ref[...]


def router_matrix(param_ref, experts):
    rows = param_ref[0:SMALL, :]
    rows = jnp.where(live_rows(rows.shape, experts), rows, 0.0).astype(jnp.bfloat16)
    zeros = jnp.zeros((LANES - SMALL, rows.shape[1]), jnp.bfloat16)
    return jnp.concatenate([rows, zeros], axis=0)


def weights_kernel(pos_ref, in_ref, out_ref, mine_ref, first_ref, second_ref):
    half = mine_ref.shape[1]
    quarter = half // 2
    start = pl.multiple_of(pos_ref[0] * half, LANES)
    for s, rows in (
        (0, in_ref[0, :, pl.ds(start, half)].T),
        (1, out_ref[0, pl.ds(start, half), :]),
    ):
        mine_ref[s] = rows
        first_ref[s] = rows[0:quarter]
        second_ref[s] = rows[quarter:]


def chunk_kernel(
    tensors, pos_ref, tok_ref, cot_ref, ids_ref, rank_ref, router_ref, one_ref, two_ref, x_ref, pay_ref,
    param_ref, flat_ref, kept_ref,
):
    images, seq_len, width = tok_ref.shape
    chunk, experts = x_ref.shape[0], router_ref.shape[0]
    start = pl.multiple_of(pos_ref[2] * chunk, 16)
    for source, target in ((tok_ref, x_ref), (cot_ref, pay_ref)):
        flat_ref[images * seq_len :, :] = jnp.zeros(
            (flat_ref.shape[0] - images * seq_len, width), jnp.float32
        )
        for i in range(images):
            flat_ref[pl.ds(i * seq_len, seq_len), :] = source[i].astype(jnp.float32)
        target[:, :width] = flat_ref[pl.ds(start, chunk), :].astype(jnp.bfloat16)
    kept_ref[...] = jnp.zeros_like(kept_ref)
    counts = jnp.zeros((1, LANES), jnp.float32)
    for i in range(images):
        rows, all_rows = [], []
        for e in range(experts):
            named = (ids_ref[i] == e).astype(jnp.float32)
            kept = jnp.where(rank_ref[i] >= 0, named, 0.0)
            rows.append(jnp.sum(kept, axis=0, keepdims=True))
            all_rows.append(jnp.sum(named, axis=0, keepdims=True))
        for group, is_kept in ((rows, True), (all_rows, False)):
            table = jnp.concatenate(group, axis=0)
            table = jnp.concatenate(
                [table, jnp.zeros((LANES - experts, seq_len), jnp.float32)], axis=0
            )
            table = jnp.concatenate(
                [table, jnp.zeros((LANES, 2 * LANES - seq_len), jnp.float32)], axis=1
            ).T
            if is_kept:
                kept_ref[pl.ds(i * seq_len, 2 * LANES), :] = table
            else:
                counts = counts + jnp.sum(table, axis=0, keepdims=True)
    pay_ref[:, width:] = kept_ref[pl.ds(start, chunk), :].astype(jnp.bfloat16)
    param_ref[...] = jnp.zeros_like(param_ref)
    param_ref[0:experts, :] = router_ref[...].astype(jnp.float32)
    param_ref[experts : experts + 1, :] = one_ref[...].reshape(1, width)
    param_ref[experts + 1 : experts + 2, :] = two_ref[...].reshape(1, width)
    param_ref[SMALL - 1 : SMALL, :LANES] = counts * (1.0 / tensors)


def stack_kernel(pos_ref, *refs):
    count = len(refs) // 3
    for i, target in enumerate(refs[2 * count :]):
        target[0] = refs[2 * i][...]
        target[1] = refs[2 * i + 1][...]


def stack_pairs(position, *pairs):
    return kernel_call(
        stack_kernel,
        "stack",
        position,
        [value for pair in pairs for value in pair],
        [like((2, *pair[0].shape), pair[0].dtype) for pair in pairs],
        limit=4,
    )


def gain_row(param_ref, experts, which):
    return param_ref[experts + which : experts + which + 1, :]


def attention_kernel(
    heads, experts, pos_ref, tok_ref, param_ref, w_ref, wo_ref, qkv_ref, lse_ref, att_ref, *refs,
):
    *parts, flat_ref, image_ref, held_ref = refs
    images, rows, width = qkv_ref.shape[1], qkv_ref.shape[2], heads * HD
    seq_len = tok_ref.shape[1]
    masks = head_masks(rows, heads)
    keys_live = lax.broadcasted_iota(jnp.int32, (rows, rows), 1) < seq_len
    lane = lax.broadcasted_iota(jnp.int32, (rows, LANES), 1)
    flat_ref[images * seq_len :, :] = jnp.zeros(
        (flat_ref.shape[0] - images * seq_len, width), jnp.float32
    )

    @pl.loop(0, images)
    def _(i):
        entered = normalize(image_rows(tok_ref, i, image_ref), gain_row(param_ref, experts, 0))[2]
        entered = entered.astype(jnp.bfloat16)
        q, k, v = (
            contract(entered, w_ref[c * width : (c + 1) * width, :], NT).astype(jnp.bfloat16)
            for c in range(3)
        )
        qkv_ref[0, i], qkv_ref[1, i], qkv_ref[2, i] = q, k, v
        attended = jnp.zeros((rows, width), jnp.float32)
        lse_all = jnp.zeros((rows, LANES), jnp.float32)
        for h in range(heads):
            scores = contract(keep_lanes(q, masks[h]), k, NT) * (HD ** (-0.5))
            scores = jnp.where(keys_live, scores, -1e30)
            top = jnp.max(scores, axis=-1, keepdims=True)
            lse = top + jnp.log(jnp.sum(jnp.exp(scores - top), axis=-1, keepdims=True))
            probs = jnp.exp(scores - lse).astype(jnp.bfloat16)
            attended = attended + contract(probs, keep_lanes(v, masks[h]), NN)
            lse_all = jnp.where(lane == h, lse, lse_all)
        lse_ref[i] = lse_all
        held_ref[i] = attended

    for i in range(images):
        flat_ref[pl.ds(i * seq_len, seq_len), :] = held_ref[i, 0:seq_len, :]
    att_ref[...] = flat_ref[...].astype(jnp.bfloat16)
    for j, part in enumerate(parts):
        rows_j = flat_ref[chunk_of(pos_ref, j, part.shape[0]), :].astype(jnp.bfloat16)
        part[...] = contract(rows_j, wo_ref[...], NN).astype(jnp.bfloat16)


def route_kernel(experts, pos_ref, *refs):
    *got, x_ref, param_ref, res_ref, routed_ref, prob_ref = refs
    residual = x_ref[...].astype(jnp.float32)
    for part in got:
        residual = residual + part[...].astype(jnp.float32)
    res_ref[...] = residual
    routed = normalize(residual, gain_row(param_ref, experts, 1))[2].astype(jnp.bfloat16)
    routed_ref[...] = routed
    prob_ref[...] = route_probs(routed, router_matrix(param_ref, experts), experts)


def route_probs(rows, router, experts):
    logits = contract(rows, router, NT)
    lane = lax.broadcasted_iota(jnp.int32, logits.shape, 1)
    logits = jnp.where(lane < experts, logits, -1e30)
    weight = jnp.exp(logits - jnp.max(logits, axis=-1, keepdims=True))
    return weight / jnp.sum(weight, axis=-1, keepdims=True)


def gelu_parts(x):
    square = jnp.exp(-0.5 * x * x)
    share = 0.5 * (1.0 + lax.erf(x * (0.5**0.5)))
    return x * share, share + x * square * (0.5 / math.pi) ** 0.5


def expert_halves(x, rg, w_in, w_out, hidden_ref, pre_ref):
    before = contract(x, w_in, NT)
    value, slope = gelu_parts(before)
    hidden = value.astype(jnp.bfloat16)
    hidden_ref[...] = hidden
    part = contract(hidden, w_out, NN)
    pre = (contract(rg, w_out, NT) * slope).astype(jnp.bfloat16)
    pre_ref[...] = pre
    return part, contract(pre, w_in, NN)


def first_expert_kernel(experts, owners, pos_ref, *refs):
    blocks = refs[:owners]
    pay_refs, param_ref, w0_ref, xa_ref, yb_ref = refs[owners : 2 * owners], *refs[2 * owners :][:4]
    hidden_ref, pre_ref, x_ref, rg_ref, dy_ref, gate_ref, part_ref, back_ref = refs[2 * owners + 4 :]
    chunk, width = blocks[0].shape
    router = router_matrix(param_ref, experts)
    for k in range(owners):
        here = pl.ds(k * chunk, chunk)
        pay = pay_refs[k]
        rows = blocks[k][...]
        x_ref[here, :] = rows
        prob = route_probs(rows, router, experts)
        mine = lax.broadcasted_iota(jnp.int32, prob.shape, 1) == pos_ref[1]
        kept = pay[:, width:].astype(jnp.float32)
        kept = jnp.sum(jnp.where(mine, kept, 0.0), axis=-1, keepdims=True)
        gate = jnp.sum(jnp.where(mine, prob, 0.0), axis=-1, keepdims=True) * kept
        gate_ref[here, :LANES] = jnp.broadcast_to(gate, (chunk, LANES))
        gate_ref[here, LANES:] = jnp.broadcast_to(kept, (chunk, LANES))
        dy = pay[:, :width]
        dy_ref[here, :] = dy
        rg_ref[here, :] = (gate * dy.astype(jnp.float32)).astype(jnp.bfloat16)
    w_in, w_out = (
        jnp.concatenate([w0_ref[s], xa_ref[s], yb_ref[s]], axis=0) for s in range(2)
    )
    part_ref[...], back_ref[...] = expert_halves(
        x_ref[...], rg_ref[...], w_in, w_out, hidden_ref, pre_ref
    )


def second_expert_kernel(
    owners, pos_ref, x_ref, rg_ref, dy_ref, gate_ref, part_in_ref, back_in_ref, pair_y_ref,
    pair_x_ref, hidden_ref, pre_ref, gated_ref, back_ref, part_ref,
):
    width = x_ref.shape[1]
    chunk = x_ref.shape[0] // owners
    w_in, w_out = (
        jnp.concatenate([ref[r, s] for ref in (pair_y_ref, pair_x_ref) for r in range(2)], axis=0)
        for s in range(2)
    )
    part, back = expert_halves(x_ref[...], rg_ref[...], w_in, w_out, hidden_ref, pre_ref)
    part_ref[...] = part_in_ref[...] + part
    back_ref[:, :width] = back_in_ref[...] + back
    for k in range(owners):
        here = pl.ds(k * chunk, chunk)
        total = part_ref[here, :]
        gated_ref[here, :] = (gate_ref[here, 0:1] * total).astype(jnp.bfloat16)
        inner = jnp.sum(total * dy_ref[here, :].astype(jnp.float32), axis=-1, keepdims=True)
        back_ref[here, width:] = gate_ref[here, LANES:] * inner


def first_expert_pass(position, blocks, payload, params, weights, experts):
    chunk, width = blocks[0].shape
    count, hidden = len(blocks) * chunk, 2 * weights[0].shape[1]
    return kernel_call(
        functools.partial(first_expert_kernel, experts, len(blocks)),
        "experts_first",
        position,
        [*blocks, *payload, params, *weights],
        [
            like((count, hidden), jnp.bfloat16),
            like((count, hidden), jnp.bfloat16),
            like((count, width), jnp.bfloat16),
            like((count, width), jnp.bfloat16),
            like((count, width), jnp.bfloat16),
            like((count, 2 * LANES), jnp.float32),
            like((count, width), jnp.float32),
            like((count, width), jnp.float32),
        ],
        limit=16,
    )


def second_expert_pass(position, first, weights, owners):
    x, rg, dy, gate, part, back = first[2:]
    count, width = x.shape
    hidden = 4 * weights[0].shape[2]
    return kernel_call(
        functools.partial(second_expert_kernel, owners),
        "experts_second",
        position,
        [x, rg, dy, gate, part, back, *weights],
        [
            like((count, hidden), jnp.bfloat16),
            like((count, hidden), jnp.bfloat16),
            like((count, width), jnp.bfloat16),
            like((count, width + LANES), jnp.float32),
        ],
        [pltpu.VMEM((count, width), jnp.float32)],
        limit=16,
    )


def join_kernel(pos_ref, back_ref, other_ref, gated_ref, gated_other_ref, *outs):
    owners = len(outs) // 2
    chunk, width = outs[owners].shape
    for k in range(owners):
        here = pl.ds(k * chunk, chunk)
        total = back_ref[here, :] + other_ref[here, :]
        outs[k][0:chunk, :] = total[:, :width].astype(jnp.bfloat16)
        inner = jnp.concatenate(
            [total[:, width:], jnp.zeros((2 * LANES - chunk, LANES), jnp.float32)], axis=0
        ).T
        high, low = split_high_low(inner[0:SMALL, :])
        outs[k][chunk:, : 2 * LANES] = jnp.concatenate([high, low], axis=0)
        outs[k][chunk:, 2 * LANES :] = jnp.zeros((2 * SMALL, width - 2 * LANES), jnp.bfloat16)
        outs[owners + k][...] = (
            gated_ref[here, :].astype(jnp.float32) + gated_other_ref[here, :].astype(jnp.float32)
        ).astype(jnp.bfloat16)


def expert_grad_kernel(pos_ref, *refs):
    *sources, first_ref, second_ref = refs
    part_rows = first_ref.shape[2]
    for j, out in enumerate((first_ref, second_ref)):
        columns = slice(2 * j * part_rows, 2 * (j + 1) * part_rows)
        for s in range(2):
            left_a, right_a, left_b, right_b = sources[4 * s : 4 * s + 4]
            grad = contract(left_a[:, columns], right_a[...], TN)
            grad = grad + contract(left_b[:, columns], right_b[...], TN)
            grad = grad.astype(jnp.bfloat16)
            out[0, s] = grad[0:part_rows]
            out[1, s] = grad[part_rows:]


def expert_grads(position, a, b, rows_a, rows_b):
    width, total = rows_a[0].shape[1], a[0].shape[1]
    return kernel_call(
        expert_grad_kernel,
        "expert_grads",
        position,
        [a[1], rows_a[0], b[1], rows_b[0], a[0], rows_a[1], b[0], rows_b[1]],
        [like((2, 2, total // 4, width), jnp.bfloat16)] * 2,
        limit=10,
    )


def route_back_kernel(
    experts, token_rows, owners, pos_ref, *refs
):
    backs = refs[:owners]
    prob_ref, res_ref, pay_ref, param_ref = refs[owners : owners + 4]
    grad_ref, up_ref, small_ref = refs[owners + 4 :]
    chunk, width = res_ref.shape
    prob = prob_ref[...]
    lane = lax.broadcasted_iota(jnp.int32, prob.shape, 1)
    route_grad = jnp.zeros_like(prob)
    routed_grad = jnp.zeros((chunk, width), jnp.float32)
    for k, back in enumerate(backs):
        owner = lax.bitwise_xor(pos_ref[1], k)
        inner = back[chunk : chunk + SMALL, : 2 * LANES].astype(jnp.float32)
        inner = inner + back[chunk + SMALL :, : 2 * LANES].astype(jnp.float32)
        inner = jnp.concatenate([inner] * (LANES // SMALL), axis=0).T[0:chunk]
        route_grad = jnp.where(lane == owner, inner, route_grad)
        routed_grad = routed_grad + back[0:chunk, :].astype(jnp.float32)
    mean = jnp.sum(route_grad * prob, axis=-1, keepdims=True)
    logit_grad = (prob * (route_grad - mean)).astype(jnp.bfloat16)
    routed_grad = routed_grad + contract(
        logit_grad, router_matrix(param_ref, experts), NN
    )
    normed, inverse, mixed = normalize(res_ref[...], gain_row(param_ref, experts, 1))
    from_norm, gain_grad = normalize_back(
        routed_grad, normed, inverse, gain_row(param_ref, experts, 1)
    )
    total = pay_ref[:, :width].astype(jnp.float32) + from_norm
    grad_ref[...] = total
    up_ref[...] = total.astype(jnp.bfloat16)
    live = live_rows(prob.shape, token_rows, pos_ref[2] * chunk)
    prob_sum = jnp.sum(jnp.where(live, prob, 0.0), axis=0, keepdims=True)
    grad_router = contract(logit_grad, mixed.astype(jnp.bfloat16), TN)
    small_ref[0:SMALL, :] = grad_router[0:SMALL]
    small_ref[experts : experts + 1, :] = gain_grad[None]
    small_ref[experts + 1 : experts + 2, :] = jnp.zeros((1, width), jnp.float32)
    small_ref[experts + 1 : experts + 2, :LANES] = prob_sum
    small_ref[experts + 2 : experts + 3, :] = param_ref[SMALL - 1 : SMALL, :]


def attention_back_kernel(
    heads, experts, owners, pos_ref, tok_ref, param_ref, w_ref, wo_ref, qkv_ref, lse_ref, att_ref,
    up_ref, small_ref, keep_ref, send_ref, *refs,
):
    *parts, hg_ref, flat_ref, big_ref, image_ref, held_ref, sum_ref, gain_ref = refs
    images, rows, width = qkv_ref.shape[1], qkv_ref.shape[2], heads * HD
    seq_len = tok_ref.shape[1]
    scale = HD ** (-0.5)
    padded, model = up_ref.shape
    chunk = padded // len(parts)
    masks = head_masks(rows, heads)
    keys_live = lax.broadcasted_iota(jnp.int32, (rows, rows), 1) < seq_len
    lane = lax.broadcasted_iota(jnp.int32, (rows, LANES), 1)
    up = up_ref[...]
    hg_ref[0:padded, :] = contract(up, wo_ref[...], NT)
    hg_ref[padded:, :] = jnp.zeros((hg_ref.shape[0] - padded, width), jnp.float32)
    big_ref[3 * width :, :] = contract(att_ref[...], up, TN)
    flat_ref[images * seq_len :, :] = jnp.zeros(
        (flat_ref.shape[0] - images * seq_len, model), jnp.float32
    )
    for i in range(images):
        held_ref[i] = hg_ref[pl.ds(i * seq_len, rows), :]
    big_ref[0 : 3 * width, :] = jnp.zeros((3 * width, model), jnp.float32)

    @pl.loop(0, images)
    def _(i):
        normed, _, mixed = normalize(
            image_rows(tok_ref, i, image_ref), gain_row(param_ref, experts, 0)
        )
        entered = mixed.astype(jnp.bfloat16)
        q, k, v = qkv_ref[0, i], qkv_ref[1, i], qkv_ref[2, i]
        heads_grad = held_ref[i]
        heads_grad = jnp.where(live_rows(heads_grad.shape, seq_len), heads_grad, 0.0)
        heads_grad = heads_grad.astype(jnp.bfloat16)
        dq = jnp.zeros((rows, width), jnp.float32)
        dk, dv = dq, dq
        for h in range(heads):
            q_h, k_h = keep_lanes(q, masks[h]), keep_lanes(k, masks[h])
            up_h = keep_lanes(heads_grad, masks[h])
            scores = contract(q_h, k, NT) * scale
            lse = jnp.sum(jnp.where(lane == h, lse_ref[i], 0.0), axis=-1, keepdims=True)
            probs = jnp.where(keys_live, jnp.exp(scores - lse), 0.0)
            prob_grad = contract(up_h, v, NT)
            total = jnp.sum(prob_grad * probs, axis=-1, keepdims=True)
            score_grad = (probs * (prob_grad - total)).astype(jnp.bfloat16)
            dv = dv + contract(probs.astype(jnp.bfloat16), up_h, TN)
            dq = dq + contract(score_grad, k_h, NN)
            dk = dk + contract(score_grad, q_h, TN)
        grads = [g.astype(jnp.bfloat16) for g in (dq * scale, dk * scale, dv)]
        part = jnp.zeros((rows, model), jnp.float32)
        for c in range(3):
            here = slice(c * width, (c + 1) * width)
            part = part + contract(grads[c], w_ref[here, :], NN)
            big_ref[here, :] += contract(grads[c], entered, TN)
        sum_ref[i] = part
        gain_ref[i] = jnp.broadcast_to(
            jnp.sum(part * normed, axis=0, keepdims=True), gain_ref.shape[1:]
        )

    gain_grad = jnp.zeros((1, model), jnp.float32)
    for i in range(images):
        flat_ref[pl.ds(i * seq_len, seq_len), :] = sum_ref[i, 0:seq_len, :]
        gain_grad = gain_grad + gain_ref[i, 0:1, :]
    high, low = split_high_low(
        jnp.concatenate([small_ref[0 : SMALL - 1, :], gain_grad], axis=0)
    )
    for j, part in enumerate(parts):
        part[0:chunk, :] = flat_ref[chunk_of(pos_ref, j, chunk), :].astype(jnp.bfloat16)
        part[chunk:, :] = jnp.concatenate([high, low], axis=0)
    me, core = pos_ref[1], pos_ref[0]
    piece = keep_ref.shape[1]
    for k in range(owners):
        place = lax.bitwise_xor(me, k) * piece
        mine = pl.ds(pl.multiple_of(core * owners * piece + place, 8), piece)
        other = pl.ds(pl.multiple_of((1 - core) * owners * piece + place, 8), piece)
        keep_ref[k] = big_ref[mine, :]
        send_ref[k] = big_ref[other, :].astype(jnp.bfloat16)


def norm_back_kernel(experts, tensors, pos_ref, *refs):
    got = refs[:tensors]
    x_ref, res_ref, param_ref, own_ref, *parts, grad_ref, out_ref, small_ref = refs[tensors:]
    chunk, width = x_ref.shape
    upstream = jnp.zeros((chunk, width), jnp.float32)
    for j, part in enumerate(got):
        upstream = upstream + part[0:chunk, :].astype(jnp.float32)
        small_ref[lax.bitwise_xor(pos_ref[2], j)] = part[chunk : chunk + SMALL, :].astype(
            jnp.float32
        ) + part[chunk + SMALL :, :].astype(jnp.float32)
    small = small_ref[0]
    for j in range(1, tensors):
        small = small + small_ref[j]
    gain = gain_row(param_ref, experts, 0)
    normed, inverse, _ = normalize(x_ref[...].astype(jnp.float32), gain)
    from_norm = normalize_back(upstream, normed, inverse, gain)[0]
    grad_ref[...] = (res_ref[...] + from_norm).astype(jnp.bfloat16)
    piece = own_ref.shape[0]
    total = own_ref[...]
    for part in parts:
        total = total + part[...].astype(jnp.float32)
    out_ref[0:piece, :] = total.astype(jnp.bfloat16)
    out_ref[piece:, :] = jnp.concatenate(split_high_low(small), axis=0)


def second_step_kernel(pos_ref, near_ref, from_y, from_x, x_ref, y_ref):
    for target, row, other in ((x_ref, 0, from_y), (y_ref, 1, from_x)):
        total = near_ref[row].astype(jnp.float32) + other[1].astype(jnp.float32)
        target[...] = total.astype(jnp.bfloat16)


def weight_sum_kernel(pos_ref, own_ref, from_y, from_x, last_x, last_y, out_ref):
    part_rows = last_x.shape[1]
    for row, other, last in ((0, from_y, last_x), (1, from_x, last_y)):
        total = own_ref[row].astype(jnp.float32) + other[0].astype(jnp.float32)
        total = total + last[...].astype(jnp.float32)
        out_ref[:, row * part_rows : (row + 1) * part_rows, :] = total.astype(jnp.bfloat16)


def add_core_kernel(pos_ref, keep_ref, other_ref, own_ref, *outs):
    total = keep_ref[...] + other_ref[...].astype(jnp.float32)
    own_ref[...] = total[0]
    for k, out in enumerate(outs):
        out[...] = total[k + 1].astype(jnp.bfloat16)


def spread_kernel(owners, experts, token_total, pos_ref, *refs):
    blocks = refs[: 2 * owners]
    qkv_ref, wo_ref, router_ref, one_ref, two_ref, loss_ref, big_ref, parts_ref = refs[2 * owners :]
    piece = blocks[0].shape[0] - 2 * SMALL
    core, me = pos_ref[0], pos_ref[1]
    for c in range(2):
        side = core if c == 0 else 1 - core
        for k in range(owners):
            block = blocks[c * owners + k]
            place = side * owners + lax.bitwise_xor(me, k)
            here = pl.ds(pl.multiple_of(place * piece, 8), piece)
            big_ref[here, :] = block[0:piece, :].astype(jnp.float32)
            parts_ref[place] = block[piece : piece + SMALL, :].astype(jnp.float32) + block[
                piece + SMALL :, :
            ].astype(jnp.float32)
    rows = qkv_ref.shape[0]
    qkv_ref[...] = big_ref[0:rows, :]
    wo_ref[...] = big_ref[rows:, :]
    small = parts_ref[0]
    for p in range(1, 2 * owners):
        small = small + parts_ref[p]
    router_ref[...] = small[0:experts, :]
    one_ref[...] = small[SMALL - 1 : SMALL, :].reshape(small.shape[1])
    two_ref[...] = small[experts : experts + 1, :].reshape(small.shape[1])
    product = small[experts + 1 : experts + 2, :LANES] * small[experts + 2 : experts + 3, :LANES]
    lane = lax.broadcasted_iota(jnp.int32, product.shape, 1)
    product = jnp.where(lane < experts, product, 0.0)
    loss = jnp.sum(product, axis=-1, keepdims=True)
    loss_ref[...] = jnp.broadcast_to(
        loss * (experts / (2.0 * token_total * token_total)), loss_ref.shape
    )


def images_kernel(pos_ref, *refs):
    *chunks, out_ref, flat_ref = refs
    images, seq_len, _ = out_ref.shape
    if len(chunks) == 1:
        flat_ref[...] = chunks[0][...].astype(jnp.float32)
    else:
        for j, part in enumerate(chunks):
            flat_ref[chunk_of(pos_ref, j, part.shape[0]), :] = part[...].astype(jnp.float32)
    for i in range(images):
        out_ref[i] = flat_ref[pl.ds(i * seq_len, seq_len), :].astype(out_ref.dtype)


def weight_out_kernel(pos_ref, mine_ref, other_ref, in_ref, out_ref):
    first_is_mine = pos_ref[0] == 0
    half = mine_ref.shape[1]
    for c in range(2):
        here = slice(c * half, (c + 1) * half)
        take = first_is_mine if c == 0 else jnp.logical_not(first_is_mine)
        grad_in = jnp.where(take, mine_ref[0], other_ref[0]).astype(jnp.float32)
        in_ref[0, :, here] = grad_in.T
        out_ref[0, here, :] = jnp.where(take, mine_ref[1], other_ref[1]).astype(jnp.float32)


def swap_core(value):
    return lax.ppermute(value, "dp", [(0, 1), (1, 0)])


def hop(value, bit):
    size = lax.axis_size("expert")
    return lax.ppermute(value, "expert", [(i, i ^ bit) for i in range(size)])


def cross(value, bit):
    size = lax.axis_size("tensor")
    return lax.ppermute(value, "tensor", [(i, i ^ bit) for i in range(size)])


def after(value, *others):
    return lax.optimization_barrier((value, *others))[0]


def dense_body(
    tokens,
    cotangent,
    expert_ids,
    slot_rank,
    qkv_weight,
    out_weight,
    router_weight,
    expert_in,
    expert_out,
    gain_attention,
    gain_experts,
):
    f32, b16 = jnp.float32, jnp.bfloat16
    images, seq_len, width = tokens.shape
    token_rows = images * seq_len
    local = qkv_weight.shape[2]
    heads = local // HD
    experts = router_weight.shape[1]
    owners = lax.axis_size("expert")
    tensors = lax.axis_size("tensor")
    cores = lax.axis_size("dp")
    chunk = round_up(-(-token_rows // tensors), 16)
    padded = chunk * tensors
    rows = round_up(seq_len, 16)
    flat_rows = padded + 32
    half = expert_in.shape[2] // cores
    quarter = half // 2
    position = jnp.stack(
        [lax.axis_index("dp"), lax.axis_index("expert"), lax.axis_index("tensor")]
    ).astype(jnp.int32)
    weight_rows = qkv_weight.transpose(0, 2, 1).reshape(3 * local, width)

    x_chunk, payload, params = kernel_call(
        functools.partial(chunk_kernel, tensors),
        "chunk",
        position,
        [
            tokens,
            cotangent,
            expert_ids.transpose(0, 2, 1),
            slot_rank.transpose(0, 2, 1),
            router_weight.T,
            gain_attention,
            gain_experts,
        ],
        [
            like((chunk, width), b16),
            like((chunk, width + LANES), b16),
            like((SMALL, width), f32),
        ],
        [
            pltpu.VMEM((flat_rows, width), f32),
            pltpu.VMEM((padded + 2 * LANES, LANES), f32),
        ],
        limit=56,
        loads=tuple(range(7)),
    )
    payload_mine = [payload] + [hop(payload, k) for k in range(1, owners)]
    mine, first, second = kernel_call(
        weights_kernel,
        "weights",
        after(position, payload),
        [expert_in, expert_out],
        [
            like((2, half, width), b16),
            like((2, quarter, width), b16),
            like((2, quarter, width), b16),
        ],
        limit=12,
        loads=(0, 1),
    )
    first_x = cross(first, 1)
    second_y = cross(second, 2)

    qkv, lse, attended, *parts = kernel_call(
        functools.partial(attention_kernel, heads, experts),
        "attention",
        after(position, mine),
        [tokens, params, weight_rows, out_weight],
        [
            like((3, images, rows, local), b16),
            like((images, rows, LANES), f32),
            like((padded, local), b16),
        ]
        + [like((chunk, width), b16)] * tensors,
        [
            pltpu.VMEM((padded, local), f32),
            pltpu.VMEM((rows, width), f32),
            pltpu.VMEM((images, rows, local), f32),
        ],
        limit=20,
        loads=(0, 2, 3),
    )
    arrived = [parts[0]] + [cross(parts[j], j) for j in range(1, tensors)]
    pair_first, pair_second = stack_pairs(position, (first, first_x), (second, second_y))

    residual, routed, prob = kernel_call(
        functools.partial(route_kernel, experts),
        "route",
        after(position, pair_first, payload_mine),
        [*arrived, x_chunk, params],
        [like((chunk, width), f32), like((chunk, width), b16), like((chunk, LANES), f32)],
        limit=8,
    )
    blocks = [routed] + [hop(routed, k) for k in range(1, owners)]
    pair_first, pair_second = after((pair_first, pair_second), routed)
    pair_y = cross(pair_first, 2)
    pair_x = cross(pair_second, 1)
    other_blocks = [swap_core(b) for b in blocks]
    payload_other = [swap_core(p) for p in payload_mine]

    near_weights, far_weights = (mine, first_x, second_y), (pair_y, pair_x)
    first_a = first_expert_pass(position, blocks, payload_mine, params, near_weights, experts)
    first_b = first_expert_pass(
        after(position, first_a[2]), other_blocks, payload_other, params, near_weights, experts
    )
    second_b = second_expert_pass(
        after(position, first_b[2]), first_b, far_weights, owners
    )
    back_other, gated_other = swap_core(second_b[3]), swap_core(second_b[2])
    second_a = second_expert_pass(
        after(position, second_b[0]), first_a, far_weights, owners
    )
    joined = kernel_call(
        join_kernel,
        "join",
        position,
        [second_a[3], back_other, second_a[2], gated_other],
        [like((chunk + 2 * SMALL, width), b16)] * owners + [like((chunk, width), b16)] * owners,
        limit=8,
    )
    backs = [joined[0]] + [hop(joined[k], k) for k in range(1, owners)]

    grad_pos = after(position, joined[:owners])
    far_y, far_x = expert_grads(grad_pos, second_a, second_b, first_a[2:4], first_b[2:4])
    from_y, from_x = cross(far_y, 2), cross(far_x, 1)
    own_grad, near_grad = expert_grads(
        after(grad_pos, far_y, backs[1]), first_a, first_b, first_a[2:4], first_b[2:4]
    )

    residual_grad, attn_grad, small = kernel_call(
        functools.partial(route_back_kernel, experts, token_rows, owners),
        "route_back",
        after(position, own_grad),
        [*backs, prob, residual, payload, params],
        [like((chunk, width), f32), like((chunk, width), b16), like((SMALL, width), f32)],
        flops=40_000_000_000,
        limit=8,
    )
    gated_back = [joined[owners]]
    for k in range(1, owners):
        gated_back.append(hop(after(joined[owners + k], attn_grad), k))
    attn_grad = lax.all_gather(attn_grad, "tensor", axis=0, tiled=True)
    piece = 4 * local // (2 * owners)
    keep, send, *parts = kernel_call(
        functools.partial(attention_back_kernel, heads, experts, owners),
        "attention_back",
        after(position, from_y, from_x, gated_back[1:]),
        [tokens, params, weight_rows, out_weight, qkv, lse, attended, attn_grad, small],
        [
            like((owners, piece, width), f32),
            like((owners, piece, width), b16),
        ]
        + [like((chunk + 2 * SMALL, width), b16)] * tensors,
        [
            pltpu.VMEM((flat_rows, local), f32),
            pltpu.VMEM((flat_rows, width), f32),
            pltpu.VMEM((4 * local, width), f32),
            pltpu.VMEM((rows, width), f32),
            pltpu.VMEM((images, rows, local), f32),
            pltpu.VMEM((images, rows, width), f32),
            pltpu.VMEM((images, SMALL, width), f32),
        ],
        limit=20,
        flops=6_000_000_000,
    )
    own_piece, *pieces = kernel_call(
        add_core_kernel,
        "add_core",
        position,
        [keep, swap_core(send)],
        [like((piece, width), f32)] + [like((piece, width), b16)] * (owners - 1),
        limit=8,
    )
    reduced = [hop(p, k + 1) for k, p in enumerate(pieces)]
    got = [parts[0]] + [cross(parts[j], j) for j in range(1, tensors)]
    up_x, up_y = kernel_call(
        second_step_kernel,
        "second_step",
        after(position, got[1:], own_piece),
        [near_grad, from_y, from_x],
        [like((2, quarter, width), b16)] * 2,
        limit=8,
    )
    last_x, last_y = cross(up_x, 1), cross(up_y, 2)

    grad_chunk, summed = kernel_call(
        functools.partial(norm_back_kernel, experts, tensors),
        "norm_back",
        position,
        [*got, x_chunk, residual_grad, params, own_piece, *reduced],
        [like((chunk, width), b16), like((piece + 2 * SMALL, width), b16)],
        [pltpu.VMEM((tensors, SMALL, width), f32)],
        flops=40_000_000_000,
        limit=8,
    )
    around = [summed] + [hop(summed, k) for k in range(1, owners)]
    grad_rows = lax.all_gather(grad_chunk, "tensor", axis=0, tiled=True)
    combined = residual
    for part in gated_back:
        combined = combined + part.astype(f32)
    combined = combined.astype(b16)
    combined = after(combined, grad_rows)
    block_parts = [combined] + [cross(combined, j) for j in range(1, tensors)]

    grad_tokens = kernel_call(
        images_kernel,
        "grad_tokens",
        after(position, around, last_x, last_y),
        [grad_rows],
        [like(tokens.shape, f32)],
        [pltpu.VMEM((padded, width), f32)],
        limit=8,
    )[0]
    grad_half = kernel_call(
        weight_sum_kernel,
        "weight_sum",
        after(position, grad_tokens),
        [own_grad, from_y, from_x, last_x, last_y],
        [like((2, half, width), b16)],
        limit=8,
    )[0]
    grad_expert_in, grad_expert_out = kernel_call(
        weight_out_kernel,
        "weight_out",
        position,
        [grad_half, swap_core(grad_half)],
        [like((1, width, 2 * half), f32), like((1, 2 * half, width), f32)],
        limit=10,
    )
    token_total = token_rows * cores * owners
    grad_qkv, grad_out, grad_router, gain_one, gain_two, loss = kernel_call(
        functools.partial(spread_kernel, owners, experts, token_total),
        "spread",
        position,
        around + [swap_core(a) for a in around],
        [
            like((3 * local, width), f32),
            like((local, width), f32),
            like((experts, width), f32),
            like((width,), f32),
            like((width,), f32),
            like((1, LANES), f32),
        ],
        [
            pltpu.VMEM((4 * local, width), f32),
            pltpu.VMEM((2 * owners, SMALL, width), f32),
        ],
        limit=8,
    )
    block_out = kernel_call(
        images_kernel,
        "block_out",
        after(position, grad_tokens, grad_expert_in, grad_qkv),
        block_parts,
        [like(tokens.shape, b16)],
        [pltpu.VMEM((padded, width), f32)],
        limit=8,
    )[0]
    return (
        block_out,
        grad_tokens,
        grad_qkv.reshape(3, local, width).transpose(0, 2, 1),
        grad_out,
        grad_router.T,
        grad_expert_in,
        grad_expert_out,
        gain_one,
        gain_two,
        loss[0, 0],
    )


def solution(mesh):
    placed = (
        P(("dp", "expert"), None, None),
        P(("dp", "expert"), None, None),
        P(("dp", "expert"), None, None),
        P(("dp", "expert"), None, None),
        P(None, None, "tensor"),
        P("tensor", None),
        P(),
        P("expert", None, "tensor"),
        P("expert", "tensor", None),
        P(),
        P(),
    )
    shape = mesh.shape
    dense = shape["dp"] == 2 and shape["expert"] == 4 and shape["tensor"] == 4
    return jax.shard_map(
        dense_body if dense else body,
        mesh=mesh,
        in_specs=placed,
        out_specs=(
            P(("dp", "expert"), None, None),
            P(("dp", "expert"), None, None),
            P(None, None, "tensor"),
            P("tensor", None),
            P(),
            P("expert", None, "tensor"),
            P("expert", "tensor", None),
            P(),
            P(),
            P(),
        ),
        check_vma=False,
    )
```

```python
import functools
import math

import jax
import jax.numpy as jnp
from jax import lax
from jax.experimental import pallas as pl
from jax.experimental.pallas import tpu as pltpu
from jax.sharding import PartitionSpec as P

HD = 64


epsilon = 1e-06


def normalize(values, gain_row):
    center = values - jnp.mean(values, axis=-1, keepdims=True)
    inverse = lax.rsqrt(jnp.mean(center * center, axis=-1, keepdims=True) + epsilon)
    normed = center * inverse
    return (normed, inverse, normed * gain_row)


def normalize_back(upstream, normed, inverse, gain_row):
    scaled = upstream * gain_row
    result = inverse * (
        scaled
        - jnp.mean(scaled, axis=-1, keepdims=True)
        - normed * jnp.mean(scaled * normed, axis=-1, keepdims=True)
    )
    return (result, jnp.sum(upstream * normed, axis=0))


def exact_gelu(values):
    return jax.nn.gelu(values, approximate=False)


def body(
    tokens,
    cotangent,
    expert_ids,
    slot_rank,
    qkv_weight,
    out_weight,
    router_weight,
    expert_in,
    expert_out,
    gain_attention,
    gain_experts,
):
    images, seq_len, model_width = tokens.shape
    token_rows = images * seq_len
    local_width = qkv_weight.shape[2]
    local_heads = local_width // HD
    slice_width = model_width // lax.axis_size("tensor")
    experts = router_weight.shape[1]
    capacity = 5 * token_rows // (2 * experts)
    owners = lax.axis_size("expert")
    per_owner = experts // owners
    slot_total = experts * capacity
    score_scale = HD ** (-0.5)
    inputs = tokens.reshape(token_rows, model_width).astype(jnp.float32)
    normed_one, inverse_one, mixed_one = normalize(inputs, gain_attention)
    entered = mixed_one.astype(jnp.bfloat16)
    project = jnp.einsum(
        "td,cdf->ctf", entered, qkv_weight, preferred_element_type=jnp.float32
    ).astype(jnp.bfloat16)
    projected_heads = project.reshape(3, images, seq_len, local_heads, HD)
    queries, key_rows, value_rows = (projected_heads[0], projected_heads[1], projected_heads[2])
    scores = (
        jnp.einsum("ishe,ithe->ihst", queries, key_rows, preferred_element_type=jnp.float32)
        * score_scale
    )
    log_total = jax.nn.logsumexp(scores, axis=-1, keepdims=True)
    attn_probs = jnp.exp(scores - log_total).astype(jnp.bfloat16)
    attended = jnp.einsum(
        "ihst,ithe->ishe", attn_probs, value_rows, preferred_element_type=jnp.float32
    )
    attended = attended.astype(jnp.bfloat16).reshape(token_rows, local_width)
    attn_part = jnp.dot(attended, out_weight, preferred_element_type=jnp.float32)
    residual = inputs + lax.psum(attn_part, "tensor")
    normed_two, inverse_two, mixed_two = normalize(residual, gain_experts)
    routed = mixed_two.astype(jnp.bfloat16)
    route_prob = jax.nn.softmax(
        jnp.dot(routed, router_weight, preferred_element_type=jnp.float32), axis=-1
    )
    chosen = expert_ids.reshape(token_rows, 2)
    ranked = slot_rank.reshape(token_rows, 2)
    kept_mask = (ranked >= 0).astype(jnp.float32)
    position = jnp.where(ranked >= 0, chosen * capacity + ranked, slot_total).reshape(-1)
    send_rows = (
        jnp.zeros((slot_total, model_width), jnp.bfloat16)
        .at[position]
        .set(jnp.repeat(routed, 2, axis=0), mode="drop")
        .reshape(experts, capacity, model_width)
    )
    fragment = lax.all_to_all(send_rows, "expert", split_axis=0, concat_axis=0, tiled=True)
    grouped = fragment.reshape(owners, per_owner, fragment.shape[1], model_width)
    before = jnp.einsum("sjcd,jdf->sjcf", grouped, expert_in, preferred_element_type=jnp.float32)
    hidden = exact_gelu(before).astype(jnp.bfloat16)
    expert_part = jnp.einsum(
        "sjcf,jfd->sjcd", hidden, expert_out, preferred_element_type=jnp.float32
    )
    produced = lax.psum_scatter(expert_part, "tensor", scatter_dimension=3, tiled=True).astype(
        jnp.bfloat16
    )
    returned = lax.all_to_all(
        produced.reshape(experts, capacity, slice_width),
        "expert",
        split_axis=0,
        concat_axis=0,
        tiled=True,
    )
    returned = lax.all_gather(returned, "tensor", axis=2, tiled=True).reshape(
        slot_total, model_width
    )
    safe_index = jnp.minimum(position, slot_total - 1)
    picked = returned[safe_index].reshape(token_rows, 2, model_width).astype(jnp.float32)
    gate_values = jnp.take_along_axis(route_prob, chosen, axis=1) * kept_mask
    output = residual + jnp.sum(gate_values[:, :, None] * picked, axis=1)
    block_out = output.astype(jnp.bfloat16).reshape(images, seq_len, model_width)
    upstream = cotangent.reshape(token_rows, model_width).astype(jnp.float32)
    gate_grad = jnp.sum(upstream[:, None, :] * picked, axis=-1) * kept_mask
    member = (chosen[:, :, None] == jnp.arange(experts)[None, None, :]).astype(jnp.float32)
    route_grad = jnp.sum(member * gate_grad[:, :, None], axis=1)
    logit_grad = (
        route_prob * (route_grad - jnp.sum(route_grad * route_prob, axis=-1, keepdims=True))
    ).astype(jnp.bfloat16)
    row_grad = (
        (gate_values[:, :, None] * upstream[:, None, :])
        .astype(jnp.bfloat16)
        .reshape(2 * token_rows, model_width)
    )
    grad_send = (
        jnp.zeros((slot_total, model_width), jnp.bfloat16)
        .at[position]
        .set(row_grad, mode="drop")
        .reshape(experts, capacity, model_width)
    )
    grad_arrived = lax.all_to_all(grad_send, "expert", split_axis=0, concat_axis=0, tiled=True)
    grad_arrived = grad_arrived.reshape(owners, per_owner, capacity, model_width)
    hidden_grad = jnp.einsum(
        "sjcd,jfd->sjcf", grad_arrived, expert_out, preferred_element_type=jnp.float32
    )
    grad_expert_out = jnp.einsum(
        "sjcf,sjcd->jfd", hidden, grad_arrived, preferred_element_type=jnp.float32
    )
    pre_grad = jax.vjp(exact_gelu, before)[1](hidden_grad)[0].astype(jnp.bfloat16)
    grad_expert_in = jnp.einsum(
        "sjcd,sjcf->jdf", grouped, pre_grad, preferred_element_type=jnp.float32
    )
    buffer_part = jnp.einsum(
        "sjcf,jdf->sjcd", pre_grad, expert_in, preferred_element_type=jnp.float32
    )
    buffer_share = lax.psum_scatter(buffer_part, "tensor", scatter_dimension=3, tiled=True).astype(
        jnp.bfloat16
    )
    buffer_back = lax.all_to_all(
        buffer_share.reshape(experts, capacity, slice_width),
        "expert",
        split_axis=0,
        concat_axis=0,
        tiled=True,
    )
    buffer_grad = lax.all_gather(buffer_back, "tensor", axis=2, tiled=True).reshape(
        slot_total, model_width
    )
    routed_grad = jnp.sum(
        buffer_grad[safe_index].reshape(token_rows, 2, model_width).astype(jnp.float32)
        * kept_mask[:, :, None],
        axis=1,
    )
    routed_grad = routed_grad + jnp.dot(
        logit_grad, router_weight.T, preferred_element_type=jnp.float32
    )
    grad_router = jnp.einsum("td,te->de", routed, logit_grad, preferred_element_type=jnp.float32)
    from_norm_two, grad_gain_experts = normalize_back(
        routed_grad, normed_two, inverse_two, gain_experts
    )
    residual_grad = upstream + from_norm_two
    attn_grad = residual_grad.astype(jnp.bfloat16)
    grad_out = jnp.einsum("tf,td->fd", attended, attn_grad, preferred_element_type=jnp.float32)
    heads_grad = jnp.dot(attn_grad, out_weight.T, preferred_element_type=jnp.float32).astype(
        jnp.bfloat16
    )
    heads_grad = heads_grad.reshape(images, seq_len, local_heads, HD)
    again = (
        jnp.einsum("ishe,ithe->ihst", queries, key_rows, preferred_element_type=jnp.float32)
        * score_scale
    )
    probs_full = jnp.exp(again - log_total)
    prob_grad = jnp.einsum(
        "ishe,ithe->ihst", heads_grad, value_rows, preferred_element_type=jnp.float32
    )
    value_grad = jnp.einsum(
        "ihst,ishe->ithe",
        probs_full.astype(jnp.bfloat16),
        heads_grad,
        preferred_element_type=jnp.float32,
    )
    score_grad = (
        probs_full * (prob_grad - jnp.sum(prob_grad * probs_full, axis=-1, keepdims=True))
    ).astype(jnp.bfloat16)
    query_grad = (
        jnp.einsum("ihst,ithe->ishe", score_grad, key_rows, preferred_element_type=jnp.float32)
        * score_scale
    )
    key_grad = (
        jnp.einsum("ihst,ishe->ithe", score_grad, queries, preferred_element_type=jnp.float32)
        * score_scale
    )
    project_grad = (
        jnp.stack([query_grad, key_grad, value_grad])
        .astype(jnp.bfloat16)
        .reshape(3, token_rows, local_width)
    )
    grad_qkv = jnp.einsum("td,ctf->cdf", entered, project_grad, preferred_element_type=jnp.float32)
    entered_part = jnp.einsum(
        "ctf,cdf->td", project_grad, qkv_weight, preferred_element_type=jnp.float32
    )
    entered_grad = lax.psum(entered_part.astype(jnp.bfloat16), "tensor").astype(jnp.float32)
    from_norm_one, grad_gain_attention = normalize_back(
        entered_grad, normed_one, inverse_one, gain_attention
    )
    grad_tokens = (residual_grad + from_norm_one).reshape(images, seq_len, model_width)
    counts = jnp.sum(member, axis=(0, 1))
    prob_sum = jnp.sum(route_prob, axis=0)
    grad_qkv, grad_out, grad_router, grad_gain_attention, grad_gain_experts, counts, prob_sum = (
        lax.psum(
            (
                grad_qkv,
                grad_out,
                grad_router,
                grad_gain_attention,
                grad_gain_experts,
                counts,
                prob_sum,
            ),
            ("dp", "expert"),
        )
    )
    grad_expert_in, grad_expert_out = (
        lax.psum(grad_expert_in.astype(jnp.bfloat16), "dp").astype(jnp.float32),
        lax.psum(grad_expert_out.astype(jnp.bfloat16), "dp").astype(jnp.float32),
    )
    token_total = token_rows * lax.axis_size("dp") * lax.axis_size("expert")
    balance_loss = experts * jnp.sum(counts / (2.0 * token_total) * prob_sum / token_total)
    return (
        block_out,
        grad_tokens,
        grad_qkv,
        grad_out,
        grad_router,
        grad_expert_in,
        grad_expert_out,
        grad_gain_attention,
        grad_gain_experts,
        balance_loss,
    )


NN = ((1,), (0,))
NT = ((1,), (1,))
TN = ((0,), (0,))
LANES = 128
SMALL = 8


def round_up(value, step):
    return -(-value // step) * step


def contract(a, b, dims):
    return lax.dot_general(a, b, (dims, ((), ())), preferred_element_type=jnp.float32)


def load_then(kernel, loads, count, *refs):
    pos_ref, *refs = refs
    *refs, sem = refs
    buffers = refs[len(refs) - len(loads) :]
    refs = refs[: len(refs) - len(loads)]
    copies = [
        pltpu.make_async_copy(refs[index], buffer, sem.at[i])
        for i, (index, buffer) in enumerate(zip(loads, buffers))
    ]
    for copy in copies:
        copy.start()
    for copy in copies:
        copy.wait()
    for index, buffer in zip(loads, buffers):
        refs[index] = buffer
    kernel(pos_ref, *refs)


def kernel_call(kernel, name, position, args, outs, scratch=(), flops=0, limit=24, loads=()):
    if loads:
        kernel = functools.partial(load_then, kernel, loads, len(args))
        scratch = [
            *scratch,
            *(pltpu.VMEM(args[i].shape, args[i].dtype) for i in loads),
            pltpu.SemaphoreType.DMA((len(loads),)),
        ]
    places = [pltpu.HBM if i in loads else pltpu.VMEM for i in range(len(args))]
    return pl.pallas_call(
        kernel,
        in_specs=[pl.BlockSpec(memory_space=pltpu.SMEM)]
        + [pl.BlockSpec(memory_space=place) for place in places],
        out_specs=[pl.BlockSpec(memory_space=pltpu.VMEM)] * len(outs),
        out_shape=list(outs),
        scratch_shapes=list(scratch),
        compiler_params=pltpu.CompilerParams(vmem_limit_bytes=limit << 20),
        cost_estimate=pl.CostEstimate(flops=flops, bytes_accessed=0, transcendentals=0),
        name=name,
    )(position, *args)


def like(shape, dtype):
    return jax.ShapeDtypeStruct(shape, dtype)


def live_rows(shape, limit, offset=0):
    return lax.broadcasted_iota(jnp.int32, shape, 0) + offset < limit


def chunk_of(pos_ref, j, size):
    return pl.ds(pl.multiple_of(lax.bitwise_xor(lax.axis_index("tensor"), j) * size, 16), size)


def head_masks(rows, heads):
    lane = lax.broadcasted_iota(jnp.int32, (rows, heads * HD), 1)
    return [(lane >= h * HD) & (lane < (h + 1) * HD) for h in range(heads)]


def keep_lanes(value, mask):
    return jnp.where(mask, value, jnp.zeros_like(value))


def split_high_low(value):
    high = value.astype(jnp.bfloat16)
    return high, (value - high.astype(jnp.float32)).astype(jnp.bfloat16)


def image_rows(ref, i, scratch_ref):
    seq_len = ref.shape[1]
    scratch_ref[seq_len:, :] = jnp.zeros((scratch_ref.shape[0] - seq_len, ref.shape[2]), jnp.float32)
    scratch_ref[0:seq_len, :] = ref[i].astype(jnp.float32)
    return scratch_ref[...]


def router_matrix(param_ref, experts):
    rows = param_ref[0:SMALL, :]
    rows = jnp.where(live_rows(rows.shape, experts), rows, 0.0).astype(jnp.bfloat16)
    zeros = jnp.zeros((LANES - SMALL, rows.shape[1]), jnp.bfloat16)
    return jnp.concatenate([rows, zeros], axis=0)


def chunk_kernel(
    tensors, pos_ref, tok_ref, cot_ref, ids_ref, rank_ref, router_ref, one_ref, two_ref, in_ref, out_ref,
    x_ref, pay_ref, param_ref, mine_ref, first_ref, second_ref, flat_ref, kept_ref,
):
    half = mine_ref.shape[1]
    core = pl.multiple_of(lax.axis_index("dp") * half, LANES)
    for s, part in ((0, in_ref[0, :, pl.ds(core, half)].T), (1, out_ref[0, pl.ds(core, half), :])):
        mine_ref[s] = part
        first_ref[s] = part[0 : half // 2]
        second_ref[s] = part[half // 2 :]
    images, seq_len, width = tok_ref.shape
    chunk, experts = x_ref.shape[0], router_ref.shape[0]
    start = pl.multiple_of(lax.axis_index("tensor") * chunk, 16)
    for source, target in ((tok_ref, x_ref), (cot_ref, pay_ref)):
        flat_ref[images * seq_len :, :] = jnp.zeros(
            (flat_ref.shape[0] - images * seq_len, width), jnp.float32
        )
        for i in range(images):
            flat_ref[pl.ds(i * seq_len, seq_len), :] = source[i].astype(jnp.float32)
        target[:, :width] = flat_ref[pl.ds(start, chunk), :].astype(jnp.bfloat16)
    kept_ref[...] = jnp.zeros_like(kept_ref)
    counts = jnp.zeros((1, LANES), jnp.float32)
    for i in range(images):
        rows, all_rows = [], []
        for e in range(experts):
            named = (ids_ref[i] == e).astype(jnp.float32)
            kept = jnp.where(rank_ref[i] >= 0, named, 0.0)
            rows.append(jnp.sum(kept, axis=0, keepdims=True))
            all_rows.append(jnp.sum(named, axis=0, keepdims=True))
        for group, is_kept in ((rows, True), (all_rows, False)):
            table = jnp.concatenate(group, axis=0)
            table = jnp.concatenate(
                [table, jnp.zeros((LANES - experts, seq_len), jnp.float32)], axis=0
            )
            table = jnp.concatenate(
                [table, jnp.zeros((LANES, 2 * LANES - seq_len), jnp.float32)], axis=1
            ).T
            if is_kept:
                kept_ref[pl.ds(i * seq_len, 2 * LANES), :] = table
            else:
                counts = counts + jnp.sum(table, axis=0, keepdims=True)
    pay_ref[:, width:] = kept_ref[pl.ds(start, chunk), :].astype(jnp.bfloat16)
    param_ref[...] = jnp.zeros_like(param_ref)
    param_ref[0:experts, :] = router_ref[...].astype(jnp.float32)
    param_ref[experts : experts + 1, :] = one_ref[...].reshape(1, width)
    param_ref[experts + 1 : experts + 2, :] = two_ref[...].reshape(1, width)
    param_ref[SMALL - 1 : SMALL, :LANES] = counts * (1.0 / tensors)


def stack_kernel(pos_ref, *refs):
    count = len(refs) // 3
    for i, target in enumerate(refs[2 * count :]):
        target[0] = refs[2 * i][...]
        target[1] = refs[2 * i + 1][...]


def stack_pairs(position, *pairs):
    return kernel_call(
        stack_kernel,
        "stack",
        position,
        [value for pair in pairs for value in pair],
        [like((2, *pair[0].shape), pair[0].dtype) for pair in pairs],
        limit=4,
    )


def lay_kernel(pos_ref, *refs):
    *blocks, out_ref = refs
    chunk = blocks[0].shape[0]
    for k, block in enumerate(blocks):
        out_ref[k * chunk : (k + 1) * chunk, :] = block[...]


def lay_rows(position, name, blocks):
    chunk, width = blocks[0].shape
    return kernel_call(
        lay_kernel,
        name,
        position,
        blocks,
        [like((len(blocks) * chunk, width), blocks[0].dtype)],
        limit=4,
    )[0]


def gain_row(param_ref, experts, which):
    return param_ref[experts + which : experts + which + 1, :]


def attention_kernel(
    heads, experts, pos_ref, tok_ref, param_ref, w_ref, wo_ref, qkv_ref, lse_ref, att_ref, *refs,
):
    *parts, flat_ref, image_ref, held_ref = refs
    images, rows, width = qkv_ref.shape[1], qkv_ref.shape[2], heads * HD
    seq_len = tok_ref.shape[1]
    masks = head_masks(rows, heads)
    keys_live = lax.broadcasted_iota(jnp.int32, (rows, rows), 1) < seq_len
    lane = lax.broadcasted_iota(jnp.int32, (rows, LANES), 1)
    flat_ref[images * seq_len :, :] = jnp.zeros(
        (flat_ref.shape[0] - images * seq_len, width), jnp.float32
    )

    @pl.loop(0, images)
    def _(i):
        entered = normalize(image_rows(tok_ref, i, image_ref), gain_row(param_ref, experts, 0))[2]
        entered = entered.astype(jnp.bfloat16)
        q, k, v = (
            contract(entered, w_ref[c * width : (c + 1) * width, :], NT).astype(jnp.bfloat16)
            for c in range(3)
        )
        qkv_ref[0, i], qkv_ref[1, i], qkv_ref[2, i] = q, k, v
        attended = jnp.zeros((rows, width), jnp.float32)
        lse_all = jnp.zeros((rows, LANES), jnp.float32)
        for h in range(heads):
            scores = contract(keep_lanes(q, masks[h]), k, NT) * (HD ** (-0.5))
            scores = jnp.where(keys_live, scores, -1e30)
            top = jnp.max(scores, axis=-1, keepdims=True)
            lse = top + jnp.log(jnp.sum(jnp.exp(scores - top), axis=-1, keepdims=True))
            probs = jnp.exp(scores - lse).astype(jnp.bfloat16)
            attended = attended + contract(probs, keep_lanes(v, masks[h]), NN)
            lse_all = jnp.where(lane == h, lse, lse_all)
        lse_ref[i] = lse_all
        held_ref[i] = attended

    for i in range(images):
        flat_ref[pl.ds(i * seq_len, seq_len), :] = held_ref[i, 0:seq_len, :]
    att_ref[...] = flat_ref[...].astype(jnp.bfloat16)
    for j, part in enumerate(parts):
        rows_j = flat_ref[chunk_of(pos_ref, j, part.shape[0]), :].astype(jnp.bfloat16)
        part[...] = contract(rows_j, wo_ref[...], NN).astype(jnp.bfloat16)


def route_kernel(experts, pos_ref, *refs):
    *got, x_ref, param_ref, res_ref, routed_ref, prob_ref = refs
    residual = x_ref[...].astype(jnp.float32)
    for part in got:
        residual = residual + part[...].astype(jnp.float32)
    res_ref[...] = residual
    routed = normalize(residual, gain_row(param_ref, experts, 1))[2].astype(jnp.bfloat16)
    routed_ref[...] = routed
    prob_ref[...] = route_probs(routed, router_matrix(param_ref, experts), experts)


def route_probs(rows, router, experts):
    logits = contract(rows, router, NT)
    lane = lax.broadcasted_iota(jnp.int32, logits.shape, 1)
    logits = jnp.where(lane < experts, logits, -1e30)
    weight = jnp.exp(logits - jnp.max(logits, axis=-1, keepdims=True))
    return weight / jnp.sum(weight, axis=-1, keepdims=True)


def gelu_parts(x):
    square = jnp.exp(-0.5 * x * x)
    share = 0.5 * (1.0 + lax.erf(x * (0.5**0.5)))
    return x * share, share + x * square * (0.5 / math.pi) ** 0.5


def expert_halves(x, rg, w_in, w_out, hidden_ref, pre_ref):
    before = contract(x, w_in, NT)
    value, slope = gelu_parts(before)
    hidden = value.astype(jnp.bfloat16)
    hidden_ref[...] = hidden
    part = contract(hidden, w_out, NN)
    pre = (contract(rg, w_out, NT) * slope).astype(jnp.bfloat16)
    pre_ref[...] = pre
    return part, contract(pre, w_in, NN)


def first_expert_kernel(
    experts, pos_ref, x_ref, pay_ref, param_ref, w0_ref, xa_ref, yb_ref, hidden_ref, pre_ref, rg_ref,
    gate_ref, part_ref, back_ref,
):
    count, width = x_ref.shape
    prob = route_probs(x_ref[...], router_matrix(param_ref, experts), experts)
    mine = lax.broadcasted_iota(jnp.int32, prob.shape, 1) == lax.axis_index("expert")
    kept = pay_ref[:, width:].astype(jnp.float32)
    kept = jnp.sum(jnp.where(mine, kept, 0.0), axis=-1, keepdims=True)
    gate = jnp.sum(jnp.where(mine, prob, 0.0), axis=-1, keepdims=True) * kept
    gate_ref[:, :LANES] = jnp.broadcast_to(gate, (count, LANES))
    gate_ref[:, LANES:] = jnp.broadcast_to(kept, (count, LANES))
    rg_ref[...] = (gate * pay_ref[:, :width].astype(jnp.float32)).astype(jnp.bfloat16)
    w_in, w_out = (
        jnp.concatenate([w0_ref[s], xa_ref[s], yb_ref[s]], axis=0) for s in range(2)
    )
    part_ref[...], back_ref[...] = expert_halves(
        x_ref[...], rg_ref[...], w_in, w_out, hidden_ref, pre_ref
    )


def second_expert_kernel(
    pos_ref, x_ref, pay_ref, rg_ref, gate_ref, part_in_ref, back_in_ref, pair_y_ref, pair_x_ref,
    hidden_ref, pre_ref, gated_ref, back_ref,
):
    width = x_ref.shape[1]
    w_in, w_out = (
        jnp.concatenate([ref[r, s] for ref in (pair_y_ref, pair_x_ref) for r in range(2)], axis=0)
        for s in range(2)
    )
    part, back = expert_halves(x_ref[...], rg_ref[...], w_in, w_out, hidden_ref, pre_ref)
    back_ref[:, :width] = back_in_ref[...] + back
    part = part_in_ref[...] + part
    gated_ref[...] = (gate_ref[:, 0:1] * part).astype(jnp.bfloat16)
    inner = jnp.sum(part * pay_ref[:, :width].astype(jnp.float32), axis=-1, keepdims=True)
    back_ref[:, width:] = gate_ref[:, LANES:] * inner


def first_expert_pass(position, rows, payload, params, weights, experts):
    count, width = rows.shape
    hidden = 2 * weights[0].shape[1]
    return kernel_call(
        functools.partial(first_expert_kernel, experts),
        "experts_first",
        position,
        [rows, payload, params, *weights],
        [
            like((count, hidden), jnp.bfloat16),
            like((count, hidden), jnp.bfloat16),
            like((count, width), jnp.bfloat16),
            like((count, 2 * LANES), jnp.float32),
            like((count, width), jnp.float32),
            like((count, width), jnp.float32),
        ],
        limit=18,
    )


def second_expert_pass(position, rows, payload, first, weights):
    count, width = rows.shape
    hidden = 4 * weights[0].shape[2]
    return kernel_call(
        second_expert_kernel,
        "experts_second",
        position,
        [rows, payload, *first[2:], *weights],
        [
            like((count, hidden), jnp.bfloat16),
            like((count, hidden), jnp.bfloat16),
            like((count, width), jnp.bfloat16),
            like((count, width + LANES), jnp.float32),
        ],
        limit=18,
    )


def join_kernel(pos_ref, back_ref, other_ref, gated_ref, gated_other_ref, *outs):
    owners = len(outs) // 2
    chunk, width = outs[owners].shape
    for k in range(owners):
        here = pl.ds(k * chunk, chunk)
        total = back_ref[here, :] + other_ref[here, :]
        outs[k][0:chunk, :] = total[:, :width].astype(jnp.bfloat16)
        inner = jnp.concatenate(
            [total[:, width:], jnp.zeros((2 * LANES - chunk, LANES), jnp.float32)], axis=0
        ).T
        high, low = split_high_low(inner[0:SMALL, :])
        outs[k][chunk:, : 2 * LANES] = jnp.concatenate([high, low], axis=0)
        outs[k][chunk:, 2 * LANES :] = jnp.zeros((2 * SMALL, width - 2 * LANES), jnp.bfloat16)
        outs[owners + k][...] = (
            gated_ref[here, :].astype(jnp.float32) + gated_other_ref[here, :].astype(jnp.float32)
        ).astype(jnp.bfloat16)


def expert_grad_kernel(pos_ref, *refs):
    *sources, first_ref, second_ref = refs
    part_rows = first_ref.shape[2]
    for j, out in enumerate((first_ref, second_ref)):
        columns = slice(2 * j * part_rows, 2 * (j + 1) * part_rows)
        for s in range(2):
            left_a, right_a, left_b, right_b = sources[4 * s : 4 * s + 4]
            grad = contract(left_a[:, columns], right_a[...], TN)
            grad = grad + contract(left_b[:, columns], right_b[...], TN)
            grad = grad.astype(jnp.bfloat16)
            out[0, s] = grad[0:part_rows]
            out[1, s] = grad[part_rows:]


def expert_grads(position, a, b, rows_a, rows_b):
    width, total = rows_a[0].shape[1], a[0].shape[1]
    return kernel_call(
        expert_grad_kernel,
        "expert_grads",
        position,
        [a[1], rows_a[0], b[1], rows_b[0], a[0], rows_a[1], b[0], rows_b[1]],
        [like((2, 2, total // 4, width), jnp.bfloat16)] * 2,
        limit=10,
    )


def route_back_kernel(
    experts, token_rows, owners, pos_ref, *refs
):
    backs = refs[:owners]
    prob_ref, res_ref, pay_ref, param_ref = refs[owners : owners + 4]
    grad_ref, up_ref, small_ref = refs[owners + 4 :]
    chunk, width = res_ref.shape
    prob = prob_ref[...]
    lane = lax.broadcasted_iota(jnp.int32, prob.shape, 1)
    route_grad = jnp.zeros_like(prob)
    routed_grad = jnp.zeros((chunk, width), jnp.float32)
    for k, back in enumerate(backs):
        owner = lax.bitwise_xor(lax.axis_index("expert"), k)
        inner = back[chunk : chunk + SMALL, : 2 * LANES].astype(jnp.float32)
        inner = inner + back[chunk + SMALL :, : 2 * LANES].astype(jnp.float32)
        inner = jnp.concatenate([inner] * (LANES // SMALL), axis=0).T[0:chunk]
        route_grad = jnp.where(lane == owner, inner, route_grad)
        routed_grad = routed_grad + back[0:chunk, :].astype(jnp.float32)
    mean = jnp.sum(route_grad * prob, axis=-1, keepdims=True)
    logit_grad = (prob * (route_grad - mean)).astype(jnp.bfloat16)
    routed_grad = routed_grad + contract(
        logit_grad, router_matrix(param_ref, experts), NN
    )
    normed, inverse, mixed = normalize(res_ref[...], gain_row(param_ref, experts, 1))
    from_norm, gain_grad = normalize_back(
        routed_grad, normed, inverse, gain_row(param_ref, experts, 1)
    )
    total = pay_ref[:, :width].astype(jnp.float32) + from_norm
    grad_ref[...] = total
    up_ref[...] = total.astype(jnp.bfloat16)
    live = live_rows(prob.shape, token_rows, lax.axis_index("tensor") * chunk)
    prob_sum = jnp.sum(jnp.where(live, prob, 0.0), axis=0, keepdims=True)
    grad_router = contract(logit_grad, mixed.astype(jnp.bfloat16), TN)
    small_ref[0:SMALL, :] = grad_router[0:SMALL]
    small_ref[experts : experts + 1, :] = gain_grad[None]
    small_ref[experts + 1 : experts + 2, :] = jnp.zeros((1, width), jnp.float32)
    small_ref[experts + 1 : experts + 2, :LANES] = prob_sum
    small_ref[experts + 2 : experts + 3, :] = param_ref[SMALL - 1 : SMALL, :]


def attention_back_kernel(
    heads, experts, owners, pos_ref, tok_ref, param_ref, w_ref, wo_ref, qkv_ref, lse_ref, att_ref,
    up_ref, small_ref, keep_ref, send_ref, *refs,
):
    *parts, hg_ref, flat_ref, big_ref, image_ref, held_ref, sum_ref, gain_ref = refs
    images, rows, width = qkv_ref.shape[1], qkv_ref.shape[2], heads * HD
    seq_len = tok_ref.shape[1]
    scale = HD ** (-0.5)
    padded, model = up_ref.shape
    chunk = padded // len(parts)
    masks = head_masks(rows, heads)
    keys_live = lax.broadcasted_iota(jnp.int32, (rows, rows), 1) < seq_len
    lane = lax.broadcasted_iota(jnp.int32, (rows, LANES), 1)
    up = up_ref[...]
    hg_ref[0:padded, :] = contract(up, wo_ref[...], NT)
    hg_ref[padded:, :] = jnp.zeros((hg_ref.shape[0] - padded, width), jnp.float32)
    big_ref[3 * width :, :] = contract(att_ref[...], up, TN)
    flat_ref[images * seq_len :, :] = jnp.zeros(
        (flat_ref.shape[0] - images * seq_len, model), jnp.float32
    )
    for i in range(images):
        held_ref[i] = hg_ref[pl.ds(i * seq_len, rows), :]
    big_ref[0 : 3 * width, :] = jnp.zeros((3 * width, model), jnp.float32)

    @pl.loop(0, images, unroll=True)
    def _(i):
        normed, _, mixed = normalize(
            image_rows(tok_ref, i, image_ref), gain_row(param_ref, experts, 0)
        )
        entered = mixed.astype(jnp.bfloat16)
        q, k, v = qkv_ref[0, i], qkv_ref[1, i], qkv_ref[2, i]
        heads_grad = held_ref[i]
        heads_grad = jnp.where(live_rows(heads_grad.shape, seq_len), heads_grad, 0.0)
        heads_grad = heads_grad.astype(jnp.bfloat16)
        dq = jnp.zeros((rows, width), jnp.float32)
        dk, dv = dq, dq
        for h in range(heads):
            q_h, k_h = keep_lanes(q, masks[h]), keep_lanes(k, masks[h])
            up_h = keep_lanes(heads_grad, masks[h])
            scores = contract(q_h, k, NT) * scale
            lse = jnp.sum(jnp.where(lane == h, lse_ref[i], 0.0), axis=-1, keepdims=True)
            probs = jnp.where(keys_live, jnp.exp(scores - lse), 0.0)
            prob_grad = contract(up_h, v, NT)
            total = jnp.sum(prob_grad * probs, axis=-1, keepdims=True)
            score_grad = (probs * (prob_grad - total)).astype(jnp.bfloat16)
            dv = dv + contract(probs.astype(jnp.bfloat16), up_h, TN)
            dq = dq + contract(score_grad, k_h, NN)
            dk = dk + contract(score_grad, q_h, TN)
        grads = [g.astype(jnp.bfloat16) for g in (dq * scale, dk * scale, dv)]
        part = jnp.zeros((rows, model), jnp.float32)
        for c in range(3):
            here = slice(c * width, (c + 1) * width)
            part = part + contract(grads[c], w_ref[here, :], NN)
            big_ref[here, :] += contract(grads[c], entered, TN)
        sum_ref[i] = part
        gain_ref[i] = jnp.broadcast_to(
            jnp.sum(part * normed, axis=0, keepdims=True), gain_ref.shape[1:]
        )

    gain_grad = jnp.zeros((1, model), jnp.float32)
    for i in range(images):
        flat_ref[pl.ds(i * seq_len, seq_len), :] = sum_ref[i, 0:seq_len, :]
        gain_grad = gain_grad + gain_ref[i, 0:1, :]
    high, low = split_high_low(
        jnp.concatenate([small_ref[0 : SMALL - 1, :], gain_grad], axis=0)
    )
    for j, part in enumerate(parts):
        part[0:chunk, :] = flat_ref[chunk_of(pos_ref, j, chunk), :].astype(jnp.bfloat16)
        part[chunk:, :] = jnp.concatenate([high, low], axis=0)
    me, core = lax.axis_index("expert"), lax.axis_index("dp")
    piece = keep_ref.shape[1]
    for k in range(owners):
        place = lax.bitwise_xor(me, k) * piece
        mine = pl.ds(pl.multiple_of(core * owners * piece + place, 8), piece)
        other = pl.ds(pl.multiple_of((1 - core) * owners * piece + place, 8), piece)
        keep_ref[k] = big_ref[mine, :]
        send_ref[k] = big_ref[other, :].astype(jnp.bfloat16)


def norm_back_kernel(experts, tensors, pos_ref, *refs):
    got = refs[:tensors]
    x_ref, res_ref, param_ref, own_ref, *parts, grad_ref, out_ref, small_ref = refs[tensors:]
    chunk, width = x_ref.shape
    upstream = jnp.zeros((chunk, width), jnp.float32)
    for j, part in enumerate(got):
        upstream = upstream + part[0:chunk, :].astype(jnp.float32)
        small_ref[lax.bitwise_xor(lax.axis_index("tensor"), j)] = part[chunk : chunk + SMALL, :].astype(
            jnp.float32
        ) + part[chunk + SMALL :, :].astype(jnp.float32)
    small = small_ref[0]
    for j in range(1, tensors):
        small = small + small_ref[j]
    gain = gain_row(param_ref, experts, 0)
    normed, inverse, _ = normalize(x_ref[...].astype(jnp.float32), gain)
    from_norm = normalize_back(upstream, normed, inverse, gain)[0]
    grad_ref[...] = (res_ref[...] + from_norm).astype(jnp.bfloat16)
    piece = own_ref.shape[0]
    total = own_ref[...]
    for part in parts:
        total = total + part[...].astype(jnp.float32)
    out_ref[0:piece, :] = total.astype(jnp.bfloat16)
    out_ref[piece:, :] = jnp.concatenate(split_high_low(small), axis=0)


def second_step_kernel(pos_ref, near_ref, from_y, from_x, x_ref, y_ref):
    for target, row, other in ((x_ref, 0, from_y), (y_ref, 1, from_x)):
        total = near_ref[row].astype(jnp.float32) + other[1].astype(jnp.float32)
        target[...] = total.astype(jnp.bfloat16)


def weight_sum_kernel(pos_ref, own_ref, from_y, from_x, last_x, last_y, out_ref):
    part_rows = last_x.shape[1]
    for row, other, last in ((0, from_y, last_x), (1, from_x, last_y)):
        total = own_ref[row].astype(jnp.float32) + other[0].astype(jnp.float32)
        total = total + last[...].astype(jnp.float32)
        out_ref[:, row * part_rows : (row + 1) * part_rows, :] = total.astype(jnp.bfloat16)


def add_core_kernel(pos_ref, keep_ref, other_ref, own_ref, *outs):
    total = keep_ref[...] + other_ref[...].astype(jnp.float32)
    own_ref[...] = total[0]
    for k, out in enumerate(outs):
        out[...] = total[k + 1].astype(jnp.bfloat16)


def spread_kernel(owners, experts, token_total, pos_ref, *refs):
    blocks = refs[: 2 * owners]
    qkv_ref, wo_ref, router_ref, one_ref, two_ref, loss_ref, big_ref, parts_ref = refs[2 * owners :]
    piece = blocks[0].shape[0] - 2 * SMALL
    core, me = lax.axis_index("dp"), lax.axis_index("expert")
    for c in range(2):
        side = core if c == 0 else 1 - core
        for k in range(owners):
            block = blocks[c * owners + k]
            place = side * owners + lax.bitwise_xor(me, k)
            here = pl.ds(pl.multiple_of(place * piece, 8), piece)
            big_ref[here, :] = block[0:piece, :].astype(jnp.float32)
            parts_ref[place] = block[piece : piece + SMALL, :].astype(jnp.float32) + block[
                piece + SMALL :, :
            ].astype(jnp.float32)
    rows = qkv_ref.shape[0]
    qkv_ref[...] = big_ref[0:rows, :]
    wo_ref[...] = big_ref[rows:, :]
    small = parts_ref[0]
    for p in range(1, 2 * owners):
        small = small + parts_ref[p]
    router_ref[...] = small[0:experts, :]
    one_ref[...] = small[SMALL - 1 : SMALL, :].reshape(small.shape[1])
    two_ref[...] = small[experts : experts + 1, :].reshape(small.shape[1])
    product = small[experts + 1 : experts + 2, :LANES] * small[experts + 2 : experts + 3, :LANES]
    lane = lax.broadcasted_iota(jnp.int32, product.shape, 1)
    product = jnp.where(lane < experts, product, 0.0)
    loss = jnp.sum(product, axis=-1, keepdims=True)
    loss_ref[...] = jnp.broadcast_to(
        loss * (experts / (2.0 * token_total * token_total)), loss_ref.shape
    )


def images_kernel(pos_ref, *refs):
    *chunks, out_ref, flat_ref = refs
    images, seq_len, _ = out_ref.shape
    if len(chunks) == 1:
        flat_ref[...] = chunks[0][...].astype(jnp.float32)
    else:
        for j, part in enumerate(chunks):
            flat_ref[chunk_of(pos_ref, j, part.shape[0]), :] = part[...].astype(jnp.float32)
    for i in range(images):
        out_ref[i] = flat_ref[pl.ds(i * seq_len, seq_len), :].astype(out_ref.dtype)


def weight_out_kernel(pos_ref, mine_ref, other_ref, in_ref, out_ref):
    first_is_mine = lax.axis_index("dp") == 0
    half = mine_ref.shape[1]
    for c in range(2):
        here = slice(c * half, (c + 1) * half)
        take = first_is_mine if c == 0 else jnp.logical_not(first_is_mine)
        grad_in = jnp.where(take, mine_ref[0], other_ref[0]).astype(jnp.float32)
        in_ref[0, :, here] = grad_in.T
        out_ref[0, here, :] = jnp.where(take, mine_ref[1], other_ref[1]).astype(jnp.float32)


def swap_core(value):
    return lax.ppermute(value, "dp", [(0, 1), (1, 0)])


def hop(value, bit):
    size = lax.axis_size("expert")
    return lax.ppermute(value, "expert", [(i, i ^ bit) for i in range(size)])


def cross(value, bit):
    size = lax.axis_size("tensor")
    return lax.ppermute(value, "tensor", [(i, i ^ bit) for i in range(size)])


def after(value, *others):
    return lax.optimization_barrier((value, *others))[0]


def dense_body(
    tokens,
    cotangent,
    expert_ids,
    slot_rank,
    qkv_weight,
    out_weight,
    router_weight,
    expert_in,
    expert_out,
    gain_attention,
    gain_experts,
):
    f32, b16 = jnp.float32, jnp.bfloat16
    images, seq_len, width = tokens.shape
    token_rows = images * seq_len
    local = qkv_weight.shape[2]
    heads = local // HD
    experts = router_weight.shape[1]
    owners = lax.axis_size("expert")
    tensors = lax.axis_size("tensor")
    cores = lax.axis_size("dp")
    chunk = round_up(-(-token_rows // tensors), 16)
    padded = chunk * tensors
    rows = round_up(seq_len, 16)
    flat_rows = padded + 32
    half = expert_in.shape[2] // cores
    quarter = half // 2
    position = jnp.zeros((1,), jnp.int32)
    weight_rows = qkv_weight.transpose(0, 2, 1).reshape(3 * local, width)

    x_chunk, payload, params, mine, first, second = kernel_call(
        functools.partial(chunk_kernel, tensors),
        "chunk",
        position,
        [
            tokens,
            cotangent,
            expert_ids.transpose(0, 2, 1),
            slot_rank.transpose(0, 2, 1),
            router_weight.T,
            gain_attention,
            gain_experts,
            expert_in,
            expert_out,
        ],
        [
            like((chunk, width), b16),
            like((chunk, width + LANES), b16),
            like((SMALL, width), f32),
            like((2, half, width), b16),
            like((2, quarter, width), b16),
            like((2, quarter, width), b16),
        ],
        [
            pltpu.VMEM((flat_rows, width), f32),
            pltpu.VMEM((padded + 2 * LANES, LANES), f32),
        ],
        limit=56,
        loads=tuple(range(9)),
    )
    payload_mine = [payload] + [hop(payload, k) for k in range(1, owners)]
    first_x = cross(first, 1)
    second_y = cross(second, 2)

    qkv, lse, attended, *parts = kernel_call(
        functools.partial(attention_kernel, heads, experts),
        "attention",
        after(position, mine),
        [tokens, params, weight_rows, out_weight],
        [
            like((3, images, rows, local), b16),
            like((images, rows, LANES), f32),
            like((padded, local), b16),
        ]
        + [like((chunk, width), b16)] * tensors,
        [
            pltpu.VMEM((padded, local), f32),
            pltpu.VMEM((rows, width), f32),
            pltpu.VMEM((images, rows, local), f32),
        ],
        limit=20,
        loads=(0, 2, 3),
    )
    arrived = [parts[0]] + [cross(parts[j], j) for j in range(1, tensors)]
    pair_first, pair_second = stack_pairs(position, (first, first_x), (second, second_y))

    residual, routed, prob = kernel_call(
        functools.partial(route_kernel, experts),
        "route",
        after(position, pair_first, payload_mine[::-1]),
        [*arrived, x_chunk, params],
        [like((chunk, width), f32), like((chunk, width), b16), like((chunk, LANES), f32)],
        limit=8,
    )
    blocks = [routed] + [hop(routed, k) for k in range(1, owners)]
    pair_first, pair_second = after((pair_first, pair_second), routed)
    pair_y = cross(pair_first, 2)
    pair_x = cross(pair_second, 1)
    payload_mine = lay_rows(after(position, routed), "lay_payload", payload_mine)
    payload_other = swap_core(payload_mine)
    rows_mine = lay_rows(position, "lay_rows", blocks)
    rows_other = swap_core(rows_mine)

    near_weights, far_weights = (mine, first_x, second_y), (pair_y, pair_x)
    first_a = first_expert_pass(position, rows_mine, payload_mine, params, near_weights, experts)
    first_b = first_expert_pass(
        after(position, first_a[2]), rows_other, payload_other, params, near_weights, experts
    )
    second_b = second_expert_pass(
        after(position, first_b[2]), rows_other, payload_other, first_b, far_weights
    )
    back_other, gated_other = swap_core(second_b[3]), swap_core(second_b[2])
    second_a = second_expert_pass(
        after(position, second_b[0]), rows_mine, payload_mine, first_a, far_weights
    )
    joined = kernel_call(
        join_kernel,
        "join",
        position,
        [second_a[3], back_other, second_a[2], gated_other],
        [like((chunk + 2 * SMALL, width), b16)] * owners + [like((chunk, width), b16)] * owners,
        limit=8,
    )
    backs = [joined[0]] + [hop(joined[k], k) for k in range(1, owners)]

    grad_pos = after(position, joined[:owners])
    far_y, far_x = expert_grads(grad_pos, second_a, second_b, (rows_mine, first_a[2]), (rows_other, first_b[2]))
    from_y, from_x = cross(far_y, 2), cross(far_x, 1)
    own_grad, near_grad = expert_grads(
        after(grad_pos, far_y, backs[1]), first_a, first_b, (rows_mine, first_a[2]), (rows_other, first_b[2])
    )

    residual_grad, attn_grad, small = kernel_call(
        functools.partial(route_back_kernel, experts, token_rows, owners),
        "route_back",
        after(position, own_grad),
        [*backs, prob, residual, payload, params],
        [like((chunk, width), f32), like((chunk, width), b16), like((SMALL, width), f32)],
        flops=40_000_000_000,
        limit=8,
    )
    gated_back = [joined[owners]]
    for k in range(1, owners):
        gated_back.append(hop(after(joined[owners + k], attn_grad), k))
    attn_grad = lax.all_gather(attn_grad, "tensor", axis=0, tiled=True)
    piece = 4 * local // (2 * owners)
    keep, send, *parts = kernel_call(
        functools.partial(attention_back_kernel, heads, experts, owners),
        "attention_back",
        after(position, from_y, from_x, gated_back[1:]),
        [tokens, params, weight_rows, out_weight, qkv, lse, attended, attn_grad, small],
        [
            like((owners, piece, width), f32),
            like((owners, piece, width), b16),
        ]
        + [like((chunk + 2 * SMALL, width), b16)] * tensors,
        [
            pltpu.VMEM((flat_rows, local), f32),
            pltpu.VMEM((flat_rows, width), f32),
            pltpu.VMEM((4 * local, width), f32),
            pltpu.VMEM((rows, width), f32),
            pltpu.VMEM((images, rows, local), f32),
            pltpu.VMEM((images, rows, width), f32),
            pltpu.VMEM((images, SMALL, width), f32),
        ],
        limit=20,
        flops=6_000_000_000,
    )
    own_piece, *pieces = kernel_call(
        add_core_kernel,
        "add_core",
        position,
        [keep, swap_core(send)],
        [like((piece, width), f32)] + [like((piece, width), b16)] * (owners - 1),
        limit=8,
    )
    reduced = [hop(p, k + 1) for k, p in enumerate(pieces)]
    got = [parts[0]] + [cross(parts[j], j) for j in range(1, tensors)]
    up_x, up_y = kernel_call(
        second_step_kernel,
        "second_step",
        after(position, got[1:], own_piece),
        [near_grad, from_y, from_x],
        [like((2, quarter, width), b16)] * 2,
        limit=8,
    )
    last_x, last_y = cross(up_x, 1), cross(up_y, 2)

    grad_chunk, summed = kernel_call(
        functools.partial(norm_back_kernel, experts, tensors),
        "norm_back",
        position,
        [*got, x_chunk, residual_grad, params, own_piece, *reduced],
        [like((chunk, width), b16), like((piece + 2 * SMALL, width), b16)],
        [pltpu.VMEM((tensors, SMALL, width), f32)],
        flops=40_000_000_000,
        limit=8,
    )
    around = [summed] + [hop(summed, k) for k in range(1, owners)]
    grad_rows = lax.all_gather(grad_chunk, "tensor", axis=0, tiled=True)
    combined = residual
    for part in gated_back:
        combined = combined + part.astype(f32)
    combined = combined.astype(b16)
    combined = after(combined, grad_rows)
    block_parts = [combined] + [cross(combined, j) for j in range(1, tensors)]

    grad_tokens = kernel_call(
        images_kernel,
        "grad_tokens",
        after(position, around, last_x, last_y),
        [grad_rows],
        [like(tokens.shape, f32)],
        [pltpu.VMEM((padded, width), f32)],
        limit=8,
    )[0]
    grad_half = kernel_call(
        weight_sum_kernel,
        "weight_sum",
        after(position, grad_tokens),
        [own_grad, from_y, from_x, last_x, last_y],
        [like((2, half, width), b16)],
        limit=8,
    )[0]
    grad_expert_in, grad_expert_out = kernel_call(
        weight_out_kernel,
        "weight_out",
        position,
        [grad_half, swap_core(grad_half)],
        [like((1, width, 2 * half), f32), like((1, 2 * half, width), f32)],
        limit=10,
    )
    token_total = token_rows * cores * owners
    grad_qkv, grad_out, grad_router, gain_one, gain_two, loss = kernel_call(
        functools.partial(spread_kernel, owners, experts, token_total),
        "spread",
        position,
        around + [swap_core(a) for a in around],
        [
            like((3 * local, width), f32),
            like((local, width), f32),
            like((experts, width), f32),
            like((width,), f32),
            like((width,), f32),
            like((1, LANES), f32),
        ],
        [
            pltpu.VMEM((4 * local, width), f32),
            pltpu.VMEM((2 * owners, SMALL, width), f32),
        ],
        limit=8,
    )
    block_out = kernel_call(
        images_kernel,
        "block_out",
        after(position, grad_tokens, grad_expert_in, grad_qkv),
        block_parts,
        [like(tokens.shape, b16)],
        [pltpu.VMEM((padded, width), f32)],
        limit=8,
    )[0]
    return (
        block_out,
        grad_tokens,
        grad_qkv.reshape(3, local, width).transpose(0, 2, 1),
        grad_out,
        grad_router.T,
        grad_expert_in,
        grad_expert_out,
        gain_one,
        gain_two,
        loss[0, 0],
    )


def solution(mesh):
    placed = (
        P(("dp", "expert"), None, None),
        P(("dp", "expert"), None, None),
        P(("dp", "expert"), None, None),
        P(("dp", "expert"), None, None),
        P(None, None, "tensor"),
        P("tensor", None),
        P(),
        P("expert", None, "tensor"),
        P("expert", "tensor", None),
        P(),
        P(),
    )
    shape = mesh.shape
    dense = shape["dp"] == 2 and shape["expert"] == 4 and shape["tensor"] == 4
    return jax.shard_map(
        dense_body if dense else body,
        mesh=mesh,
        in_specs=placed,
        out_specs=(
            P(("dp", "expert"), None, None),
            P(("dp", "expert"), None, None),
            P(None, None, "tensor"),
            P("tensor", None),
            P(),
            P("expert", None, "tensor"),
            P("expert", "tensor", None),
            P(),
            P(),
            P(),
        ),
        check_vma=False,
    )
```

```python
import functools
import math

import jax
import jax.numpy as jnp
from jax import lax
from jax.experimental import pallas as pl
from jax.experimental.pallas import tpu as pltpu
from jax.sharding import PartitionSpec as P

HD = 64


epsilon = 1e-06


def normalize(values, gain_row):
    center = values - jnp.mean(values, axis=-1, keepdims=True)
    inverse = lax.rsqrt(jnp.mean(center * center, axis=-1, keepdims=True) + epsilon)
    normed = center * inverse
    return (normed, inverse, normed * gain_row)


def normalize_back(upstream, normed, inverse, gain_row):
    scaled = upstream * gain_row
    result = inverse * (
        scaled
        - jnp.mean(scaled, axis=-1, keepdims=True)
        - normed * jnp.mean(scaled * normed, axis=-1, keepdims=True)
    )
    return (result, jnp.sum(upstream * normed, axis=0))


def exact_gelu(values):
    return jax.nn.gelu(values, approximate=False)


def body(
    tokens,
    cotangent,
    expert_ids,
    slot_rank,
    qkv_weight,
    out_weight,
    router_weight,
    expert_in,
    expert_out,
    gain_attention,
    gain_experts,
):
    images, seq_len, model_width = tokens.shape
    token_rows = images * seq_len
    local_width = qkv_weight.shape[2]
    local_heads = local_width // HD
    slice_width = model_width // lax.axis_size("tensor")
    experts = router_weight.shape[1]
    capacity = 5 * token_rows // (2 * experts)
    owners = lax.axis_size("expert")
    per_owner = experts // owners
    slot_total = experts * capacity
    score_scale = HD ** (-0.5)
    inputs = tokens.reshape(token_rows, model_width).astype(jnp.float32)
    normed_one, inverse_one, mixed_one = normalize(inputs, gain_attention)
    entered = mixed_one.astype(jnp.bfloat16)
    project = jnp.einsum(
        "td,cdf->ctf", entered, qkv_weight, preferred_element_type=jnp.float32
    ).astype(jnp.bfloat16)
    projected_heads = project.reshape(3, images, seq_len, local_heads, HD)
    queries, key_rows, value_rows = (projected_heads[0], projected_heads[1], projected_heads[2])
    scores = (
        jnp.einsum("ishe,ithe->ihst", queries, key_rows, preferred_element_type=jnp.float32)
        * score_scale
    )
    log_total = jax.nn.logsumexp(scores, axis=-1, keepdims=True)
    attn_probs = jnp.exp(scores - log_total).astype(jnp.bfloat16)
    attended = jnp.einsum(
        "ihst,ithe->ishe", attn_probs, value_rows, preferred_element_type=jnp.float32
    )
    attended = attended.astype(jnp.bfloat16).reshape(token_rows, local_width)
    attn_part = jnp.dot(attended, out_weight, preferred_element_type=jnp.float32)
    residual = inputs + lax.psum(attn_part, "tensor")
    normed_two, inverse_two, mixed_two = normalize(residual, gain_experts)
    routed = mixed_two.astype(jnp.bfloat16)
    route_prob = jax.nn.softmax(
        jnp.dot(routed, router_weight, preferred_element_type=jnp.float32), axis=-1
    )
    chosen = expert_ids.reshape(token_rows, 2)
    ranked = slot_rank.reshape(token_rows, 2)
    kept_mask = (ranked >= 0).astype(jnp.float32)
    position = jnp.where(ranked >= 0, chosen * capacity + ranked, slot_total).reshape(-1)
    send_rows = (
        jnp.zeros((slot_total, model_width), jnp.bfloat16)
        .at[position]
        .set(jnp.repeat(routed, 2, axis=0), mode="drop")
        .reshape(experts, capacity, model_width)
    )
    fragment = lax.all_to_all(send_rows, "expert", split_axis=0, concat_axis=0, tiled=True)
    grouped = fragment.reshape(owners, per_owner, fragment.shape[1], model_width)
    before = jnp.einsum("sjcd,jdf->sjcf", grouped, expert_in, preferred_element_type=jnp.float32)
    hidden = exact_gelu(before).astype(jnp.bfloat16)
    expert_part = jnp.einsum(
        "sjcf,jfd->sjcd", hidden, expert_out, preferred_element_type=jnp.float32
    )
    produced = lax.psum_scatter(expert_part, "tensor", scatter_dimension=3, tiled=True).astype(
        jnp.bfloat16
    )
    returned = lax.all_to_all(
        produced.reshape(experts, capacity, slice_width),
        "expert",
        split_axis=0,
        concat_axis=0,
        tiled=True,
    )
    returned = lax.all_gather(returned, "tensor", axis=2, tiled=True).reshape(
        slot_total, model_width
    )
    safe_index = jnp.minimum(position, slot_total - 1)
    picked = returned[safe_index].reshape(token_rows, 2, model_width).astype(jnp.float32)
    gate_values = jnp.take_along_axis(route_prob, chosen, axis=1) * kept_mask
    output = residual + jnp.sum(gate_values[:, :, None] * picked, axis=1)
    block_out = output.astype(jnp.bfloat16).reshape(images, seq_len, model_width)
    upstream = cotangent.reshape(token_rows, model_width).astype(jnp.float32)
    gate_grad = jnp.sum(upstream[:, None, :] * picked, axis=-1) * kept_mask
    member = (chosen[:, :, None] == jnp.arange(experts)[None, None, :]).astype(jnp.float32)
    route_grad = jnp.sum(member * gate_grad[:, :, None], axis=1)
    logit_grad = (
        route_prob * (route_grad - jnp.sum(route_grad * route_prob, axis=-1, keepdims=True))
    ).astype(jnp.bfloat16)
    row_grad = (
        (gate_values[:, :, None] * upstream[:, None, :])
        .astype(jnp.bfloat16)
        .reshape(2 * token_rows, model_width)
    )
    grad_send = (
        jnp.zeros((slot_total, model_width), jnp.bfloat16)
        .at[position]
        .set(row_grad, mode="drop")
        .reshape(experts, capacity, model_width)
    )
    grad_arrived = lax.all_to_all(grad_send, "expert", split_axis=0, concat_axis=0, tiled=True)
    grad_arrived = grad_arrived.reshape(owners, per_owner, capacity, model_width)
    hidden_grad = jnp.einsum(
        "sjcd,jfd->sjcf", grad_arrived, expert_out, preferred_element_type=jnp.float32
    )
    grad_expert_out = jnp.einsum(
        "sjcf,sjcd->jfd", hidden, grad_arrived, preferred_element_type=jnp.float32
    )
    pre_grad = jax.vjp(exact_gelu, before)[1](hidden_grad)[0].astype(jnp.bfloat16)
    grad_expert_in = jnp.einsum(
        "sjcd,sjcf->jdf", grouped, pre_grad, preferred_element_type=jnp.float32
    )
    buffer_part = jnp.einsum(
        "sjcf,jdf->sjcd", pre_grad, expert_in, preferred_element_type=jnp.float32
    )
    buffer_share = lax.psum_scatter(buffer_part, "tensor", scatter_dimension=3, tiled=True).astype(
        jnp.bfloat16
    )
    buffer_back = lax.all_to_all(
        buffer_share.reshape(experts, capacity, slice_width),
        "expert",
        split_axis=0,
        concat_axis=0,
        tiled=True,
    )
    buffer_grad = lax.all_gather(buffer_back, "tensor", axis=2, tiled=True).reshape(
        slot_total, model_width
    )
    routed_grad = jnp.sum(
        buffer_grad[safe_index].reshape(token_rows, 2, model_width).astype(jnp.float32)
        * kept_mask[:, :, None],
        axis=1,
    )
    routed_grad = routed_grad + jnp.dot(
        logit_grad, router_weight.T, preferred_element_type=jnp.float32
    )
    grad_router = jnp.einsum("td,te->de", routed, logit_grad, preferred_element_type=jnp.float32)
    from_norm_two, grad_gain_experts = normalize_back(
        routed_grad, normed_two, inverse_two, gain_experts
    )
    residual_grad = upstream + from_norm_two
    attn_grad = residual_grad.astype(jnp.bfloat16)
    grad_out = jnp.einsum("tf,td->fd", attended, attn_grad, preferred_element_type=jnp.float32)
    heads_grad = jnp.dot(attn_grad, out_weight.T, preferred_element_type=jnp.float32).astype(
        jnp.bfloat16
    )
    heads_grad = heads_grad.reshape(images, seq_len, local_heads, HD)
    again = (
        jnp.einsum("ishe,ithe->ihst", queries, key_rows, preferred_element_type=jnp.float32)
        * score_scale
    )
    probs_full = jnp.exp(again - log_total)
    prob_grad = jnp.einsum(
        "ishe,ithe->ihst", heads_grad, value_rows, preferred_element_type=jnp.float32
    )
    value_grad = jnp.einsum(
        "ihst,ishe->ithe",
        probs_full.astype(jnp.bfloat16),
        heads_grad,
        preferred_element_type=jnp.float32,
    )
    score_grad = (
        probs_full * (prob_grad - jnp.sum(prob_grad * probs_full, axis=-1, keepdims=True))
    ).astype(jnp.bfloat16)
    query_grad = (
        jnp.einsum("ihst,ithe->ishe", score_grad, key_rows, preferred_element_type=jnp.float32)
        * score_scale
    )
    key_grad = (
        jnp.einsum("ihst,ishe->ithe", score_grad, queries, preferred_element_type=jnp.float32)
        * score_scale
    )
    project_grad = (
        jnp.stack([query_grad, key_grad, value_grad])
        .astype(jnp.bfloat16)
        .reshape(3, token_rows, local_width)
    )
    grad_qkv = jnp.einsum("td,ctf->cdf", entered, project_grad, preferred_element_type=jnp.float32)
    entered_part = jnp.einsum(
        "ctf,cdf->td", project_grad, qkv_weight, preferred_element_type=jnp.float32
    )
    entered_grad = lax.psum(entered_part.astype(jnp.bfloat16), "tensor").astype(jnp.float32)
    from_norm_one, grad_gain_attention = normalize_back(
        entered_grad, normed_one, inverse_one, gain_attention
    )
    grad_tokens = (residual_grad + from_norm_one).reshape(images, seq_len, model_width)
    counts = jnp.sum(member, axis=(0, 1))
    prob_sum = jnp.sum(route_prob, axis=0)
    grad_qkv, grad_out, grad_router, grad_gain_attention, grad_gain_experts, counts, prob_sum = (
        lax.psum(
            (
                grad_qkv,
                grad_out,
                grad_router,
                grad_gain_attention,
                grad_gain_experts,
                counts,
                prob_sum,
            ),
            ("dp", "expert"),
        )
    )
    grad_expert_in, grad_expert_out = (
        lax.psum(grad_expert_in.astype(jnp.bfloat16), "dp").astype(jnp.float32),
        lax.psum(grad_expert_out.astype(jnp.bfloat16), "dp").astype(jnp.float32),
    )
    token_total = token_rows * lax.axis_size("dp") * lax.axis_size("expert")
    balance_loss = experts * jnp.sum(counts / (2.0 * token_total) * prob_sum / token_total)
    return (
        block_out,
        grad_tokens,
        grad_qkv,
        grad_out,
        grad_router,
        grad_expert_in,
        grad_expert_out,
        grad_gain_attention,
        grad_gain_experts,
        balance_loss,
    )


NN = ((1,), (0,))
NT = ((1,), (1,))
TN = ((0,), (0,))
LANES = 128
SMALL = 8


def round_up(value, step):
    return -(-value // step) * step


def contract(a, b, dims):
    return lax.dot_general(a, b, (dims, ((), ())), preferred_element_type=jnp.float32)


def load_then(kernel, loads, count, *refs):
    pos_ref, *refs = refs
    *refs, sem = refs
    buffers = refs[len(refs) - len(loads) :]
    refs = refs[: len(refs) - len(loads)]
    copies = [
        pltpu.make_async_copy(refs[index], buffer, sem.at[i])
        for i, (index, buffer) in enumerate(zip(loads, buffers))
    ]
    for copy in copies:
        copy.start()
    for index, buffer in zip(loads, buffers):
        refs[index] = buffer

    def arrive(*indices):
        for index in indices:
            copies[loads.index(index)].wait()

    kernel(arrive, pos_ref, *refs)


def kernel_call(kernel, name, position, args, outs, scratch=(), flops=0, limit=24, loads=()):
    if loads:
        kernel = functools.partial(load_then, kernel, loads, len(args))
        scratch = [
            *scratch,
            *(pltpu.VMEM(args[i].shape, args[i].dtype) for i in loads),
            pltpu.SemaphoreType.DMA((len(loads),)),
        ]
    places = [pltpu.HBM if i in loads else pltpu.VMEM for i in range(len(args))]
    return pl.pallas_call(
        kernel,
        in_specs=[pl.BlockSpec(memory_space=pltpu.SMEM)]
        + [pl.BlockSpec(memory_space=place) for place in places],
        out_specs=[pl.BlockSpec(memory_space=pltpu.VMEM)] * len(outs),
        out_shape=list(outs),
        scratch_shapes=list(scratch),
        compiler_params=pltpu.CompilerParams(vmem_limit_bytes=limit << 20),
        cost_estimate=pl.CostEstimate(flops=flops, bytes_accessed=0, transcendentals=0),
        name=name,
    )(position, *args)


def like(shape, dtype):
    return jax.ShapeDtypeStruct(shape, dtype)


def live_rows(shape, limit, offset=0):
    return lax.broadcasted_iota(jnp.int32, shape, 0) + offset < limit


def chunk_of(pos_ref, j, size):
    return pl.ds(pl.multiple_of(lax.bitwise_xor(lax.axis_index("tensor"), j) * size, 16), size)


def head_masks(rows, heads):
    lane = lax.broadcasted_iota(jnp.int32, (rows, heads * HD), 1)
    return [(lane >= h * HD) & (lane < (h + 1) * HD) for h in range(heads)]


def keep_lanes(value, mask):
    return jnp.where(mask, value, jnp.zeros_like(value))


def split_high_low(value):
    high = value.astype(jnp.bfloat16)
    return high, (value - high.astype(jnp.float32)).astype(jnp.bfloat16)


def image_rows(ref, i, scratch_ref):
    seq_len = ref.shape[1]
    scratch_ref[seq_len:, :] = jnp.zeros((scratch_ref.shape[0] - seq_len, ref.shape[2]), jnp.float32)
    scratch_ref[0:seq_len, :] = ref[i].astype(jnp.float32)
    return scratch_ref[...]


def router_matrix(param_ref, experts):
    rows = param_ref[0:SMALL, :]
    rows = jnp.where(live_rows(rows.shape, experts), rows, 0.0).astype(jnp.bfloat16)
    zeros = jnp.zeros((LANES - SMALL, rows.shape[1]), jnp.bfloat16)
    return jnp.concatenate([rows, zeros], axis=0)


def chunk_kernel(
    tensors, arrive, pos_ref, tok_ref, cot_ref, ids_ref, rank_ref, router_ref, one_ref, two_ref, in_ref, out_ref,
    x_ref, pay_ref, param_ref, mine_ref, first_ref, second_ref, flat_ref, kept_ref,
):
    images, seq_len, width = tok_ref.shape
    chunk, experts = x_ref.shape[0], router_ref.shape[0]
    start = pl.multiple_of(lax.axis_index("tensor") * chunk, 16)
    for index, source, target in ((0, tok_ref, x_ref), (1, cot_ref, pay_ref)):
        arrive(index)
        flat_ref[images * seq_len :, :] = jnp.zeros(
            (flat_ref.shape[0] - images * seq_len, width), jnp.float32
        )
        for i in range(images):
            flat_ref[pl.ds(i * seq_len, seq_len), :] = source[i].astype(jnp.float32)
        target[0:chunk, :] = flat_ref[pl.ds(start, chunk), :].astype(jnp.bfloat16)
    arrive(2, 3, 4, 5, 6)
    kept_ref[...] = jnp.zeros_like(kept_ref)
    counts = jnp.zeros((1, LANES), jnp.float32)
    for i in range(images):
        rows, all_rows = [], []
        for e in range(experts):
            named = (ids_ref[i] == e).astype(jnp.float32)
            kept = jnp.where(rank_ref[i] >= 0, named, 0.0)
            rows.append(jnp.sum(kept, axis=0, keepdims=True))
            all_rows.append(jnp.sum(named, axis=0, keepdims=True))
        for group, is_kept in ((rows, True), (all_rows, False)):
            table = jnp.concatenate(group, axis=0)
            table = jnp.concatenate(
                [table, jnp.zeros((LANES - experts, seq_len), jnp.float32)], axis=0
            )
            table = jnp.concatenate(
                [table, jnp.zeros((LANES, 2 * LANES - seq_len), jnp.float32)], axis=1
            ).T
            if is_kept:
                kept_ref[pl.ds(i * seq_len, 2 * LANES), :] = table
            else:
                counts = counts + jnp.sum(table, axis=0, keepdims=True)
    kept = jnp.concatenate(
        [kept_ref[pl.ds(start, chunk), :], jnp.zeros((2 * LANES - chunk, LANES), jnp.float32)], axis=0
    ).T
    pay_ref[chunk:, : 2 * LANES] = kept[0 : 2 * SMALL].astype(jnp.bfloat16)
    pay_ref[chunk:, 2 * LANES :] = jnp.zeros((2 * SMALL, width - 2 * LANES), jnp.bfloat16)
    param_ref[...] = jnp.zeros_like(param_ref)
    param_ref[0:experts, :] = router_ref[...].astype(jnp.float32)
    param_ref[experts : experts + 1, :] = one_ref[...].reshape(1, width)
    param_ref[experts + 1 : experts + 2, :] = two_ref[...].reshape(1, width)
    param_ref[SMALL - 1 : SMALL, :LANES] = counts * (1.0 / tensors)
    arrive(7, 8)
    half = mine_ref.shape[1]
    core = pl.multiple_of(lax.axis_index("dp") * half, LANES)
    for s, part in ((0, in_ref[0, :, pl.ds(core, half)].T), (1, out_ref[0, pl.ds(core, half), :])):
        mine_ref[s] = part
        first_ref[s] = part[0 : half // 2]
        second_ref[s] = part[half // 2 :]


def stack_kernel(pos_ref, *refs):
    count = len(refs) // 3
    for i, target in enumerate(refs[2 * count :]):
        target[0] = refs[2 * i][...]
        target[1] = refs[2 * i + 1][...]


def stack_pairs(position, *pairs):
    return kernel_call(
        stack_kernel,
        "stack",
        position,
        [value for pair in pairs for value in pair],
        [like((2, *pair[0].shape), pair[0].dtype) for pair in pairs],
        limit=4,
    )


def lay_kernel(pos_ref, *refs):
    *blocks, out_ref = refs
    chunk = blocks[0].shape[0]
    for k, block in enumerate(blocks):
        out_ref[k * chunk : (k + 1) * chunk, :] = block[...]


def lay_payload_kernel(pos_ref, *refs):
    *blocks, out_ref = refs
    chunk = out_ref.shape[0] // len(blocks)
    width = blocks[0].shape[1]
    for k, block in enumerate(blocks):
        here = slice(k * chunk, (k + 1) * chunk)
        out_ref[here, :width] = block[0:chunk, :]
        kept = block[chunk:, : 2 * LANES].astype(jnp.float32)
        kept = jnp.concatenate([kept] * (LANES // kept.shape[0]), axis=0).T[0:chunk]
        out_ref[here, width:] = kept.astype(jnp.bfloat16)


def lay_rows(position, name, blocks):
    chunk, width = blocks[0].shape
    return kernel_call(
        lay_kernel,
        name,
        position,
        blocks,
        [like((len(blocks) * chunk, width), blocks[0].dtype)],
        limit=4,
    )[0]


def gain_row(param_ref, experts, which):
    return param_ref[experts + which : experts + which + 1, :]


def attention_kernel(
    heads, experts, arrive, pos_ref, tok_ref, param_ref, w_ref, wo_ref, qkv_ref, lse_ref, att_ref,
    *refs,
):
    *parts, flat_ref, image_ref, held_ref = refs
    images, rows, width = qkv_ref.shape[1], qkv_ref.shape[2], heads * HD
    seq_len = tok_ref.shape[1]
    masks = head_masks(rows, heads)
    keys_live = lax.broadcasted_iota(jnp.int32, (rows, rows), 1) < seq_len
    lane = lax.broadcasted_iota(jnp.int32, (rows, LANES), 1)
    flat_ref[images * seq_len :, :] = jnp.zeros(
        (flat_ref.shape[0] - images * seq_len, width), jnp.float32
    )
    arrive(0, 1, 2)

    @pl.loop(0, images)
    def _(i):
        entered = normalize(image_rows(tok_ref, i, image_ref), gain_row(param_ref, experts, 0))[2]
        entered = entered.astype(jnp.bfloat16)
        q, k, v = (
            contract(entered, w_ref[c * width : (c + 1) * width, :], NT).astype(jnp.bfloat16)
            for c in range(3)
        )
        qkv_ref[0, i], qkv_ref[1, i], qkv_ref[2, i] = q, k, v
        attended = jnp.zeros((rows, width), jnp.float32)
        lse_all = jnp.zeros((rows, LANES), jnp.float32)
        for h in range(heads):
            scores = contract(keep_lanes(q, masks[h]), k, NT) * (HD ** (-0.5))
            scores = jnp.where(keys_live, scores, -1e30)
            top = jnp.max(scores, axis=-1, keepdims=True)
            lse = top + jnp.log(jnp.sum(jnp.exp(scores - top), axis=-1, keepdims=True))
            probs = jnp.exp(scores - lse).astype(jnp.bfloat16)
            attended = attended + contract(probs, keep_lanes(v, masks[h]), NN)
            lse_all = jnp.where(lane == h, lse, lse_all)
        lse_ref[i] = lse_all
        held_ref[i] = attended

    for i in range(images):
        flat_ref[pl.ds(i * seq_len, seq_len), :] = held_ref[i, 0:seq_len, :]
    arrive(3)
    att_ref[...] = flat_ref[...].astype(jnp.bfloat16)
    for j, part in enumerate(parts):
        rows_j = flat_ref[chunk_of(pos_ref, j, part.shape[0]), :].astype(jnp.bfloat16)
        part[...] = contract(rows_j, wo_ref[...], NN).astype(jnp.bfloat16)


def route_kernel(experts, pos_ref, *refs):
    *got, x_ref, param_ref, res_ref, routed_ref, prob_ref = refs
    residual = x_ref[...].astype(jnp.float32)
    for part in got:
        residual = residual + part[...].astype(jnp.float32)
    res_ref[...] = residual
    routed = normalize(residual, gain_row(param_ref, experts, 1))[2].astype(jnp.bfloat16)
    routed_ref[...] = routed
    prob_ref[...] = route_probs(routed, router_matrix(param_ref, experts), experts)


def route_probs(rows, router, experts):
    logits = contract(rows, router, NT)
    lane = lax.broadcasted_iota(jnp.int32, logits.shape, 1)
    logits = jnp.where(lane < experts, logits, -1e30)
    weight = jnp.exp(logits - jnp.max(logits, axis=-1, keepdims=True))
    return weight / jnp.sum(weight, axis=-1, keepdims=True)


def gelu_parts(x):
    square = jnp.exp(-0.5 * x * x)
    share = 0.5 * (1.0 + lax.erf(x * (0.5**0.5)))
    return x * share, share + x * square * (0.5 / math.pi) ** 0.5


def expert_halves(x, rg, w_in, w_out, hidden_ref, pre_ref):
    before = contract(x, w_in, NT)
    value, slope = gelu_parts(before)
    hidden = value.astype(jnp.bfloat16)
    hidden_ref[...] = hidden
    part = contract(hidden, w_out, NN)
    pre = (contract(rg, w_out, NT) * slope).astype(jnp.bfloat16)
    pre_ref[...] = pre
    return part, contract(pre, w_in, NN)


def first_expert_kernel(
    experts, pos_ref, x_ref, pay_ref, param_ref, w0_ref, xa_ref, yb_ref, hidden_ref, pre_ref, rg_ref,
    gate_ref, part_ref, back_ref,
):
    count, width = x_ref.shape
    prob = route_probs(x_ref[...], router_matrix(param_ref, experts), experts)
    mine = lax.broadcasted_iota(jnp.int32, prob.shape, 1) == lax.axis_index("expert")
    kept = pay_ref[:, width:].astype(jnp.float32)
    kept = jnp.sum(jnp.where(mine, kept, 0.0), axis=-1, keepdims=True)
    gate = jnp.sum(jnp.where(mine, prob, 0.0), axis=-1, keepdims=True) * kept
    gate_ref[:, :LANES] = jnp.broadcast_to(gate, (count, LANES))
    gate_ref[:, LANES:] = jnp.broadcast_to(kept, (count, LANES))
    rg_ref[...] = (gate * pay_ref[:, :width].astype(jnp.float32)).astype(jnp.bfloat16)
    w_in, w_out = (
        jnp.concatenate([w0_ref[s], xa_ref[s], yb_ref[s]], axis=0) for s in range(2)
    )
    part_ref[...], back_ref[...] = expert_halves(
        x_ref[...], rg_ref[...], w_in, w_out, hidden_ref, pre_ref
    )


def second_expert_kernel(
    pos_ref, x_ref, pay_ref, rg_ref, gate_ref, part_in_ref, back_in_ref, pair_y_ref, pair_x_ref,
    hidden_ref, pre_ref, gated_ref, back_ref,
):
    width = x_ref.shape[1]
    w_in, w_out = (
        jnp.concatenate([ref[r, s] for ref in (pair_y_ref, pair_x_ref) for r in range(2)], axis=0)
        for s in range(2)
    )
    part, back = expert_halves(x_ref[...], rg_ref[...], w_in, w_out, hidden_ref, pre_ref)
    back_ref[:, :width] = back_in_ref[...] + back
    part = part_in_ref[...] + part
    gated_ref[...] = (gate_ref[:, 0:1] * part).astype(jnp.bfloat16)
    inner = jnp.sum(part * pay_ref[:, :width].astype(jnp.float32), axis=-1, keepdims=True)
    back_ref[:, width:] = gate_ref[:, LANES:] * inner


def first_expert_pass(position, rows, payload, params, weights, experts):
    count, width = rows.shape
    hidden = 2 * weights[0].shape[1]
    return kernel_call(
        functools.partial(first_expert_kernel, experts),
        "experts_first",
        position,
        [rows, payload, params, *weights],
        [
            like((count, hidden), jnp.bfloat16),
            like((count, hidden), jnp.bfloat16),
            like((count, width), jnp.bfloat16),
            like((count, 2 * LANES), jnp.float32),
            like((count, width), jnp.float32),
            like((count, width), jnp.float32),
        ],
        limit=18,
    )


def second_expert_pass(position, rows, payload, first, weights):
    count, width = rows.shape
    hidden = 4 * weights[0].shape[2]
    return kernel_call(
        second_expert_kernel,
        "experts_second",
        position,
        [rows, payload, *first[2:], *weights],
        [
            like((count, hidden), jnp.bfloat16),
            like((count, hidden), jnp.bfloat16),
            like((count, width), jnp.bfloat16),
            like((count, width + LANES), jnp.float32),
        ],
        limit=18,
    )


def join_kernel(pos_ref, back_ref, other_ref, gated_ref, gated_other_ref, *outs):
    *backs, own_ref, pair_ref, far_ref = outs
    chunk, width = own_ref.shape
    for k, out in enumerate(backs):
        here = pl.ds(k * chunk, chunk)
        total = back_ref[here, :] + other_ref[here, :]
        out[0:chunk, :] = total[:, :width].astype(jnp.bfloat16)
        inner = jnp.concatenate(
            [total[:, width:], jnp.zeros((2 * LANES - chunk, LANES), jnp.float32)], axis=0
        ).T
        high, low = split_high_low(inner[0:SMALL, :])
        both = jnp.where(
            live_rows(high.shape, SMALL // 2), high.astype(jnp.float32), low.astype(jnp.float32)
        )
        out[chunk:, : 2 * LANES] = both.astype(jnp.bfloat16)
        out[chunk:, 2 * LANES :] = jnp.zeros((SMALL, width - 2 * LANES), jnp.bfloat16)
        gated = gated_ref[here, :].astype(jnp.float32) + gated_other_ref[here, :].astype(jnp.float32)
        gated = gated.astype(jnp.bfloat16)
        if k % 2:
            pair_ref[k // 2] = gated
        else:
            (own_ref, far_ref)[k // 2][...] = gated


def pair_sum_kernel(pos_ref, base_ref, own_ref, far_ref, got_ref, sum_ref, send_ref):
    total = base_ref[...] + own_ref[...].astype(jnp.float32) + got_ref[0].astype(jnp.float32)
    sum_ref[...] = total
    send_ref[...] = (far_ref[...].astype(jnp.float32) + got_ref[1].astype(jnp.float32)).astype(
        jnp.bfloat16
    )


def expert_grad_kernel(pos_ref, *refs):
    *sources, first_ref, second_ref = refs
    part_rows = first_ref.shape[2]
    for j, out in enumerate((first_ref, second_ref)):
        columns = slice(2 * j * part_rows, 2 * (j + 1) * part_rows)
        for s in range(2):
            left_a, right_a, left_b, right_b = sources[4 * s : 4 * s + 4]
            grad = contract(left_a[:, columns], right_a[...], TN)
            grad = grad + contract(left_b[:, columns], right_b[...], TN)
            grad = grad.astype(jnp.bfloat16)
            out[0, s] = grad[0:part_rows]
            out[1, s] = grad[part_rows:]


def expert_grads(position, a, b, rows_a, rows_b, flops=0):
    width, total = rows_a[0].shape[1], a[0].shape[1]
    return kernel_call(
        expert_grad_kernel,
        "expert_grads",
        position,
        [a[1], rows_a[0], b[1], rows_b[0], a[0], rows_a[1], b[0], rows_b[1]],
        [like((2, 2, total // 4, width), jnp.bfloat16)] * 2,
        flops=flops,
        limit=10,
    )


def route_back_kernel(
    experts, token_rows, owners, pos_ref, *refs
):
    backs = refs[:owners]
    prob_ref, res_ref, pay_ref, param_ref = refs[owners : owners + 4]
    grad_ref, up_ref, small_ref = refs[owners + 4 :]
    chunk, width = res_ref.shape
    prob = prob_ref[...]
    lane = lax.broadcasted_iota(jnp.int32, prob.shape, 1)
    route_grad = jnp.zeros_like(prob)
    routed_grad = jnp.zeros((chunk, width), jnp.float32)
    for k, back in enumerate(backs):
        owner = lax.bitwise_xor(lax.axis_index("expert"), k)
        inner = back[chunk:, : 2 * LANES].astype(jnp.float32)
        inner = jnp.concatenate([inner] * (LANES // SMALL), axis=0).T[0:chunk]
        inner = jnp.sum(inner, axis=-1, keepdims=True) * (2.0 / LANES)
        route_grad = jnp.where(lane == owner, inner, route_grad)
        routed_grad = routed_grad + back[0:chunk, :].astype(jnp.float32)
    mean = jnp.sum(route_grad * prob, axis=-1, keepdims=True)
    logit_grad = (prob * (route_grad - mean)).astype(jnp.bfloat16)
    routed_grad = routed_grad + contract(
        logit_grad, router_matrix(param_ref, experts), NN
    )
    normed, inverse, mixed = normalize(res_ref[...], gain_row(param_ref, experts, 1))
    from_norm, gain_grad = normalize_back(
        routed_grad, normed, inverse, gain_row(param_ref, experts, 1)
    )
    total = pay_ref[0:chunk, :].astype(jnp.float32) + from_norm
    grad_ref[...] = total
    up_ref[...] = total.astype(jnp.bfloat16)
    live = live_rows(prob.shape, token_rows, lax.axis_index("tensor") * chunk)
    prob_sum = jnp.sum(jnp.where(live, prob, 0.0), axis=0, keepdims=True)
    grad_router = contract(logit_grad, mixed.astype(jnp.bfloat16), TN)
    small_ref[0:SMALL, :] = grad_router[0:SMALL]
    small_ref[experts : experts + 1, :] = gain_grad[None]
    small_ref[experts + 1 : experts + 2, :] = jnp.zeros((1, width), jnp.float32)
    small_ref[experts + 1 : experts + 2, :LANES] = prob_sum
    small_ref[experts + 2 : experts + 3, :] = param_ref[SMALL - 1 : SMALL, :]


def attention_back_kernel(
    heads, experts, owners, pos_ref, tok_ref, param_ref, w_ref, wo_ref, qkv_ref, lse_ref, att_ref,
    up_ref, small_ref, keep_ref, send_ref, *refs,
):
    *parts, hg_ref, flat_ref, big_ref, image_ref, held_ref, sum_ref, gain_ref = refs
    images, rows, width = qkv_ref.shape[1], qkv_ref.shape[2], heads * HD
    seq_len = tok_ref.shape[1]
    scale = HD ** (-0.5)
    padded, model = up_ref.shape
    chunk = padded // len(parts)
    masks = head_masks(rows, heads)
    keys_live = lax.broadcasted_iota(jnp.int32, (rows, rows), 1) < seq_len
    lane = lax.broadcasted_iota(jnp.int32, (rows, LANES), 1)
    up = up_ref[...]
    hg_ref[0:padded, :] = contract(up, wo_ref[...], NT)
    hg_ref[padded:, :] = jnp.zeros((hg_ref.shape[0] - padded, width), jnp.float32)
    big_ref[3 * width :, :] = contract(att_ref[...], up, TN)
    flat_ref[images * seq_len :, :] = jnp.zeros(
        (flat_ref.shape[0] - images * seq_len, model), jnp.float32
    )
    for i in range(images):
        held_ref[i] = hg_ref[pl.ds(i * seq_len, rows), :]
    big_ref[0 : 3 * width, :] = jnp.zeros((3 * width, model), jnp.float32)

    @pl.loop(0, images, unroll=True)
    def _(i):
        normed, _, mixed = normalize(
            image_rows(tok_ref, i, image_ref), gain_row(param_ref, experts, 0)
        )
        entered = mixed.astype(jnp.bfloat16)
        q, k, v = qkv_ref[0, i], qkv_ref[1, i], qkv_ref[2, i]
        heads_grad = held_ref[i]
        heads_grad = jnp.where(live_rows(heads_grad.shape, seq_len), heads_grad, 0.0)
        heads_grad = heads_grad.astype(jnp.bfloat16)
        dq = jnp.zeros((rows, width), jnp.float32)
        dk, dv = dq, dq
        for h in range(heads):
            q_h, k_h = keep_lanes(q, masks[h]), keep_lanes(k, masks[h])
            up_h = keep_lanes(heads_grad, masks[h])
            scores = contract(q_h, k, NT) * scale
            lse = jnp.sum(jnp.where(lane == h, lse_ref[i], 0.0), axis=-1, keepdims=True)
            probs = jnp.where(keys_live, jnp.exp(scores - lse), 0.0)
            prob_grad = contract(up_h, v, NT)
            total = jnp.sum(prob_grad * probs, axis=-1, keepdims=True)
            score_grad = (probs * (prob_grad - total)).astype(jnp.bfloat16)
            dv = dv + contract(probs.astype(jnp.bfloat16), up_h, TN)
            dq = dq + contract(score_grad, k_h, NN)
            dk = dk + contract(score_grad, q_h, TN)
        grads = [g.astype(jnp.bfloat16) for g in (dq * scale, dk * scale, dv)]
        part = jnp.zeros((rows, model), jnp.float32)
        for c in range(3):
            here = slice(c * width, (c + 1) * width)
            part = part + contract(grads[c], w_ref[here, :], NN)
            big_ref[here, :] += contract(grads[c], entered, TN)
        sum_ref[i] = part
        gain_ref[i] = jnp.broadcast_to(
            jnp.sum(part * normed, axis=0, keepdims=True), gain_ref.shape[1:]
        )

    gain_grad = jnp.zeros((1, model), jnp.float32)
    for i in range(images):
        flat_ref[pl.ds(i * seq_len, seq_len), :] = sum_ref[i, 0:seq_len, :]
        gain_grad = gain_grad + gain_ref[i, 0:1, :]
    high, low = split_high_low(
        jnp.concatenate([small_ref[0 : SMALL - 1, :], gain_grad], axis=0)
    )
    for j, part in enumerate(parts):
        part[0:chunk, :] = flat_ref[chunk_of(pos_ref, j, chunk), :].astype(jnp.bfloat16)
        part[chunk:, :] = jnp.concatenate([high, low], axis=0)
    me, core = lax.axis_index("expert"), lax.axis_index("dp")
    piece = keep_ref.shape[1]
    for k in range(owners):
        place = lax.bitwise_xor(me, k) * piece
        mine = pl.ds(pl.multiple_of(core * owners * piece + place, 8), piece)
        other = pl.ds(pl.multiple_of((1 - core) * owners * piece + place, 8), piece)
        keep_ref[k] = big_ref[mine, :]
        send_ref[k] = big_ref[other, :].astype(jnp.bfloat16)


def norm_back_kernel(experts, tensors, pos_ref, *refs):
    got = refs[:tensors]
    x_ref, res_ref, param_ref, own_ref, *parts, grad_ref, out_ref, small_ref = refs[tensors:]
    chunk, width = x_ref.shape
    upstream = jnp.zeros((chunk, width), jnp.float32)
    for j, part in enumerate(got):
        upstream = upstream + part[0:chunk, :].astype(jnp.float32)
        small_ref[lax.bitwise_xor(lax.axis_index("tensor"), j)] = part[chunk : chunk + SMALL, :].astype(
            jnp.float32
        ) + part[chunk + SMALL :, :].astype(jnp.float32)
    small = small_ref[0]
    for j in range(1, tensors):
        small = small + small_ref[j]
    gain = gain_row(param_ref, experts, 0)
    normed, inverse, _ = normalize(x_ref[...].astype(jnp.float32), gain)
    from_norm = normalize_back(upstream, normed, inverse, gain)[0]
    grad_ref[...] = (res_ref[...] + from_norm).astype(jnp.bfloat16)
    piece = own_ref.shape[0]
    total = own_ref[...]
    for part in parts:
        total = total + part[...].astype(jnp.float32)
    out_ref[0:piece, :] = total.astype(jnp.bfloat16)
    out_ref[piece:, :] = jnp.concatenate(split_high_low(small), axis=0)


def second_step_kernel(pos_ref, near_ref, from_y, from_x, x_ref, y_ref):
    for target, row, other in ((x_ref, 0, from_y), (y_ref, 1, from_x)):
        total = near_ref[row].astype(jnp.float32) + other[1].astype(jnp.float32)
        target[...] = total.astype(jnp.bfloat16)


def weight_sum_kernel(pos_ref, own_ref, from_y, from_x, last_x, last_y, out_ref):
    part_rows = last_x.shape[1]
    for row, other, last in ((0, from_y, last_x), (1, from_x, last_y)):
        total = own_ref[row].astype(jnp.float32) + other[0].astype(jnp.float32)
        total = total + last[...].astype(jnp.float32)
        out_ref[:, row * part_rows : (row + 1) * part_rows, :] = total.astype(jnp.bfloat16)


def add_core_kernel(pos_ref, keep_ref, other_ref, own_ref, *outs):
    total = keep_ref[...] + other_ref[...].astype(jnp.float32)
    own_ref[...] = total[0]
    for k, out in enumerate(outs):
        out[...] = total[k + 1].astype(jnp.bfloat16)


def spread_kernel(owners, experts, token_total, pos_ref, *refs):
    sides = refs[:2]
    qkv_ref, wo_ref, router_ref, one_ref, two_ref, loss_ref, big_ref, parts_ref = refs[2:]
    span = sides[0].shape[0] // owners
    piece = span - 2 * SMALL
    core, me = lax.axis_index("dp"), lax.axis_index("expert")
    for c in range(2):
        side = core if c == 0 else 1 - core
        for k in range(owners):
            block = sides[c].at[k * span : (k + 1) * span]
            place = side * owners + lax.bitwise_xor(me, k)
            here = pl.ds(pl.multiple_of(place * piece, 8), piece)
            big_ref[here, :] = block[0:piece, :].astype(jnp.float32)
            parts_ref[place] = block[piece : piece + SMALL, :].astype(jnp.float32) + block[
                piece + SMALL :, :
            ].astype(jnp.float32)
    rows = qkv_ref.shape[0]
    qkv_ref[...] = big_ref[0:rows, :]
    wo_ref[...] = big_ref[rows:, :]
    small = parts_ref[0]
    for p in range(1, 2 * owners):
        small = small + parts_ref[p]
    router_ref[...] = small[0:experts, :]
    one_ref[...] = small[SMALL - 1 : SMALL, :].reshape(small.shape[1])
    two_ref[...] = small[experts : experts + 1, :].reshape(small.shape[1])
    product = small[experts + 1 : experts + 2, :LANES] * small[experts + 2 : experts + 3, :LANES]
    lane = lax.broadcasted_iota(jnp.int32, product.shape, 1)
    product = jnp.where(lane < experts, product, 0.0)
    loss = jnp.sum(product, axis=-1, keepdims=True)
    loss_ref[...] = jnp.broadcast_to(
        loss * (experts / (2.0 * token_total * token_total)), loss_ref.shape
    )


def images_kernel(pos_ref, *refs):
    *chunks, out_ref, flat_ref = refs
    images, seq_len, _ = out_ref.shape
    if len(chunks) == 1:
        flat_ref[...] = chunks[0][...].astype(jnp.float32)
    else:
        for j, part in enumerate(chunks):
            flat_ref[chunk_of(pos_ref, j, part.shape[0]), :] = part[...].astype(jnp.float32)
    for i in range(images):
        out_ref[i] = flat_ref[pl.ds(i * seq_len, seq_len), :].astype(out_ref.dtype)


def weight_out_kernel(pos_ref, mine_ref, other_ref, in_ref, out_ref):
    first_is_mine = lax.axis_index("dp") == 0
    half = mine_ref.shape[1]
    for c in range(2):
        here = slice(c * half, (c + 1) * half)
        take = first_is_mine if c == 0 else jnp.logical_not(first_is_mine)
        grad_in = jnp.where(take, mine_ref[0], other_ref[0]).astype(jnp.float32)
        in_ref[0, :, here] = grad_in.T
        out_ref[0, here, :] = jnp.where(take, mine_ref[1], other_ref[1]).astype(jnp.float32)


def swap_core(value):
    return lax.ppermute(value, "dp", [(0, 1), (1, 0)])


def hop(value, bit):
    size = lax.axis_size("expert")
    return lax.ppermute(value, "expert", [(i, i ^ bit) for i in range(size)])


def cross(value, bit):
    size = lax.axis_size("tensor")
    return lax.ppermute(value, "tensor", [(i, i ^ bit) for i in range(size)])


def after(value, *others):
    return lax.optimization_barrier((value, *others))[0]


def dense_body(
    tokens,
    cotangent,
    expert_ids,
    slot_rank,
    qkv_weight,
    out_weight,
    router_weight,
    expert_in,
    expert_out,
    gain_attention,
    gain_experts,
):
    f32, b16 = jnp.float32, jnp.bfloat16
    images, seq_len, width = tokens.shape
    token_rows = images * seq_len
    local = qkv_weight.shape[2]
    heads = local // HD
    experts = router_weight.shape[1]
    owners = lax.axis_size("expert")
    tensors = lax.axis_size("tensor")
    cores = lax.axis_size("dp")
    chunk = round_up(-(-token_rows // tensors), 16)
    padded = chunk * tensors
    rows = round_up(seq_len, 16)
    flat_rows = padded + 32
    half = expert_in.shape[2] // cores
    quarter = half // 2
    position = jnp.zeros((1,), jnp.int32)
    weight_rows = qkv_weight.transpose(0, 2, 1).reshape(3 * local, width)

    x_chunk, payload, params, mine, first, second = kernel_call(
        functools.partial(chunk_kernel, tensors),
        "chunk",
        position,
        [
            tokens,
            cotangent,
            expert_ids.transpose(0, 2, 1),
            slot_rank.transpose(0, 2, 1),
            router_weight.T,
            gain_attention,
            gain_experts,
            expert_in,
            expert_out,
        ],
        [
            like((chunk, width), b16),
            like((chunk + 2 * SMALL, width), b16),
            like((SMALL, width), f32),
            like((2, half, width), b16),
            like((2, quarter, width), b16),
            like((2, quarter, width), b16),
        ],
        [
            pltpu.VMEM((flat_rows, width), f32),
            pltpu.VMEM((padded + 2 * LANES, LANES), f32),
        ],
        limit=56,
        loads=tuple(range(9)),
    )
    payload_mine = [payload] + [hop(payload, k) for k in range(1, owners)]
    first_x = cross(first, 1)
    second_y = cross(second, 2)

    qkv, lse, attended, *parts = kernel_call(
        functools.partial(attention_kernel, heads, experts),
        "attention",
        after(position, mine),
        [tokens, params, weight_rows, out_weight],
        [
            like((3, images, rows, local), b16),
            like((images, rows, LANES), f32),
            like((padded, local), b16),
        ]
        + [like((chunk, width), b16)] * tensors,
        [
            pltpu.VMEM((padded, local), f32),
            pltpu.VMEM((rows, width), f32),
            pltpu.VMEM((images, rows, local), f32),
        ],
        flops=40_000_000_000,
        limit=20,
        loads=(0, 1, 2, 3),
    )
    arrived = [parts[0]] + [cross(parts[j], j) for j in range(1, tensors)]
    pair_first, pair_second = stack_pairs(position, (first, first_x), (second, second_y))

    residual, routed, prob = kernel_call(
        functools.partial(route_kernel, experts),
        "route",
        after(position, pair_first, payload_mine[::-1]),
        [*arrived, x_chunk, params],
        [like((chunk, width), f32), like((chunk, width), b16), like((chunk, LANES), f32)],
        limit=8,
    )
    blocks = [routed] + [hop(routed, k) for k in range(1, owners)]
    pair_first, pair_second = after((pair_first, pair_second), routed)
    pair_y = cross(pair_first, 2)
    pair_x = cross(pair_second, 1)
    payload_mine = kernel_call(
        lay_payload_kernel,
        "lay_payload",
        after(position, routed),
        payload_mine,
        [like((owners * chunk, width + LANES), b16)],
        limit=6,
    )[0]
    payload_other = swap_core(payload_mine)
    rows_mine = lay_rows(position, "lay_rows", blocks)
    rows_other = swap_core(rows_mine)

    near_weights, far_weights = (mine, first_x, second_y), (pair_y, pair_x)
    first_a = first_expert_pass(position, rows_mine, payload_mine, params, near_weights, experts)
    first_b = first_expert_pass(
        after(position, first_a[2]), rows_other, payload_other, params, near_weights, experts
    )
    second_b = second_expert_pass(
        after(position, first_b[2]), rows_other, payload_other, first_b, far_weights
    )
    back_other, gated_other = swap_core(second_b[3]), swap_core(second_b[2])
    second_a = second_expert_pass(
        after(position, second_b[0]), rows_mine, payload_mine, first_a, far_weights
    )
    *joined, gated_own, gated_pair, gated_far = kernel_call(
        join_kernel,
        "join",
        position,
        [second_a[3], back_other, second_a[2], gated_other],
        [like((chunk + SMALL, width), b16)] * owners
        + [like((chunk, width), b16), like((2, chunk, width), b16), like((chunk, width), b16)],
        limit=8,
    )
    backs = [joined[0]] + [hop(joined[k], k) for k in range(1, owners)]

    grad_pos = after(position, joined)
    far_y, far_x = expert_grads(grad_pos, second_a, second_b, (rows_mine, first_a[2]), (rows_other, first_b[2]))
    from_y, from_x = cross(far_y, 2), cross(far_x, 1)
    residual_grad, attn_grad, small = kernel_call(
        functools.partial(route_back_kernel, experts, token_rows, owners),
        "route_back",
        position,
        [*backs, prob, residual, payload, params],
        [like((chunk, width), f32), like((chunk, width), b16), like((SMALL, width), f32)],
        flops=40_000_000_000,
        limit=8,
    )
    own_grad, near_grad = expert_grads(
        after(position, attn_grad), first_a, first_b, (rows_mine, first_a[2]), (rows_other, first_b[2]),
    )
    gated_near = hop(after(gated_pair, backs[1]), 1)
    block_sum, gated_far = kernel_call(
        pair_sum_kernel,
        "pair_sum",
        after(position, own_grad),
        [residual, gated_own, gated_far, gated_near],
        [like((chunk, width), f32), like((chunk, width), b16)],
        limit=4,
    )
    attn_grad, gated_far = lax.optimization_barrier((attn_grad, gated_far))
    gated_last = hop(gated_far, 2)
    attn_grad = lax.all_gather(attn_grad, "tensor", axis=0, tiled=True)
    piece = 4 * local // (2 * owners)
    keep, send, *parts = kernel_call(
        functools.partial(attention_back_kernel, heads, experts, owners),
        "attention_back",
        after(position, from_y, from_x, gated_last),
        [tokens, params, weight_rows, out_weight, qkv, lse, attended, attn_grad, small],
        [
            like((owners, piece, width), f32),
            like((owners, piece, width), b16),
        ]
        + [like((chunk + 2 * SMALL, width), b16)] * tensors,
        [
            pltpu.VMEM((flat_rows, local), f32),
            pltpu.VMEM((flat_rows, width), f32),
            pltpu.VMEM((4 * local, width), f32),
            pltpu.VMEM((rows, width), f32),
            pltpu.VMEM((images, rows, local), f32),
            pltpu.VMEM((images, rows, width), f32),
            pltpu.VMEM((images, SMALL, width), f32),
        ],
        limit=20,
        flops=6_000_000_000,
    )
    own_piece, *pieces = kernel_call(
        add_core_kernel,
        "add_core",
        position,
        [keep, swap_core(send)],
        [like((piece, width), f32)] + [like((piece, width), b16)] * (owners - 1),
        limit=8,
    )
    reduced = [hop(p, k + 1) for k, p in enumerate(pieces)]
    got = [parts[0]] + [cross(parts[j], j) for j in range(1, tensors)]

    up_x, up_y = kernel_call(
        second_step_kernel,
        "second_step",
        after(position, got[1:], own_piece),
        [near_grad, from_y, from_x],
        [like((2, quarter, width), b16)] * 2,
        limit=8,
    )
    last_x, last_y = cross(up_x, 1), cross(up_y, 2)

    grad_chunk, summed = kernel_call(
        functools.partial(norm_back_kernel, experts, tensors),
        "norm_back",
        position,
        [*got, x_chunk, residual_grad, params, own_piece, *reduced],
        [like((chunk, width), b16), like((piece + 2 * SMALL, width), b16)],
        [pltpu.VMEM((tensors, SMALL, width), f32)],
        flops=40_000_000_000,
        limit=8,
    )
    around = [summed] + [hop(summed, k) for k in range(1, owners)]
    grad_rows = lax.all_gather(grad_chunk, "tensor", axis=0, tiled=True)
    combined = (block_sum + gated_last.astype(f32)).astype(b16)
    combined = after(combined, grad_rows)
    block_parts = [combined] + [cross(combined, j) for j in range(1, tensors)]

    grad_tokens = kernel_call(
        images_kernel,
        "grad_tokens",
        position,
        [grad_rows],
        [like(tokens.shape, f32)],
        [pltpu.VMEM((padded, width), f32)],
        limit=8,
    )[0]
    grad_half = kernel_call(
        weight_sum_kernel,
        "weight_sum",
        after(position, grad_rows, around),
        [own_grad, from_y, from_x, last_x, last_y],
        [like((2, half, width), b16)],
        limit=8,
    )[0]
    grad_expert_in, grad_expert_out = kernel_call(
        weight_out_kernel,
        "weight_out",
        position,
        [grad_half, swap_core(grad_half)],
        [like((1, width, 2 * half), f32), like((1, 2 * half, width), f32)],
        limit=10,
    )
    around_rows = lay_rows(position, "lay_grads", around)
    token_total = token_rows * cores * owners
    grad_qkv, grad_out, grad_router, gain_one, gain_two, loss = kernel_call(
        functools.partial(spread_kernel, owners, experts, token_total),
        "spread",
        position,
        [around_rows, swap_core(around_rows)],
        [
            like((3 * local, width), f32),
            like((local, width), f32),
            like((experts, width), f32),
            like((width,), f32),
            like((width,), f32),
            like((1, LANES), f32),
        ],
        [
            pltpu.VMEM((4 * local, width), f32),
            pltpu.VMEM((2 * owners, SMALL, width), f32),
        ],
        limit=8,
    )
    block_out = kernel_call(
        images_kernel,
        "block_out",
        after(position, grad_tokens, grad_expert_in, grad_qkv),
        block_parts,
        [like(tokens.shape, b16)],
        [pltpu.VMEM((padded, width), f32)],
        limit=8,
    )[0]
    return (
        block_out,
        grad_tokens,
        grad_qkv.reshape(3, local, width).transpose(0, 2, 1),
        grad_out,
        grad_router.T,
        grad_expert_in,
        grad_expert_out,
        gain_one,
        gain_two,
        loss[0, 0],
    )


def solution(mesh):
    placed = (
        P(("dp", "expert"), None, None),
        P(("dp", "expert"), None, None),
        P(("dp", "expert"), None, None),
        P(("dp", "expert"), None, None),
        P(None, None, "tensor"),
        P("tensor", None),
        P(),
        P("expert", None, "tensor"),
        P("expert", "tensor", None),
        P(),
        P(),
    )
    shape = mesh.shape
    dense = shape["dp"] == 2 and shape["expert"] == 4 and shape["tensor"] == 4
    return jax.shard_map(
        dense_body if dense else body,
        mesh=mesh,
        in_specs=placed,
        out_specs=(
            P(("dp", "expert"), None, None),
            P(("dp", "expert"), None, None),
            P(None, None, "tensor"),
            P("tensor", None),
            P(),
            P("expert", None, "tensor"),
            P("expert", "tensor", None),
            P(),
            P(),
            P(),
        ),
        check_vma=False,
    )
```

```python
import functools
import math

import jax
import jax.numpy as jnp
from jax import lax
from jax.experimental import pallas as pl
from jax.experimental.pallas import tpu as pltpu
from jax.sharding import PartitionSpec as P

HD = 64


epsilon = 1e-06


def normalize(values, gain_row):
    center = values - jnp.mean(values, axis=-1, keepdims=True)
    inverse = lax.rsqrt(jnp.mean(center * center, axis=-1, keepdims=True) + epsilon)
    normed = center * inverse
    return (normed, inverse, normed * gain_row)


def normalize_back(upstream, normed, inverse, gain_row):
    scaled = upstream * gain_row
    result = inverse * (
        scaled
        - jnp.mean(scaled, axis=-1, keepdims=True)
        - normed * jnp.mean(scaled * normed, axis=-1, keepdims=True)
    )
    return (result, jnp.sum(upstream * normed, axis=0))


def exact_gelu(values):
    return jax.nn.gelu(values, approximate=False)


def body(
    tokens,
    cotangent,
    expert_ids,
    slot_rank,
    qkv_weight,
    out_weight,
    router_weight,
    expert_in,
    expert_out,
    gain_attention,
    gain_experts,
):
    images, seq_len, model_width = tokens.shape
    token_rows = images * seq_len
    local_width = qkv_weight.shape[2]
    local_heads = local_width // HD
    slice_width = model_width // lax.axis_size("tensor")
    experts = router_weight.shape[1]
    capacity = 5 * token_rows // (2 * experts)
    owners = lax.axis_size("expert")
    per_owner = experts // owners
    slot_total = experts * capacity
    score_scale = HD ** (-0.5)
    inputs = tokens.reshape(token_rows, model_width).astype(jnp.float32)
    normed_one, inverse_one, mixed_one = normalize(inputs, gain_attention)
    entered = mixed_one.astype(jnp.bfloat16)
    project = jnp.einsum(
        "td,cdf->ctf", entered, qkv_weight, preferred_element_type=jnp.float32
    ).astype(jnp.bfloat16)
    projected_heads = project.reshape(3, images, seq_len, local_heads, HD)
    queries, key_rows, value_rows = (projected_heads[0], projected_heads[1], projected_heads[2])
    scores = (
        jnp.einsum("ishe,ithe->ihst", queries, key_rows, preferred_element_type=jnp.float32)
        * score_scale
    )
    log_total = jax.nn.logsumexp(scores, axis=-1, keepdims=True)
    attn_probs = jnp.exp(scores - log_total).astype(jnp.bfloat16)
    attended = jnp.einsum(
        "ihst,ithe->ishe", attn_probs, value_rows, preferred_element_type=jnp.float32
    )
    attended = attended.astype(jnp.bfloat16).reshape(token_rows, local_width)
    attn_part = jnp.dot(attended, out_weight, preferred_element_type=jnp.float32)
    residual = inputs + lax.psum(attn_part, "tensor")
    normed_two, inverse_two, mixed_two = normalize(residual, gain_experts)
    routed = mixed_two.astype(jnp.bfloat16)
    route_prob = jax.nn.softmax(
        jnp.dot(routed, router_weight, preferred_element_type=jnp.float32), axis=-1
    )
    chosen = expert_ids.reshape(token_rows, 2)
    ranked = slot_rank.reshape(token_rows, 2)
    kept_mask = (ranked >= 0).astype(jnp.float32)
    position = jnp.where(ranked >= 0, chosen * capacity + ranked, slot_total).reshape(-1)
    send_rows = (
        jnp.zeros((slot_total, model_width), jnp.bfloat16)
        .at[position]
        .set(jnp.repeat(routed, 2, axis=0), mode="drop")
        .reshape(experts, capacity, model_width)
    )
    fragment = lax.all_to_all(send_rows, "expert", split_axis=0, concat_axis=0, tiled=True)
    grouped = fragment.reshape(owners, per_owner, fragment.shape[1], model_width)
    before = jnp.einsum("sjcd,jdf->sjcf", grouped, expert_in, preferred_element_type=jnp.float32)
    hidden = exact_gelu(before).astype(jnp.bfloat16)
    expert_part = jnp.einsum(
        "sjcf,jfd->sjcd", hidden, expert_out, preferred_element_type=jnp.float32
    )
    produced = lax.psum_scatter(expert_part, "tensor", scatter_dimension=3, tiled=True).astype(
        jnp.bfloat16
    )
    returned = lax.all_to_all(
        produced.reshape(experts, capacity, slice_width),
        "expert",
        split_axis=0,
        concat_axis=0,
        tiled=True,
    )
    returned = lax.all_gather(returned, "tensor", axis=2, tiled=True).reshape(
        slot_total, model_width
    )
    safe_index = jnp.minimum(position, slot_total - 1)
    picked = returned[safe_index].reshape(token_rows, 2, model_width).astype(jnp.float32)
    gate_values = jnp.take_along_axis(route_prob, chosen, axis=1) * kept_mask
    output = residual + jnp.sum(gate_values[:, :, None] * picked, axis=1)
    block_out = output.astype(jnp.bfloat16).reshape(images, seq_len, model_width)
    upstream = cotangent.reshape(token_rows, model_width).astype(jnp.float32)
    gate_grad = jnp.sum(upstream[:, None, :] * picked, axis=-1) * kept_mask
    member = (chosen[:, :, None] == jnp.arange(experts)[None, None, :]).astype(jnp.float32)
    route_grad = jnp.sum(member * gate_grad[:, :, None], axis=1)
    logit_grad = (
        route_prob * (route_grad - jnp.sum(route_grad * route_prob, axis=-1, keepdims=True))
    ).astype(jnp.bfloat16)
    row_grad = (
        (gate_values[:, :, None] * upstream[:, None, :])
        .astype(jnp.bfloat16)
        .reshape(2 * token_rows, model_width)
    )
    grad_send = (
        jnp.zeros((slot_total, model_width), jnp.bfloat16)
        .at[position]
        .set(row_grad, mode="drop")
        .reshape(experts, capacity, model_width)
    )
    grad_arrived = lax.all_to_all(grad_send, "expert", split_axis=0, concat_axis=0, tiled=True)
    grad_arrived = grad_arrived.reshape(owners, per_owner, capacity, model_width)
    hidden_grad = jnp.einsum(
        "sjcd,jfd->sjcf", grad_arrived, expert_out, preferred_element_type=jnp.float32
    )
    grad_expert_out = jnp.einsum(
        "sjcf,sjcd->jfd", hidden, grad_arrived, preferred_element_type=jnp.float32
    )
    pre_grad = jax.vjp(exact_gelu, before)[1](hidden_grad)[0].astype(jnp.bfloat16)
    grad_expert_in = jnp.einsum(
        "sjcd,sjcf->jdf", grouped, pre_grad, preferred_element_type=jnp.float32
    )
    buffer_part = jnp.einsum(
        "sjcf,jdf->sjcd", pre_grad, expert_in, preferred_element_type=jnp.float32
    )
    buffer_share = lax.psum_scatter(buffer_part, "tensor", scatter_dimension=3, tiled=True).astype(
        jnp.bfloat16
    )
    buffer_back = lax.all_to_all(
        buffer_share.reshape(experts, capacity, slice_width),
        "expert",
        split_axis=0,
        concat_axis=0,
        tiled=True,
    )
    buffer_grad = lax.all_gather(buffer_back, "tensor", axis=2, tiled=True).reshape(
        slot_total, model_width
    )
    routed_grad = jnp.sum(
        buffer_grad[safe_index].reshape(token_rows, 2, model_width).astype(jnp.float32)
        * kept_mask[:, :, None],
        axis=1,
    )
    routed_grad = routed_grad + jnp.dot(
        logit_grad, router_weight.T, preferred_element_type=jnp.float32
    )
    grad_router = jnp.einsum("td,te->de", routed, logit_grad, preferred_element_type=jnp.float32)
    from_norm_two, grad_gain_experts = normalize_back(
        routed_grad, normed_two, inverse_two, gain_experts
    )
    residual_grad = upstream + from_norm_two
    attn_grad = residual_grad.astype(jnp.bfloat16)
    grad_out = jnp.einsum("tf,td->fd", attended, attn_grad, preferred_element_type=jnp.float32)
    heads_grad = jnp.dot(attn_grad, out_weight.T, preferred_element_type=jnp.float32).astype(
        jnp.bfloat16
    )
    heads_grad = heads_grad.reshape(images, seq_len, local_heads, HD)
    again = (
        jnp.einsum("ishe,ithe->ihst", queries, key_rows, preferred_element_type=jnp.float32)
        * score_scale
    )
    probs_full = jnp.exp(again - log_total)
    prob_grad = jnp.einsum(
        "ishe,ithe->ihst", heads_grad, value_rows, preferred_element_type=jnp.float32
    )
    value_grad = jnp.einsum(
        "ihst,ishe->ithe",
        probs_full.astype(jnp.bfloat16),
        heads_grad,
        preferred_element_type=jnp.float32,
    )
    score_grad = (
        probs_full * (prob_grad - jnp.sum(prob_grad * probs_full, axis=-1, keepdims=True))
    ).astype(jnp.bfloat16)
    query_grad = (
        jnp.einsum("ihst,ithe->ishe", score_grad, key_rows, preferred_element_type=jnp.float32)
        * score_scale
    )
    key_grad = (
        jnp.einsum("ihst,ishe->ithe", score_grad, queries, preferred_element_type=jnp.float32)
        * score_scale
    )
    project_grad = (
        jnp.stack([query_grad, key_grad, value_grad])
        .astype(jnp.bfloat16)
        .reshape(3, token_rows, local_width)
    )
    grad_qkv = jnp.einsum("td,ctf->cdf", entered, project_grad, preferred_element_type=jnp.float32)
    entered_part = jnp.einsum(
        "ctf,cdf->td", project_grad, qkv_weight, preferred_element_type=jnp.float32
    )
    entered_grad = lax.psum(entered_part.astype(jnp.bfloat16), "tensor").astype(jnp.float32)
    from_norm_one, grad_gain_attention = normalize_back(
        entered_grad, normed_one, inverse_one, gain_attention
    )
    grad_tokens = (residual_grad + from_norm_one).reshape(images, seq_len, model_width)
    counts = jnp.sum(member, axis=(0, 1))
    prob_sum = jnp.sum(route_prob, axis=0)
    grad_qkv, grad_out, grad_router, grad_gain_attention, grad_gain_experts, counts, prob_sum = (
        lax.psum(
            (
                grad_qkv,
                grad_out,
                grad_router,
                grad_gain_attention,
                grad_gain_experts,
                counts,
                prob_sum,
            ),
            ("dp", "expert"),
        )
    )
    grad_expert_in, grad_expert_out = (
        lax.psum(grad_expert_in.astype(jnp.bfloat16), "dp").astype(jnp.float32),
        lax.psum(grad_expert_out.astype(jnp.bfloat16), "dp").astype(jnp.float32),
    )
    token_total = token_rows * lax.axis_size("dp") * lax.axis_size("expert")
    balance_loss = experts * jnp.sum(counts / (2.0 * token_total) * prob_sum / token_total)
    return (
        block_out,
        grad_tokens,
        grad_qkv,
        grad_out,
        grad_router,
        grad_expert_in,
        grad_expert_out,
        grad_gain_attention,
        grad_gain_experts,
        balance_loss,
    )


NN = ((1,), (0,))
NT = ((1,), (1,))
TN = ((0,), (0,))
LANES = 128
SMALL = 8


def round_up(value, step):
    return -(-value // step) * step


def contract(a, b, dims):
    return lax.dot_general(a, b, (dims, ((), ())), preferred_element_type=jnp.float32)


def load_then(kernel, loads, count, *refs):
    pos_ref, *refs = refs
    *refs, sem = refs
    buffers = refs[len(refs) - len(loads) :]
    refs = refs[: len(refs) - len(loads)]
    copies = [
        pltpu.make_async_copy(refs[index], buffer, sem.at[i])
        for i, (index, buffer) in enumerate(zip(loads, buffers))
    ]
    for copy in copies:
        copy.start()
    for index, buffer in zip(loads, buffers):
        refs[index] = buffer

    def arrive(*indices):
        for index in indices:
            copies[loads.index(index)].wait()

    kernel(arrive, pos_ref, *refs)


def kernel_call(kernel, name, position, args, outs, scratch=(), flops=0, limit=24, loads=()):
    if loads:
        kernel = functools.partial(load_then, kernel, loads, len(args))
        scratch = [
            *scratch,
            *(pltpu.VMEM(args[i].shape, args[i].dtype) for i in loads),
            pltpu.SemaphoreType.DMA((len(loads),)),
        ]
    places = [pltpu.HBM if i in loads else pltpu.VMEM for i in range(len(args))]
    return pl.pallas_call(
        kernel,
        in_specs=[pl.BlockSpec(memory_space=pltpu.SMEM)]
        + [pl.BlockSpec(memory_space=place) for place in places],
        out_specs=[pl.BlockSpec(memory_space=pltpu.VMEM)] * len(outs),
        out_shape=list(outs),
        scratch_shapes=list(scratch),
        compiler_params=pltpu.CompilerParams(vmem_limit_bytes=limit << 20),
        cost_estimate=pl.CostEstimate(flops=flops, bytes_accessed=0, transcendentals=0),
        name=name,
    )(position, *args)


def like(shape, dtype):
    return jax.ShapeDtypeStruct(shape, dtype)


def live_rows(shape, limit, offset=0):
    return lax.broadcasted_iota(jnp.int32, shape, 0) + offset < limit


def chunk_of(pos_ref, j, size):
    return pl.ds(pl.multiple_of(lax.bitwise_xor(lax.axis_index("tensor"), j) * size, 16), size)


def head_masks(rows, heads):
    lane = lax.broadcasted_iota(jnp.int32, (rows, heads * HD), 1)
    return [(lane >= h * HD) & (lane < (h + 1) * HD) for h in range(heads)]


def keep_lanes(value, mask):
    return jnp.where(mask, value, jnp.zeros_like(value))


def split_high_low(value):
    high = value.astype(jnp.bfloat16)
    return high, (value - high.astype(jnp.float32)).astype(jnp.bfloat16)


def image_rows(ref, i, scratch_ref):
    seq_len = ref.shape[1]
    scratch_ref[seq_len:, :] = jnp.zeros((scratch_ref.shape[0] - seq_len, ref.shape[2]), jnp.float32)
    scratch_ref[0:seq_len, :] = ref[i].astype(jnp.float32)
    return scratch_ref[...]


def router_matrix(param_ref, experts):
    rows = param_ref[0:SMALL, :]
    rows = jnp.where(live_rows(rows.shape, experts), rows, 0.0).astype(jnp.bfloat16)
    zeros = jnp.zeros((LANES - SMALL, rows.shape[1]), jnp.bfloat16)
    return jnp.concatenate([rows, zeros], axis=0)


def chunk_kernel(
    tensors, arrive, pos_ref, tok_ref, cot_ref, ids_ref, rank_ref, router_ref, one_ref, two_ref, in_ref, out_ref,
    x_ref, pay_ref, param_ref, mine_ref, first_ref, second_ref, flat_ref, kept_ref,
):
    images, seq_len, width = tok_ref.shape
    chunk, experts = x_ref.shape[0], router_ref.shape[0]
    start = pl.multiple_of(lax.axis_index("tensor") * chunk, 16)
    for index, source, target in ((0, tok_ref, x_ref), (1, cot_ref, pay_ref)):
        arrive(index)
        flat_ref[images * seq_len :, :] = jnp.zeros(
            (flat_ref.shape[0] - images * seq_len, width), jnp.float32
        )
        for i in range(images):
            flat_ref[pl.ds(i * seq_len, seq_len), :] = source[i].astype(jnp.float32)
        target[0:chunk, :] = flat_ref[pl.ds(start, chunk), :].astype(jnp.bfloat16)
    arrive(2, 3, 4, 5, 6)
    kept_ref[...] = jnp.zeros_like(kept_ref)
    counts = jnp.zeros((1, LANES), jnp.float32)
    for i in range(images):
        rows, all_rows = [], []
        for e in range(experts):
            named = (ids_ref[i] == e).astype(jnp.float32)
            kept = jnp.where(rank_ref[i] >= 0, named, 0.0)
            rows.append(jnp.sum(kept, axis=0, keepdims=True))
            all_rows.append(jnp.sum(named, axis=0, keepdims=True))
        for group, is_kept in ((rows, True), (all_rows, False)):
            table = jnp.concatenate(group, axis=0)
            table = jnp.concatenate(
                [table, jnp.zeros((LANES - experts, seq_len), jnp.float32)], axis=0
            )
            table = jnp.concatenate(
                [table, jnp.zeros((LANES, 2 * LANES - seq_len), jnp.float32)], axis=1
            ).T
            if is_kept:
                kept_ref[pl.ds(i * seq_len, 2 * LANES), :] = table
            else:
                counts = counts + jnp.sum(table, axis=0, keepdims=True)
    kept = jnp.concatenate(
        [kept_ref[pl.ds(start, chunk), :], jnp.zeros((2 * LANES - chunk, LANES), jnp.float32)], axis=0
    ).T
    pay_ref[chunk:, : 2 * LANES] = kept[0 : 2 * SMALL].astype(jnp.bfloat16)
    pay_ref[chunk:, 2 * LANES :] = jnp.zeros((2 * SMALL, width - 2 * LANES), jnp.bfloat16)
    param_ref[...] = jnp.zeros_like(param_ref)
    param_ref[0:experts, :] = router_ref[...].astype(jnp.float32)
    param_ref[experts : experts + 1, :] = one_ref[...].reshape(1, width)
    param_ref[experts + 1 : experts + 2, :] = two_ref[...].reshape(1, width)
    param_ref[SMALL - 1 : SMALL, :LANES] = counts * (1.0 / tensors)
    arrive(7, 8)
    half = mine_ref.shape[1]
    core = pl.multiple_of(lax.axis_index("dp") * half, LANES)
    for s, part in ((0, in_ref[0, :, pl.ds(core, half)].T), (1, out_ref[0, pl.ds(core, half), :])):
        mine_ref[s] = part
        first_ref[s] = part[0 : half // 2]
        second_ref[s] = part[half // 2 :]


def stack_kernel(pos_ref, *refs):
    count = len(refs) // 3
    for i, target in enumerate(refs[2 * count :]):
        target[0] = refs[2 * i][...]
        target[1] = refs[2 * i + 1][...]


def stack_pairs(position, *pairs):
    return kernel_call(
        stack_kernel,
        "stack",
        position,
        [value for pair in pairs for value in pair],
        [like((2, *pair[0].shape), pair[0].dtype) for pair in pairs],
        limit=4,
    )


def lay_kernel(pos_ref, *refs):
    *blocks, out_ref = refs
    chunk = blocks[0].shape[0]
    for k, block in enumerate(blocks):
        out_ref[k * chunk : (k + 1) * chunk, :] = block[...]


def lay_payload_kernel(pos_ref, near_ref, far_ref, out_ref):
    chunk = out_ref.shape[0] // 4
    width = near_ref.shape[2]
    for k in range(4):
        block = (near_ref, far_ref)[k % 2].at[k // 2]
        here = slice(k * chunk, (k + 1) * chunk)
        out_ref[here, :width] = block[0:chunk, :]
        kept = block[chunk:, : 2 * LANES].astype(jnp.float32)
        kept = jnp.concatenate([kept] * (LANES // kept.shape[0]), axis=0).T[0:chunk]
        out_ref[here, width:] = kept.astype(jnp.bfloat16)


def lay_rows(position, name, blocks):
    chunk, width = blocks[0].shape
    return kernel_call(
        lay_kernel,
        name,
        position,
        blocks,
        [like((len(blocks) * chunk, width), blocks[0].dtype)],
        limit=4,
    )[0]


def gain_row(param_ref, experts, which):
    return param_ref[experts + which : experts + which + 1, :]


def attention_kernel(
    heads, experts, arrive, pos_ref, tok_ref, param_ref, w_ref, wo_ref, qkv_ref, lse_ref, att_ref,
    *refs,
):
    *parts, flat_ref, image_ref, held_ref = refs
    images, rows, width = qkv_ref.shape[1], qkv_ref.shape[2], heads * HD
    seq_len = tok_ref.shape[1]
    masks = head_masks(rows, heads)
    keys_live = lax.broadcasted_iota(jnp.int32, (rows, rows), 1) < seq_len
    lane = lax.broadcasted_iota(jnp.int32, (rows, LANES), 1)
    flat_ref[images * seq_len :, :] = jnp.zeros(
        (flat_ref.shape[0] - images * seq_len, width), jnp.float32
    )
    arrive(0, 1, 2)

    @pl.loop(0, images)
    def _(i):
        entered = normalize(image_rows(tok_ref, i, image_ref), gain_row(param_ref, experts, 0))[2]
        entered = entered.astype(jnp.bfloat16)
        q, k, v = (
            contract(entered, w_ref[c * width : (c + 1) * width, :], NT).astype(jnp.bfloat16)
            for c in range(3)
        )
        qkv_ref[0, i], qkv_ref[1, i], qkv_ref[2, i] = q, k, v
        attended = jnp.zeros((rows, width), jnp.float32)
        lse_all = jnp.zeros((rows, LANES), jnp.float32)
        for h in range(heads):
            scores = contract(keep_lanes(q, masks[h]), k, NT) * (HD ** (-0.5))
            scores = jnp.where(keys_live, scores, -1e30)
            top = jnp.max(scores, axis=-1, keepdims=True)
            lse = top + jnp.log(jnp.sum(jnp.exp(scores - top), axis=-1, keepdims=True))
            probs = jnp.exp(scores - lse).astype(jnp.bfloat16)
            attended = attended + contract(probs, keep_lanes(v, masks[h]), NN)
            lse_all = jnp.where(lane == h, lse, lse_all)
        lse_ref[i] = lse_all
        held_ref[i] = attended

    for i in range(images):
        flat_ref[pl.ds(i * seq_len, seq_len), :] = held_ref[i, 0:seq_len, :]
    arrive(3)
    att_ref[...] = flat_ref[...].astype(jnp.bfloat16)
    for j, part in enumerate(parts):
        rows_j = flat_ref[chunk_of(pos_ref, j, part.shape[0]), :].astype(jnp.bfloat16)
        part[...] = contract(rows_j, wo_ref[...], NN).astype(jnp.bfloat16)


def route_kernel(experts, pos_ref, *refs):
    *got, x_ref, param_ref, res_ref, routed_ref, prob_ref = refs
    residual = x_ref[...].astype(jnp.float32)
    for part in got:
        residual = residual + part[...].astype(jnp.float32)
    res_ref[...] = residual
    routed = normalize(residual, gain_row(param_ref, experts, 1))[2].astype(jnp.bfloat16)
    routed_ref[...] = routed
    prob_ref[...] = route_probs(routed, router_matrix(param_ref, experts), experts)


def route_probs(rows, router, experts):
    logits = contract(rows, router, NT)
    lane = lax.broadcasted_iota(jnp.int32, logits.shape, 1)
    logits = jnp.where(lane < experts, logits, -1e30)
    weight = jnp.exp(logits - jnp.max(logits, axis=-1, keepdims=True))
    return weight / jnp.sum(weight, axis=-1, keepdims=True)


def gelu_parts(x):
    square = jnp.exp(-0.5 * x * x)
    share = 0.5 * (1.0 + lax.erf(x * (0.5**0.5)))
    return x * share, share + x * square * (0.5 / math.pi) ** 0.5


def expert_halves(x, rg, w_in, w_out, hidden_ref, pre_ref):
    before = contract(x, w_in, NT)
    value, slope = gelu_parts(before)
    hidden = value.astype(jnp.bfloat16)
    hidden_ref[...] = hidden
    part = contract(hidden, w_out, NN)
    pre = (contract(rg, w_out, NT) * slope).astype(jnp.bfloat16)
    pre_ref[...] = pre
    return part, contract(pre, w_in, NN)


def first_expert_kernel(
    experts, pos_ref, x_ref, pay_ref, param_ref, w0_ref, xa_ref, yb_ref, hidden_ref, pre_ref, rg_ref,
    gate_ref, part_ref, back_ref,
):
    count, width = x_ref.shape
    prob = route_probs(x_ref[...], router_matrix(param_ref, experts), experts)
    mine = lax.broadcasted_iota(jnp.int32, prob.shape, 1) == lax.axis_index("expert")
    kept = pay_ref[:, width:].astype(jnp.float32)
    kept = jnp.sum(jnp.where(mine, kept, 0.0), axis=-1, keepdims=True)
    gate = jnp.sum(jnp.where(mine, prob, 0.0), axis=-1, keepdims=True) * kept
    gate_ref[:, :LANES] = jnp.broadcast_to(gate, (count, LANES))
    gate_ref[:, LANES:] = jnp.broadcast_to(kept, (count, LANES))
    rg_ref[...] = (gate * pay_ref[:, :width].astype(jnp.float32)).astype(jnp.bfloat16)
    w_in, w_out = (
        jnp.concatenate([w0_ref[s], xa_ref[s], yb_ref[s]], axis=0) for s in range(2)
    )
    part_ref[...], back_ref[...] = expert_halves(
        x_ref[...], rg_ref[...], w_in, w_out, hidden_ref, pre_ref
    )


def second_expert_kernel(
    pos_ref, x_ref, pay_ref, rg_ref, gate_ref, part_in_ref, back_in_ref, pair_y_ref, pair_x_ref,
    hidden_ref, pre_ref, gated_ref, back_ref,
):
    width = x_ref.shape[1]
    w_in, w_out = (
        jnp.concatenate([ref[r, s] for ref in (pair_y_ref, pair_x_ref) for r in range(2)], axis=0)
        for s in range(2)
    )
    part, back = expert_halves(x_ref[...], rg_ref[...], w_in, w_out, hidden_ref, pre_ref)
    back_ref[:, :width] = (back_in_ref[...] + back).astype(back_ref.dtype)
    part = part_in_ref[...] + part
    gated_ref[...] = (gate_ref[:, 0:1] * part).astype(jnp.bfloat16)
    inner = jnp.sum(part * pay_ref[:, :width].astype(jnp.float32), axis=-1, keepdims=True)
    inner = gate_ref[:, LANES:] * inner
    if back_ref.dtype == jnp.bfloat16:
        high, low = split_high_low(inner)
        upper = lax.broadcasted_iota(jnp.int32, inner.shape, 1) < LANES // 2
        inner = jnp.where(upper, high.astype(jnp.float32), low.astype(jnp.float32))
    back_ref[:, width:] = inner.astype(back_ref.dtype)


def first_expert_pass(position, rows, payload, params, weights, experts):
    count, width = rows.shape
    hidden = 2 * weights[0].shape[1]
    return kernel_call(
        functools.partial(first_expert_kernel, experts),
        "experts_first",
        position,
        [rows, payload, params, *weights],
        [
            like((count, hidden), jnp.bfloat16),
            like((count, hidden), jnp.bfloat16),
            like((count, width), jnp.bfloat16),
            like((count, 2 * LANES), jnp.float32),
            like((count, width), jnp.float32),
            like((count, width), jnp.float32),
        ],
        limit=18,
    )


def second_expert_pass(position, rows, payload, first, weights, back_dtype):
    count, width = rows.shape
    hidden = 4 * weights[0].shape[2]
    return kernel_call(
        second_expert_kernel,
        "experts_second",
        position,
        [rows, payload, *first[2:], *weights],
        [
            like((count, hidden), jnp.bfloat16),
            like((count, hidden), jnp.bfloat16),
            like((count, width), jnp.bfloat16),
            like((count, width + LANES), back_dtype),
        ],
        limit=18,
    )


def join_kernel(pos_ref, back_ref, other_ref, gated_ref, gated_other_ref, *outs):
    *backs, own_ref, pair_ref, far_ref = outs
    chunk, width = own_ref.shape
    for k, out in enumerate(backs):
        here = pl.ds(k * chunk, chunk)
        other = other_ref[here, :].astype(jnp.float32)
        out[0:chunk, :] = (back_ref[here, :width] + other[:, :width]).astype(jnp.bfloat16)
        inner = jnp.sum(other[:, width:], axis=-1, keepdims=True) * (2.0 / LANES)
        inner = back_ref[here, width:] + inner
        inner = jnp.concatenate(
            [inner, jnp.zeros((2 * LANES - chunk, LANES), jnp.float32)], axis=0
        ).T
        high, low = split_high_low(inner[0:SMALL, :])
        both = jnp.where(
            live_rows(high.shape, SMALL // 2), high.astype(jnp.float32), low.astype(jnp.float32)
        )
        out[chunk:, : 2 * LANES] = both.astype(jnp.bfloat16)
        out[chunk:, 2 * LANES :] = jnp.zeros((SMALL, width - 2 * LANES), jnp.bfloat16)
        gated = gated_ref[here, :].astype(jnp.float32) + gated_other_ref[here, :].astype(jnp.float32)
        gated = gated.astype(jnp.bfloat16)
        if k % 2:
            pair_ref[k // 2] = gated
        else:
            (own_ref, far_ref)[k // 2][...] = gated


def pair_sum_kernel(pos_ref, base_ref, own_ref, far_ref, got_ref, sum_ref, send_ref):
    total = base_ref[...] + own_ref[...].astype(jnp.float32) + got_ref[0].astype(jnp.float32)
    sum_ref[...] = total
    send_ref[...] = (far_ref[...].astype(jnp.float32) + got_ref[1].astype(jnp.float32)).astype(
        jnp.bfloat16
    )


def expert_grad_kernel(pos_ref, *refs):
    *sources, first_ref, second_ref = refs
    part_rows = first_ref.shape[2]
    for j, out in enumerate((first_ref, second_ref)):
        columns = slice(2 * j * part_rows, 2 * (j + 1) * part_rows)
        for s in range(2):
            left_a, right_a, left_b, right_b = sources[4 * s : 4 * s + 4]
            grad = contract(left_a[:, columns], right_a[...], TN)
            grad = grad + contract(left_b[:, columns], right_b[...], TN)
            grad = grad.astype(jnp.bfloat16)
            out[0, s] = grad[0:part_rows]
            out[1, s] = grad[part_rows:]


def expert_grads(position, a, b, rows_a, rows_b, flops=0):
    width, total = rows_a[0].shape[1], a[0].shape[1]
    return kernel_call(
        expert_grad_kernel,
        "expert_grads",
        position,
        [a[1], rows_a[0], b[1], rows_b[0], a[0], rows_a[1], b[0], rows_b[1]],
        [like((2, 2, total // 4, width), jnp.bfloat16)] * 2,
        flops=flops,
        limit=10,
    )


def route_back_kernel(
    experts, token_rows, owners, pos_ref, *refs
):
    backs = refs[:owners]
    prob_ref, res_ref, pay_ref, param_ref = refs[owners : owners + 4]
    grad_ref, up_ref, small_ref = refs[owners + 4 :]
    chunk, width = res_ref.shape
    prob = prob_ref[...]
    lane = lax.broadcasted_iota(jnp.int32, prob.shape, 1)
    route_grad = jnp.zeros_like(prob)
    routed_grad = jnp.zeros((chunk, width), jnp.float32)
    for k, back in enumerate(backs):
        owner = lax.bitwise_xor(lax.axis_index("expert"), k)
        inner = back[chunk:, : 2 * LANES].astype(jnp.float32)
        inner = jnp.concatenate([inner] * (LANES // SMALL), axis=0).T[0:chunk]
        inner = jnp.sum(inner, axis=-1, keepdims=True) * (2.0 / LANES)
        route_grad = jnp.where(lane == owner, inner, route_grad)
        routed_grad = routed_grad + back[0:chunk, :].astype(jnp.float32)
    mean = jnp.sum(route_grad * prob, axis=-1, keepdims=True)
    logit_grad = (prob * (route_grad - mean)).astype(jnp.bfloat16)
    routed_grad = routed_grad + contract(
        logit_grad, router_matrix(param_ref, experts), NN
    )
    normed, inverse, mixed = normalize(res_ref[...], gain_row(param_ref, experts, 1))
    from_norm, gain_grad = normalize_back(
        routed_grad, normed, inverse, gain_row(param_ref, experts, 1)
    )
    total = pay_ref[0:chunk, :].astype(jnp.float32) + from_norm
    grad_ref[...] = total
    up_ref[...] = total.astype(jnp.bfloat16)
    live = live_rows(prob.shape, token_rows, lax.axis_index("tensor") * chunk)
    prob_sum = jnp.sum(jnp.where(live, prob, 0.0), axis=0, keepdims=True)
    grad_router = contract(logit_grad, mixed.astype(jnp.bfloat16), TN)
    small_ref[0:SMALL, :] = grad_router[0:SMALL]
    small_ref[experts : experts + 1, :] = gain_grad[None]
    small_ref[experts + 1 : experts + 2, :] = jnp.zeros((1, width), jnp.float32)
    small_ref[experts + 1 : experts + 2, :LANES] = prob_sum
    small_ref[experts + 2 : experts + 3, :] = param_ref[SMALL - 1 : SMALL, :]


def attention_back_kernel(
    heads, experts, owners, pos_ref, tok_ref, param_ref, w_ref, wo_ref, qkv_ref, lse_ref, att_ref,
    up_ref, small_ref, keep_ref, send_ref, *refs,
):
    *parts, hg_ref, flat_ref, big_ref, image_ref, held_ref, sum_ref, gain_ref = refs
    images, rows, width = qkv_ref.shape[1], qkv_ref.shape[2], heads * HD
    seq_len = tok_ref.shape[1]
    scale = HD ** (-0.5)
    padded, model = up_ref.shape
    chunk = padded // len(parts)
    masks = head_masks(rows, heads)
    keys_live = lax.broadcasted_iota(jnp.int32, (rows, rows), 1) < seq_len
    lane = lax.broadcasted_iota(jnp.int32, (rows, LANES), 1)
    up = up_ref[...]
    hg_ref[0:padded, :] = contract(up, wo_ref[...], NT)
    hg_ref[padded:, :] = jnp.zeros((hg_ref.shape[0] - padded, width), jnp.float32)
    big_ref[3 * width :, :] = contract(att_ref[...], up, TN)
    flat_ref[images * seq_len :, :] = jnp.zeros(
        (flat_ref.shape[0] - images * seq_len, model), jnp.float32
    )
    for i in range(images):
        held_ref[i] = hg_ref[pl.ds(i * seq_len, rows), :]
    big_ref[0 : 3 * width, :] = jnp.zeros((3 * width, model), jnp.float32)

    @pl.loop(0, images, unroll=True)
    def _(i):
        normed, _, mixed = normalize(
            image_rows(tok_ref, i, image_ref), gain_row(param_ref, experts, 0)
        )
        entered = mixed.astype(jnp.bfloat16)
        q, k, v = qkv_ref[0, i], qkv_ref[1, i], qkv_ref[2, i]
        heads_grad = held_ref[i]
        heads_grad = jnp.where(live_rows(heads_grad.shape, seq_len), heads_grad, 0.0)
        heads_grad = heads_grad.astype(jnp.bfloat16)
        dq = jnp.zeros((rows, width), jnp.float32)
        dk, dv = dq, dq
        for h in range(heads):
            q_h, k_h = keep_lanes(q, masks[h]), keep_lanes(k, masks[h])
            up_h = keep_lanes(heads_grad, masks[h])
            scores = contract(q_h, k, NT) * scale
            lse = jnp.sum(jnp.where(lane == h, lse_ref[i], 0.0), axis=-1, keepdims=True)
            probs = jnp.where(keys_live, jnp.exp(scores - lse), 0.0)
            prob_grad = contract(up_h, v, NT)
            total = jnp.sum(prob_grad * probs, axis=-1, keepdims=True)
            score_grad = (probs * (prob_grad - total)).astype(jnp.bfloat16)
            dv = dv + contract(probs.astype(jnp.bfloat16), up_h, TN)
            dq = dq + contract(score_grad, k_h, NN)
            dk = dk + contract(score_grad, q_h, TN)
        grads = [g.astype(jnp.bfloat16) for g in (dq * scale, dk * scale, dv)]
        part = jnp.zeros((rows, model), jnp.float32)
        for c in range(3):
            here = slice(c * width, (c + 1) * width)
            part = part + contract(grads[c], w_ref[here, :], NN)
            big_ref[here, :] += contract(grads[c], entered, TN)
        sum_ref[i] = part
        gain_ref[i] = jnp.broadcast_to(
            jnp.sum(part * normed, axis=0, keepdims=True), gain_ref.shape[1:]
        )

    gain_grad = jnp.zeros((1, model), jnp.float32)
    for i in range(images):
        flat_ref[pl.ds(i * seq_len, seq_len), :] = sum_ref[i, 0:seq_len, :]
        gain_grad = gain_grad + gain_ref[i, 0:1, :]
    high, low = split_high_low(
        jnp.concatenate([small_ref[0 : SMALL - 1, :], gain_grad], axis=0)
    )
    for j, part in enumerate(parts):
        part[0:chunk, :] = flat_ref[chunk_of(pos_ref, j, chunk), :].astype(jnp.bfloat16)
        part[chunk:, :] = jnp.concatenate([high, low], axis=0)
    me, core = lax.axis_index("expert"), lax.axis_index("dp")
    piece = keep_ref.shape[1]
    for k in range(owners):
        place = lax.bitwise_xor(me, k) * piece
        mine = pl.ds(pl.multiple_of(core * owners * piece + place, 8), piece)
        other = pl.ds(pl.multiple_of((1 - core) * owners * piece + place, 8), piece)
        keep_ref[k] = big_ref[mine, :]
        send_ref[k] = big_ref[other, :].astype(jnp.bfloat16)


def norm_back_kernel(experts, tensors, pos_ref, *refs):
    got = refs[:tensors]
    x_ref, res_ref, param_ref, own_ref, *parts, grad_ref, out_ref, small_ref = refs[tensors:]
    chunk, width = x_ref.shape
    upstream = jnp.zeros((chunk, width), jnp.float32)
    for j, part in enumerate(got):
        upstream = upstream + part[0:chunk, :].astype(jnp.float32)
        small_ref[lax.bitwise_xor(lax.axis_index("tensor"), j)] = part[chunk : chunk + SMALL, :].astype(
            jnp.float32
        ) + part[chunk + SMALL :, :].astype(jnp.float32)
    small = small_ref[0]
    for j in range(1, tensors):
        small = small + small_ref[j]
    gain = gain_row(param_ref, experts, 0)
    normed, inverse, _ = normalize(x_ref[...].astype(jnp.float32), gain)
    from_norm = normalize_back(upstream, normed, inverse, gain)[0]
    grad_ref[...] = (res_ref[...] + from_norm).astype(jnp.bfloat16)
    piece = own_ref.shape[0]
    total = own_ref[...]
    for part in parts:
        total = total + part[...].astype(jnp.float32)
    out_ref[0:piece, :] = total.astype(jnp.bfloat16)
    out_ref[piece:, :] = jnp.concatenate(split_high_low(small), axis=0)


def second_step_kernel(pos_ref, near_ref, from_y, from_x, x_ref, y_ref):
    for target, row, other in ((x_ref, 0, from_y), (y_ref, 1, from_x)):
        total = near_ref[row].astype(jnp.float32) + other[1].astype(jnp.float32)
        target[...] = total.astype(jnp.bfloat16)


def weight_sum_kernel(pos_ref, own_ref, from_y, from_x, last_x, last_y, out_ref):
    part_rows = last_x.shape[1]
    for row, other, last in ((0, from_y, last_x), (1, from_x, last_y)):
        total = own_ref[row].astype(jnp.float32) + other[0].astype(jnp.float32)
        total = total + last[...].astype(jnp.float32)
        out_ref[:, row * part_rows : (row + 1) * part_rows, :] = total.astype(jnp.bfloat16)


def add_core_kernel(pos_ref, keep_ref, other_ref, own_ref, *outs):
    total = keep_ref[...] + other_ref[...].astype(jnp.float32)
    own_ref[...] = total[0]
    for k, out in enumerate(outs):
        out[...] = total[k + 1].astype(jnp.bfloat16)


def spread_kernel(owners, experts, token_total, pos_ref, *refs):
    sides = refs[:2]
    qkv_ref, wo_ref, router_ref, one_ref, two_ref, loss_ref, big_ref, parts_ref = refs[2:]
    span = sides[0].shape[0] // owners
    piece = span - 2 * SMALL
    core, me = lax.axis_index("dp"), lax.axis_index("expert")
    for c in range(2):
        side = core if c == 0 else 1 - core
        for k in range(owners):
            block = sides[c].at[k * span : (k + 1) * span]
            place = side * owners + lax.bitwise_xor(me, k)
            here = pl.ds(pl.multiple_of(place * piece, 8), piece)
            big_ref[here, :] = block[0:piece, :].astype(jnp.float32)
            parts_ref[place] = block[piece : piece + SMALL, :].astype(jnp.float32) + block[
                piece + SMALL :, :
            ].astype(jnp.float32)
    rows = qkv_ref.shape[0]
    qkv_ref[...] = big_ref[0:rows, :]
    wo_ref[...] = big_ref[rows:, :]
    small = parts_ref[0]
    for p in range(1, 2 * owners):
        small = small + parts_ref[p]
    router_ref[...] = small[0:experts, :]
    one_ref[...] = small[SMALL - 1 : SMALL, :].reshape(small.shape[1])
    two_ref[...] = small[experts : experts + 1, :].reshape(small.shape[1])
    product = small[experts + 1 : experts + 2, :LANES] * small[experts + 2 : experts + 3, :LANES]
    lane = lax.broadcasted_iota(jnp.int32, product.shape, 1)
    product = jnp.where(lane < experts, product, 0.0)
    loss = jnp.sum(product, axis=-1, keepdims=True)
    loss_ref[...] = jnp.broadcast_to(
        loss * (experts / (2.0 * token_total * token_total)), loss_ref.shape
    )


def images_kernel(pos_ref, *refs):
    *chunks, out_ref, flat_ref = refs
    images, seq_len, _ = out_ref.shape
    if len(chunks) == 1:
        flat_ref[...] = chunks[0][...].astype(jnp.float32)
    else:
        for j, part in enumerate(chunks):
            flat_ref[chunk_of(pos_ref, j, part.shape[0]), :] = part[...].astype(jnp.float32)
    for i in range(images):
        out_ref[i] = flat_ref[pl.ds(i * seq_len, seq_len), :].astype(out_ref.dtype)


def weight_out_kernel(pos_ref, mine_ref, other_ref, in_ref, out_ref):
    first_is_mine = lax.axis_index("dp") == 0
    half = mine_ref.shape[1]
    for c in range(2):
        here = slice(c * half, (c + 1) * half)
        take = first_is_mine if c == 0 else jnp.logical_not(first_is_mine)
        grad_in = jnp.where(take, mine_ref[0], other_ref[0]).astype(jnp.float32)
        in_ref[0, :, here] = grad_in.T
        out_ref[0, here, :] = jnp.where(take, mine_ref[1], other_ref[1]).astype(jnp.float32)


def swap_core(value):
    return lax.ppermute(value, "dp", [(0, 1), (1, 0)])


def hop(value, bit):
    size = lax.axis_size("expert")
    return lax.ppermute(value, "expert", [(i, i ^ bit) for i in range(size)])


def cross(value, bit):
    size = lax.axis_size("tensor")
    return lax.ppermute(value, "tensor", [(i, i ^ bit) for i in range(size)])


def after(value, *others):
    return lax.optimization_barrier((value, *others))[0]


def dense_body(
    tokens,
    cotangent,
    expert_ids,
    slot_rank,
    qkv_weight,
    out_weight,
    router_weight,
    expert_in,
    expert_out,
    gain_attention,
    gain_experts,
):
    f32, b16 = jnp.float32, jnp.bfloat16
    images, seq_len, width = tokens.shape
    token_rows = images * seq_len
    local = qkv_weight.shape[2]
    heads = local // HD
    experts = router_weight.shape[1]
    owners = lax.axis_size("expert")
    tensors = lax.axis_size("tensor")
    cores = lax.axis_size("dp")
    chunk = round_up(-(-token_rows // tensors), 16)
    padded = chunk * tensors
    rows = round_up(seq_len, 16)
    flat_rows = padded + 32
    half = expert_in.shape[2] // cores
    quarter = half // 2
    position = jnp.zeros((1,), jnp.int32)
    weight_rows = qkv_weight.transpose(0, 2, 1).reshape(3 * local, width)

    x_chunk, payload, params, mine, first, second = kernel_call(
        functools.partial(chunk_kernel, tensors),
        "chunk",
        position,
        [
            tokens,
            cotangent,
            expert_ids.transpose(0, 2, 1),
            slot_rank.transpose(0, 2, 1),
            router_weight.T,
            gain_attention,
            gain_experts,
            expert_in,
            expert_out,
        ],
        [
            like((chunk, width), b16),
            like((chunk + 2 * SMALL, width), b16),
            like((SMALL, width), f32),
            like((2, half, width), b16),
            like((2, quarter, width), b16),
            like((2, quarter, width), b16),
        ],
        [
            pltpu.VMEM((flat_rows, width), f32),
            pltpu.VMEM((padded + 2 * LANES, LANES), f32),
        ],
        limit=56,
        loads=tuple(range(9)),
    )
    payload_two = hop(payload, 2)
    first_x = cross(first, 1)
    second_y = cross(second, 2)

    qkv, lse, attended, *parts = kernel_call(
        functools.partial(attention_kernel, heads, experts),
        "attention",
        after(position, mine),
        [tokens, params, weight_rows, out_weight],
        [
            like((3, images, rows, local), b16),
            like((images, rows, LANES), f32),
            like((padded, local), b16),
        ]
        + [like((chunk, width), b16)] * tensors,
        [
            pltpu.VMEM((padded, local), f32),
            pltpu.VMEM((rows, width), f32),
            pltpu.VMEM((images, rows, local), f32),
        ],
        flops=40_000_000_000,
        limit=20,
        loads=(0, 1, 2, 3),
    )
    arrived = [parts[0]] + [cross(parts[j], j) for j in range(1, tensors)]
    pair_first, pair_second = stack_pairs(
        after(position, parts[0]), (first, first_x), (second, second_y)
    )
    (payload_near,) = stack_pairs(after(position, pair_first), (payload, payload_two))
    payload_far = hop(payload_near, 1)

    residual, routed, prob = kernel_call(
        functools.partial(route_kernel, experts),
        "route",
        after(position, pair_first, payload_near),
        [*arrived, x_chunk, params],
        [like((chunk, width), f32), like((chunk, width), b16), like((chunk, LANES), f32)],
        limit=8,
    )
    blocks = [routed] + [hop(routed, k) for k in range(1, owners)]
    pair_first, pair_second = after((pair_first, pair_second), routed)
    pair_y = cross(pair_first, 2)
    pair_x = cross(pair_second, 1)
    payload_mine = kernel_call(
        lay_payload_kernel,
        "lay_payload",
        after(position, routed),
        [payload_near, payload_far],
        [like((owners * chunk, width + LANES), b16)],
        limit=6,
    )[0]
    payload_other = swap_core(payload_mine)
    rows_mine = lay_rows(position, "lay_rows", blocks)
    rows_other = swap_core(rows_mine)

    near_weights, far_weights = (mine, first_x, second_y), (pair_y, pair_x)
    first_a = first_expert_pass(position, rows_mine, payload_mine, params, near_weights, experts)
    first_b = first_expert_pass(
        after(position, first_a[2]), rows_other, payload_other, params, near_weights, experts
    )
    second_b = second_expert_pass(
        after(position, first_b[2]), rows_other, payload_other, first_b, far_weights, b16
    )
    back_other, gated_other = swap_core(second_b[3]), swap_core(second_b[2])
    second_a = second_expert_pass(
        after(position, second_b[0]), rows_mine, payload_mine, first_a, far_weights, f32
    )
    *joined, gated_own, gated_pair, gated_far = kernel_call(
        join_kernel,
        "join",
        position,
        [second_a[3], back_other, second_a[2], gated_other],
        [like((chunk + SMALL, width), b16)] * owners
        + [like((chunk, width), b16), like((2, chunk, width), b16), like((chunk, width), b16)],
        limit=8,
    )
    backs = [joined[0]] + [hop(joined[k], k) for k in range(1, owners)]

    grad_pos = after(position, joined)
    far_y, far_x = expert_grads(grad_pos, second_a, second_b, (rows_mine, first_a[2]), (rows_other, first_b[2]))
    from_y, from_x = cross(far_y, 2), cross(far_x, 1)
    residual_grad, attn_grad, small = kernel_call(
        functools.partial(route_back_kernel, experts, token_rows, owners),
        "route_back",
        position,
        [*backs, prob, residual, payload, params],
        [like((chunk, width), f32), like((chunk, width), b16), like((SMALL, width), f32)],
        flops=40_000_000_000,
        limit=8,
    )
    own_grad, near_grad = expert_grads(
        after(position, attn_grad), first_a, first_b, (rows_mine, first_a[2]), (rows_other, first_b[2]),
    )
    gated_near = hop(after(gated_pair, backs[1]), 1)
    block_sum, gated_far = kernel_call(
        pair_sum_kernel,
        "pair_sum",
        after(position, own_grad),
        [residual, gated_own, gated_far, gated_near],
        [like((chunk, width), f32), like((chunk, width), b16)],
        limit=4,
    )
    attn_grad, gated_far = lax.optimization_barrier((attn_grad, gated_far))
    gated_last = hop(gated_far, 2)
    attn_grad = lax.all_gather(attn_grad, "tensor", axis=0, tiled=True)
    piece = 4 * local // (2 * owners)
    keep, send, *parts = kernel_call(
        functools.partial(attention_back_kernel, heads, experts, owners),
        "attention_back",
        after(position, from_y, from_x, gated_last),
        [tokens, params, weight_rows, out_weight, qkv, lse, attended, attn_grad, small],
        [
            like((owners, piece, width), f32),
            like((owners, piece, width), b16),
        ]
        + [like((chunk + 2 * SMALL, width), b16)] * tensors,
        [
            pltpu.VMEM((flat_rows, local), f32),
            pltpu.VMEM((flat_rows, width), f32),
            pltpu.VMEM((4 * local, width), f32),
            pltpu.VMEM((rows, width), f32),
            pltpu.VMEM((images, rows, local), f32),
            pltpu.VMEM((images, rows, width), f32),
            pltpu.VMEM((images, SMALL, width), f32),
        ],
        limit=20,
        flops=6_000_000_000,
    )
    own_piece, *pieces = kernel_call(
        add_core_kernel,
        "add_core",
        position,
        [keep, swap_core(send)],
        [like((piece, width), f32)] + [like((piece, width), b16)] * (owners - 1),
        limit=8,
    )
    reduced = [hop(p, k + 1) for k, p in enumerate(pieces)]
    got = [parts[0]] + [cross(parts[j], j) for j in range(1, tensors)]

    up_x, up_y = kernel_call(
        second_step_kernel,
        "second_step",
        after(position, got[1:], own_piece),
        [near_grad, from_y, from_x],
        [like((2, quarter, width), b16)] * 2,
        limit=8,
    )
    last_x, last_y = cross(up_x, 1), cross(up_y, 2)

    grad_chunk, summed = kernel_call(
        functools.partial(norm_back_kernel, experts, tensors),
        "norm_back",
        position,
        [*got, x_chunk, residual_grad, params, own_piece, *reduced],
        [like((chunk, width), b16), like((piece + 2 * SMALL, width), b16)],
        [pltpu.VMEM((tensors, SMALL, width), f32)],
        flops=40_000_000_000,
        limit=8,
    )
    around = [summed] + [hop(summed, k) for k in range(1, owners)]
    grad_rows = lax.all_gather(grad_chunk, "tensor", axis=0, tiled=True)
    combined = (block_sum + gated_last.astype(f32)).astype(b16)
    combined = after(combined, grad_rows)
    block_parts = [combined] + [cross(combined, j) for j in range(1, tensors)]

    grad_tokens = kernel_call(
        images_kernel,
        "grad_tokens",
        position,
        [grad_rows],
        [like(tokens.shape, f32)],
        [pltpu.VMEM((padded, width), f32)],
        limit=8,
    )[0]
    grad_half = kernel_call(
        weight_sum_kernel,
        "weight_sum",
        after(position, grad_rows, around),
        [own_grad, from_y, from_x, last_x, last_y],
        [like((2, half, width), b16)],
        limit=8,
    )[0]
    grad_expert_in, grad_expert_out = kernel_call(
        weight_out_kernel,
        "weight_out",
        position,
        [grad_half, swap_core(grad_half)],
        [like((1, width, 2 * half), f32), like((1, 2 * half, width), f32)],
        limit=10,
    )
    around_rows = lay_rows(position, "lay_grads", around)
    token_total = token_rows * cores * owners
    grad_qkv, grad_out, grad_router, gain_one, gain_two, loss = kernel_call(
        functools.partial(spread_kernel, owners, experts, token_total),
        "spread",
        position,
        [around_rows, swap_core(around_rows)],
        [
            like((3 * local, width), f32),
            like((local, width), f32),
            like((experts, width), f32),
            like((width,), f32),
            like((width,), f32),
            like((1, LANES), f32),
        ],
        [
            pltpu.VMEM((4 * local, width), f32),
            pltpu.VMEM((2 * owners, SMALL, width), f32),
        ],
        limit=8,
    )
    block_out = kernel_call(
        images_kernel,
        "block_out",
        after(position, grad_tokens, grad_expert_in, grad_qkv),
        block_parts,
        [like(tokens.shape, b16)],
        [pltpu.VMEM((padded, width), f32)],
        limit=8,
    )[0]
    return (
        block_out,
        grad_tokens,
        grad_qkv.reshape(3, local, width).transpose(0, 2, 1),
        grad_out,
        grad_router.T,
        grad_expert_in,
        grad_expert_out,
        gain_one,
        gain_two,
        loss[0, 0],
    )


def solution(mesh):
    placed = (
        P(("dp", "expert"), None, None),
        P(("dp", "expert"), None, None),
        P(("dp", "expert"), None, None),
        P(("dp", "expert"), None, None),
        P(None, None, "tensor"),
        P("tensor", None),
        P(),
        P("expert", None, "tensor"),
        P("expert", "tensor", None),
        P(),
        P(),
    )
    shape = mesh.shape
    dense = shape["dp"] == 2 and shape["expert"] == 4 and shape["tensor"] == 4
    return jax.shard_map(
        dense_body if dense else body,
        mesh=mesh,
        in_specs=placed,
        out_specs=(
            P(("dp", "expert"), None, None),
            P(("dp", "expert"), None, None),
            P(None, None, "tensor"),
            P("tensor", None),
            P(),
            P("expert", None, "tensor"),
            P("expert", "tensor", None),
            P(),
            P(),
            P(),
        ),
        check_vma=False,
    )
```

```python
import functools
import math

import jax
import jax.numpy as jnp
from jax import lax
from jax.experimental import pallas as pl
from jax.experimental.pallas import tpu as pltpu
from jax.sharding import PartitionSpec as P

HD = 64


epsilon = 1e-06


def normalize(values, gain_row):
    center = values - jnp.mean(values, axis=-1, keepdims=True)
    inverse = lax.rsqrt(jnp.mean(center * center, axis=-1, keepdims=True) + epsilon)
    normed = center * inverse
    return (normed, inverse, normed * gain_row)


def normalize_back(upstream, normed, inverse, gain_row):
    scaled = upstream * gain_row
    result = inverse * (
        scaled
        - jnp.mean(scaled, axis=-1, keepdims=True)
        - normed * jnp.mean(scaled * normed, axis=-1, keepdims=True)
    )
    return (result, jnp.sum(upstream * normed, axis=0))


def exact_gelu(values):
    return jax.nn.gelu(values, approximate=False)


def body(
    tokens,
    cotangent,
    expert_ids,
    slot_rank,
    qkv_weight,
    out_weight,
    router_weight,
    expert_in,
    expert_out,
    gain_attention,
    gain_experts,
):
    images, seq_len, model_width = tokens.shape
    token_rows = images * seq_len
    local_width = qkv_weight.shape[2]
    local_heads = local_width // HD
    slice_width = model_width // lax.axis_size("tensor")
    experts = router_weight.shape[1]
    capacity = 5 * token_rows // (2 * experts)
    owners = lax.axis_size("expert")
    per_owner = experts // owners
    slot_total = experts * capacity
    score_scale = HD ** (-0.5)
    inputs = tokens.reshape(token_rows, model_width).astype(jnp.float32)
    normed_one, inverse_one, mixed_one = normalize(inputs, gain_attention)
    entered = mixed_one.astype(jnp.bfloat16)
    project = jnp.einsum(
        "td,cdf->ctf", entered, qkv_weight, preferred_element_type=jnp.float32
    ).astype(jnp.bfloat16)
    projected_heads = project.reshape(3, images, seq_len, local_heads, HD)
    queries, key_rows, value_rows = (projected_heads[0], projected_heads[1], projected_heads[2])
    scores = (
        jnp.einsum("ishe,ithe->ihst", queries, key_rows, preferred_element_type=jnp.float32)
        * score_scale
    )
    log_total = jax.nn.logsumexp(scores, axis=-1, keepdims=True)
    attn_probs = jnp.exp(scores - log_total).astype(jnp.bfloat16)
    attended = jnp.einsum(
        "ihst,ithe->ishe", attn_probs, value_rows, preferred_element_type=jnp.float32
    )
    attended = attended.astype(jnp.bfloat16).reshape(token_rows, local_width)
    attn_part = jnp.dot(attended, out_weight, preferred_element_type=jnp.float32)
    residual = inputs + lax.psum(attn_part, "tensor")
    normed_two, inverse_two, mixed_two = normalize(residual, gain_experts)
    routed = mixed_two.astype(jnp.bfloat16)
    route_prob = jax.nn.softmax(
        jnp.dot(routed, router_weight, preferred_element_type=jnp.float32), axis=-1
    )
    chosen = expert_ids.reshape(token_rows, 2)
    ranked = slot_rank.reshape(token_rows, 2)
    kept_mask = (ranked >= 0).astype(jnp.float32)
    position = jnp.where(ranked >= 0, chosen * capacity + ranked, slot_total).reshape(-1)
    send_rows = (
        jnp.zeros((slot_total, model_width), jnp.bfloat16)
        .at[position]
        .set(jnp.repeat(routed, 2, axis=0), mode="drop")
        .reshape(experts, capacity, model_width)
    )
    fragment = lax.all_to_all(send_rows, "expert", split_axis=0, concat_axis=0, tiled=True)
    grouped = fragment.reshape(owners, per_owner, fragment.shape[1], model_width)
    before = jnp.einsum("sjcd,jdf->sjcf", grouped, expert_in, preferred_element_type=jnp.float32)
    hidden = exact_gelu(before).astype(jnp.bfloat16)
    expert_part = jnp.einsum(
        "sjcf,jfd->sjcd", hidden, expert_out, preferred_element_type=jnp.float32
    )
    produced = lax.psum_scatter(expert_part, "tensor", scatter_dimension=3, tiled=True).astype(
        jnp.bfloat16
    )
    returned = lax.all_to_all(
        produced.reshape(experts, capacity, slice_width),
        "expert",
        split_axis=0,
        concat_axis=0,
        tiled=True,
    )
    returned = lax.all_gather(returned, "tensor", axis=2, tiled=True).reshape(
        slot_total, model_width
    )
    safe_index = jnp.minimum(position, slot_total - 1)
    picked = returned[safe_index].reshape(token_rows, 2, model_width).astype(jnp.float32)
    gate_values = jnp.take_along_axis(route_prob, chosen, axis=1) * kept_mask
    output = residual + jnp.sum(gate_values[:, :, None] * picked, axis=1)
    block_out = output.astype(jnp.bfloat16).reshape(images, seq_len, model_width)
    upstream = cotangent.reshape(token_rows, model_width).astype(jnp.float32)
    gate_grad = jnp.sum(upstream[:, None, :] * picked, axis=-1) * kept_mask
    member = (chosen[:, :, None] == jnp.arange(experts)[None, None, :]).astype(jnp.float32)
    route_grad = jnp.sum(member * gate_grad[:, :, None], axis=1)
    logit_grad = (
        route_prob * (route_grad - jnp.sum(route_grad * route_prob, axis=-1, keepdims=True))
    ).astype(jnp.bfloat16)
    row_grad = (
        (gate_values[:, :, None] * upstream[:, None, :])
        .astype(jnp.bfloat16)
        .reshape(2 * token_rows, model_width)
    )
    grad_send = (
        jnp.zeros((slot_total, model_width), jnp.bfloat16)
        .at[position]
        .set(row_grad, mode="drop")
        .reshape(experts, capacity, model_width)
    )
    grad_arrived = lax.all_to_all(grad_send, "expert", split_axis=0, concat_axis=0, tiled=True)
    grad_arrived = grad_arrived.reshape(owners, per_owner, capacity, model_width)
    hidden_grad = jnp.einsum(
        "sjcd,jfd->sjcf", grad_arrived, expert_out, preferred_element_type=jnp.float32
    )
    grad_expert_out = jnp.einsum(
        "sjcf,sjcd->jfd", hidden, grad_arrived, preferred_element_type=jnp.float32
    )
    pre_grad = jax.vjp(exact_gelu, before)[1](hidden_grad)[0].astype(jnp.bfloat16)
    grad_expert_in = jnp.einsum(
        "sjcd,sjcf->jdf", grouped, pre_grad, preferred_element_type=jnp.float32
    )
    buffer_part = jnp.einsum(
        "sjcf,jdf->sjcd", pre_grad, expert_in, preferred_element_type=jnp.float32
    )
    buffer_share = lax.psum_scatter(buffer_part, "tensor", scatter_dimension=3, tiled=True).astype(
        jnp.bfloat16
    )
    buffer_back = lax.all_to_all(
        buffer_share.reshape(experts, capacity, slice_width),
        "expert",
        split_axis=0,
        concat_axis=0,
        tiled=True,
    )
    buffer_grad = lax.all_gather(buffer_back, "tensor", axis=2, tiled=True).reshape(
        slot_total, model_width
    )
    routed_grad = jnp.sum(
        buffer_grad[safe_index].reshape(token_rows, 2, model_width).astype(jnp.float32)
        * kept_mask[:, :, None],
        axis=1,
    )
    routed_grad = routed_grad + jnp.dot(
        logit_grad, router_weight.T, preferred_element_type=jnp.float32
    )
    grad_router = jnp.einsum("td,te->de", routed, logit_grad, preferred_element_type=jnp.float32)
    from_norm_two, grad_gain_experts = normalize_back(
        routed_grad, normed_two, inverse_two, gain_experts
    )
    residual_grad = upstream + from_norm_two
    attn_grad = residual_grad.astype(jnp.bfloat16)
    grad_out = jnp.einsum("tf,td->fd", attended, attn_grad, preferred_element_type=jnp.float32)
    heads_grad = jnp.dot(attn_grad, out_weight.T, preferred_element_type=jnp.float32).astype(
        jnp.bfloat16
    )
    heads_grad = heads_grad.reshape(images, seq_len, local_heads, HD)
    again = (
        jnp.einsum("ishe,ithe->ihst", queries, key_rows, preferred_element_type=jnp.float32)
        * score_scale
    )
    probs_full = jnp.exp(again - log_total)
    prob_grad = jnp.einsum(
        "ishe,ithe->ihst", heads_grad, value_rows, preferred_element_type=jnp.float32
    )
    value_grad = jnp.einsum(
        "ihst,ishe->ithe",
        probs_full.astype(jnp.bfloat16),
        heads_grad,
        preferred_element_type=jnp.float32,
    )
    score_grad = (
        probs_full * (prob_grad - jnp.sum(prob_grad * probs_full, axis=-1, keepdims=True))
    ).astype(jnp.bfloat16)
    query_grad = (
        jnp.einsum("ihst,ithe->ishe", score_grad, key_rows, preferred_element_type=jnp.float32)
        * score_scale
    )
    key_grad = (
        jnp.einsum("ihst,ishe->ithe", score_grad, queries, preferred_element_type=jnp.float32)
        * score_scale
    )
    project_grad = (
        jnp.stack([query_grad, key_grad, value_grad])
        .astype(jnp.bfloat16)
        .reshape(3, token_rows, local_width)
    )
    grad_qkv = jnp.einsum("td,ctf->cdf", entered, project_grad, preferred_element_type=jnp.float32)
    entered_part = jnp.einsum(
        "ctf,cdf->td", project_grad, qkv_weight, preferred_element_type=jnp.float32
    )
    entered_grad = lax.psum(entered_part.astype(jnp.bfloat16), "tensor").astype(jnp.float32)
    from_norm_one, grad_gain_attention = normalize_back(
        entered_grad, normed_one, inverse_one, gain_attention
    )
    grad_tokens = (residual_grad + from_norm_one).reshape(images, seq_len, model_width)
    counts = jnp.sum(member, axis=(0, 1))
    prob_sum = jnp.sum(route_prob, axis=0)
    grad_qkv, grad_out, grad_router, grad_gain_attention, grad_gain_experts, counts, prob_sum = (
        lax.psum(
            (
                grad_qkv,
                grad_out,
                grad_router,
                grad_gain_attention,
                grad_gain_experts,
                counts,
                prob_sum,
            ),
            ("dp", "expert"),
        )
    )
    grad_expert_in, grad_expert_out = (
        lax.psum(grad_expert_in.astype(jnp.bfloat16), "dp").astype(jnp.float32),
        lax.psum(grad_expert_out.astype(jnp.bfloat16), "dp").astype(jnp.float32),
    )
    token_total = token_rows * lax.axis_size("dp") * lax.axis_size("expert")
    balance_loss = experts * jnp.sum(counts / (2.0 * token_total) * prob_sum / token_total)
    return (
        block_out,
        grad_tokens,
        grad_qkv,
        grad_out,
        grad_router,
        grad_expert_in,
        grad_expert_out,
        grad_gain_attention,
        grad_gain_experts,
        balance_loss,
    )


NN = ((1,), (0,))
NT = ((1,), (1,))
TN = ((0,), (0,))
LANES = 128
SMALL = 8


def round_up(value, step):
    return -(-value // step) * step


def contract(a, b, dims):
    return lax.dot_general(a, b, (dims, ((), ())), preferred_element_type=jnp.float32)


def load_then(kernel, loads, count, *refs):
    pos_ref, *refs = refs
    *refs, sem = refs
    buffers = refs[len(refs) - len(loads) :]
    refs = refs[: len(refs) - len(loads)]
    copies = [
        pltpu.make_async_copy(refs[index], buffer, sem.at[i])
        for i, (index, buffer) in enumerate(zip(loads, buffers))
    ]
    for copy in copies:
        copy.start()
    for index, buffer in zip(loads, buffers):
        refs[index] = buffer

    def arrive(*indices):
        for index in indices:
            copies[loads.index(index)].wait()

    kernel(arrive, pos_ref, *refs)


def kernel_call(kernel, name, position, args, outs, scratch=(), flops=0, limit=24, loads=()):
    if loads:
        kernel = functools.partial(load_then, kernel, loads, len(args))
        scratch = [
            *scratch,
            *(pltpu.VMEM(args[i].shape, args[i].dtype) for i in loads),
            pltpu.SemaphoreType.DMA((len(loads),)),
        ]
    places = [pltpu.HBM if i in loads else pltpu.VMEM for i in range(len(args))]
    return pl.pallas_call(
        kernel,
        in_specs=[pl.BlockSpec(memory_space=pltpu.SMEM)]
        + [pl.BlockSpec(memory_space=place) for place in places],
        out_specs=[pl.BlockSpec(memory_space=pltpu.VMEM)] * len(outs),
        out_shape=list(outs),
        scratch_shapes=list(scratch),
        compiler_params=pltpu.CompilerParams(vmem_limit_bytes=limit << 20),
        cost_estimate=pl.CostEstimate(flops=flops, bytes_accessed=0, transcendentals=0),
        name=name,
    )(position, *args)


def like(shape, dtype):
    return jax.ShapeDtypeStruct(shape, dtype)


def live_rows(shape, limit, offset=0):
    return lax.broadcasted_iota(jnp.int32, shape, 0) + offset < limit


def chunk_of(pos_ref, j, size):
    return pl.ds(pl.multiple_of(lax.bitwise_xor(lax.axis_index("tensor"), j) * size, 8), size)


def head_masks(rows, heads):
    lane = lax.broadcasted_iota(jnp.int32, (rows, heads * HD), 1)
    return [(lane >= h * HD) & (lane < (h + 1) * HD) for h in range(heads)]


def keep_lanes(value, mask):
    return jnp.where(mask, value, jnp.zeros_like(value))


def split_high_low(value):
    high = value.astype(jnp.bfloat16)
    return high, (value - high.astype(jnp.float32)).astype(jnp.bfloat16)


def image_rows(ref, i, scratch_ref):
    seq_len = ref.shape[1]
    scratch_ref[seq_len:, :] = jnp.zeros((scratch_ref.shape[0] - seq_len, ref.shape[2]), jnp.float32)
    scratch_ref[0:seq_len, :] = ref[i].astype(jnp.float32)
    return scratch_ref[...]


def router_matrix(param_ref, experts):
    rows = param_ref[0:SMALL, :]
    rows = jnp.where(live_rows(rows.shape, experts), rows, 0.0).astype(jnp.bfloat16)
    zeros = jnp.zeros((LANES - SMALL, rows.shape[1]), jnp.bfloat16)
    return jnp.concatenate([rows, zeros], axis=0)


def chunk_kernel(
    tensors, arrive, pos_ref, tok_ref, cot_ref, ids_ref, rank_ref, router_ref, one_ref, two_ref, in_ref, out_ref,
    x_ref, pay_ref, param_ref, mine_ref, first_ref, second_ref, flat_ref, kept_ref,
):
    images, seq_len, width = tok_ref.shape
    chunk, experts = x_ref.shape[0], router_ref.shape[0]
    start = pl.multiple_of(lax.axis_index("tensor") * chunk, 8)
    for index, source, target in ((0, tok_ref, x_ref), (1, cot_ref, pay_ref)):
        arrive(index)
        flat_ref[images * seq_len :, :] = jnp.zeros(
            (flat_ref.shape[0] - images * seq_len, width), jnp.float32
        )
        for i in range(images):
            flat_ref[pl.ds(i * seq_len, seq_len), :] = source[i].astype(jnp.float32)
        target[0:chunk, :] = flat_ref[pl.ds(start, chunk), :].astype(jnp.bfloat16)
    arrive(2, 3, 4, 5, 6)
    kept_ref[...] = jnp.zeros_like(kept_ref)
    counts = jnp.zeros((1, LANES), jnp.float32)
    for i in range(images):
        rows, all_rows = [], []
        for e in range(experts):
            named = (ids_ref[i] == e).astype(jnp.float32)
            kept = jnp.where(rank_ref[i] >= 0, named, 0.0)
            rows.append(jnp.sum(kept, axis=0, keepdims=True))
            all_rows.append(jnp.sum(named, axis=0, keepdims=True))
        for group, is_kept in ((rows, True), (all_rows, False)):
            table = jnp.concatenate(group, axis=0)
            table = jnp.concatenate(
                [table, jnp.zeros((LANES - experts, seq_len), jnp.float32)], axis=0
            )
            table = jnp.concatenate(
                [table, jnp.zeros((LANES, 2 * LANES - seq_len), jnp.float32)], axis=1
            ).T
            if is_kept:
                kept_ref[pl.ds(i * seq_len, 2 * LANES), :] = table
            else:
                counts = counts + jnp.sum(table, axis=0, keepdims=True)
    kept = jnp.concatenate(
        [kept_ref[pl.ds(start, chunk), :], jnp.zeros((2 * LANES - chunk, LANES), jnp.float32)], axis=0
    ).T
    pay_ref[chunk:, : 2 * LANES] = kept[0 : 2 * SMALL].astype(jnp.bfloat16)
    pay_ref[chunk:, 2 * LANES :] = jnp.zeros((2 * SMALL, width - 2 * LANES), jnp.bfloat16)
    param_ref[...] = jnp.zeros_like(param_ref)
    param_ref[0:experts, :] = router_ref[...].astype(jnp.float32)
    param_ref[experts : experts + 1, :] = one_ref[...].reshape(1, width)
    param_ref[experts + 1 : experts + 2, :] = two_ref[...].reshape(1, width)
    param_ref[SMALL - 1 : SMALL, :LANES] = counts * (1.0 / tensors)
    arrive(7, 8)
    half = mine_ref.shape[1]
    core = pl.multiple_of(lax.axis_index("dp") * half, LANES)
    for s, part in ((0, in_ref[0, :, pl.ds(core, half)].T), (1, out_ref[0, pl.ds(core, half), :])):
        mine_ref[s] = part
        first_ref[s] = part[0 : half // 2]
        second_ref[s] = part[half // 2 :]


def stack_kernel(pos_ref, *refs):
    count = len(refs) // 3
    for i, target in enumerate(refs[2 * count :]):
        target[0] = refs[2 * i][...]
        target[1] = refs[2 * i + 1][...]


def stack_pairs(position, *pairs):
    return kernel_call(
        stack_kernel,
        "stack",
        position,
        [value for pair in pairs for value in pair],
        [like((2, *pair[0].shape), pair[0].dtype) for pair in pairs],
        limit=4,
    )


def lay_kernel(pos_ref, *refs):
    *blocks, out_ref = refs
    chunk = blocks[0].shape[0]
    for k, block in enumerate(blocks):
        out_ref[k * chunk : (k + 1) * chunk, :] = block[...]


def lay_payload_kernel(pos_ref, near_ref, far_ref, out_ref):
    chunk = out_ref.shape[0] // 4
    width = near_ref.shape[2]
    for k in range(4):
        block = (near_ref, far_ref)[k % 2].at[k // 2]
        here = slice(k * chunk, (k + 1) * chunk)
        out_ref[here, :width] = block[0:chunk, :]
        kept = block[chunk:, : 2 * LANES].astype(jnp.float32)
        kept = jnp.concatenate([kept] * (LANES // kept.shape[0]), axis=0).T[0:chunk]
        out_ref[here, width:] = kept.astype(jnp.bfloat16)


def lay_rows(position, name, blocks):
    chunk, width = blocks[0].shape
    return kernel_call(
        lay_kernel,
        name,
        position,
        blocks,
        [like((len(blocks) * chunk, width), blocks[0].dtype)],
        limit=4,
    )[0]


def gain_row(param_ref, experts, which):
    return param_ref[experts + which : experts + which + 1, :]


def attention_kernel(
    heads, experts, arrive, pos_ref, tok_ref, param_ref, w_ref, wo_ref, qkv_ref, lse_ref, att_ref,
    *refs,
):
    *parts, flat_ref, image_ref, held_ref = refs
    images, rows, width = qkv_ref.shape[1], qkv_ref.shape[2], heads * HD
    seq_len = tok_ref.shape[1]
    masks = head_masks(rows, heads)
    keys_live = lax.broadcasted_iota(jnp.int32, (rows, rows), 1) < seq_len
    lane = lax.broadcasted_iota(jnp.int32, (rows, LANES), 1)
    flat_ref[images * seq_len :, :] = jnp.zeros(
        (flat_ref.shape[0] - images * seq_len, width), jnp.float32
    )
    arrive(0, 1, 2)

    @pl.loop(0, images)
    def _(i):
        entered = normalize(image_rows(tok_ref, i, image_ref), gain_row(param_ref, experts, 0))[2]
        entered = entered.astype(jnp.bfloat16)
        q, k, v = (
            contract(entered, w_ref[c * width : (c + 1) * width, :], NT).astype(jnp.bfloat16)
            for c in range(3)
        )
        qkv_ref[0, i], qkv_ref[1, i], qkv_ref[2, i] = q, k, v
        attended = jnp.zeros((rows, width), jnp.float32)
        lse_all = jnp.zeros((rows, LANES), jnp.float32)
        for h in range(heads):
            scores = contract(keep_lanes(q, masks[h]), k, NT) * (HD ** (-0.5))
            scores = jnp.where(keys_live, scores, -1e30)
            top = jnp.max(scores, axis=-1, keepdims=True)
            lse = top + jnp.log(jnp.sum(jnp.exp(scores - top), axis=-1, keepdims=True))
            probs = jnp.exp(scores - lse).astype(jnp.bfloat16)
            attended = attended + contract(probs, keep_lanes(v, masks[h]), NN)
            lse_all = jnp.where(lane == h, lse, lse_all)
        lse_ref[i] = lse_all
        held_ref[i] = attended

    for i in range(images):
        flat_ref[pl.ds(i * seq_len, seq_len), :] = held_ref[i, 0:seq_len, :]
    arrive(3)
    att_ref[...] = flat_ref[...].astype(jnp.bfloat16)
    for j, part in enumerate(parts):
        rows_j = flat_ref[chunk_of(pos_ref, j, part.shape[0]), :].astype(jnp.bfloat16)
        part[...] = contract(rows_j, wo_ref[...], NN).astype(jnp.bfloat16)


def route_kernel(experts, pos_ref, *refs):
    *got, x_ref, param_ref, res_ref, routed_ref, prob_ref = refs
    residual = x_ref[...].astype(jnp.float32)
    for part in got:
        residual = residual + part[...].astype(jnp.float32)
    res_ref[...] = residual
    routed = normalize(residual, gain_row(param_ref, experts, 1))[2].astype(jnp.bfloat16)
    routed_ref[...] = routed
    prob_ref[...] = route_probs(routed, router_matrix(param_ref, experts), experts)


def route_probs(rows, router, experts):
    logits = contract(rows, router, NT)
    lane = lax.broadcasted_iota(jnp.int32, logits.shape, 1)
    logits = jnp.where(lane < experts, logits, -1e30)
    weight = jnp.exp(logits - jnp.max(logits, axis=-1, keepdims=True))
    return weight / jnp.sum(weight, axis=-1, keepdims=True)


def gelu_parts(x):
    square = jnp.exp(-0.5 * x * x)
    share = 0.5 * (1.0 + lax.erf(x * (0.5**0.5)))
    return x * share, share + x * square * (0.5 / math.pi) ** 0.5


def expert_halves(x, rg, w_in, w_out, hidden_ref, pre_ref):
    before = contract(x, w_in, NT)
    value, slope = gelu_parts(before)
    hidden = value.astype(jnp.bfloat16)
    hidden_ref[...] = hidden
    part = contract(hidden, w_out, NN)
    pre = (contract(rg, w_out, NT) * slope).astype(jnp.bfloat16)
    pre_ref[...] = pre
    return part, contract(pre, w_in, NN)


def first_expert_kernel(
    experts, pos_ref, x_ref, pay_ref, param_ref, w0_ref, xa_ref, yb_ref, hidden_ref, pre_ref, rg_ref,
    gate_ref, part_ref, back_ref,
):
    count, width = x_ref.shape
    prob = route_probs(x_ref[...], router_matrix(param_ref, experts), experts)
    mine = lax.broadcasted_iota(jnp.int32, prob.shape, 1) == lax.axis_index("expert")
    kept = pay_ref[:, width:].astype(jnp.float32)
    kept = jnp.sum(jnp.where(mine, kept, 0.0), axis=-1, keepdims=True)
    gate = jnp.sum(jnp.where(mine, prob, 0.0), axis=-1, keepdims=True) * kept
    gate_ref[:, :LANES] = jnp.broadcast_to(gate, (count, LANES))
    gate_ref[:, LANES:] = jnp.broadcast_to(kept, (count, LANES))
    rg_ref[...] = (gate * pay_ref[:, :width].astype(jnp.float32)).astype(jnp.bfloat16)
    w_in, w_out = (
        jnp.concatenate([w0_ref[s], xa_ref[s], yb_ref[s]], axis=0) for s in range(2)
    )
    part_ref[...], back_ref[...] = expert_halves(
        x_ref[...], rg_ref[...], w_in, w_out, hidden_ref, pre_ref
    )


def second_expert_kernel(
    pos_ref, x_ref, pay_ref, rg_ref, gate_ref, part_in_ref, back_in_ref, pair_y_ref, pair_x_ref,
    hidden_ref, pre_ref, gated_ref, back_ref,
):
    width = x_ref.shape[1]
    w_in, w_out = (
        jnp.concatenate([ref[r, s] for ref in (pair_y_ref, pair_x_ref) for r in range(2)], axis=0)
        for s in range(2)
    )
    part, back = expert_halves(x_ref[...], rg_ref[...], w_in, w_out, hidden_ref, pre_ref)
    back_ref[:, :width] = (back_in_ref[...] + back).astype(back_ref.dtype)
    part = part_in_ref[...] + part
    gated_ref[...] = (gate_ref[:, 0:1] * part).astype(jnp.bfloat16)
    inner = jnp.sum(part * pay_ref[:, :width].astype(jnp.float32), axis=-1, keepdims=True)
    inner = gate_ref[:, LANES:] * inner
    if back_ref.dtype == jnp.bfloat16:
        high, low = split_high_low(inner)
        upper = lax.broadcasted_iota(jnp.int32, inner.shape, 1) < LANES // 2
        inner = jnp.where(upper, high.astype(jnp.float32), low.astype(jnp.float32))
    back_ref[:, width:] = inner.astype(back_ref.dtype)


def first_expert_pass(position, rows, payload, params, weights, experts):
    count, width = rows.shape
    hidden = 2 * weights[0].shape[1]
    return kernel_call(
        functools.partial(first_expert_kernel, experts),
        "experts_first",
        position,
        [rows, payload, params, *weights],
        [
            like((count, hidden), jnp.bfloat16),
            like((count, hidden), jnp.bfloat16),
            like((count, width), jnp.bfloat16),
            like((count, 2 * LANES), jnp.float32),
            like((count, width), jnp.float32),
            like((count, width), jnp.float32),
        ],
        limit=18,
    )


def second_expert_pass(position, rows, payload, first, weights, back_dtype):
    count, width = rows.shape
    hidden = 4 * weights[0].shape[2]
    return kernel_call(
        second_expert_kernel,
        "experts_second",
        position,
        [rows, payload, *first[2:], *weights],
        [
            like((count, hidden), jnp.bfloat16),
            like((count, hidden), jnp.bfloat16),
            like((count, width), jnp.bfloat16),
            like((count, width + LANES), back_dtype),
        ],
        limit=18,
    )


def join_kernel(pos_ref, back_ref, other_ref, gated_ref, gated_other_ref, *outs):
    *backs, own_ref, pair_ref, far_ref = outs
    chunk, width = own_ref.shape
    for k, out in enumerate(backs):
        here = pl.ds(k * chunk, chunk)
        other = other_ref[here, :].astype(jnp.float32)
        out[0:chunk, :] = (back_ref[here, :width] + other[:, :width]).astype(jnp.bfloat16)
        inner = jnp.sum(other[:, width:], axis=-1, keepdims=True) * (2.0 / LANES)
        inner = back_ref[here, width:] + inner
        inner = jnp.concatenate(
            [inner, jnp.zeros((2 * LANES - chunk, LANES), jnp.float32)], axis=0
        ).T
        high, low = split_high_low(inner[0:SMALL, :])
        both = jnp.where(
            live_rows(high.shape, SMALL // 2), high.astype(jnp.float32), low.astype(jnp.float32)
        )
        out[chunk:, : 2 * LANES] = both.astype(jnp.bfloat16)
        out[chunk:, 2 * LANES :] = jnp.zeros((SMALL, width - 2 * LANES), jnp.bfloat16)
        gated = gated_ref[here, :].astype(jnp.float32) + gated_other_ref[here, :].astype(jnp.float32)
        gated = gated.astype(jnp.bfloat16)
        if k % 2:
            pair_ref[k // 2] = gated
        else:
            (own_ref, far_ref)[k // 2][...] = gated


def pair_sum_kernel(pos_ref, base_ref, own_ref, far_ref, got_ref, sum_ref, send_ref):
    total = base_ref[...] + own_ref[...].astype(jnp.float32) + got_ref[0].astype(jnp.float32)
    sum_ref[...] = total
    send_ref[...] = (far_ref[...].astype(jnp.float32) + got_ref[1].astype(jnp.float32)).astype(
        jnp.bfloat16
    )


def expert_grad_kernel(first, pos_ref, *refs):
    outs = refs[8:]
    part_rows = outs[0].shape[2]
    for j, out in enumerate(outs):
        start = 2 * (first + j) * part_rows
        columns = slice(start, start + 2 * part_rows)
        for s in range(2):
            left_a, right_a, left_b, right_b = refs[4 * s : 4 * s + 4]
            grad = contract(left_a[:, columns], right_a[...], TN)
            grad = grad + contract(left_b[:, columns], right_b[...], TN)
            grad = grad.astype(jnp.bfloat16)
            out[0, s] = grad[0:part_rows]
            out[1, s] = grad[part_rows:]


def expert_grads(position, a, b, rows_a, rows_b, first=0, count=2, flops=0):
    width, total = rows_a[0].shape[1], a[0].shape[1]
    return kernel_call(
        functools.partial(expert_grad_kernel, first),
        "expert_grads",
        position,
        [a[1], rows_a[0], b[1], rows_b[0], a[0], rows_a[1], b[0], rows_b[1]],
        [like((2, 2, total // 4, width), jnp.bfloat16)] * count,
        flops=flops,
        limit=10,
    )


def route_back_kernel(
    experts, token_rows, owners, pos_ref, *refs
):
    backs = refs[:owners]
    prob_ref, res_ref, pay_ref, param_ref = refs[owners : owners + 4]
    grad_ref, up_ref, small_ref = refs[owners + 4 :]
    chunk, width = res_ref.shape
    prob = prob_ref[...]
    lane = lax.broadcasted_iota(jnp.int32, prob.shape, 1)
    route_grad = jnp.zeros_like(prob)
    routed_grad = jnp.zeros((chunk, width), jnp.float32)
    for k, back in enumerate(backs):
        owner = lax.bitwise_xor(lax.axis_index("expert"), k)
        inner = back[chunk:, : 2 * LANES].astype(jnp.float32)
        inner = jnp.concatenate([inner] * (LANES // SMALL), axis=0).T[0:chunk]
        inner = jnp.sum(inner, axis=-1, keepdims=True) * (2.0 / LANES)
        route_grad = jnp.where(lane == owner, inner, route_grad)
        routed_grad = routed_grad + back[0:chunk, :].astype(jnp.float32)
    mean = jnp.sum(route_grad * prob, axis=-1, keepdims=True)
    logit_grad = (prob * (route_grad - mean)).astype(jnp.bfloat16)
    routed_grad = routed_grad + contract(
        logit_grad, router_matrix(param_ref, experts), NN
    )
    normed, inverse, mixed = normalize(res_ref[...], gain_row(param_ref, experts, 1))
    from_norm, gain_grad = normalize_back(
        routed_grad, normed, inverse, gain_row(param_ref, experts, 1)
    )
    total = pay_ref[0:chunk, :].astype(jnp.float32) + from_norm
    grad_ref[...] = total
    up_ref[...] = total.astype(jnp.bfloat16)
    live = live_rows(prob.shape, token_rows, lax.axis_index("tensor") * chunk)
    prob_sum = jnp.sum(jnp.where(live, prob, 0.0), axis=0, keepdims=True)
    grad_router = contract(logit_grad, mixed.astype(jnp.bfloat16), TN)
    small_ref[0:SMALL, :] = grad_router[0:SMALL]
    small_ref[experts : experts + 1, :] = gain_grad[None]
    small_ref[experts + 1 : experts + 2, :] = jnp.zeros((1, width), jnp.float32)
    small_ref[experts + 1 : experts + 2, :LANES] = prob_sum
    small_ref[experts + 2 : experts + 3, :] = param_ref[SMALL - 1 : SMALL, :]


def attention_back_kernel(
    heads, experts, owners, pos_ref, tok_ref, param_ref, w_ref, wo_ref, qkv_ref, lse_ref, att_ref,
    up_ref, small_ref, keep_ref, send_ref, *refs,
):
    *parts, hg_ref, flat_ref, big_ref, image_ref, held_ref, sum_ref, gain_ref = refs
    images, rows, width = qkv_ref.shape[1], qkv_ref.shape[2], heads * HD
    seq_len = tok_ref.shape[1]
    scale = HD ** (-0.5)
    padded, model = up_ref.shape
    chunk = padded // len(parts)
    masks = head_masks(rows, heads)
    keys_live = lax.broadcasted_iota(jnp.int32, (rows, rows), 1) < seq_len
    lane = lax.broadcasted_iota(jnp.int32, (rows, LANES), 1)
    up = up_ref[...]
    hg_ref[0:padded, :] = contract(up, wo_ref[...], NT)
    hg_ref[padded:, :] = jnp.zeros((hg_ref.shape[0] - padded, width), jnp.float32)
    big_ref[3 * width :, :] = contract(att_ref[...], up, TN)
    flat_ref[images * seq_len :, :] = jnp.zeros(
        (flat_ref.shape[0] - images * seq_len, model), jnp.float32
    )
    for i in range(images):
        held_ref[i] = hg_ref[pl.ds(i * seq_len, rows), :]
    big_ref[0 : 3 * width, :] = jnp.zeros((3 * width, model), jnp.float32)

    @pl.loop(0, images, unroll=True)
    def _(i):
        normed, _, mixed = normalize(
            image_rows(tok_ref, i, image_ref), gain_row(param_ref, experts, 0)
        )
        entered = mixed.astype(jnp.bfloat16)
        q, k, v = qkv_ref[0, i], qkv_ref[1, i], qkv_ref[2, i]
        heads_grad = held_ref[i]
        heads_grad = jnp.where(live_rows(heads_grad.shape, seq_len), heads_grad, 0.0)
        heads_grad = heads_grad.astype(jnp.bfloat16)
        dq = jnp.zeros((rows, width), jnp.float32)
        dk, dv = dq, dq
        for h in range(heads):
            q_h, k_h = keep_lanes(q, masks[h]), keep_lanes(k, masks[h])
            up_h = keep_lanes(heads_grad, masks[h])
            scores = contract(q_h, k, NT) * scale
            lse = jnp.sum(jnp.where(lane == h, lse_ref[i], 0.0), axis=-1, keepdims=True)
            probs = jnp.where(keys_live, jnp.exp(scores - lse), 0.0)
            prob_grad = contract(up_h, v, NT)
            total = jnp.sum(prob_grad * probs, axis=-1, keepdims=True)
            score_grad = (probs * (prob_grad - total)).astype(jnp.bfloat16)
            dv = dv + contract(probs.astype(jnp.bfloat16), up_h, TN)
            dq = dq + contract(score_grad, k_h, NN)
            dk = dk + contract(score_grad, q_h, TN)
        grads = [g.astype(jnp.bfloat16) for g in (dq * scale, dk * scale, dv)]
        part = jnp.zeros((rows, model), jnp.float32)
        for c in range(3):
            here = slice(c * width, (c + 1) * width)
            part = part + contract(grads[c], w_ref[here, :], NN)
            big_ref[here, :] += contract(grads[c], entered, TN)
        sum_ref[i] = part
        gain_ref[i] = jnp.broadcast_to(
            jnp.sum(part * normed, axis=0, keepdims=True), gain_ref.shape[1:]
        )

    gain_grad = jnp.zeros((1, model), jnp.float32)
    for i in range(images):
        flat_ref[pl.ds(i * seq_len, seq_len), :] = sum_ref[i, 0:seq_len, :]
        gain_grad = gain_grad + gain_ref[i, 0:1, :]
    high, low = split_high_low(
        jnp.concatenate([small_ref[0 : SMALL - 1, :], gain_grad], axis=0)
    )
    for j, part in enumerate(parts):
        part[0:chunk, :] = flat_ref[chunk_of(pos_ref, j, chunk), :].astype(jnp.bfloat16)
        part[chunk:, :] = jnp.concatenate([high, low], axis=0)
    me, core = lax.axis_index("expert"), lax.axis_index("dp")
    piece = keep_ref.shape[1]
    for k in range(owners):
        place = lax.bitwise_xor(me, k) * piece
        mine = pl.ds(pl.multiple_of(core * owners * piece + place, 8), piece)
        other = pl.ds(pl.multiple_of((1 - core) * owners * piece + place, 8), piece)
        keep_ref[k] = big_ref[mine, :]
        send_ref[k] = big_ref[other, :].astype(jnp.bfloat16)


def norm_back_kernel(experts, tensors, pos_ref, *refs):
    got = refs[:tensors]
    x_ref, res_ref, param_ref, own_ref, *parts, grad_ref, out_ref, small_ref = refs[tensors:]
    chunk, width = x_ref.shape
    upstream = jnp.zeros((chunk, width), jnp.float32)
    for j, part in enumerate(got):
        upstream = upstream + part[0:chunk, :].astype(jnp.float32)
        small_ref[lax.bitwise_xor(lax.axis_index("tensor"), j)] = part[chunk : chunk + SMALL, :].astype(
            jnp.float32
        ) + part[chunk + SMALL :, :].astype(jnp.float32)
    small = small_ref[0]
    for j in range(1, tensors):
        small = small + small_ref[j]
    gain = gain_row(param_ref, experts, 0)
    normed, inverse, _ = normalize(x_ref[...].astype(jnp.float32), gain)
    from_norm = normalize_back(upstream, normed, inverse, gain)[0]
    grad_ref[...] = (res_ref[...] + from_norm).astype(jnp.bfloat16)
    piece = own_ref.shape[0]
    total = own_ref[...]
    for part in parts:
        total = total + part[...].astype(jnp.float32)
    out_ref[0:piece, :] = total.astype(jnp.bfloat16)
    out_ref[piece:, :] = jnp.concatenate(split_high_low(small), axis=0)


def second_step_kernel(pos_ref, near_ref, from_y, from_x, x_ref, y_ref):
    for target, row, other in ((x_ref, 0, from_y), (y_ref, 1, from_x)):
        total = near_ref[row].astype(jnp.float32) + other[1].astype(jnp.float32)
        target[...] = total.astype(jnp.bfloat16)


def weight_sum_kernel(pos_ref, own_ref, from_y, from_x, last_x, last_y, out_ref):
    part_rows = last_x.shape[1]
    for row, other, last in ((0, from_y, last_x), (1, from_x, last_y)):
        total = own_ref[row].astype(jnp.float32) + other[0].astype(jnp.float32)
        total = total + last[...].astype(jnp.float32)
        out_ref[:, row * part_rows : (row + 1) * part_rows, :] = total.astype(jnp.bfloat16)


def add_core_kernel(pos_ref, keep_ref, other_ref, own_ref, *outs):
    total = keep_ref[...] + other_ref[...].astype(jnp.float32)
    own_ref[...] = total[0]
    for k, out in enumerate(outs):
        out[...] = total[k + 1].astype(jnp.bfloat16)


def spread_kernel(owners, experts, token_total, pos_ref, *refs):
    sides = refs[:2]
    qkv_ref, wo_ref, router_ref, one_ref, two_ref, loss_ref, big_ref, parts_ref = refs[2:]
    span = sides[0].shape[0] // owners
    piece = span - 2 * SMALL
    core, me = lax.axis_index("dp"), lax.axis_index("expert")
    for c in range(2):
        side = core if c == 0 else 1 - core
        for k in range(owners):
            block = sides[c].at[k * span : (k + 1) * span]
            place = side * owners + lax.bitwise_xor(me, k)
            here = pl.ds(pl.multiple_of(place * piece, 8), piece)
            big_ref[here, :] = block[0:piece, :].astype(jnp.float32)
            parts_ref[place] = block[piece : piece + SMALL, :].astype(jnp.float32) + block[
                piece + SMALL :, :
            ].astype(jnp.float32)
    rows = qkv_ref.shape[0]
    qkv_ref[...] = big_ref[0:rows, :]
    wo_ref[...] = big_ref[rows:, :]
    small = parts_ref[0]
    for p in range(1, 2 * owners):
        small = small + parts_ref[p]
    router_ref[...] = small[0:experts, :]
    one_ref[...] = small[SMALL - 1 : SMALL, :].reshape(small.shape[1])
    two_ref[...] = small[experts : experts + 1, :].reshape(small.shape[1])
    product = small[experts + 1 : experts + 2, :LANES] * small[experts + 2 : experts + 3, :LANES]
    lane = lax.broadcasted_iota(jnp.int32, product.shape, 1)
    product = jnp.where(lane < experts, product, 0.0)
    loss = jnp.sum(product, axis=-1, keepdims=True)
    loss_ref[...] = jnp.broadcast_to(
        loss * (experts / (2.0 * token_total * token_total)), loss_ref.shape
    )


def images_kernel(pos_ref, *refs):
    *chunks, out_ref, flat_ref = refs
    images, seq_len, _ = out_ref.shape
    if len(chunks) == 1:
        flat_ref[...] = chunks[0][...].astype(jnp.float32)
    else:
        for j, part in enumerate(chunks):
            flat_ref[chunk_of(pos_ref, j, part.shape[0]), :] = part[...].astype(jnp.float32)
    for i in range(images):
        out_ref[i] = flat_ref[pl.ds(i * seq_len, seq_len), :].astype(out_ref.dtype)


def weight_out_kernel(pos_ref, mine_ref, other_ref, in_ref, out_ref):
    first_is_mine = lax.axis_index("dp") == 0
    half = mine_ref.shape[1]
    for c in range(2):
        here = slice(c * half, (c + 1) * half)
        take = first_is_mine if c == 0 else jnp.logical_not(first_is_mine)
        grad_in = jnp.where(take, mine_ref[0], other_ref[0]).astype(jnp.float32)
        in_ref[0, :, here] = grad_in.T
        out_ref[0, here, :] = jnp.where(take, mine_ref[1], other_ref[1]).astype(jnp.float32)


def swap_core(value):
    return lax.ppermute(value, "dp", [(0, 1), (1, 0)])


def hop(value, bit):
    size = lax.axis_size("expert")
    return lax.ppermute(value, "expert", [(i, i ^ bit) for i in range(size)])


def cross(value, bit):
    size = lax.axis_size("tensor")
    return lax.ppermute(value, "tensor", [(i, i ^ bit) for i in range(size)])


def after(value, *others):
    return lax.optimization_barrier((value, *others))[0]


def dense_body(
    tokens,
    cotangent,
    expert_ids,
    slot_rank,
    qkv_weight,
    out_weight,
    router_weight,
    expert_in,
    expert_out,
    gain_attention,
    gain_experts,
):
    f32, b16 = jnp.float32, jnp.bfloat16
    images, seq_len, width = tokens.shape
    token_rows = images * seq_len
    local = qkv_weight.shape[2]
    heads = local // HD
    experts = router_weight.shape[1]
    owners = lax.axis_size("expert")
    tensors = lax.axis_size("tensor")
    cores = lax.axis_size("dp")
    chunk = round_up(-(-token_rows // tensors), 8)
    padded = chunk * tensors
    rows = round_up(seq_len, 16)
    flat_rows = padded + 32
    half = expert_in.shape[2] // cores
    quarter = half // 2
    position = jnp.zeros((1,), jnp.int32)
    weight_rows = qkv_weight.transpose(0, 2, 1).reshape(3 * local, width)

    x_chunk, payload, params, mine, first, second = kernel_call(
        functools.partial(chunk_kernel, tensors),
        "chunk",
        position,
        [
            tokens,
            cotangent,
            expert_ids.transpose(0, 2, 1),
            slot_rank.transpose(0, 2, 1),
            router_weight.T,
            gain_attention,
            gain_experts,
            expert_in,
            expert_out,
        ],
        [
            like((chunk, width), b16),
            like((chunk + 2 * SMALL, width), b16),
            like((SMALL, width), f32),
            like((2, half, width), b16),
            like((2, quarter, width), b16),
            like((2, quarter, width), b16),
        ],
        [
            pltpu.VMEM((flat_rows, width), f32),
            pltpu.VMEM((padded + 2 * LANES, LANES), f32),
        ],
        limit=56,
        loads=tuple(range(9)),
    )
    payload_two = hop(payload, 2)
    first_x = cross(first, 1)
    second_y = cross(second, 2)

    qkv, lse, attended, *parts = kernel_call(
        functools.partial(attention_kernel, heads, experts),
        "attention",
        after(position, mine),
        [tokens, params, weight_rows, out_weight],
        [
            like((3, images, rows, local), b16),
            like((images, rows, LANES), f32),
            like((padded, local), b16),
        ]
        + [like((chunk, width), b16)] * tensors,
        [
            pltpu.VMEM((padded, local), f32),
            pltpu.VMEM((rows, width), f32),
            pltpu.VMEM((images, rows, local), f32),
        ],
        flops=40_000_000_000,
        limit=20,
        loads=(0, 1, 2, 3),
    )
    arrived = [parts[0]] + [cross(parts[j], j) for j in range(1, tensors)]
    pair_first, pair_second = stack_pairs(
        after(position, parts[0]), (first, first_x), (second, second_y)
    )
    (payload_near,) = stack_pairs(after(position, pair_first), (payload, payload_two))
    payload_far = hop(payload_near, 1)

    residual, routed, prob = kernel_call(
        functools.partial(route_kernel, experts),
        "route",
        after(position, pair_first, payload_near),
        [*arrived, x_chunk, params],
        [like((chunk, width), f32), like((chunk, width), b16), like((chunk, LANES), f32)],
        limit=8,
    )
    blocks = [routed] + [hop(routed, k) for k in range(1, owners)]
    pair_first, pair_second = after((pair_first, pair_second), routed)
    pair_y = cross(pair_first, 2)
    pair_x = cross(pair_second, 1)
    payload_mine = kernel_call(
        lay_payload_kernel,
        "lay_payload",
        after(position, routed),
        [payload_near, payload_far],
        [like((owners * chunk, width + LANES), b16)],
        limit=6,
    )[0]
    payload_other = swap_core(payload_mine)
    rows_mine = lay_rows(position, "lay_rows", blocks)
    rows_other = swap_core(rows_mine)

    near_weights, far_weights = (mine, first_x, second_y), (pair_y, pair_x)
    first_a = first_expert_pass(position, rows_mine, payload_mine, params, near_weights, experts)
    first_b = first_expert_pass(
        after(position, first_a[2]), rows_other, payload_other, params, near_weights, experts
    )
    second_b = second_expert_pass(
        after(position, first_b[2]), rows_other, payload_other, first_b, far_weights, b16
    )
    back_other, gated_other = swap_core(second_b[3]), swap_core(second_b[2])
    second_a = second_expert_pass(
        after(position, second_b[0]), rows_mine, payload_mine, first_a, far_weights, f32
    )
    *joined, gated_own, gated_pair, gated_far = kernel_call(
        join_kernel,
        "join",
        position,
        [second_a[3], back_other, second_a[2], gated_other],
        [like((chunk + SMALL, width), b16)] * owners
        + [like((chunk, width), b16), like((2, chunk, width), b16), like((chunk, width), b16)],
        limit=8,
    )
    backs = [joined[0]] + [hop(joined[k], k) for k in range(1, owners)]

    grad_pos = after(position, joined)
    far_rows = (rows_mine, first_a[2]), (rows_other, first_b[2])
    (far_y,) = expert_grads(grad_pos, second_a, second_b, *far_rows, first=0, count=1)
    (far_x,) = expert_grads(
        after(grad_pos, far_y), second_a, second_b, *far_rows, first=1, count=1, flops=0
    )
    from_y, from_x = cross(far_y, 2), cross(far_x, 1)
    residual_grad, attn_grad, small = kernel_call(
        functools.partial(route_back_kernel, experts, token_rows, owners),
        "route_back",
        position,
        [*backs, prob, residual, payload, params],
        [like((chunk, width), f32), like((chunk, width), b16), like((SMALL, width), f32)],
        flops=40_000_000_000,
        limit=8,
    )
    own_grad, near_grad = expert_grads(
        after(position, attn_grad), first_a, first_b, (rows_mine, first_a[2]), (rows_other, first_b[2]),
    )
    gated_near = hop(after(gated_pair, backs[1]), 1)
    block_sum, gated_far = kernel_call(
        pair_sum_kernel,
        "pair_sum",
        after(position, own_grad),
        [residual, gated_own, gated_far, gated_near],
        [like((chunk, width), f32), like((chunk, width), b16)],
        limit=4,
    )
    attn_grad, gated_far = lax.optimization_barrier((attn_grad, gated_far))
    gated_last = hop(gated_far, 2)
    attn_grad = lax.all_gather(attn_grad, "tensor", axis=0, tiled=True)
    piece = 4 * local // (2 * owners)
    keep, send, *parts = kernel_call(
        functools.partial(attention_back_kernel, heads, experts, owners),
        "attention_back",
        after(position, from_y, from_x, gated_last),
        [tokens, params, weight_rows, out_weight, qkv, lse, attended, attn_grad, small],
        [
            like((owners, piece, width), f32),
            like((owners, piece, width), b16),
        ]
        + [like((chunk + 2 * SMALL, width), b16)] * tensors,
        [
            pltpu.VMEM((flat_rows, local), f32),
            pltpu.VMEM((flat_rows, width), f32),
            pltpu.VMEM((4 * local, width), f32),
            pltpu.VMEM((rows, width), f32),
            pltpu.VMEM((images, rows, local), f32),
            pltpu.VMEM((images, rows, width), f32),
            pltpu.VMEM((images, SMALL, width), f32),
        ],
        limit=20,
        flops=6_000_000_000,
    )
    own_piece, *pieces = kernel_call(
        add_core_kernel,
        "add_core",
        position,
        [keep, swap_core(send)],
        [like((piece, width), f32)] + [like((piece, width), b16)] * (owners - 1),
        limit=8,
    )
    reduced = [hop(p, k + 1) for k, p in enumerate(pieces)]
    got = [parts[0]] + [cross(parts[j], j) for j in range(1, tensors)]

    up_x, up_y = kernel_call(
        second_step_kernel,
        "second_step",
        after(position, own_piece),
        [near_grad, from_y, from_x],
        [like((2, quarter, width), b16)] * 2,
        limit=8,
    )
    up_x, up_y = after((up_x, up_y), got[1:])
    last_x, last_y = cross(up_x, 1), cross(up_y, 2)

    grad_chunk, summed = kernel_call(
        functools.partial(norm_back_kernel, experts, tensors),
        "norm_back",
        position,
        [*got, x_chunk, residual_grad, params, own_piece, *reduced],
        [like((chunk, width), b16), like((piece + 2 * SMALL, width), b16)],
        [pltpu.VMEM((tensors, SMALL, width), f32)],
        flops=40_000_000_000,
        limit=8,
    )
    around = [summed] + [hop(summed, k) for k in range(1, owners)]
    grad_rows = lax.all_gather(grad_chunk, "tensor", axis=0, tiled=True)
    combined = (block_sum + gated_last.astype(f32)).astype(b16)
    combined = after(combined, grad_rows)
    block_parts = [combined] + [cross(combined, j) for j in range(1, tensors)]

    grad_tokens = kernel_call(
        images_kernel,
        "grad_tokens",
        position,
        [grad_rows],
        [like(tokens.shape, f32)],
        [pltpu.VMEM((padded, width), f32)],
        limit=8,
    )[0]
    grad_half = kernel_call(
        weight_sum_kernel,
        "weight_sum",
        after(position, grad_rows, around),
        [own_grad, from_y, from_x, last_x, last_y],
        [like((2, half, width), b16)],
        limit=8,
    )[0]
    grad_expert_in, grad_expert_out = kernel_call(
        weight_out_kernel,
        "weight_out",
        position,
        [grad_half, swap_core(grad_half)],
        [like((1, width, 2 * half), f32), like((1, 2 * half, width), f32)],
        limit=10,
    )
    around_rows = lay_rows(position, "lay_grads", around)
    token_total = token_rows * cores * owners
    grad_qkv, grad_out, grad_router, gain_one, gain_two, loss = kernel_call(
        functools.partial(spread_kernel, owners, experts, token_total),
        "spread",
        position,
        [around_rows, swap_core(around_rows)],
        [
            like((3 * local, width), f32),
            like((local, width), f32),
            like((experts, width), f32),
            like((width,), f32),
            like((width,), f32),
            like((1, LANES), f32),
        ],
        [
            pltpu.VMEM((4 * local, width), f32),
            pltpu.VMEM((2 * owners, SMALL, width), f32),
        ],
        limit=8,
    )
    block_out = kernel_call(
        images_kernel,
        "block_out",
        after(position, grad_tokens, grad_expert_in, grad_qkv),
        block_parts,
        [like(tokens.shape, b16)],
        [pltpu.VMEM((padded, width), f32)],
        limit=8,
    )[0]
    return (
        block_out,
        grad_tokens,
        grad_qkv.reshape(3, local, width).transpose(0, 2, 1),
        grad_out,
        grad_router.T,
        grad_expert_in,
        grad_expert_out,
        gain_one,
        gain_two,
        loss[0, 0],
    )


def solution(mesh):
    placed = (
        P(("dp", "expert"), None, None),
        P(("dp", "expert"), None, None),
        P(("dp", "expert"), None, None),
        P(("dp", "expert"), None, None),
        P(None, None, "tensor"),
        P("tensor", None),
        P(),
        P("expert", None, "tensor"),
        P("expert", "tensor", None),
        P(),
        P(),
    )
    shape = mesh.shape
    dense = shape["dp"] == 2 and shape["expert"] == 4 and shape["tensor"] == 4
    return jax.shard_map(
        dense_body if dense else body,
        mesh=mesh,
        in_specs=placed,
        out_specs=(
            P(("dp", "expert"), None, None),
            P(("dp", "expert"), None, None),
            P(None, None, "tensor"),
            P("tensor", None),
            P(),
            P("expert", None, "tensor"),
            P("expert", "tensor", None),
            P(),
            P(),
            P(),
        ),
        check_vma=False,
    )
```

```python
import functools
import math

import jax
import jax.numpy as jnp
from jax import lax
from jax.experimental import pallas as pl
from jax.experimental.pallas import tpu as pltpu
from jax.sharding import PartitionSpec as P

HD = 64


epsilon = 1e-06


def normalize(values, gain_row):
    center = values - jnp.mean(values, axis=-1, keepdims=True)
    inverse = lax.rsqrt(jnp.mean(center * center, axis=-1, keepdims=True) + epsilon)
    normed = center * inverse
    return (normed, inverse, normed * gain_row)


def normalize_back(upstream, normed, inverse, gain_row):
    scaled = upstream * gain_row
    result = inverse * (
        scaled
        - jnp.mean(scaled, axis=-1, keepdims=True)
        - normed * jnp.mean(scaled * normed, axis=-1, keepdims=True)
    )
    return (result, jnp.sum(upstream * normed, axis=0))


def exact_gelu(values):
    return jax.nn.gelu(values, approximate=False)


def body(
    tokens,
    cotangent,
    expert_ids,
    slot_rank,
    qkv_weight,
    out_weight,
    router_weight,
    expert_in,
    expert_out,
    gain_attention,
    gain_experts,
):
    images, seq_len, model_width = tokens.shape
    token_rows = images * seq_len
    local_width = qkv_weight.shape[2]
    local_heads = local_width // HD
    slice_width = model_width // lax.axis_size("tensor")
    experts = router_weight.shape[1]
    capacity = 5 * token_rows // (2 * experts)
    owners = lax.axis_size("expert")
    per_owner = experts // owners
    slot_total = experts * capacity
    score_scale = HD ** (-0.5)
    inputs = tokens.reshape(token_rows, model_width).astype(jnp.float32)
    normed_one, inverse_one, mixed_one = normalize(inputs, gain_attention)
    entered = mixed_one.astype(jnp.bfloat16)
    project = jnp.einsum(
        "td,cdf->ctf", entered, qkv_weight, preferred_element_type=jnp.float32
    ).astype(jnp.bfloat16)
    projected_heads = project.reshape(3, images, seq_len, local_heads, HD)
    queries, key_rows, value_rows = (projected_heads[0], projected_heads[1], projected_heads[2])
    scores = (
        jnp.einsum("ishe,ithe->ihst", queries, key_rows, preferred_element_type=jnp.float32)
        * score_scale
    )
    log_total = jax.nn.logsumexp(scores, axis=-1, keepdims=True)
    attn_probs = jnp.exp(scores - log_total).astype(jnp.bfloat16)
    attended = jnp.einsum(
        "ihst,ithe->ishe", attn_probs, value_rows, preferred_element_type=jnp.float32
    )
    attended = attended.astype(jnp.bfloat16).reshape(token_rows, local_width)
    attn_part = jnp.dot(attended, out_weight, preferred_element_type=jnp.float32)
    residual = inputs + lax.psum(attn_part, "tensor")
    normed_two, inverse_two, mixed_two = normalize(residual, gain_experts)
    routed = mixed_two.astype(jnp.bfloat16)
    route_prob = jax.nn.softmax(
        jnp.dot(routed, router_weight, preferred_element_type=jnp.float32), axis=-1
    )
    chosen = expert_ids.reshape(token_rows, 2)
    ranked = slot_rank.reshape(token_rows, 2)
    kept_mask = (ranked >= 0).astype(jnp.float32)
    position = jnp.where(ranked >= 0, chosen * capacity + ranked, slot_total).reshape(-1)
    send_rows = (
        jnp.zeros((slot_total, model_width), jnp.bfloat16)
        .at[position]
        .set(jnp.repeat(routed, 2, axis=0), mode="drop")
        .reshape(experts, capacity, model_width)
    )
    fragment = lax.all_to_all(send_rows, "expert", split_axis=0, concat_axis=0, tiled=True)
    grouped = fragment.reshape(owners, per_owner, fragment.shape[1], model_width)
    before = jnp.einsum("sjcd,jdf->sjcf", grouped, expert_in, preferred_element_type=jnp.float32)
    hidden = exact_gelu(before).astype(jnp.bfloat16)
    expert_part = jnp.einsum(
        "sjcf,jfd->sjcd", hidden, expert_out, preferred_element_type=jnp.float32
    )
    produced = lax.psum_scatter(expert_part, "tensor", scatter_dimension=3, tiled=True).astype(
        jnp.bfloat16
    )
    returned = lax.all_to_all(
        produced.reshape(experts, capacity, slice_width),
        "expert",
        split_axis=0,
        concat_axis=0,
        tiled=True,
    )
    returned = lax.all_gather(returned, "tensor", axis=2, tiled=True).reshape(
        slot_total, model_width
    )
    safe_index = jnp.minimum(position, slot_total - 1)
    picked = returned[safe_index].reshape(token_rows, 2, model_width).astype(jnp.float32)
    gate_values = jnp.take_along_axis(route_prob, chosen, axis=1) * kept_mask
    output = residual + jnp.sum(gate_values[:, :, None] * picked, axis=1)
    block_out = output.astype(jnp.bfloat16).reshape(images, seq_len, model_width)
    upstream = cotangent.reshape(token_rows, model_width).astype(jnp.float32)
    gate_grad = jnp.sum(upstream[:, None, :] * picked, axis=-1) * kept_mask
    member = (chosen[:, :, None] == jnp.arange(experts)[None, None, :]).astype(jnp.float32)
    route_grad = jnp.sum(member * gate_grad[:, :, None], axis=1)
    logit_grad = (
        route_prob * (route_grad - jnp.sum(route_grad * route_prob, axis=-1, keepdims=True))
    ).astype(jnp.bfloat16)
    row_grad = (
        (gate_values[:, :, None] * upstream[:, None, :])
        .astype(jnp.bfloat16)
        .reshape(2 * token_rows, model_width)
    )
    grad_send = (
        jnp.zeros((slot_total, model_width), jnp.bfloat16)
        .at[position]
        .set(row_grad, mode="drop")
        .reshape(experts, capacity, model_width)
    )
    grad_arrived = lax.all_to_all(grad_send, "expert", split_axis=0, concat_axis=0, tiled=True)
    grad_arrived = grad_arrived.reshape(owners, per_owner, capacity, model_width)
    hidden_grad = jnp.einsum(
        "sjcd,jfd->sjcf", grad_arrived, expert_out, preferred_element_type=jnp.float32
    )
    grad_expert_out = jnp.einsum(
        "sjcf,sjcd->jfd", hidden, grad_arrived, preferred_element_type=jnp.float32
    )
    pre_grad = jax.vjp(exact_gelu, before)[1](hidden_grad)[0].astype(jnp.bfloat16)
    grad_expert_in = jnp.einsum(
        "sjcd,sjcf->jdf", grouped, pre_grad, preferred_element_type=jnp.float32
    )
    buffer_part = jnp.einsum(
        "sjcf,jdf->sjcd", pre_grad, expert_in, preferred_element_type=jnp.float32
    )
    buffer_share = lax.psum_scatter(buffer_part, "tensor", scatter_dimension=3, tiled=True).astype(
        jnp.bfloat16
    )
    buffer_back = lax.all_to_all(
        buffer_share.reshape(experts, capacity, slice_width),
        "expert",
        split_axis=0,
        concat_axis=0,
        tiled=True,
    )
    buffer_grad = lax.all_gather(buffer_back, "tensor", axis=2, tiled=True).reshape(
        slot_total, model_width
    )
    routed_grad = jnp.sum(
        buffer_grad[safe_index].reshape(token_rows, 2, model_width).astype(jnp.float32)
        * kept_mask[:, :, None],
        axis=1,
    )
    routed_grad = routed_grad + jnp.dot(
        logit_grad, router_weight.T, preferred_element_type=jnp.float32
    )
    grad_router = jnp.einsum("td,te->de", routed, logit_grad, preferred_element_type=jnp.float32)
    from_norm_two, grad_gain_experts = normalize_back(
        routed_grad, normed_two, inverse_two, gain_experts
    )
    residual_grad = upstream + from_norm_two
    attn_grad = residual_grad.astype(jnp.bfloat16)
    grad_out = jnp.einsum("tf,td->fd", attended, attn_grad, preferred_element_type=jnp.float32)
    heads_grad = jnp.dot(attn_grad, out_weight.T, preferred_element_type=jnp.float32).astype(
        jnp.bfloat16
    )
    heads_grad = heads_grad.reshape(images, seq_len, local_heads, HD)
    again = (
        jnp.einsum("ishe,ithe->ihst", queries, key_rows, preferred_element_type=jnp.float32)
        * score_scale
    )
    probs_full = jnp.exp(again - log_total)
    prob_grad = jnp.einsum(
        "ishe,ithe->ihst", heads_grad, value_rows, preferred_element_type=jnp.float32
    )
    value_grad = jnp.einsum(
        "ihst,ishe->ithe",
        probs_full.astype(jnp.bfloat16),
        heads_grad,
        preferred_element_type=jnp.float32,
    )
    score_grad = (
        probs_full * (prob_grad - jnp.sum(prob_grad * probs_full, axis=-1, keepdims=True))
    ).astype(jnp.bfloat16)
    query_grad = (
        jnp.einsum("ihst,ithe->ishe", score_grad, key_rows, preferred_element_type=jnp.float32)
        * score_scale
    )
    key_grad = (
        jnp.einsum("ihst,ishe->ithe", score_grad, queries, preferred_element_type=jnp.float32)
        * score_scale
    )
    project_grad = (
        jnp.stack([query_grad, key_grad, value_grad])
        .astype(jnp.bfloat16)
        .reshape(3, token_rows, local_width)
    )
    grad_qkv = jnp.einsum("td,ctf->cdf", entered, project_grad, preferred_element_type=jnp.float32)
    entered_part = jnp.einsum(
        "ctf,cdf->td", project_grad, qkv_weight, preferred_element_type=jnp.float32
    )
    entered_grad = lax.psum(entered_part.astype(jnp.bfloat16), "tensor").astype(jnp.float32)
    from_norm_one, grad_gain_attention = normalize_back(
        entered_grad, normed_one, inverse_one, gain_attention
    )
    grad_tokens = (residual_grad + from_norm_one).reshape(images, seq_len, model_width)
    counts = jnp.sum(member, axis=(0, 1))
    prob_sum = jnp.sum(route_prob, axis=0)
    grad_qkv, grad_out, grad_router, grad_gain_attention, grad_gain_experts, counts, prob_sum = (
        lax.psum(
            (
                grad_qkv,
                grad_out,
                grad_router,
                grad_gain_attention,
                grad_gain_experts,
                counts,
                prob_sum,
            ),
            ("dp", "expert"),
        )
    )
    grad_expert_in, grad_expert_out = (
        lax.psum(grad_expert_in.astype(jnp.bfloat16), "dp").astype(jnp.float32),
        lax.psum(grad_expert_out.astype(jnp.bfloat16), "dp").astype(jnp.float32),
    )
    token_total = token_rows * lax.axis_size("dp") * lax.axis_size("expert")
    balance_loss = experts * jnp.sum(counts / (2.0 * token_total) * prob_sum / token_total)
    return (
        block_out,
        grad_tokens,
        grad_qkv,
        grad_out,
        grad_router,
        grad_expert_in,
        grad_expert_out,
        grad_gain_attention,
        grad_gain_experts,
        balance_loss,
    )


NN = ((1,), (0,))
NT = ((1,), (1,))
TN = ((0,), (0,))
LANES = 128
SMALL = 8


def round_up(value, step):
    return -(-value // step) * step


def contract(a, b, dims):
    return lax.dot_general(a, b, (dims, ((), ())), preferred_element_type=jnp.float32)


def load_then(kernel, loads, count, *refs):
    pos_ref, *refs = refs
    *refs, sem = refs
    buffers = refs[len(refs) - len(loads) :]
    refs = refs[: len(refs) - len(loads)]
    copies = [
        pltpu.make_async_copy(refs[index], buffer, sem.at[i])
        for i, (index, buffer) in enumerate(zip(loads, buffers))
    ]
    for copy in copies:
        copy.start()
    for index, buffer in zip(loads, buffers):
        refs[index] = buffer

    def arrive(*indices):
        for index in indices:
            copies[loads.index(index)].wait()

    kernel(arrive, pos_ref, *refs)


def kernel_call(kernel, name, position, args, outs, scratch=(), flops=0, limit=24, loads=()):
    if loads:
        kernel = functools.partial(load_then, kernel, loads, len(args))
        scratch = [
            *scratch,
            *(pltpu.VMEM(args[i].shape, args[i].dtype) for i in loads),
            pltpu.SemaphoreType.DMA((len(loads),)),
        ]
    places = [pltpu.HBM if i in loads else pltpu.VMEM for i in range(len(args))]
    return pl.pallas_call(
        kernel,
        in_specs=[pl.BlockSpec(memory_space=pltpu.SMEM)]
        + [pl.BlockSpec(memory_space=place) for place in places],
        out_specs=[pl.BlockSpec(memory_space=pltpu.VMEM)] * len(outs),
        out_shape=list(outs),
        scratch_shapes=list(scratch),
        compiler_params=pltpu.CompilerParams(vmem_limit_bytes=limit << 20),
        cost_estimate=pl.CostEstimate(flops=flops, bytes_accessed=0, transcendentals=0),
        name=name,
    )(position, *args)


def like(shape, dtype):
    return jax.ShapeDtypeStruct(shape, dtype)


def live_rows(shape, limit, offset=0):
    return lax.broadcasted_iota(jnp.int32, shape, 0) + offset < limit


def chunk_of(pos_ref, j, size):
    return pl.ds(pl.multiple_of(lax.bitwise_xor(lax.axis_index("tensor"), j) * size, 8), size)


def head_masks(rows, heads):
    lane = lax.broadcasted_iota(jnp.int32, (rows, heads * HD), 1)
    return [(lane >= h * HD) & (lane < (h + 1) * HD) for h in range(heads)]


def keep_lanes(value, mask):
    return jnp.where(mask, value, jnp.zeros_like(value))


def split_high_low(value):
    high = value.astype(jnp.bfloat16)
    return high, (value - high.astype(jnp.float32)).astype(jnp.bfloat16)


def image_rows(ref, i, scratch_ref):
    seq_len = ref.shape[1]
    scratch_ref[seq_len:, :] = jnp.zeros((scratch_ref.shape[0] - seq_len, ref.shape[2]), jnp.float32)
    scratch_ref[0:seq_len, :] = ref[i].astype(jnp.float32)
    return scratch_ref[...]


def router_matrix(param_ref, experts):
    rows = param_ref[0:SMALL, :]
    rows = jnp.where(live_rows(rows.shape, experts), rows, 0.0).astype(jnp.bfloat16)
    zeros = jnp.zeros((LANES - SMALL, rows.shape[1]), jnp.bfloat16)
    return jnp.concatenate([rows, zeros], axis=0)


def chunk_kernel(
    tensors, arrive, pos_ref, tok_ref, cot_ref, ids_ref, rank_ref, router_ref, one_ref, two_ref, in_ref, out_ref,
    x_ref, pay_ref, param_ref, mine_ref, first_ref, second_ref, flat_ref, kept_ref,
):
    images, seq_len, width = tok_ref.shape
    chunk, experts = x_ref.shape[0], router_ref.shape[0]
    start = pl.multiple_of(lax.axis_index("tensor") * chunk, 8)
    for index, source, target in ((0, tok_ref, x_ref), (1, cot_ref, pay_ref)):
        arrive(index)
        flat_ref[images * seq_len :, :] = jnp.zeros(
            (flat_ref.shape[0] - images * seq_len, width), jnp.float32
        )
        for i in range(images):
            flat_ref[pl.ds(i * seq_len, seq_len), :] = source[i].astype(jnp.float32)
        target[0:chunk, :] = flat_ref[pl.ds(start, chunk), :].astype(jnp.bfloat16)
    arrive(2, 3, 4, 5, 6)
    kept_ref[...] = jnp.zeros_like(kept_ref)
    counts = jnp.zeros((1, LANES), jnp.float32)
    for i in range(images):
        rows, all_rows = [], []
        for e in range(experts):
            named = (ids_ref[i] == e).astype(jnp.float32)
            kept = jnp.where(rank_ref[i] >= 0, named, 0.0)
            rows.append(jnp.sum(kept, axis=0, keepdims=True))
            all_rows.append(jnp.sum(named, axis=0, keepdims=True))
        for group, is_kept in ((rows, True), (all_rows, False)):
            table = jnp.concatenate(group, axis=0)
            table = jnp.concatenate(
                [table, jnp.zeros((LANES - experts, seq_len), jnp.float32)], axis=0
            )
            table = jnp.concatenate(
                [table, jnp.zeros((LANES, 2 * LANES - seq_len), jnp.float32)], axis=1
            ).T
            if is_kept:
                kept_ref[pl.ds(i * seq_len, 2 * LANES), :] = table
            else:
                counts = counts + jnp.sum(table, axis=0, keepdims=True)
    kept = jnp.concatenate(
        [kept_ref[pl.ds(start, chunk), :], jnp.zeros((2 * LANES - chunk, LANES), jnp.float32)], axis=0
    ).T
    pay_ref[chunk:, : 2 * LANES] = kept[0:SMALL].astype(jnp.bfloat16)
    pay_ref[chunk:, 2 * LANES :] = jnp.zeros((SMALL, width - 2 * LANES), jnp.bfloat16)
    param_ref[...] = jnp.zeros_like(param_ref)
    param_ref[0:experts, :] = router_ref[...].astype(jnp.float32)
    param_ref[experts : experts + 1, :] = one_ref[...].reshape(1, width)
    param_ref[experts + 1 : experts + 2, :] = two_ref[...].reshape(1, width)
    param_ref[SMALL - 1 : SMALL, :LANES] = counts * (1.0 / tensors)
    arrive(7, 8)
    half = mine_ref.shape[1]
    core = pl.multiple_of(lax.axis_index("dp") * half, LANES)
    for s, part in ((0, in_ref[0, :, pl.ds(core, half)].T), (1, out_ref[0, pl.ds(core, half), :])):
        mine_ref[s] = part
        first_ref[s] = part[0 : half // 2]
        second_ref[s] = part[half // 2 :]


def stack_kernel(pos_ref, *refs):
    count = len(refs) // 3
    for i, target in enumerate(refs[2 * count :]):
        target[0] = refs[2 * i][...]
        target[1] = refs[2 * i + 1][...]


def stack_pairs(position, *pairs):
    return kernel_call(
        stack_kernel,
        "stack",
        position,
        [value for pair in pairs for value in pair],
        [like((2, *pair[0].shape), pair[0].dtype) for pair in pairs],
        limit=4,
    )


def lay_kernel(pos_ref, *refs):
    *blocks, out_ref = refs
    chunk = blocks[0].shape[0]
    for k, block in enumerate(blocks):
        out_ref[k * chunk : (k + 1) * chunk, :] = block[...]


def lay_payload_kernel(pos_ref, near_ref, far_ref, out_ref):
    chunk = out_ref.shape[0] // 4
    width = near_ref.shape[2]
    for k in range(4):
        block = (near_ref, far_ref)[k % 2].at[k // 2]
        here = slice(k * chunk, (k + 1) * chunk)
        out_ref[here, :width] = block[0:chunk, :]
        kept = block[chunk:, : 2 * LANES].astype(jnp.float32)
        kept = jnp.concatenate([kept] * (LANES // kept.shape[0]), axis=0).T[0:chunk]
        out_ref[here, width:] = kept.astype(jnp.bfloat16)


def lay_rows(position, name, blocks):
    chunk, width = blocks[0].shape
    return kernel_call(
        lay_kernel,
        name,
        position,
        blocks,
        [like((len(blocks) * chunk, width), blocks[0].dtype)],
        limit=4,
    )[0]


def pack_small(small, experts):
    high, low = split_high_low(small)
    row = lax.broadcasted_iota(jnp.int32, (SMALL, LANES), 0)
    loss_rows = (row == experts + 1) | (row == experts + 2)
    low = jnp.where(loss_rows, low[:, :LANES].astype(jnp.float32), 0.0)
    high = high.astype(jnp.float32)
    packed = [high[:, :LANES], high[:, LANES : 2 * LANES] + low, high[:, 2 * LANES :]]
    return jnp.concatenate(packed, axis=1).astype(jnp.bfloat16)


def unpack_small(rows, experts):
    rows = rows.astype(jnp.float32)
    row = lax.broadcasted_iota(jnp.int32, (SMALL, LANES), 0)
    loss_rows = (row == experts + 1) | (row == experts + 2)
    low = rows[:, LANES : 2 * LANES]
    first = rows[:, :LANES] + jnp.where(loss_rows, low, 0.0)
    return jnp.concatenate([first, jnp.where(loss_rows, 0.0, low), rows[:, 2 * LANES :]], axis=1)


def gain_row(param_ref, experts, which):
    return param_ref[experts + which : experts + which + 1, :]


def attention_kernel(
    heads, experts, arrive, pos_ref, tok_ref, param_ref, w_ref, wo_ref, qkv_ref, lse_ref, att_ref,
    *refs,
):
    *parts, flat_ref, image_ref, held_ref = refs
    images, rows, width = qkv_ref.shape[1], qkv_ref.shape[2], heads * HD
    seq_len = tok_ref.shape[1]
    masks = head_masks(rows, heads)
    keys_live = lax.broadcasted_iota(jnp.int32, (rows, rows), 1) < seq_len
    lane = lax.broadcasted_iota(jnp.int32, (rows, LANES), 1)
    flat_ref[images * seq_len :, :] = jnp.zeros(
        (flat_ref.shape[0] - images * seq_len, width), jnp.float32
    )
    arrive(0, 1, 2)

    @pl.loop(0, images)
    def _(i):
        entered = normalize(image_rows(tok_ref, i, image_ref), gain_row(param_ref, experts, 0))[2]
        entered = entered.astype(jnp.bfloat16)
        q, k, v = (
            contract(entered, w_ref[c * width : (c + 1) * width, :], NT).astype(jnp.bfloat16)
            for c in range(3)
        )
        qkv_ref[0, i], qkv_ref[1, i], qkv_ref[2, i] = q, k, v
        attended = jnp.zeros((rows, width), jnp.float32)
        lse_all = jnp.zeros((rows, LANES), jnp.float32)
        for h in range(heads):
            scores = contract(keep_lanes(q, masks[h]), k, NT) * (HD ** (-0.5))
            scores = jnp.where(keys_live, scores, -1e30)
            top = jnp.max(scores, axis=-1, keepdims=True)
            lse = top + jnp.log(jnp.sum(jnp.exp(scores - top), axis=-1, keepdims=True))
            probs = jnp.exp(scores - lse).astype(jnp.bfloat16)
            attended = attended + contract(probs, keep_lanes(v, masks[h]), NN)
            lse_all = jnp.where(lane == h, lse, lse_all)
        lse_ref[i] = lse_all
        held_ref[i] = attended

    for i in range(images):
        flat_ref[pl.ds(i * seq_len, seq_len), :] = held_ref[i, 0:seq_len, :]
    arrive(3)
    att_ref[...] = flat_ref[...].astype(jnp.bfloat16)
    for j, part in enumerate(parts):
        rows_j = flat_ref[chunk_of(pos_ref, j, part.shape[0]), :].astype(jnp.bfloat16)
        part[...] = contract(rows_j, wo_ref[...], NN).astype(jnp.bfloat16)


def route_kernel(experts, pos_ref, *refs):
    *got, x_ref, param_ref, res_ref, routed_ref, prob_ref = refs
    residual = x_ref[...].astype(jnp.float32)
    for part in got:
        residual = residual + part[...].astype(jnp.float32)
    res_ref[...] = residual
    routed = normalize(residual, gain_row(param_ref, experts, 1))[2].astype(jnp.bfloat16)
    routed_ref[...] = routed
    prob_ref[...] = route_probs(routed, router_matrix(param_ref, experts), experts)


def route_probs(rows, router, experts):
    logits = contract(rows, router, NT)
    lane = lax.broadcasted_iota(jnp.int32, logits.shape, 1)
    logits = jnp.where(lane < experts, logits, -1e30)
    weight = jnp.exp(logits - jnp.max(logits, axis=-1, keepdims=True))
    return weight / jnp.sum(weight, axis=-1, keepdims=True)


def gelu_parts(x):
    square = jnp.exp(-0.5 * x * x)
    share = 0.5 * (1.0 + lax.erf(x * (0.5**0.5)))
    return x * share, share + x * square * (0.5 / math.pi) ** 0.5


def expert_halves(x, rg, w_in, w_out, hidden_ref, pre_ref):
    before = contract(x, w_in, NT)
    value, slope = gelu_parts(before)
    hidden = value.astype(jnp.bfloat16)
    hidden_ref[...] = hidden
    part = contract(hidden, w_out, NN)
    pre = (contract(rg, w_out, NT) * slope).astype(jnp.bfloat16)
    pre_ref[...] = pre
    return part, contract(pre, w_in, NN)


def first_expert_kernel(
    experts, pos_ref, x_ref, pay_ref, param_ref, w0_ref, xa_ref, yb_ref, hidden_ref, pre_ref, rg_ref,
    gate_ref, part_ref, back_ref,
):
    count, width = x_ref.shape
    prob = route_probs(x_ref[...], router_matrix(param_ref, experts), experts)
    mine = lax.broadcasted_iota(jnp.int32, prob.shape, 1) == lax.axis_index("expert")
    kept = pay_ref[:, width:].astype(jnp.float32)
    kept = jnp.sum(jnp.where(mine, kept, 0.0), axis=-1, keepdims=True)
    gate = jnp.sum(jnp.where(mine, prob, 0.0), axis=-1, keepdims=True) * kept
    gate_ref[:, :LANES] = jnp.broadcast_to(gate, (count, LANES))
    gate_ref[:, LANES:] = jnp.broadcast_to(kept, (count, LANES))
    rg_ref[...] = (gate * pay_ref[:, :width].astype(jnp.float32)).astype(jnp.bfloat16)
    w_in, w_out = (
        jnp.concatenate([w0_ref[s], xa_ref[s], yb_ref[s]], axis=0) for s in range(2)
    )
    part_ref[...], back_ref[...] = expert_halves(
        x_ref[...], rg_ref[...], w_in, w_out, hidden_ref, pre_ref
    )


def second_expert_kernel(
    pos_ref, x_ref, pay_ref, rg_ref, gate_ref, part_in_ref, back_in_ref, pair_y_ref, pair_x_ref,
    hidden_ref, pre_ref, gated_ref, back_ref,
):
    width = x_ref.shape[1]
    w_in, w_out = (
        jnp.concatenate([ref[r, s] for ref in (pair_y_ref, pair_x_ref) for r in range(2)], axis=0)
        for s in range(2)
    )
    part, back = expert_halves(x_ref[...], rg_ref[...], w_in, w_out, hidden_ref, pre_ref)
    back_ref[:, :width] = (back_in_ref[...] + back).astype(back_ref.dtype)
    part = part_in_ref[...] + part
    gated_ref[...] = (gate_ref[:, 0:1] * part).astype(jnp.bfloat16)
    inner = jnp.sum(part * pay_ref[:, :width].astype(jnp.float32), axis=-1, keepdims=True)
    inner = gate_ref[:, LANES:] * inner
    if back_ref.dtype == jnp.bfloat16:
        high, low = split_high_low(inner)
        upper = lax.broadcasted_iota(jnp.int32, inner.shape, 1) < LANES // 2
        inner = jnp.where(upper, high.astype(jnp.float32), low.astype(jnp.float32))
    back_ref[:, width:] = inner.astype(back_ref.dtype)


def first_expert_pass(position, rows, payload, params, weights, experts):
    count, width = rows.shape
    hidden = 2 * weights[0].shape[1]
    return kernel_call(
        functools.partial(first_expert_kernel, experts),
        "experts_first",
        position,
        [rows, payload, params, *weights],
        [
            like((count, hidden), jnp.bfloat16),
            like((count, hidden), jnp.bfloat16),
            like((count, width), jnp.bfloat16),
            like((count, 2 * LANES), jnp.float32),
            like((count, width), jnp.float32),
            like((count, width), jnp.float32),
        ],
        limit=18,
    )


def second_expert_pass(position, rows, payload, first, weights, back_dtype):
    count, width = rows.shape
    hidden = 4 * weights[0].shape[2]
    return kernel_call(
        second_expert_kernel,
        "experts_second",
        position,
        [rows, payload, *first[2:], *weights],
        [
            like((count, hidden), jnp.bfloat16),
            like((count, hidden), jnp.bfloat16),
            like((count, width), jnp.bfloat16),
            like((count, width + LANES), back_dtype),
        ],
        limit=18,
    )


def join_kernel(pos_ref, back_ref, other_ref, gated_ref, gated_other_ref, *outs):
    *backs, own_ref, pair_ref, far_ref = outs
    chunk, width = own_ref.shape
    for k, out in enumerate(backs):
        here = pl.ds(k * chunk, chunk)
        other = other_ref[here, :].astype(jnp.float32)
        out[0:chunk, :] = (back_ref[here, :width] + other[:, :width]).astype(jnp.bfloat16)
        inner = jnp.sum(other[:, width:], axis=-1, keepdims=True) * (2.0 / LANES)
        inner = back_ref[here, width:] + inner
        inner = jnp.concatenate(
            [inner, jnp.zeros((2 * LANES - chunk, LANES), jnp.float32)], axis=0
        ).T
        high, low = split_high_low(inner[0:SMALL, :])
        both = jnp.where(
            live_rows(high.shape, SMALL // 2), high.astype(jnp.float32), low.astype(jnp.float32)
        )
        out[chunk:, : 2 * LANES] = both.astype(jnp.bfloat16)
        out[chunk:, 2 * LANES :] = jnp.zeros((SMALL, width - 2 * LANES), jnp.bfloat16)
        gated = gated_ref[here, :].astype(jnp.float32) + gated_other_ref[here, :].astype(jnp.float32)
        gated = gated.astype(jnp.bfloat16)
        if k % 2:
            pair_ref[k // 2] = gated
        else:
            (own_ref, far_ref)[k // 2][...] = gated


def pair_sum_kernel(pos_ref, base_ref, own_ref, far_ref, got_ref, sum_ref, send_ref):
    total = base_ref[...] + own_ref[...].astype(jnp.float32) + got_ref[0].astype(jnp.float32)
    sum_ref[...] = total
    send_ref[...] = (far_ref[...].astype(jnp.float32) + got_ref[1].astype(jnp.float32)).astype(
        jnp.bfloat16
    )


def expert_grad_kernel(first, pos_ref, *refs):
    outs = refs[8:]
    part_rows = outs[0].shape[2]
    for j, out in enumerate(outs):
        start = 2 * (first + j) * part_rows
        columns = slice(start, start + 2 * part_rows)
        for s in range(2):
            left_a, right_a, left_b, right_b = refs[4 * s : 4 * s + 4]
            grad = contract(left_a[:, columns], right_a[...], TN)
            grad = grad + contract(left_b[:, columns], right_b[...], TN)
            grad = grad.astype(jnp.bfloat16)
            out[0, s] = grad[0:part_rows]
            out[1, s] = grad[part_rows:]


def expert_grads(position, a, b, rows_a, rows_b, first=0, count=2, flops=0):
    width, total = rows_a[0].shape[1], a[0].shape[1]
    return kernel_call(
        functools.partial(expert_grad_kernel, first),
        "expert_grads",
        position,
        [a[1], rows_a[0], b[1], rows_b[0], a[0], rows_a[1], b[0], rows_b[1]],
        [like((2, 2, total // 4, width), jnp.bfloat16)] * count,
        flops=flops,
        limit=10,
    )


def route_back_kernel(
    experts, token_rows, owners, pos_ref, *refs
):
    backs = refs[:owners]
    prob_ref, res_ref, pay_ref, param_ref = refs[owners : owners + 4]
    grad_ref, up_ref, small_ref = refs[owners + 4 :]
    chunk, width = res_ref.shape
    prob = prob_ref[...]
    lane = lax.broadcasted_iota(jnp.int32, prob.shape, 1)
    route_grad = jnp.zeros_like(prob)
    routed_grad = jnp.zeros((chunk, width), jnp.float32)
    for k, back in enumerate(backs):
        owner = lax.bitwise_xor(lax.axis_index("expert"), k)
        inner = back[chunk:, : 2 * LANES].astype(jnp.float32)
        inner = jnp.concatenate([inner] * (LANES // SMALL), axis=0).T[0:chunk]
        inner = jnp.sum(inner, axis=-1, keepdims=True) * (2.0 / LANES)
        route_grad = jnp.where(lane == owner, inner, route_grad)
        routed_grad = routed_grad + back[0:chunk, :].astype(jnp.float32)
    mean = jnp.sum(route_grad * prob, axis=-1, keepdims=True)
    logit_grad = (prob * (route_grad - mean)).astype(jnp.bfloat16)
    routed_grad = routed_grad + contract(
        logit_grad, router_matrix(param_ref, experts), NN
    )
    normed, inverse, mixed = normalize(res_ref[...], gain_row(param_ref, experts, 1))
    from_norm, gain_grad = normalize_back(
        routed_grad, normed, inverse, gain_row(param_ref, experts, 1)
    )
    total = pay_ref[0:chunk, :].astype(jnp.float32) + from_norm
    grad_ref[...] = total
    up_ref[...] = total.astype(jnp.bfloat16)
    live = live_rows(prob.shape, token_rows, lax.axis_index("tensor") * chunk)
    prob_sum = jnp.sum(jnp.where(live, prob, 0.0), axis=0, keepdims=True)
    grad_router = contract(logit_grad, mixed.astype(jnp.bfloat16), TN)
    small_ref[0:SMALL, :] = grad_router[0:SMALL]
    small_ref[experts : experts + 1, :] = gain_grad[None]
    small_ref[experts + 1 : experts + 2, :] = jnp.zeros((1, width), jnp.float32)
    small_ref[experts + 1 : experts + 2, :LANES] = prob_sum
    small_ref[experts + 2 : experts + 3, :] = param_ref[SMALL - 1 : SMALL, :]


def attention_back_kernel(
    heads, experts, owners, pos_ref, tok_ref, param_ref, w_ref, wo_ref, qkv_ref, lse_ref, att_ref,
    up_ref, small_ref, keep_ref, send_ref, *refs,
):
    *parts, hg_ref, flat_ref, big_ref, image_ref, held_ref, sum_ref, gain_ref = refs
    images, rows, width = qkv_ref.shape[1], qkv_ref.shape[2], heads * HD
    seq_len = tok_ref.shape[1]
    scale = HD ** (-0.5)
    padded, model = up_ref.shape
    chunk = padded // len(parts)
    masks = head_masks(rows, heads)
    keys_live = lax.broadcasted_iota(jnp.int32, (rows, rows), 1) < seq_len
    lane = lax.broadcasted_iota(jnp.int32, (rows, LANES), 1)
    up = up_ref[...]
    hg_ref[0:padded, :] = contract(up, wo_ref[...], NT)
    hg_ref[padded:, :] = jnp.zeros((hg_ref.shape[0] - padded, width), jnp.float32)
    big_ref[3 * width :, :] = contract(att_ref[...], up, TN)
    flat_ref[images * seq_len :, :] = jnp.zeros(
        (flat_ref.shape[0] - images * seq_len, model), jnp.float32
    )
    for i in range(images):
        held_ref[i] = hg_ref[pl.ds(i * seq_len, rows), :]
    big_ref[0 : 3 * width, :] = jnp.zeros((3 * width, model), jnp.float32)

    @pl.loop(0, images, unroll=True)
    def _(i):
        normed, _, mixed = normalize(
            image_rows(tok_ref, i, image_ref), gain_row(param_ref, experts, 0)
        )
        entered = mixed.astype(jnp.bfloat16)
        q, k, v = qkv_ref[0, i], qkv_ref[1, i], qkv_ref[2, i]
        heads_grad = held_ref[i]
        heads_grad = jnp.where(live_rows(heads_grad.shape, seq_len), heads_grad, 0.0)
        heads_grad = heads_grad.astype(jnp.bfloat16)
        dq = jnp.zeros((rows, width), jnp.float32)
        dk, dv = dq, dq
        for h in range(heads):
            q_h, k_h = keep_lanes(q, masks[h]), keep_lanes(k, masks[h])
            up_h = keep_lanes(heads_grad, masks[h])
            scores = contract(q_h, k, NT) * scale
            lse = jnp.sum(jnp.where(lane == h, lse_ref[i], 0.0), axis=-1, keepdims=True)
            probs = jnp.where(keys_live, jnp.exp(scores - lse), 0.0)
            prob_grad = contract(up_h, v, NT)
            total = jnp.sum(prob_grad * probs, axis=-1, keepdims=True)
            score_grad = (probs * (prob_grad - total)).astype(jnp.bfloat16)
            dv = dv + contract(probs.astype(jnp.bfloat16), up_h, TN)
            dq = dq + contract(score_grad, k_h, NN)
            dk = dk + contract(score_grad, q_h, TN)
        grads = [g.astype(jnp.bfloat16) for g in (dq * scale, dk * scale, dv)]
        part = jnp.zeros((rows, model), jnp.float32)
        for c in range(3):
            here = slice(c * width, (c + 1) * width)
            part = part + contract(grads[c], w_ref[here, :], NN)
            big_ref[here, :] += contract(grads[c], entered, TN)
        sum_ref[i] = part
        gain_ref[i] = jnp.broadcast_to(
            jnp.sum(part * normed, axis=0, keepdims=True), gain_ref.shape[1:]
        )

    gain_grad = jnp.zeros((1, model), jnp.float32)
    for i in range(images):
        flat_ref[pl.ds(i * seq_len, seq_len), :] = sum_ref[i, 0:seq_len, :]
        gain_grad = gain_grad + gain_ref[i, 0:1, :]
    small = pack_small(
        jnp.concatenate([small_ref[0 : SMALL - 1, :], gain_grad], axis=0), experts
    )
    for j, part in enumerate(parts):
        part[0:chunk, :] = flat_ref[chunk_of(pos_ref, j, chunk), :].astype(jnp.bfloat16)
        part[chunk:, :] = small
    me, core = lax.axis_index("expert"), lax.axis_index("dp")
    piece = keep_ref.shape[1]
    for k in range(owners):
        place = lax.bitwise_xor(me, k) * piece
        mine = pl.ds(pl.multiple_of(core * owners * piece + place, 8), piece)
        other = pl.ds(pl.multiple_of((1 - core) * owners * piece + place, 8), piece)
        keep_ref[k] = big_ref[mine, :]
        send_ref[k] = big_ref[other, :].astype(jnp.bfloat16)


def norm_back_kernel(experts, tensors, pos_ref, *refs):
    got = refs[:tensors]
    x_ref, res_ref, param_ref, own_ref, *parts, grad_ref, out_ref, small_ref = refs[tensors:]
    chunk, width = x_ref.shape
    upstream = jnp.zeros((chunk, width), jnp.float32)
    for j, part in enumerate(got):
        upstream = upstream + part[0:chunk, :].astype(jnp.float32)
        small_ref[lax.bitwise_xor(lax.axis_index("tensor"), j)] = unpack_small(
            part[chunk:, :], experts
        )
    small = small_ref[0]
    for j in range(1, tensors):
        small = small + small_ref[j]
    gain = gain_row(param_ref, experts, 0)
    normed, inverse, _ = normalize(x_ref[...].astype(jnp.float32), gain)
    from_norm = normalize_back(upstream, normed, inverse, gain)[0]
    grad_ref[...] = (res_ref[...] + from_norm).astype(jnp.bfloat16)
    piece = own_ref.shape[0]
    total = own_ref[...]
    for part in parts:
        total = total + part[...].astype(jnp.float32)
    out_ref[0:piece, :] = total.astype(jnp.bfloat16)
    out_ref[piece:, :] = pack_small(small, experts)


def second_step_kernel(pos_ref, near_ref, from_y, from_x, x_ref, y_ref):
    for target, row, other in ((x_ref, 0, from_y), (y_ref, 1, from_x)):
        total = near_ref[row].astype(jnp.float32) + other[1].astype(jnp.float32)
        target[...] = total.astype(jnp.bfloat16)


def weight_sum_kernel(pos_ref, own_ref, from_y, from_x, last_x, last_y, out_ref):
    part_rows = last_x.shape[1]
    for row, other, last in ((0, from_y, last_x), (1, from_x, last_y)):
        total = own_ref[row].astype(jnp.float32) + other[0].astype(jnp.float32)
        total = total + last[...].astype(jnp.float32)
        out_ref[:, row * part_rows : (row + 1) * part_rows, :] = total.astype(jnp.bfloat16)


def add_core_kernel(pos_ref, keep_ref, other_ref, own_ref, *outs):
    total = keep_ref[...] + other_ref[...].astype(jnp.float32)
    own_ref[...] = total[0]
    for k, out in enumerate(outs):
        out[...] = total[k + 1].astype(jnp.bfloat16)


def spread_kernel(owners, experts, token_total, pos_ref, *refs):
    sides = refs[:2]
    qkv_ref, wo_ref, router_ref, one_ref, two_ref, loss_ref, big_ref, parts_ref = refs[2:]
    span = sides[0].shape[0] // owners
    piece = span - SMALL
    core, me = lax.axis_index("dp"), lax.axis_index("expert")
    for c in range(2):
        side = core if c == 0 else 1 - core
        for k in range(owners):
            block = sides[c].at[k * span : (k + 1) * span]
            place = side * owners + lax.bitwise_xor(me, k)
            here = pl.ds(pl.multiple_of(place * piece, 8), piece)
            big_ref[here, :] = block[0:piece, :].astype(jnp.float32)
            parts_ref[place] = unpack_small(block[piece:, :], experts)
    rows = qkv_ref.shape[0]
    qkv_ref[...] = big_ref[0:rows, :]
    wo_ref[...] = big_ref[rows:, :]
    small = parts_ref[0]
    for p in range(1, 2 * owners):
        small = small + parts_ref[p]
    router_ref[...] = small[0:experts, :]
    one_ref[...] = small[SMALL - 1 : SMALL, :].reshape(small.shape[1])
    two_ref[...] = small[experts : experts + 1, :].reshape(small.shape[1])
    product = small[experts + 1 : experts + 2, :LANES] * small[experts + 2 : experts + 3, :LANES]
    lane = lax.broadcasted_iota(jnp.int32, product.shape, 1)
    product = jnp.where(lane < experts, product, 0.0)
    loss = jnp.sum(product, axis=-1, keepdims=True)
    loss_ref[...] = jnp.broadcast_to(
        loss * (experts / (2.0 * token_total * token_total)), loss_ref.shape
    )


def images_kernel(pos_ref, *refs):
    *chunks, out_ref, flat_ref = refs
    images, seq_len, _ = out_ref.shape
    if len(chunks) == 1:
        flat_ref[...] = chunks[0][...].astype(jnp.float32)
    else:
        for j, part in enumerate(chunks):
            flat_ref[chunk_of(pos_ref, j, part.shape[0]), :] = part[...].astype(jnp.float32)
    for i in range(images):
        out_ref[i] = flat_ref[pl.ds(i * seq_len, seq_len), :].astype(out_ref.dtype)


def weight_out_kernel(pos_ref, mine_ref, other_ref, in_ref, out_ref):
    first_is_mine = lax.axis_index("dp") == 0
    half = mine_ref.shape[1]
    for c in range(2):
        here = slice(c * half, (c + 1) * half)
        take = first_is_mine if c == 0 else jnp.logical_not(first_is_mine)
        grad_in = jnp.where(take, mine_ref[0], other_ref[0]).astype(jnp.float32)
        in_ref[0, :, here] = grad_in.T
        out_ref[0, here, :] = jnp.where(take, mine_ref[1], other_ref[1]).astype(jnp.float32)


def swap_core(value):
    return lax.ppermute(value, "dp", [(0, 1), (1, 0)])


def hop(value, bit):
    size = lax.axis_size("expert")
    return lax.ppermute(value, "expert", [(i, i ^ bit) for i in range(size)])


def cross(value, bit):
    size = lax.axis_size("tensor")
    return lax.ppermute(value, "tensor", [(i, i ^ bit) for i in range(size)])


def after(value, *others):
    return lax.optimization_barrier((value, *others))[0]


def dense_body(
    tokens,
    cotangent,
    expert_ids,
    slot_rank,
    qkv_weight,
    out_weight,
    router_weight,
    expert_in,
    expert_out,
    gain_attention,
    gain_experts,
):
    f32, b16 = jnp.float32, jnp.bfloat16
    images, seq_len, width = tokens.shape
    token_rows = images * seq_len
    local = qkv_weight.shape[2]
    heads = local // HD
    experts = router_weight.shape[1]
    owners = lax.axis_size("expert")
    tensors = lax.axis_size("tensor")
    cores = lax.axis_size("dp")
    chunk = round_up(-(-token_rows // tensors), 8)
    padded = chunk * tensors
    rows = round_up(seq_len, 16)
    flat_rows = padded + 32
    half = expert_in.shape[2] // cores
    quarter = half // 2
    position = jnp.zeros((1,), jnp.int32)
    weight_rows = qkv_weight.transpose(0, 2, 1).reshape(3 * local, width)

    x_chunk, payload, params, mine, first, second = kernel_call(
        functools.partial(chunk_kernel, tensors),
        "chunk",
        position,
        [
            tokens,
            cotangent,
            expert_ids.transpose(0, 2, 1),
            slot_rank.transpose(0, 2, 1),
            router_weight.T,
            gain_attention,
            gain_experts,
            expert_in,
            expert_out,
        ],
        [
            like((chunk, width), b16),
            like((chunk + SMALL, width), b16),
            like((SMALL, width), f32),
            like((2, half, width), b16),
            like((2, quarter, width), b16),
            like((2, quarter, width), b16),
        ],
        [
            pltpu.VMEM((flat_rows, width), f32),
            pltpu.VMEM((padded + 2 * LANES, LANES), f32),
        ],
        limit=56,
        loads=tuple(range(9)),
    )
    payload_two = hop(payload, 2)
    first_x = cross(first, 1)
    second_y = cross(second, 2)

    qkv, lse, attended, *parts = kernel_call(
        functools.partial(attention_kernel, heads, experts),
        "attention",
        after(position, mine),
        [tokens, params, weight_rows, out_weight],
        [
            like((3, images, rows, local), b16),
            like((images, rows, LANES), f32),
            like((padded, local), b16),
        ]
        + [like((chunk, width), b16)] * tensors,
        [
            pltpu.VMEM((padded, local), f32),
            pltpu.VMEM((rows, width), f32),
            pltpu.VMEM((images, rows, local), f32),
        ],
        flops=40_000_000_000,
        limit=20,
        loads=(0, 1, 2, 3),
    )
    arrived = [parts[0]] + [cross(parts[j], j) for j in range(1, tensors)]
    pair_first, pair_second = stack_pairs(
        after(position, parts[0]), (first, first_x), (second, second_y)
    )
    (payload_near,) = stack_pairs(after(position, pair_first), (payload, payload_two))
    payload_far = hop(payload_near, 1)

    residual, routed, prob = kernel_call(
        functools.partial(route_kernel, experts),
        "route",
        after(position, pair_first, payload_near),
        [*arrived, x_chunk, params],
        [like((chunk, width), f32), like((chunk, width), b16), like((chunk, LANES), f32)],
        limit=8,
    )
    blocks = [routed] + [hop(routed, k) for k in range(1, owners)]
    pair_first, pair_second = after((pair_first, pair_second), routed)
    pair_y = cross(pair_first, 2)
    pair_x = cross(pair_second, 1)
    payload_mine = kernel_call(
        lay_payload_kernel,
        "lay_payload",
        after(position, routed),
        [payload_near, payload_far],
        [like((owners * chunk, width + LANES), b16)],
        limit=6,
    )[0]
    payload_other = swap_core(payload_mine)
    rows_mine = lay_rows(position, "lay_rows", blocks)
    rows_other = swap_core(rows_mine)

    near_weights, far_weights = (mine, first_x, second_y), (pair_y, pair_x)
    first_a = first_expert_pass(position, rows_mine, payload_mine, params, near_weights, experts)
    first_b = first_expert_pass(
        after(position, first_a[2]), rows_other, payload_other, params, near_weights, experts
    )
    second_b = second_expert_pass(
        after(position, first_b[2]), rows_other, payload_other, first_b, far_weights, b16
    )
    back_other, gated_other = swap_core(second_b[3]), swap_core(second_b[2])
    second_a = second_expert_pass(
        after(position, second_b[0]), rows_mine, payload_mine, first_a, far_weights, f32
    )
    *joined, gated_own, gated_pair, gated_far = kernel_call(
        join_kernel,
        "join",
        position,
        [second_a[3], back_other, second_a[2], gated_other],
        [like((chunk + SMALL, width), b16)] * owners
        + [like((chunk, width), b16), like((2, chunk, width), b16), like((chunk, width), b16)],
        limit=8,
    )
    backs = [joined[0]] + [hop(joined[k], k) for k in range(1, owners)]

    grad_pos = after(position, joined)
    far_rows = (rows_mine, first_a[2]), (rows_other, first_b[2])
    (far_y,) = expert_grads(grad_pos, second_a, second_b, *far_rows, first=0, count=1)
    (far_x,) = expert_grads(
        after(grad_pos, far_y), second_a, second_b, *far_rows, first=1, count=1, flops=0
    )
    from_y, from_x = cross(far_y, 2), cross(far_x, 1)
    residual_grad, attn_grad, small = kernel_call(
        functools.partial(route_back_kernel, experts, token_rows, owners),
        "route_back",
        position,
        [*backs, prob, residual, payload, params],
        [like((chunk, width), f32), like((chunk, width), b16), like((SMALL, width), f32)],
        flops=40_000_000_000,
        limit=8,
    )
    own_grad, near_grad = expert_grads(
        after(position, attn_grad), first_a, first_b, (rows_mine, first_a[2]), (rows_other, first_b[2]),
    )
    gated_near = hop(after(gated_pair, backs[1]), 1)
    block_sum, gated_far = kernel_call(
        pair_sum_kernel,
        "pair_sum",
        after(position, own_grad),
        [residual, gated_own, gated_far, gated_near],
        [like((chunk, width), f32), like((chunk, width), b16)],
        limit=4,
    )
    attn_grad, gated_far = lax.optimization_barrier((attn_grad, gated_far))
    gated_last = hop(gated_far, 2)
    attn_grad = lax.all_gather(attn_grad, "tensor", axis=0, tiled=True)
    piece = 4 * local // (2 * owners)
    keep, send, *parts = kernel_call(
        functools.partial(attention_back_kernel, heads, experts, owners),
        "attention_back",
        after(position, from_y, from_x, gated_last),
        [tokens, params, weight_rows, out_weight, qkv, lse, attended, attn_grad, small],
        [
            like((owners, piece, width), f32),
            like((owners, piece, width), b16),
        ]
        + [like((chunk + SMALL, width), b16)] * tensors,
        [
            pltpu.VMEM((flat_rows, local), f32),
            pltpu.VMEM((flat_rows, width), f32),
            pltpu.VMEM((4 * local, width), f32),
            pltpu.VMEM((rows, width), f32),
            pltpu.VMEM((images, rows, local), f32),
            pltpu.VMEM((images, rows, width), f32),
            pltpu.VMEM((images, SMALL, width), f32),
        ],
        limit=20,
        flops=6_000_000_000,
    )
    own_piece, *pieces = kernel_call(
        add_core_kernel,
        "add_core",
        position,
        [keep, swap_core(send)],
        [like((piece, width), f32)] + [like((piece, width), b16)] * (owners - 1),
        limit=8,
    )
    reduced = [hop(p, k + 1) for k, p in enumerate(pieces)]
    got = [parts[0]] + [cross(parts[j], j) for j in range(1, tensors)]

    up_x, up_y = kernel_call(
        second_step_kernel,
        "second_step",
        after(position, own_piece),
        [near_grad, from_y, from_x],
        [like((2, quarter, width), b16)] * 2,
        limit=8,
    )
    up_x, up_y = after((up_x, up_y), got[1:])
    last_x, last_y = cross(up_x, 1), cross(up_y, 2)

    grad_chunk, summed = kernel_call(
        functools.partial(norm_back_kernel, experts, tensors),
        "norm_back",
        position,
        [*got, x_chunk, residual_grad, params, own_piece, *reduced],
        [like((chunk, width), b16), like((piece + SMALL, width), b16)],
        [pltpu.VMEM((tensors, SMALL, width), f32)],
        flops=40_000_000_000,
        limit=8,
    )
    around = [summed] + [hop(summed, k) for k in range(1, owners)]
    grad_rows = lax.all_gather(grad_chunk, "tensor", axis=0, tiled=True)
    combined = (block_sum + gated_last.astype(f32)).astype(b16)
    combined = after(combined, grad_rows)
    block_parts = [combined] + [cross(combined, j) for j in range(1, tensors)]

    grad_tokens = kernel_call(
        images_kernel,
        "grad_tokens",
        position,
        [grad_rows],
        [like(tokens.shape, f32)],
        [pltpu.VMEM((padded, width), f32)],
        limit=8,
    )[0]
    grad_half = kernel_call(
        weight_sum_kernel,
        "weight_sum",
        after(position, grad_rows, around),
        [own_grad, from_y, from_x, last_x, last_y],
        [like((2, half, width), b16)],
        limit=8,
    )[0]
    grad_expert_in, grad_expert_out = kernel_call(
        weight_out_kernel,
        "weight_out",
        position,
        [grad_half, swap_core(grad_half)],
        [like((1, width, 2 * half), f32), like((1, 2 * half, width), f32)],
        limit=10,
    )
    around_rows = lay_rows(position, "lay_grads", around)
    token_total = token_rows * cores * owners
    grad_qkv, grad_out, grad_router, gain_one, gain_two, loss = kernel_call(
        functools.partial(spread_kernel, owners, experts, token_total),
        "spread",
        position,
        [around_rows, swap_core(around_rows)],
        [
            like((3 * local, width), f32),
            like((local, width), f32),
            like((experts, width), f32),
            like((width,), f32),
            like((width,), f32),
            like((1, LANES), f32),
        ],
        [
            pltpu.VMEM((4 * local, width), f32),
            pltpu.VMEM((2 * owners, SMALL, width), f32),
        ],
        limit=8,
    )
    block_out = kernel_call(
        images_kernel,
        "block_out",
        after(position, grad_tokens, grad_expert_in, grad_qkv),
        block_parts,
        [like(tokens.shape, b16)],
        [pltpu.VMEM((padded, width), f32)],
        limit=8,
    )[0]
    return (
        block_out,
        grad_tokens,
        grad_qkv.reshape(3, local, width).transpose(0, 2, 1),
        grad_out,
        grad_router.T,
        grad_expert_in,
        grad_expert_out,
        gain_one,
        gain_two,
        loss[0, 0],
    )


def solution(mesh):
    placed = (
        P(("dp", "expert"), None, None),
        P(("dp", "expert"), None, None),
        P(("dp", "expert"), None, None),
        P(("dp", "expert"), None, None),
        P(None, None, "tensor"),
        P("tensor", None),
        P(),
        P("expert", None, "tensor"),
        P("expert", "tensor", None),
        P(),
        P(),
    )
    shape = mesh.shape
    dense = shape["dp"] == 2 and shape["expert"] == 4 and shape["tensor"] == 4
    return jax.shard_map(
        dense_body if dense else body,
        mesh=mesh,
        in_specs=placed,
        out_specs=(
            P(("dp", "expert"), None, None),
            P(("dp", "expert"), None, None),
            P(None, None, "tensor"),
            P("tensor", None),
            P(),
            P("expert", None, "tensor"),
            P("expert", "tensor", None),
            P(),
            P(),
            P(),
        ),
        check_vma=False,
    )
```

```python
import functools
import math

import jax
import jax.numpy as jnp
from jax import lax
from jax.experimental import pallas as pl
from jax.experimental.pallas import tpu as pltpu
from jax.sharding import PartitionSpec as P

HD = 64


epsilon = 1e-06


def normalize(values, gain_row):
    center = values - jnp.mean(values, axis=-1, keepdims=True)
    inverse = lax.rsqrt(jnp.mean(center * center, axis=-1, keepdims=True) + epsilon)
    normed = center * inverse
    return (normed, inverse, normed * gain_row)


def normalize_back(upstream, normed, inverse, gain_row):
    scaled = upstream * gain_row
    result = inverse * (
        scaled
        - jnp.mean(scaled, axis=-1, keepdims=True)
        - normed * jnp.mean(scaled * normed, axis=-1, keepdims=True)
    )
    return (result, jnp.sum(upstream * normed, axis=0))


def exact_gelu(values):
    return jax.nn.gelu(values, approximate=False)


def body(
    tokens,
    cotangent,
    expert_ids,
    slot_rank,
    qkv_weight,
    out_weight,
    router_weight,
    expert_in,
    expert_out,
    gain_attention,
    gain_experts,
):
    images, seq_len, model_width = tokens.shape
    token_rows = images * seq_len
    local_width = qkv_weight.shape[2]
    local_heads = local_width // HD
    slice_width = model_width // lax.axis_size("tensor")
    experts = router_weight.shape[1]
    capacity = 5 * token_rows // (2 * experts)
    owners = lax.axis_size("expert")
    per_owner = experts // owners
    slot_total = experts * capacity
    score_scale = HD ** (-0.5)
    inputs = tokens.reshape(token_rows, model_width).astype(jnp.float32)
    normed_one, inverse_one, mixed_one = normalize(inputs, gain_attention)
    entered = mixed_one.astype(jnp.bfloat16)
    project = jnp.einsum(
        "td,cdf->ctf", entered, qkv_weight, preferred_element_type=jnp.float32
    ).astype(jnp.bfloat16)
    projected_heads = project.reshape(3, images, seq_len, local_heads, HD)
    queries, key_rows, value_rows = (projected_heads[0], projected_heads[1], projected_heads[2])
    scores = (
        jnp.einsum("ishe,ithe->ihst", queries, key_rows, preferred_element_type=jnp.float32)
        * score_scale
    )
    log_total = jax.nn.logsumexp(scores, axis=-1, keepdims=True)
    attn_probs = jnp.exp(scores - log_total).astype(jnp.bfloat16)
    attended = jnp.einsum(
        "ihst,ithe->ishe", attn_probs, value_rows, preferred_element_type=jnp.float32
    )
    attended = attended.astype(jnp.bfloat16).reshape(token_rows, local_width)
    attn_part = jnp.dot(attended, out_weight, preferred_element_type=jnp.float32)
    residual = inputs + lax.psum(attn_part, "tensor")
    normed_two, inverse_two, mixed_two = normalize(residual, gain_experts)
    routed = mixed_two.astype(jnp.bfloat16)
    route_prob = jax.nn.softmax(
        jnp.dot(routed, router_weight, preferred_element_type=jnp.float32), axis=-1
    )
    chosen = expert_ids.reshape(token_rows, 2)
    ranked = slot_rank.reshape(token_rows, 2)
    kept_mask = (ranked >= 0).astype(jnp.float32)
    position = jnp.where(ranked >= 0, chosen * capacity + ranked, slot_total).reshape(-1)
    send_rows = (
        jnp.zeros((slot_total, model_width), jnp.bfloat16)
        .at[position]
        .set(jnp.repeat(routed, 2, axis=0), mode="drop")
        .reshape(experts, capacity, model_width)
    )
    fragment = lax.all_to_all(send_rows, "expert", split_axis=0, concat_axis=0, tiled=True)
    grouped = fragment.reshape(owners, per_owner, fragment.shape[1], model_width)
    before = jnp.einsum("sjcd,jdf->sjcf", grouped, expert_in, preferred_element_type=jnp.float32)
    hidden = exact_gelu(before).astype(jnp.bfloat16)
    expert_part = jnp.einsum(
        "sjcf,jfd->sjcd", hidden, expert_out, preferred_element_type=jnp.float32
    )
    produced = lax.psum_scatter(expert_part, "tensor", scatter_dimension=3, tiled=True).astype(
        jnp.bfloat16
    )
    returned = lax.all_to_all(
        produced.reshape(experts, capacity, slice_width),
        "expert",
        split_axis=0,
        concat_axis=0,
        tiled=True,
    )
    returned = lax.all_gather(returned, "tensor", axis=2, tiled=True).reshape(
        slot_total, model_width
    )
    safe_index = jnp.minimum(position, slot_total - 1)
    picked = returned[safe_index].reshape(token_rows, 2, model_width).astype(jnp.float32)
    gate_values = jnp.take_along_axis(route_prob, chosen, axis=1) * kept_mask
    output = residual + jnp.sum(gate_values[:, :, None] * picked, axis=1)
    block_out = output.astype(jnp.bfloat16).reshape(images, seq_len, model_width)
    upstream = cotangent.reshape(token_rows, model_width).astype(jnp.float32)
    gate_grad = jnp.sum(upstream[:, None, :] * picked, axis=-1) * kept_mask
    member = (chosen[:, :, None] == jnp.arange(experts)[None, None, :]).astype(jnp.float32)
    route_grad = jnp.sum(member * gate_grad[:, :, None], axis=1)
    logit_grad = (
        route_prob * (route_grad - jnp.sum(route_grad * route_prob, axis=-1, keepdims=True))
    ).astype(jnp.bfloat16)
    row_grad = (
        (gate_values[:, :, None] * upstream[:, None, :])
        .astype(jnp.bfloat16)
        .reshape(2 * token_rows, model_width)
    )
    grad_send = (
        jnp.zeros((slot_total, model_width), jnp.bfloat16)
        .at[position]
        .set(row_grad, mode="drop")
        .reshape(experts, capacity, model_width)
    )
    grad_arrived = lax.all_to_all(grad_send, "expert", split_axis=0, concat_axis=0, tiled=True)
    grad_arrived = grad_arrived.reshape(owners, per_owner, capacity, model_width)
    hidden_grad = jnp.einsum(
        "sjcd,jfd->sjcf", grad_arrived, expert_out, preferred_element_type=jnp.float32
    )
    grad_expert_out = jnp.einsum(
        "sjcf,sjcd->jfd", hidden, grad_arrived, preferred_element_type=jnp.float32
    )
    pre_grad = jax.vjp(exact_gelu, before)[1](hidden_grad)[0].astype(jnp.bfloat16)
    grad_expert_in = jnp.einsum(
        "sjcd,sjcf->jdf", grouped, pre_grad, preferred_element_type=jnp.float32
    )
    buffer_part = jnp.einsum(
        "sjcf,jdf->sjcd", pre_grad, expert_in, preferred_element_type=jnp.float32
    )
    buffer_share = lax.psum_scatter(buffer_part, "tensor", scatter_dimension=3, tiled=True).astype(
        jnp.bfloat16
    )
    buffer_back = lax.all_to_all(
        buffer_share.reshape(experts, capacity, slice_width),
        "expert",
        split_axis=0,
        concat_axis=0,
        tiled=True,
    )
    buffer_grad = lax.all_gather(buffer_back, "tensor", axis=2, tiled=True).reshape(
        slot_total, model_width
    )
    routed_grad = jnp.sum(
        buffer_grad[safe_index].reshape(token_rows, 2, model_width).astype(jnp.float32)
        * kept_mask[:, :, None],
        axis=1,
    )
    routed_grad = routed_grad + jnp.dot(
        logit_grad, router_weight.T, preferred_element_type=jnp.float32
    )
    grad_router = jnp.einsum("td,te->de", routed, logit_grad, preferred_element_type=jnp.float32)
    from_norm_two, grad_gain_experts = normalize_back(
        routed_grad, normed_two, inverse_two, gain_experts
    )
    residual_grad = upstream + from_norm_two
    attn_grad = residual_grad.astype(jnp.bfloat16)
    grad_out = jnp.einsum("tf,td->fd", attended, attn_grad, preferred_element_type=jnp.float32)
    heads_grad = jnp.dot(attn_grad, out_weight.T, preferred_element_type=jnp.float32).astype(
        jnp.bfloat16
    )
    heads_grad = heads_grad.reshape(images, seq_len, local_heads, HD)
    again = (
        jnp.einsum("ishe,ithe->ihst", queries, key_rows, preferred_element_type=jnp.float32)
        * score_scale
    )
    probs_full = jnp.exp(again - log_total)
    prob_grad = jnp.einsum(
        "ishe,ithe->ihst", heads_grad, value_rows, preferred_element_type=jnp.float32
    )
    value_grad = jnp.einsum(
        "ihst,ishe->ithe",
        probs_full.astype(jnp.bfloat16),
        heads_grad,
        preferred_element_type=jnp.float32,
    )
    score_grad = (
        probs_full * (prob_grad - jnp.sum(prob_grad * probs_full, axis=-1, keepdims=True))
    ).astype(jnp.bfloat16)
    query_grad = (
        jnp.einsum("ihst,ithe->ishe", score_grad, key_rows, preferred_element_type=jnp.float32)
        * score_scale
    )
    key_grad = (
        jnp.einsum("ihst,ishe->ithe", score_grad, queries, preferred_element_type=jnp.float32)
        * score_scale
    )
    project_grad = (
        jnp.stack([query_grad, key_grad, value_grad])
        .astype(jnp.bfloat16)
        .reshape(3, token_rows, local_width)
    )
    grad_qkv = jnp.einsum("td,ctf->cdf", entered, project_grad, preferred_element_type=jnp.float32)
    entered_part = jnp.einsum(
        "ctf,cdf->td", project_grad, qkv_weight, preferred_element_type=jnp.float32
    )
    entered_grad = lax.psum(entered_part.astype(jnp.bfloat16), "tensor").astype(jnp.float32)
    from_norm_one, grad_gain_attention = normalize_back(
        entered_grad, normed_one, inverse_one, gain_attention
    )
    grad_tokens = (residual_grad + from_norm_one).reshape(images, seq_len, model_width)
    counts = jnp.sum(member, axis=(0, 1))
    prob_sum = jnp.sum(route_prob, axis=0)
    grad_qkv, grad_out, grad_router, grad_gain_attention, grad_gain_experts, counts, prob_sum = (
        lax.psum(
            (
                grad_qkv,
                grad_out,
                grad_router,
                grad_gain_attention,
                grad_gain_experts,
                counts,
                prob_sum,
            ),
            ("dp", "expert"),
        )
    )
    grad_expert_in, grad_expert_out = (
        lax.psum(grad_expert_in.astype(jnp.bfloat16), "dp").astype(jnp.float32),
        lax.psum(grad_expert_out.astype(jnp.bfloat16), "dp").astype(jnp.float32),
    )
    token_total = token_rows * lax.axis_size("dp") * lax.axis_size("expert")
    balance_loss = experts * jnp.sum(counts / (2.0 * token_total) * prob_sum / token_total)
    return (
        block_out,
        grad_tokens,
        grad_qkv,
        grad_out,
        grad_router,
        grad_expert_in,
        grad_expert_out,
        grad_gain_attention,
        grad_gain_experts,
        balance_loss,
    )


NN = ((1,), (0,))
NT = ((1,), (1,))
TN = ((0,), (0,))
LANES = 128
SMALL = 8


def round_up(value, step):
    return -(-value // step) * step


def contract(a, b, dims):
    return lax.dot_general(a, b, (dims, ((), ())), preferred_element_type=jnp.float32)


def load_then(kernel, loads, count, *refs):
    pos_ref, *refs = refs
    *refs, sem = refs
    buffers = refs[len(refs) - len(loads) :]
    refs = refs[: len(refs) - len(loads)]
    copies = [
        pltpu.make_async_copy(refs[index], buffer, sem.at[i])
        for i, (index, buffer) in enumerate(zip(loads, buffers))
    ]
    for copy in copies:
        copy.start()
    for index, buffer in zip(loads, buffers):
        refs[index] = buffer

    def arrive(*indices):
        for index in indices:
            copies[loads.index(index)].wait()

    kernel(arrive, pos_ref, *refs)


def kernel_call(kernel, name, position, args, outs, scratch=(), flops=0, limit=24, loads=()):
    if loads:
        kernel = functools.partial(load_then, kernel, loads, len(args))
        scratch = [
            *scratch,
            *(pltpu.VMEM(args[i].shape, args[i].dtype) for i in loads),
            pltpu.SemaphoreType.DMA((len(loads),)),
        ]
    places = [pltpu.HBM if i in loads else pltpu.VMEM for i in range(len(args))]
    return pl.pallas_call(
        kernel,
        in_specs=[pl.BlockSpec(memory_space=pltpu.SMEM)]
        + [pl.BlockSpec(memory_space=place) for place in places],
        out_specs=[pl.BlockSpec(memory_space=pltpu.VMEM)] * len(outs),
        out_shape=list(outs),
        scratch_shapes=list(scratch),
        compiler_params=pltpu.CompilerParams(vmem_limit_bytes=limit << 20),
        cost_estimate=pl.CostEstimate(flops=flops, bytes_accessed=0, transcendentals=0),
        name=name,
    )(position, *args)


def like(shape, dtype):
    return jax.ShapeDtypeStruct(shape, dtype)


def live_rows(shape, limit, offset=0):
    return lax.broadcasted_iota(jnp.int32, shape, 0) + offset < limit


def chunk_of(pos_ref, j, size):
    return pl.ds(pl.multiple_of(lax.bitwise_xor(lax.axis_index("tensor"), j) * size, 8), size)


def head_masks(rows, heads):
    lane = lax.broadcasted_iota(jnp.int32, (rows, heads * HD), 1)
    return [(lane >= h * HD) & (lane < (h + 1) * HD) for h in range(heads)]


def keep_lanes(value, mask):
    return jnp.where(mask, value, jnp.zeros_like(value))


def split_high_low(value):
    high = value.astype(jnp.bfloat16)
    return high, (value - high.astype(jnp.float32)).astype(jnp.bfloat16)


def image_rows(ref, i, scratch_ref):
    seq_len = ref.shape[1]
    scratch_ref[seq_len:, :] = jnp.zeros((scratch_ref.shape[0] - seq_len, ref.shape[2]), jnp.float32)
    scratch_ref[0:seq_len, :] = ref[i].astype(jnp.float32)
    return scratch_ref[...]


def router_matrix(param_ref, experts):
    rows = param_ref[0:SMALL, :]
    rows = jnp.where(live_rows(rows.shape, experts), rows, 0.0).astype(jnp.bfloat16)
    zeros = jnp.zeros((LANES - SMALL, rows.shape[1]), jnp.bfloat16)
    return jnp.concatenate([rows, zeros], axis=0)


def chunk_kernel(
    tensors, arrive, pos_ref, tok_ref, cot_ref, ids_ref, rank_ref, router_ref, one_ref, two_ref, in_ref, out_ref,
    x_ref, pay_ref, param_ref, first_ref, second_ref, flat_ref, kept_ref,
):
    images, seq_len, width = tok_ref.shape
    chunk, experts = x_ref.shape[0], router_ref.shape[0]
    start = pl.multiple_of(lax.axis_index("tensor") * chunk, 8)
    for index, source, target in ((0, tok_ref, x_ref), (1, cot_ref, pay_ref)):
        arrive(index)
        flat_ref[images * seq_len :, :] = jnp.zeros(
            (flat_ref.shape[0] - images * seq_len, width), jnp.float32
        )
        for i in range(images):
            flat_ref[pl.ds(i * seq_len, seq_len), :] = source[i].astype(jnp.float32)
        target[0:chunk, :] = flat_ref[pl.ds(start, chunk), :].astype(jnp.bfloat16)
    arrive(2, 3, 4, 5, 6)
    kept_ref[...] = jnp.zeros_like(kept_ref)
    counts = jnp.zeros((1, LANES), jnp.float32)
    for i in range(images):
        rows, all_rows = [], []
        for e in range(experts):
            named = (ids_ref[i] == e).astype(jnp.float32)
            kept = jnp.where(rank_ref[i] >= 0, named, 0.0)
            rows.append(jnp.sum(kept, axis=0, keepdims=True))
            all_rows.append(jnp.sum(named, axis=0, keepdims=True))
        for group, is_kept in ((rows, True), (all_rows, False)):
            table = jnp.concatenate(group, axis=0)
            table = jnp.concatenate(
                [table, jnp.zeros((LANES - experts, seq_len), jnp.float32)], axis=0
            )
            table = jnp.concatenate(
                [table, jnp.zeros((LANES, 2 * LANES - seq_len), jnp.float32)], axis=1
            ).T
            if is_kept:
                kept_ref[pl.ds(i * seq_len, 2 * LANES), :] = table
            else:
                counts = counts + jnp.sum(table, axis=0, keepdims=True)
    kept = jnp.concatenate(
        [kept_ref[pl.ds(start, chunk), :], jnp.zeros((2 * LANES - chunk, LANES), jnp.float32)], axis=0
    ).T
    pay_ref[chunk:, : 2 * LANES] = kept[0:SMALL].astype(jnp.bfloat16)
    pay_ref[chunk:, 2 * LANES :] = jnp.zeros((SMALL, width - 2 * LANES), jnp.bfloat16)
    param_ref[...] = jnp.zeros_like(param_ref)
    param_ref[0:experts, :] = router_ref[...].astype(jnp.float32)
    param_ref[experts : experts + 1, :] = one_ref[...].reshape(1, width)
    param_ref[experts + 1 : experts + 2, :] = two_ref[...].reshape(1, width)
    param_ref[SMALL - 1 : SMALL, :LANES] = counts * (1.0 / tensors)
    arrive(7, 8)
    half = 2 * first_ref.shape[1]
    core = pl.multiple_of(lax.axis_index("dp") * half, LANES)
    for s, part in ((0, in_ref[0, :, pl.ds(core, half)].T), (1, out_ref[0, pl.ds(core, half), :])):
        first_ref[s] = part[0 : half // 2]
        second_ref[s] = part[half // 2 :]


def stack_kernel(pos_ref, *refs):
    count = len(refs) // 3
    for i, target in enumerate(refs[2 * count :]):
        target[0] = refs[2 * i][...]
        target[1] = refs[2 * i + 1][...]


def stack_pairs(position, *pairs):
    return kernel_call(
        stack_kernel,
        "stack",
        position,
        [value for pair in pairs for value in pair],
        [like((2, *pair[0].shape), pair[0].dtype) for pair in pairs],
        limit=4,
    )


def lay_kernel(pos_ref, *refs):
    *blocks, out_ref = refs
    chunk = blocks[0].shape[0]
    for k, block in enumerate(blocks):
        out_ref[k * chunk : (k + 1) * chunk, :] = block[...]


def lay_payload_kernel(pos_ref, near_ref, far_ref, out_ref):
    chunk = out_ref.shape[0] // 4
    width = near_ref.shape[2]
    for k in range(4):
        block = (near_ref, far_ref)[k % 2].at[k // 2]
        here = slice(k * chunk, (k + 1) * chunk)
        out_ref[here, :width] = block[0:chunk, :]
        kept = block[chunk:, : 2 * LANES].astype(jnp.float32)
        kept = jnp.concatenate([kept] * (LANES // kept.shape[0]), axis=0).T[0:chunk]
        out_ref[here, width:] = kept.astype(jnp.bfloat16)


def lay_rows(position, name, blocks):
    chunk, width = blocks[0].shape
    return kernel_call(
        lay_kernel,
        name,
        position,
        blocks,
        [like((len(blocks) * chunk, width), blocks[0].dtype)],
        limit=4,
    )[0]


def pack_small(small, experts):
    high, low = split_high_low(small)
    row = lax.broadcasted_iota(jnp.int32, (SMALL, LANES), 0)
    loss_rows = (row == experts + 1) | (row == experts + 2)
    low = jnp.where(loss_rows, low[:, :LANES].astype(jnp.float32), 0.0)
    high = high.astype(jnp.float32)
    packed = [high[:, :LANES], high[:, LANES : 2 * LANES] + low, high[:, 2 * LANES :]]
    return jnp.concatenate(packed, axis=1).astype(jnp.bfloat16)


def unpack_small(rows, experts):
    rows = rows.astype(jnp.float32)
    row = lax.broadcasted_iota(jnp.int32, (SMALL, LANES), 0)
    loss_rows = (row == experts + 1) | (row == experts + 2)
    low = rows[:, LANES : 2 * LANES]
    first = rows[:, :LANES] + jnp.where(loss_rows, low, 0.0)
    return jnp.concatenate([first, jnp.where(loss_rows, 0.0, low), rows[:, 2 * LANES :]], axis=1)


def gain_row(param_ref, experts, which):
    return param_ref[experts + which : experts + which + 1, :]


def attention_kernel(
    heads, experts, arrive, pos_ref, tok_ref, param_ref, w_ref, wo_ref, qkv_ref, lse_ref, att_ref,
    *refs,
):
    *parts, flat_ref, image_ref, held_ref = refs
    images, rows, width = qkv_ref.shape[1], qkv_ref.shape[2], heads * HD
    seq_len = tok_ref.shape[1]
    masks = head_masks(rows, heads)
    keys_live = lax.broadcasted_iota(jnp.int32, (rows, rows), 1) < seq_len
    lane = lax.broadcasted_iota(jnp.int32, (rows, LANES), 1)
    flat_ref[images * seq_len :, :] = jnp.zeros(
        (flat_ref.shape[0] - images * seq_len, width), jnp.float32
    )
    arrive(0, 1, 2)

    @pl.loop(0, images)
    def _(i):
        entered = normalize(image_rows(tok_ref, i, image_ref), gain_row(param_ref, experts, 0))[2]
        entered = entered.astype(jnp.bfloat16)
        q, k, v = (
            contract(entered, w_ref[c * width : (c + 1) * width, :], NT).astype(jnp.bfloat16)
            for c in range(3)
        )
        qkv_ref[0, i], qkv_ref[1, i], qkv_ref[2, i] = q, k, v
        attended = jnp.zeros((rows, width), jnp.float32)
        lse_all = jnp.zeros((rows, LANES), jnp.float32)
        for h in range(heads):
            scores = contract(keep_lanes(q, masks[h]), k, NT) * (HD ** (-0.5))
            scores = jnp.where(keys_live, scores, -1e30)
            top = jnp.max(scores, axis=-1, keepdims=True)
            lse = top + jnp.log(jnp.sum(jnp.exp(scores - top), axis=-1, keepdims=True))
            probs = jnp.exp(scores - lse).astype(jnp.bfloat16)
            attended = attended + contract(probs, keep_lanes(v, masks[h]), NN)
            lse_all = jnp.where(lane == h, lse, lse_all)
        lse_ref[i] = lse_all
        held_ref[i] = attended

    for i in range(images):
        flat_ref[pl.ds(i * seq_len, seq_len), :] = held_ref[i, 0:seq_len, :]
    arrive(3)
    att_ref[...] = flat_ref[...].astype(jnp.bfloat16)
    for j, part in enumerate(parts):
        rows_j = flat_ref[chunk_of(pos_ref, j, part.shape[0]), :].astype(jnp.bfloat16)
        part[...] = contract(rows_j, wo_ref[...], NN).astype(jnp.bfloat16)


def route_kernel(experts, pos_ref, *refs):
    *got, x_ref, param_ref, res_ref, routed_ref, prob_ref = refs
    residual = x_ref[...].astype(jnp.float32)
    for part in got:
        residual = residual + part[...].astype(jnp.float32)
    res_ref[...] = residual
    routed = normalize(residual, gain_row(param_ref, experts, 1))[2].astype(jnp.bfloat16)
    routed_ref[...] = routed
    prob_ref[...] = route_probs(routed, router_matrix(param_ref, experts), experts)


def route_probs(rows, router, experts):
    logits = contract(rows, router, NT)
    lane = lax.broadcasted_iota(jnp.int32, logits.shape, 1)
    logits = jnp.where(lane < experts, logits, -1e30)
    weight = jnp.exp(logits - jnp.max(logits, axis=-1, keepdims=True))
    return weight / jnp.sum(weight, axis=-1, keepdims=True)


def gelu_parts(x):
    square = jnp.exp(-0.5 * x * x)
    share = 0.5 * (1.0 + lax.erf(x * (0.5**0.5)))
    return x * share, share + x * square * (0.5 / math.pi) ** 0.5


def expert_halves(x, rg, w_in, w_out, hidden_ref, pre_ref):
    before = contract(x, w_in, NT)
    value, slope = gelu_parts(before)
    hidden = value.astype(jnp.bfloat16)
    hidden_ref[...] = hidden
    part = contract(hidden, w_out, NN)
    pre = (contract(rg, w_out, NT) * slope).astype(jnp.bfloat16)
    pre_ref[...] = pre
    return part, contract(pre, w_in, NN)


def first_expert_kernel(
    experts, pos_ref, x_ref, pay_ref, param_ref, wa_ref, wb_ref, xa_ref, yb_ref, hidden_ref,
    pre_ref, rg_ref,
    gate_ref, part_ref, back_ref,
):
    count, width = x_ref.shape
    prob = route_probs(x_ref[...], router_matrix(param_ref, experts), experts)
    mine = lax.broadcasted_iota(jnp.int32, prob.shape, 1) == lax.axis_index("expert")
    kept = pay_ref[:, width:].astype(jnp.float32)
    kept = jnp.sum(jnp.where(mine, kept, 0.0), axis=-1, keepdims=True)
    gate = jnp.sum(jnp.where(mine, prob, 0.0), axis=-1, keepdims=True) * kept
    gate_ref[:, :LANES] = jnp.broadcast_to(gate, (count, LANES))
    gate_ref[:, LANES:] = jnp.broadcast_to(kept, (count, LANES))
    rg_ref[...] = (gate * pay_ref[:, :width].astype(jnp.float32)).astype(jnp.bfloat16)
    w_in, w_out = (
        jnp.concatenate([ref[s] for ref in (wa_ref, wb_ref, xa_ref, yb_ref)], axis=0)
        for s in range(2)
    )
    part_ref[...], back_ref[...] = expert_halves(
        x_ref[...], rg_ref[...], w_in, w_out, hidden_ref, pre_ref
    )


def second_expert_kernel(
    pos_ref, x_ref, pay_ref, rg_ref, gate_ref, part_in_ref, back_in_ref, pair_y_ref, pair_x_ref,
    hidden_ref, pre_ref, gated_ref, back_ref,
):
    width = x_ref.shape[1]
    w_in, w_out = (
        jnp.concatenate([ref[r, s] for ref in (pair_y_ref, pair_x_ref) for r in range(2)], axis=0)
        for s in range(2)
    )
    part, back = expert_halves(x_ref[...], rg_ref[...], w_in, w_out, hidden_ref, pre_ref)
    back_ref[:, :width] = (back_in_ref[...] + back).astype(back_ref.dtype)
    part = part_in_ref[...] + part
    gated_ref[...] = (gate_ref[:, 0:1] * part).astype(jnp.bfloat16)
    inner = jnp.sum(part * pay_ref[:, :width].astype(jnp.float32), axis=-1, keepdims=True)
    inner = gate_ref[:, LANES:] * inner
    if back_ref.dtype == jnp.bfloat16:
        high, low = split_high_low(inner)
        upper = lax.broadcasted_iota(jnp.int32, inner.shape, 1) < LANES // 2
        inner = jnp.where(upper, high.astype(jnp.float32), low.astype(jnp.float32))
    back_ref[:, width:] = inner.astype(back_ref.dtype)


def first_expert_pass(position, rows, payload, params, weights, experts):
    count, width = rows.shape
    hidden = 4 * weights[0].shape[1]
    return kernel_call(
        functools.partial(first_expert_kernel, experts),
        "experts_first",
        position,
        [rows, payload, params, *weights],
        [
            like((count, hidden), jnp.bfloat16),
            like((count, hidden), jnp.bfloat16),
            like((count, width), jnp.bfloat16),
            like((count, 2 * LANES), jnp.float32),
            like((count, width), jnp.float32),
            like((count, width), jnp.float32),
        ],
        limit=18,
    )


def second_expert_pass(position, rows, payload, first, weights, back_dtype):
    count, width = rows.shape
    hidden = 4 * weights[0].shape[2]
    return kernel_call(
        second_expert_kernel,
        "experts_second",
        position,
        [rows, payload, *first[2:], *weights],
        [
            like((count, hidden), jnp.bfloat16),
            like((count, hidden), jnp.bfloat16),
            like((count, width), jnp.bfloat16),
            like((count, width + LANES), back_dtype),
        ],
        limit=18,
    )


def join_kernel(pos_ref, back_ref, other_ref, gated_ref, gated_other_ref, *outs):
    *backs, own_ref, pair_ref, far_ref = outs
    chunk, width = own_ref.shape
    for k, out in enumerate(backs):
        here = pl.ds(k * chunk, chunk)
        other = other_ref[here, :].astype(jnp.float32)
        out[0:chunk, :] = (back_ref[here, :width] + other[:, :width]).astype(jnp.bfloat16)
        inner = jnp.sum(other[:, width:], axis=-1, keepdims=True) * (2.0 / LANES)
        inner = back_ref[here, width:] + inner
        inner = jnp.concatenate(
            [inner, jnp.zeros((2 * LANES - chunk, LANES), jnp.float32)], axis=0
        ).T
        high, low = split_high_low(inner[0:SMALL, :])
        both = jnp.where(
            live_rows(high.shape, SMALL // 2), high.astype(jnp.float32), low.astype(jnp.float32)
        )
        out[chunk:, : 2 * LANES] = both.astype(jnp.bfloat16)
        out[chunk:, 2 * LANES :] = jnp.zeros((SMALL, width - 2 * LANES), jnp.bfloat16)
        gated = gated_ref[here, :].astype(jnp.float32) + gated_other_ref[here, :].astype(jnp.float32)
        gated = gated.astype(jnp.bfloat16)
        if k % 2:
            pair_ref[k // 2] = gated
        else:
            (own_ref, far_ref)[k // 2][...] = gated


def pair_sum_kernel(pos_ref, base_ref, own_ref, far_ref, got_ref, sum_ref, send_ref):
    total = base_ref[...] + own_ref[...].astype(jnp.float32) + got_ref[0].astype(jnp.float32)
    sum_ref[...] = total
    send_ref[...] = (far_ref[...].astype(jnp.float32) + got_ref[1].astype(jnp.float32)).astype(
        jnp.bfloat16
    )


def expert_grad_kernel(first, pos_ref, *refs):
    outs = refs[8:]
    part_rows = outs[0].shape[2]
    for j, out in enumerate(outs):
        start = 2 * (first + j) * part_rows
        columns = slice(start, start + 2 * part_rows)
        for s in range(2):
            left_a, right_a, left_b, right_b = refs[4 * s : 4 * s + 4]
            grad = contract(left_a[:, columns], right_a[...], TN)
            grad = grad + contract(left_b[:, columns], right_b[...], TN)
            grad = grad.astype(jnp.bfloat16)
            out[0, s] = grad[0:part_rows]
            out[1, s] = grad[part_rows:]


def expert_grads(position, a, b, rows_a, rows_b, first=0, count=2, flops=0):
    width, total = rows_a[0].shape[1], a[0].shape[1]
    return kernel_call(
        functools.partial(expert_grad_kernel, first),
        "expert_grads",
        position,
        [a[1], rows_a[0], b[1], rows_b[0], a[0], rows_a[1], b[0], rows_b[1]],
        [like((2, 2, total // 4, width), jnp.bfloat16)] * count,
        flops=flops,
        limit=10,
    )


def route_back_kernel(
    experts, token_rows, owners, pos_ref, *refs
):
    backs = refs[:owners]
    prob_ref, res_ref, pay_ref, param_ref = refs[owners : owners + 4]
    grad_ref, up_ref, small_ref = refs[owners + 4 :]
    chunk, width = res_ref.shape
    prob = prob_ref[...]
    lane = lax.broadcasted_iota(jnp.int32, prob.shape, 1)
    route_grad = jnp.zeros_like(prob)
    routed_grad = jnp.zeros((chunk, width), jnp.float32)
    for k, back in enumerate(backs):
        owner = lax.bitwise_xor(lax.axis_index("expert"), k)
        inner = back[chunk:, : 2 * LANES].astype(jnp.float32)
        inner = jnp.concatenate([inner] * (LANES // SMALL), axis=0).T[0:chunk]
        inner = jnp.sum(inner, axis=-1, keepdims=True) * (2.0 / LANES)
        route_grad = jnp.where(lane == owner, inner, route_grad)
        routed_grad = routed_grad + back[0:chunk, :].astype(jnp.float32)
    mean = jnp.sum(route_grad * prob, axis=-1, keepdims=True)
    logit_grad = (prob * (route_grad - mean)).astype(jnp.bfloat16)
    routed_grad = routed_grad + contract(
        logit_grad, router_matrix(param_ref, experts), NN
    )
    normed, inverse, mixed = normalize(res_ref[...], gain_row(param_ref, experts, 1))
    from_norm, gain_grad = normalize_back(
        routed_grad, normed, inverse, gain_row(param_ref, experts, 1)
    )
    total = pay_ref[0:chunk, :].astype(jnp.float32) + from_norm
    grad_ref[...] = total
    up_ref[...] = total.astype(jnp.bfloat16)
    live = live_rows(prob.shape, token_rows, lax.axis_index("tensor") * chunk)
    prob_sum = jnp.sum(jnp.where(live, prob, 0.0), axis=0, keepdims=True)
    grad_router = contract(logit_grad, mixed.astype(jnp.bfloat16), TN)
    small_ref[0:SMALL, :] = grad_router[0:SMALL]
    small_ref[experts : experts + 1, :] = gain_grad[None]
    small_ref[experts + 1 : experts + 2, :] = jnp.zeros((1, width), jnp.float32)
    small_ref[experts + 1 : experts + 2, :LANES] = prob_sum
    small_ref[experts + 2 : experts + 3, :] = param_ref[SMALL - 1 : SMALL, :]


def attention_back_kernel(
    heads, experts, owners, pos_ref, tok_ref, param_ref, w_ref, wo_ref, qkv_ref, lse_ref, att_ref,
    up_ref, small_ref, keep_ref, send_ref, *refs,
):
    *parts, hg_ref, flat_ref, big_ref, image_ref, held_ref, sum_ref, gain_ref = refs
    images, rows, width = qkv_ref.shape[1], qkv_ref.shape[2], heads * HD
    seq_len = tok_ref.shape[1]
    scale = HD ** (-0.5)
    padded, model = up_ref.shape
    chunk = padded // len(parts)
    masks = head_masks(rows, heads)
    keys_live = lax.broadcasted_iota(jnp.int32, (rows, rows), 1) < seq_len
    lane = lax.broadcasted_iota(jnp.int32, (rows, LANES), 1)
    up = up_ref[...]
    hg_ref[0:padded, :] = contract(up, wo_ref[...], NT)
    hg_ref[padded:, :] = jnp.zeros((hg_ref.shape[0] - padded, width), jnp.float32)
    big_ref[3 * width :, :] = contract(att_ref[...], up, TN)
    flat_ref[images * seq_len :, :] = jnp.zeros(
        (flat_ref.shape[0] - images * seq_len, model), jnp.float32
    )
    for i in range(images):
        held_ref[i] = hg_ref[pl.ds(i * seq_len, rows), :]
    big_ref[0 : 3 * width, :] = jnp.zeros((3 * width, model), jnp.float32)

    @pl.loop(0, images, unroll=True)
    def _(i):
        normed, _, mixed = normalize(
            image_rows(tok_ref, i, image_ref), gain_row(param_ref, experts, 0)
        )
        entered = mixed.astype(jnp.bfloat16)
        q, k, v = qkv_ref[0, i], qkv_ref[1, i], qkv_ref[2, i]
        heads_grad = held_ref[i]
        heads_grad = jnp.where(live_rows(heads_grad.shape, seq_len), heads_grad, 0.0)
        heads_grad = heads_grad.astype(jnp.bfloat16)
        dq = jnp.zeros((rows, width), jnp.float32)
        dk, dv = dq, dq
        for h in range(heads):
            q_h, k_h = keep_lanes(q, masks[h]), keep_lanes(k, masks[h])
            up_h = keep_lanes(heads_grad, masks[h])
            scores = contract(q_h, k, NT) * scale
            lse = jnp.sum(jnp.where(lane == h, lse_ref[i], 0.0), axis=-1, keepdims=True)
            probs = jnp.where(keys_live, jnp.exp(scores - lse), 0.0)
            prob_grad = contract(up_h, v, NT)
            total = jnp.sum(prob_grad * probs, axis=-1, keepdims=True)
            score_grad = (probs * (prob_grad - total)).astype(jnp.bfloat16)
            dv = dv + contract(probs.astype(jnp.bfloat16), up_h, TN)
            dq = dq + contract(score_grad, k_h, NN)
            dk = dk + contract(score_grad, q_h, TN)
        grads = [g.astype(jnp.bfloat16) for g in (dq * scale, dk * scale, dv)]
        part = jnp.zeros((rows, model), jnp.float32)
        for c in range(3):
            here = slice(c * width, (c + 1) * width)
            part = part + contract(grads[c], w_ref[here, :], NN)
            big_ref[here, :] += contract(grads[c], entered, TN)
        sum_ref[i] = part
        gain_ref[i] = jnp.broadcast_to(
            jnp.sum(part * normed, axis=0, keepdims=True), gain_ref.shape[1:]
        )

    gain_grad = jnp.zeros((1, model), jnp.float32)
    for i in range(images):
        flat_ref[pl.ds(i * seq_len, seq_len), :] = sum_ref[i, 0:seq_len, :]
        gain_grad = gain_grad + gain_ref[i, 0:1, :]
    small = pack_small(
        jnp.concatenate([small_ref[0 : SMALL - 1, :], gain_grad], axis=0), experts
    )
    for j, part in enumerate(parts):
        part[0:chunk, :] = flat_ref[chunk_of(pos_ref, j, chunk), :].astype(jnp.bfloat16)
        part[chunk:, :] = small
    me, core = lax.axis_index("expert"), lax.axis_index("dp")
    piece = keep_ref.shape[1]
    for k in range(owners):
        place = lax.bitwise_xor(me, k) * piece
        mine = pl.ds(pl.multiple_of(core * owners * piece + place, 8), piece)
        other = pl.ds(pl.multiple_of((1 - core) * owners * piece + place, 8), piece)
        keep_ref[k] = big_ref[mine, :]
        send_ref[k] = big_ref[other, :].astype(jnp.bfloat16)


def norm_back_kernel(experts, tensors, pos_ref, *refs):
    got = refs[:tensors]
    x_ref, res_ref, param_ref, own_ref, *parts, grad_ref, out_ref, small_ref = refs[tensors:]
    chunk, width = x_ref.shape
    upstream = jnp.zeros((chunk, width), jnp.float32)
    for j, part in enumerate(got):
        upstream = upstream + part[0:chunk, :].astype(jnp.float32)
        small_ref[lax.bitwise_xor(lax.axis_index("tensor"), j)] = unpack_small(
            part[chunk:, :], experts
        )
    small = small_ref[0]
    for j in range(1, tensors):
        small = small + small_ref[j]
    gain = gain_row(param_ref, experts, 0)
    normed, inverse, _ = normalize(x_ref[...].astype(jnp.float32), gain)
    from_norm = normalize_back(upstream, normed, inverse, gain)[0]
    grad_ref[...] = (res_ref[...] + from_norm).astype(jnp.bfloat16)
    piece = own_ref.shape[0]
    total = own_ref[...]
    for part in parts:
        total = total + part[...].astype(jnp.float32)
    out_ref[0:piece, :] = total.astype(jnp.bfloat16)
    out_ref[piece:, :] = pack_small(small, experts)


def second_step_kernel(pos_ref, near_ref, from_y, from_x, x_ref, y_ref):
    for target, row, other in ((x_ref, 0, from_y), (y_ref, 1, from_x)):
        total = near_ref[row].astype(jnp.float32) + other[1].astype(jnp.float32)
        target[...] = total.astype(jnp.bfloat16)


def weight_sum_kernel(pos_ref, own_ref, from_y, from_x, last_x, last_y, out_ref):
    part_rows = last_x.shape[1]
    for row, other, last in ((0, from_y, last_x), (1, from_x, last_y)):
        total = own_ref[row].astype(jnp.float32) + other[0].astype(jnp.float32)
        total = total + last[...].astype(jnp.float32)
        out_ref[:, row * part_rows : (row + 1) * part_rows, :] = total.astype(jnp.bfloat16)


def add_core_kernel(pos_ref, keep_ref, other_ref, own_ref, *outs):
    total = keep_ref[...] + other_ref[...].astype(jnp.float32)
    own_ref[...] = total[0]
    for k, out in enumerate(outs):
        out[...] = total[k + 1].astype(jnp.bfloat16)


def spread_kernel(owners, experts, token_total, pos_ref, *refs):
    sides = refs[:2]
    qkv_ref, wo_ref, router_ref, one_ref, two_ref, loss_ref, big_ref, parts_ref = refs[2:]
    span = sides[0].shape[0] // owners
    piece = span - SMALL
    core, me = lax.axis_index("dp"), lax.axis_index("expert")
    for c in range(2):
        side = core if c == 0 else 1 - core
        for k in range(owners):
            block = sides[c].at[k * span : (k + 1) * span]
            place = side * owners + lax.bitwise_xor(me, k)
            here = pl.ds(pl.multiple_of(place * piece, 8), piece)
            big_ref[here, :] = block[0:piece, :].astype(jnp.float32)
            parts_ref[place] = unpack_small(block[piece:, :], experts)
    rows = qkv_ref.shape[0]
    qkv_ref[...] = big_ref[0:rows, :]
    wo_ref[...] = big_ref[rows:, :]
    small = parts_ref[0]
    for p in range(1, 2 * owners):
        small = small + parts_ref[p]
    router_ref[...] = small[0:experts, :]
    one_ref[...] = small[SMALL - 1 : SMALL, :].reshape(small.shape[1])
    two_ref[...] = small[experts : experts + 1, :].reshape(small.shape[1])
    product = small[experts + 1 : experts + 2, :LANES] * small[experts + 2 : experts + 3, :LANES]
    lane = lax.broadcasted_iota(jnp.int32, product.shape, 1)
    product = jnp.where(lane < experts, product, 0.0)
    loss = jnp.sum(product, axis=-1, keepdims=True)
    loss_ref[...] = jnp.broadcast_to(
        loss * (experts / (2.0 * token_total * token_total)), loss_ref.shape
    )


def images_kernel(pos_ref, *refs):
    *chunks, out_ref, flat_ref = refs
    images, seq_len, _ = out_ref.shape
    if len(chunks) == 1:
        flat_ref[...] = chunks[0][...].astype(jnp.float32)
    else:
        for j, part in enumerate(chunks):
            flat_ref[chunk_of(pos_ref, j, part.shape[0]), :] = part[...].astype(jnp.float32)
    for i in range(images):
        out_ref[i] = flat_ref[pl.ds(i * seq_len, seq_len), :].astype(out_ref.dtype)


def weight_out_kernel(pos_ref, mine_ref, other_ref, in_ref, out_ref):
    first_is_mine = lax.axis_index("dp") == 0
    half = mine_ref.shape[1]
    for c in range(2):
        here = slice(c * half, (c + 1) * half)
        take = first_is_mine if c == 0 else jnp.logical_not(first_is_mine)
        grad_in = jnp.where(take, mine_ref[0], other_ref[0]).astype(jnp.float32)
        in_ref[0, :, here] = grad_in.T
        out_ref[0, here, :] = jnp.where(take, mine_ref[1], other_ref[1]).astype(jnp.float32)


def swap_core(value):
    return lax.ppermute(value, "dp", [(0, 1), (1, 0)])


def hop(value, bit):
    size = lax.axis_size("expert")
    return lax.ppermute(value, "expert", [(i, i ^ bit) for i in range(size)])


def cross(value, bit):
    size = lax.axis_size("tensor")
    return lax.ppermute(value, "tensor", [(i, i ^ bit) for i in range(size)])


def after(value, *others):
    return lax.optimization_barrier((value, *others))[0]


def dense_body(
    tokens,
    cotangent,
    expert_ids,
    slot_rank,
    qkv_weight,
    out_weight,
    router_weight,
    expert_in,
    expert_out,
    gain_attention,
    gain_experts,
):
    f32, b16 = jnp.float32, jnp.bfloat16
    images, seq_len, width = tokens.shape
    token_rows = images * seq_len
    local = qkv_weight.shape[2]
    heads = local // HD
    experts = router_weight.shape[1]
    owners = lax.axis_size("expert")
    tensors = lax.axis_size("tensor")
    cores = lax.axis_size("dp")
    chunk = round_up(-(-token_rows // tensors), 8)
    padded = chunk * tensors
    rows = round_up(seq_len, 16)
    flat_rows = padded + 32
    half = expert_in.shape[2] // cores
    quarter = half // 2
    position = jnp.zeros((1,), jnp.int32)
    weight_rows = qkv_weight.transpose(0, 2, 1).reshape(3 * local, width)

    x_chunk, payload, params, first, second = kernel_call(
        functools.partial(chunk_kernel, tensors),
        "chunk",
        position,
        [
            tokens,
            cotangent,
            expert_ids.transpose(0, 2, 1),
            slot_rank.transpose(0, 2, 1),
            router_weight.T,
            gain_attention,
            gain_experts,
            expert_in,
            expert_out,
        ],
        [
            like((chunk, width), b16),
            like((chunk + SMALL, width), b16),
            like((SMALL, width), f32),
            like((2, quarter, width), b16),
            like((2, quarter, width), b16),
        ],
        [
            pltpu.VMEM((flat_rows, width), f32),
            pltpu.VMEM((padded + 2 * LANES, LANES), f32),
        ],
        limit=56,
        loads=tuple(range(9)),
    )
    payload_two = hop(payload, 2)
    first_x = cross(first, 1)
    second_y = cross(second, 2)

    qkv, lse, attended, *parts = kernel_call(
        functools.partial(attention_kernel, heads, experts),
        "attention",
        after(position, first),
        [tokens, params, weight_rows, out_weight],
        [
            like((3, images, rows, local), b16),
            like((images, rows, LANES), f32),
            like((padded, local), b16),
        ]
        + [like((chunk, width), b16)] * tensors,
        [
            pltpu.VMEM((padded, local), f32),
            pltpu.VMEM((rows, width), f32),
            pltpu.VMEM((images, rows, local), f32),
        ],
        flops=40_000_000_000,
        limit=20,
        loads=(0, 1, 2, 3),
    )
    arrived = [parts[0]] + [cross(parts[j], j) for j in range(1, tensors)]
    pair_first, pair_second = stack_pairs(
        after(position, parts[0]), (first, first_x), (second, second_y)
    )
    (payload_near,) = stack_pairs(after(position, pair_first), (payload, payload_two))
    payload_far = hop(payload_near, 1)

    residual, routed, prob = kernel_call(
        functools.partial(route_kernel, experts),
        "route",
        after(position, pair_first, payload_near),
        [*arrived, x_chunk, params],
        [like((chunk, width), f32), like((chunk, width), b16), like((chunk, LANES), f32)],
        limit=8,
    )
    blocks = [routed] + [hop(routed, k) for k in range(1, owners)]
    pair_first, pair_second = after((pair_first, pair_second), routed)
    pair_y = cross(pair_first, 2)
    pair_x = cross(pair_second, 1)
    payload_mine = kernel_call(
        lay_payload_kernel,
        "lay_payload",
        after(position, routed),
        [payload_near, payload_far],
        [like((owners * chunk, width + LANES), b16)],
        limit=6,
    )[0]
    payload_other = swap_core(payload_mine)
    rows_mine = lay_rows(position, "lay_rows", blocks)
    rows_other = swap_core(rows_mine)

    near_weights = (first, second, first_x, second_y)
    far_weights = (pair_y, pair_x)
    first_a = first_expert_pass(position, rows_mine, payload_mine, params, near_weights, experts)
    first_b = first_expert_pass(
        after(position, first_a[2]), rows_other, payload_other, params, near_weights, experts
    )
    second_b = second_expert_pass(
        after(position, first_b[2]), rows_other, payload_other, first_b, far_weights, b16
    )
    back_other, gated_other = swap_core(second_b[3]), swap_core(second_b[2])
    second_a = second_expert_pass(
        after(position, second_b[0]), rows_mine, payload_mine, first_a, far_weights, f32
    )
    *joined, gated_own, gated_pair, gated_far = kernel_call(
        join_kernel,
        "join",
        position,
        [second_a[3], back_other, second_a[2], gated_other],
        [like((chunk + SMALL, width), b16)] * owners
        + [like((chunk, width), b16), like((2, chunk, width), b16), like((chunk, width), b16)],
        limit=8,
    )
    backs = [joined[0]] + [hop(joined[k], k) for k in range(1, owners)]

    grad_pos = after(position, joined)
    far_rows = (rows_mine, first_a[2]), (rows_other, first_b[2])
    (far_y,) = expert_grads(grad_pos, second_a, second_b, *far_rows, first=0, count=1)
    (far_x,) = expert_grads(
        after(grad_pos, far_y), second_a, second_b, *far_rows, first=1, count=1, flops=0
    )
    from_y, from_x = cross(far_y, 2), cross(far_x, 1)
    residual_grad, attn_grad, small = kernel_call(
        functools.partial(route_back_kernel, experts, token_rows, owners),
        "route_back",
        position,
        [*backs, prob, residual, payload, params],
        [like((chunk, width), f32), like((chunk, width), b16), like((SMALL, width), f32)],
        flops=40_000_000_000,
        limit=8,
    )
    own_grad, near_grad = expert_grads(
        after(position, attn_grad), first_a, first_b, (rows_mine, first_a[2]), (rows_other, first_b[2]),
    )
    gated_near = hop(after(gated_pair, backs[1]), 1)
    block_sum, gated_far = kernel_call(
        pair_sum_kernel,
        "pair_sum",
        after(position, own_grad),
        [residual, gated_own, gated_far, gated_near],
        [like((chunk, width), f32), like((chunk, width), b16)],
        limit=4,
    )
    attn_grad, gated_far = lax.optimization_barrier((attn_grad, gated_far))
    gated_last = hop(gated_far, 2)
    attn_grad = lax.all_gather(attn_grad, "tensor", axis=0, tiled=True)
    piece = 4 * local // (2 * owners)
    keep, send, *parts = kernel_call(
        functools.partial(attention_back_kernel, heads, experts, owners),
        "attention_back",
        after(position, from_y, from_x, gated_last),
        [tokens, params, weight_rows, out_weight, qkv, lse, attended, attn_grad, small],
        [
            like((owners, piece, width), f32),
            like((owners, piece, width), b16),
        ]
        + [like((chunk + SMALL, width), b16)] * tensors,
        [
            pltpu.VMEM((flat_rows, local), f32),
            pltpu.VMEM((flat_rows, width), f32),
            pltpu.VMEM((4 * local, width), f32),
            pltpu.VMEM((rows, width), f32),
            pltpu.VMEM((images, rows, local), f32),
            pltpu.VMEM((images, rows, width), f32),
            pltpu.VMEM((images, SMALL, width), f32),
        ],
        limit=20,
        flops=6_000_000_000,
    )
    own_piece, *pieces = kernel_call(
        add_core_kernel,
        "add_core",
        position,
        [keep, swap_core(send)],
        [like((piece, width), f32)] + [like((piece, width), b16)] * (owners - 1),
        limit=8,
    )
    reduced = [hop(p, k + 1) for k, p in enumerate(pieces)]
    got = [parts[0]] + [cross(parts[j], j) for j in range(1, tensors)]

    up_x, up_y = kernel_call(
        second_step_kernel,
        "second_step",
        after(position, own_piece),
        [near_grad, from_y, from_x],
        [like((2, quarter, width), b16)] * 2,
        limit=8,
    )
    up_x, up_y = after((up_x, up_y), got[1:])
    last_x, last_y = cross(up_x, 1), cross(up_y, 2)

    grad_chunk, summed = kernel_call(
        functools.partial(norm_back_kernel, experts, tensors),
        "norm_back",
        position,
        [*got, x_chunk, residual_grad, params, own_piece, *reduced],
        [like((chunk, width), b16), like((piece + SMALL, width), b16)],
        [pltpu.VMEM((tensors, SMALL, width), f32)],
        flops=40_000_000_000,
        limit=8,
    )
    around = [summed] + [hop(summed, k) for k in range(1, owners)]
    grad_rows = lax.all_gather(grad_chunk, "tensor", axis=0, tiled=True)
    combined = (block_sum + gated_last.astype(f32)).astype(b16)
    combined = after(combined, grad_rows)
    block_parts = [combined] + [cross(combined, j) for j in range(1, tensors)]

    grad_tokens = kernel_call(
        images_kernel,
        "grad_tokens",
        position,
        [grad_rows],
        [like(tokens.shape, f32)],
        [pltpu.VMEM((padded, width), f32)],
        limit=8,
    )[0]
    grad_half = kernel_call(
        weight_sum_kernel,
        "weight_sum",
        after(position, grad_rows, around),
        [own_grad, from_y, from_x, last_x, last_y],
        [like((2, half, width), b16)],
        limit=8,
    )[0]
    grad_expert_in, grad_expert_out = kernel_call(
        weight_out_kernel,
        "weight_out",
        position,
        [grad_half, swap_core(grad_half)],
        [like((1, width, 2 * half), f32), like((1, 2 * half, width), f32)],
        limit=10,
    )
    around_rows = lay_rows(position, "lay_grads", around)
    token_total = token_rows * cores * owners
    grad_qkv, grad_out, grad_router, gain_one, gain_two, loss = kernel_call(
        functools.partial(spread_kernel, owners, experts, token_total),
        "spread",
        position,
        [around_rows, swap_core(around_rows)],
        [
            like((3 * local, width), f32),
            like((local, width), f32),
            like((experts, width), f32),
            like((width,), f32),
            like((width,), f32),
            like((1, LANES), f32),
        ],
        [
            pltpu.VMEM((4 * local, width), f32),
            pltpu.VMEM((2 * owners, SMALL, width), f32),
        ],
        limit=8,
    )
    block_out = kernel_call(
        images_kernel,
        "block_out",
        after(position, grad_tokens, grad_expert_in, grad_qkv),
        block_parts,
        [like(tokens.shape, b16)],
        [pltpu.VMEM((padded, width), f32)],
        limit=8,
    )[0]
    return (
        block_out,
        grad_tokens,
        grad_qkv.reshape(3, local, width).transpose(0, 2, 1),
        grad_out,
        grad_router.T,
        grad_expert_in,
        grad_expert_out,
        gain_one,
        gain_two,
        loss[0, 0],
    )


def solution(mesh):
    placed = (
        P(("dp", "expert"), None, None),
        P(("dp", "expert"), None, None),
        P(("dp", "expert"), None, None),
        P(("dp", "expert"), None, None),
        P(None, None, "tensor"),
        P("tensor", None),
        P(),
        P("expert", None, "tensor"),
        P("expert", "tensor", None),
        P(),
        P(),
    )
    shape = mesh.shape
    dense = shape["dp"] == 2 and shape["expert"] == 4 and shape["tensor"] == 4
    return jax.shard_map(
        dense_body if dense else body,
        mesh=mesh,
        in_specs=placed,
        out_specs=(
            P(("dp", "expert"), None, None),
            P(("dp", "expert"), None, None),
            P(None, None, "tensor"),
            P("tensor", None),
            P(),
            P("expert", None, "tensor"),
            P("expert", "tensor", None),
            P(),
            P(),
            P(),
        ),
        check_vma=False,
    )
```

```python
import functools
import math

import jax
import jax.numpy as jnp
from jax import lax
from jax.experimental import pallas as pl
from jax.experimental.pallas import tpu as pltpu
from jax.sharding import PartitionSpec as P

HD = 64


epsilon = 1e-06


def normalize(values, gain_row):
    center = values - jnp.mean(values, axis=-1, keepdims=True)
    inverse = lax.rsqrt(jnp.mean(center * center, axis=-1, keepdims=True) + epsilon)
    normed = center * inverse
    return (normed, inverse, normed * gain_row)


def normalize_back(upstream, normed, inverse, gain_row):
    scaled = upstream * gain_row
    result = inverse * (
        scaled
        - jnp.mean(scaled, axis=-1, keepdims=True)
        - normed * jnp.mean(scaled * normed, axis=-1, keepdims=True)
    )
    return (result, jnp.sum(upstream * normed, axis=0))


def exact_gelu(values):
    return jax.nn.gelu(values, approximate=False)


def body(
    tokens,
    cotangent,
    expert_ids,
    slot_rank,
    qkv_weight,
    out_weight,
    router_weight,
    expert_in,
    expert_out,
    gain_attention,
    gain_experts,
):
    images, seq_len, model_width = tokens.shape
    token_rows = images * seq_len
    local_width = qkv_weight.shape[2]
    local_heads = local_width // HD
    slice_width = model_width // lax.axis_size("tensor")
    experts = router_weight.shape[1]
    capacity = 5 * token_rows // (2 * experts)
    owners = lax.axis_size("expert")
    per_owner = experts // owners
    slot_total = experts * capacity
    score_scale = HD ** (-0.5)
    inputs = tokens.reshape(token_rows, model_width).astype(jnp.float32)
    normed_one, inverse_one, mixed_one = normalize(inputs, gain_attention)
    entered = mixed_one.astype(jnp.bfloat16)
    project = jnp.einsum(
        "td,cdf->ctf", entered, qkv_weight, preferred_element_type=jnp.float32
    ).astype(jnp.bfloat16)
    projected_heads = project.reshape(3, images, seq_len, local_heads, HD)
    queries, key_rows, value_rows = (projected_heads[0], projected_heads[1], projected_heads[2])
    scores = (
        jnp.einsum("ishe,ithe->ihst", queries, key_rows, preferred_element_type=jnp.float32)
        * score_scale
    )
    log_total = jax.nn.logsumexp(scores, axis=-1, keepdims=True)
    attn_probs = jnp.exp(scores - log_total).astype(jnp.bfloat16)
    attended = jnp.einsum(
        "ihst,ithe->ishe", attn_probs, value_rows, preferred_element_type=jnp.float32
    )
    attended = attended.astype(jnp.bfloat16).reshape(token_rows, local_width)
    attn_part = jnp.dot(attended, out_weight, preferred_element_type=jnp.float32)
    residual = inputs + lax.psum(attn_part, "tensor")
    normed_two, inverse_two, mixed_two = normalize(residual, gain_experts)
    routed = mixed_two.astype(jnp.bfloat16)
    route_prob = jax.nn.softmax(
        jnp.dot(routed, router_weight, preferred_element_type=jnp.float32), axis=-1
    )
    chosen = expert_ids.reshape(token_rows, 2)
    ranked = slot_rank.reshape(token_rows, 2)
    kept_mask = (ranked >= 0).astype(jnp.float32)
    position = jnp.where(ranked >= 0, chosen * capacity + ranked, slot_total).reshape(-1)
    send_rows = (
        jnp.zeros((slot_total, model_width), jnp.bfloat16)
        .at[position]
        .set(jnp.repeat(routed, 2, axis=0), mode="drop")
        .reshape(experts, capacity, model_width)
    )
    fragment = lax.all_to_all(send_rows, "expert", split_axis=0, concat_axis=0, tiled=True)
    grouped = fragment.reshape(owners, per_owner, fragment.shape[1], model_width)
    before = jnp.einsum("sjcd,jdf->sjcf", grouped, expert_in, preferred_element_type=jnp.float32)
    hidden = exact_gelu(before).astype(jnp.bfloat16)
    expert_part = jnp.einsum(
        "sjcf,jfd->sjcd", hidden, expert_out, preferred_element_type=jnp.float32
    )
    produced = lax.psum_scatter(expert_part, "tensor", scatter_dimension=3, tiled=True).astype(
        jnp.bfloat16
    )
    returned = lax.all_to_all(
        produced.reshape(experts, capacity, slice_width),
        "expert",
        split_axis=0,
        concat_axis=0,
        tiled=True,
    )
    returned = lax.all_gather(returned, "tensor", axis=2, tiled=True).reshape(
        slot_total, model_width
    )
    safe_index = jnp.minimum(position, slot_total - 1)
    picked = returned[safe_index].reshape(token_rows, 2, model_width).astype(jnp.float32)
    gate_values = jnp.take_along_axis(route_prob, chosen, axis=1) * kept_mask
    output = residual + jnp.sum(gate_values[:, :, None] * picked, axis=1)
    block_out = output.astype(jnp.bfloat16).reshape(images, seq_len, model_width)
    upstream = cotangent.reshape(token_rows, model_width).astype(jnp.float32)
    gate_grad = jnp.sum(upstream[:, None, :] * picked, axis=-1) * kept_mask
    member = (chosen[:, :, None] == jnp.arange(experts)[None, None, :]).astype(jnp.float32)
    route_grad = jnp.sum(member * gate_grad[:, :, None], axis=1)
    logit_grad = (
        route_prob * (route_grad - jnp.sum(route_grad * route_prob, axis=-1, keepdims=True))
    ).astype(jnp.bfloat16)
    row_grad = (
        (gate_values[:, :, None] * upstream[:, None, :])
        .astype(jnp.bfloat16)
        .reshape(2 * token_rows, model_width)
    )
    grad_send = (
        jnp.zeros((slot_total, model_width), jnp.bfloat16)
        .at[position]
        .set(row_grad, mode="drop")
        .reshape(experts, capacity, model_width)
    )
    grad_arrived = lax.all_to_all(grad_send, "expert", split_axis=0, concat_axis=0, tiled=True)
    grad_arrived = grad_arrived.reshape(owners, per_owner, capacity, model_width)
    hidden_grad = jnp.einsum(
        "sjcd,jfd->sjcf", grad_arrived, expert_out, preferred_element_type=jnp.float32
    )
    grad_expert_out = jnp.einsum(
        "sjcf,sjcd->jfd", hidden, grad_arrived, preferred_element_type=jnp.float32
    )
    pre_grad = jax.vjp(exact_gelu, before)[1](hidden_grad)[0].astype(jnp.bfloat16)
    grad_expert_in = jnp.einsum(
        "sjcd,sjcf->jdf", grouped, pre_grad, preferred_element_type=jnp.float32
    )
    buffer_part = jnp.einsum(
        "sjcf,jdf->sjcd", pre_grad, expert_in, preferred_element_type=jnp.float32
    )
    buffer_share = lax.psum_scatter(buffer_part, "tensor", scatter_dimension=3, tiled=True).astype(
        jnp.bfloat16
    )
    buffer_back = lax.all_to_all(
        buffer_share.reshape(experts, capacity, slice_width),
        "expert",
        split_axis=0,
        concat_axis=0,
        tiled=True,
    )
    buffer_grad = lax.all_gather(buffer_back, "tensor", axis=2, tiled=True).reshape(
        slot_total, model_width
    )
    routed_grad = jnp.sum(
        buffer_grad[safe_index].reshape(token_rows, 2, model_width).astype(jnp.float32)
        * kept_mask[:, :, None],
        axis=1,
    )
    routed_grad = routed_grad + jnp.dot(
        logit_grad, router_weight.T, preferred_element_type=jnp.float32
    )
    grad_router = jnp.einsum("td,te->de", routed, logit_grad, preferred_element_type=jnp.float32)
    from_norm_two, grad_gain_experts = normalize_back(
        routed_grad, normed_two, inverse_two, gain_experts
    )
    residual_grad = upstream + from_norm_two
    attn_grad = residual_grad.astype(jnp.bfloat16)
    grad_out = jnp.einsum("tf,td->fd", attended, attn_grad, preferred_element_type=jnp.float32)
    heads_grad = jnp.dot(attn_grad, out_weight.T, preferred_element_type=jnp.float32).astype(
        jnp.bfloat16
    )
    heads_grad = heads_grad.reshape(images, seq_len, local_heads, HD)
    again = (
        jnp.einsum("ishe,ithe->ihst", queries, key_rows, preferred_element_type=jnp.float32)
        * score_scale
    )
    probs_full = jnp.exp(again - log_total)
    prob_grad = jnp.einsum(
        "ishe,ithe->ihst", heads_grad, value_rows, preferred_element_type=jnp.float32
    )
    value_grad = jnp.einsum(
        "ihst,ishe->ithe",
        probs_full.astype(jnp.bfloat16),
        heads_grad,
        preferred_element_type=jnp.float32,
    )
    score_grad = (
        probs_full * (prob_grad - jnp.sum(prob_grad * probs_full, axis=-1, keepdims=True))
    ).astype(jnp.bfloat16)
    query_grad = (
        jnp.einsum("ihst,ithe->ishe", score_grad, key_rows, preferred_element_type=jnp.float32)
        * score_scale
    )
    key_grad = (
        jnp.einsum("ihst,ishe->ithe", score_grad, queries, preferred_element_type=jnp.float32)
        * score_scale
    )
    project_grad = (
        jnp.stack([query_grad, key_grad, value_grad])
        .astype(jnp.bfloat16)
        .reshape(3, token_rows, local_width)
    )
    grad_qkv = jnp.einsum("td,ctf->cdf", entered, project_grad, preferred_element_type=jnp.float32)
    entered_part = jnp.einsum(
        "ctf,cdf->td", project_grad, qkv_weight, preferred_element_type=jnp.float32
    )
    entered_grad = lax.psum(entered_part.astype(jnp.bfloat16), "tensor").astype(jnp.float32)
    from_norm_one, grad_gain_attention = normalize_back(
        entered_grad, normed_one, inverse_one, gain_attention
    )
    grad_tokens = (residual_grad + from_norm_one).reshape(images, seq_len, model_width)
    counts = jnp.sum(member, axis=(0, 1))
    prob_sum = jnp.sum(route_prob, axis=0)
    grad_qkv, grad_out, grad_router, grad_gain_attention, grad_gain_experts, counts, prob_sum = (
        lax.psum(
            (
                grad_qkv,
                grad_out,
                grad_router,
                grad_gain_attention,
                grad_gain_experts,
                counts,
                prob_sum,
            ),
            ("dp", "expert"),
        )
    )
    grad_expert_in, grad_expert_out = (
        lax.psum(grad_expert_in.astype(jnp.bfloat16), "dp").astype(jnp.float32),
        lax.psum(grad_expert_out.astype(jnp.bfloat16), "dp").astype(jnp.float32),
    )
    token_total = token_rows * lax.axis_size("dp") * lax.axis_size("expert")
    balance_loss = experts * jnp.sum(counts / (2.0 * token_total) * prob_sum / token_total)
    return (
        block_out,
        grad_tokens,
        grad_qkv,
        grad_out,
        grad_router,
        grad_expert_in,
        grad_expert_out,
        grad_gain_attention,
        grad_gain_experts,
        balance_loss,
    )


NN = ((1,), (0,))
NT = ((1,), (1,))
TN = ((0,), (0,))
LANES = 128
SMALL = 8


def round_up(value, step):
    return -(-value // step) * step


def contract(a, b, dims):
    return lax.dot_general(a, b, (dims, ((), ())), preferred_element_type=jnp.float32)


def load_then(kernel, loads, count, *refs):
    pos_ref, *refs = refs
    *refs, sem = refs
    buffers = refs[len(refs) - len(loads) :]
    refs = refs[: len(refs) - len(loads)]
    copies = [
        pltpu.make_async_copy(refs[index], buffer, sem.at[i])
        for i, (index, buffer) in enumerate(zip(loads, buffers))
    ]
    for copy in copies:
        copy.start()
    for index, buffer in zip(loads, buffers):
        refs[index] = buffer

    def arrive(*indices):
        for index in indices:
            copies[loads.index(index)].wait()

    kernel(arrive, pos_ref, *refs)


def kernel_call(kernel, name, position, args, outs, scratch=(), flops=0, limit=24, loads=()):
    if loads:
        kernel = functools.partial(load_then, kernel, loads, len(args))
        scratch = [
            *scratch,
            *(pltpu.VMEM(args[i].shape, args[i].dtype) for i in loads),
            pltpu.SemaphoreType.DMA((len(loads),)),
        ]
    places = [pltpu.HBM if i in loads else pltpu.VMEM for i in range(len(args))]
    return pl.pallas_call(
        kernel,
        in_specs=[pl.BlockSpec(memory_space=pltpu.SMEM)]
        + [pl.BlockSpec(memory_space=place) for place in places],
        out_specs=[pl.BlockSpec(memory_space=pltpu.VMEM)] * len(outs),
        out_shape=list(outs),
        scratch_shapes=list(scratch),
        compiler_params=pltpu.CompilerParams(vmem_limit_bytes=limit << 20),
        cost_estimate=pl.CostEstimate(flops=flops, bytes_accessed=0, transcendentals=0),
        name=name,
    )(position, *args)


def like(shape, dtype):
    return jax.ShapeDtypeStruct(shape, dtype)


def live_rows(shape, limit, offset=0):
    return lax.broadcasted_iota(jnp.int32, shape, 0) + offset < limit


def chunk_of(pos_ref, j, size):
    return pl.ds(pl.multiple_of(lax.bitwise_xor(lax.axis_index("tensor"), j) * size, 8), size)


def head_masks(rows, heads):
    lane = lax.broadcasted_iota(jnp.int32, (rows, heads * HD), 1)
    return [(lane >= h * HD) & (lane < (h + 1) * HD) for h in range(heads)]


def keep_lanes(value, mask):
    return jnp.where(mask, value, jnp.zeros_like(value))


def split_high_low(value):
    high = value.astype(jnp.bfloat16)
    return high, (value - high.astype(jnp.float32)).astype(jnp.bfloat16)


def image_rows(ref, i, scratch_ref):
    seq_len = ref.shape[1]
    scratch_ref[seq_len:, :] = jnp.zeros((scratch_ref.shape[0] - seq_len, ref.shape[2]), jnp.float32)
    scratch_ref[0:seq_len, :] = ref[i].astype(jnp.float32)
    return scratch_ref[...]


def router_matrix(param_ref, experts):
    rows = param_ref[0:SMALL, :]
    rows = jnp.where(live_rows(rows.shape, experts), rows, 0.0).astype(jnp.bfloat16)
    zeros = jnp.zeros((LANES - SMALL, rows.shape[1]), jnp.bfloat16)
    return jnp.concatenate([rows, zeros], axis=0)


def chunk_kernel(
    tensors, arrive, pos_ref, tok_ref, cot_ref, ids_ref, rank_ref, router_ref, one_ref, two_ref, in_ref, out_ref,
    x_ref, pay_ref, param_ref, first_ref, second_ref, flat_ref, kept_ref,
):
    images, seq_len, width = tok_ref.shape
    chunk, experts = x_ref.shape[0], router_ref.shape[0]
    start = pl.multiple_of(lax.axis_index("tensor") * chunk, 8)
    for index, source, target in ((0, tok_ref, x_ref), (1, cot_ref, pay_ref)):
        arrive(index)
        flat_ref[images * seq_len :, :] = jnp.zeros(
            (flat_ref.shape[0] - images * seq_len, width), jnp.float32
        )
        for i in range(images):
            flat_ref[pl.ds(i * seq_len, seq_len), :] = source[i].astype(jnp.float32)
        target[0:chunk, :] = flat_ref[pl.ds(start, chunk), :].astype(jnp.bfloat16)
    arrive(2, 3, 4, 5, 6)
    kept_ref[...] = jnp.zeros_like(kept_ref)
    counts = jnp.zeros((1, LANES), jnp.float32)
    for i in range(images):
        rows, all_rows = [], []
        for e in range(experts):
            named = (ids_ref[i] == e).astype(jnp.float32)
            kept = jnp.where(rank_ref[i] >= 0, named, 0.0)
            rows.append(jnp.sum(kept, axis=0, keepdims=True))
            all_rows.append(jnp.sum(named, axis=0, keepdims=True))
        for group, is_kept in ((rows, True), (all_rows, False)):
            table = jnp.concatenate(group, axis=0)
            table = jnp.concatenate(
                [table, jnp.zeros((LANES - experts, seq_len), jnp.float32)], axis=0
            )
            table = jnp.concatenate(
                [table, jnp.zeros((LANES, 2 * LANES - seq_len), jnp.float32)], axis=1
            ).T
            if is_kept:
                kept_ref[pl.ds(i * seq_len, 2 * LANES), :] = table
            else:
                counts = counts + jnp.sum(table, axis=0, keepdims=True)
    kept = jnp.concatenate(
        [kept_ref[pl.ds(start, chunk), :], jnp.zeros((2 * LANES - chunk, LANES), jnp.float32)], axis=0
    ).T
    pay_ref[chunk:, : 2 * LANES] = kept[0:SMALL].astype(jnp.bfloat16)
    pay_ref[chunk:, 2 * LANES :] = jnp.zeros((SMALL, width - 2 * LANES), jnp.bfloat16)
    param_ref[...] = jnp.zeros_like(param_ref)
    param_ref[0:experts, :] = router_ref[...].astype(jnp.float32)
    param_ref[experts : experts + 1, :] = one_ref[...].reshape(1, width)
    param_ref[experts + 1 : experts + 2, :] = two_ref[...].reshape(1, width)
    param_ref[SMALL - 1 : SMALL, :LANES] = counts * (1.0 / tensors)
    arrive(7, 8)
    half = 2 * first_ref.shape[1]
    core = pl.multiple_of(lax.axis_index("dp") * half, LANES)
    for s, part in ((0, in_ref[0, :, pl.ds(core, half)].T), (1, out_ref[0, pl.ds(core, half), :])):
        first_ref[s] = part[0 : half // 2]
        second_ref[s] = part[half // 2 :]


def stack_kernel(pos_ref, *refs):
    count = len(refs) // 3
    for i, target in enumerate(refs[2 * count :]):
        target[0] = refs[2 * i][...]
        target[1] = refs[2 * i + 1][...]


def stack_pairs(position, *pairs):
    return kernel_call(
        stack_kernel,
        "stack",
        position,
        [value for pair in pairs for value in pair],
        [like((2, *pair[0].shape), pair[0].dtype) for pair in pairs],
        limit=4,
    )


def lay_kernel(pos_ref, *refs):
    *blocks, out_ref = refs
    chunk = blocks[0].shape[0]
    for k, block in enumerate(blocks):
        out_ref[k * chunk : (k + 1) * chunk, :] = block[...]


def lay_payload_kernel(pos_ref, near_ref, far_ref, out_ref):
    chunk = out_ref.shape[0] // 4
    width = near_ref.shape[2]
    for k in range(4):
        block = (near_ref, far_ref)[k % 2].at[k // 2]
        here = slice(k * chunk, (k + 1) * chunk)
        out_ref[here, :width] = block[0:chunk, :]
        kept = block[chunk:, : 2 * LANES].astype(jnp.float32)
        kept = jnp.concatenate([kept] * (LANES // kept.shape[0]), axis=0).T[0:chunk]
        out_ref[here, width:] = kept.astype(jnp.bfloat16)


def lay_rows(position, name, blocks):
    chunk, width = blocks[0].shape
    return kernel_call(
        lay_kernel,
        name,
        position,
        blocks,
        [like((len(blocks) * chunk, width), blocks[0].dtype)],
        limit=4,
    )[0]


def pack_small(small, experts):
    high, low = split_high_low(small)
    row = lax.broadcasted_iota(jnp.int32, (SMALL, LANES), 0)
    loss_rows = (row == experts + 1) | (row == experts + 2)
    low = jnp.where(loss_rows, low[:, :LANES].astype(jnp.float32), 0.0)
    high = high.astype(jnp.float32)
    packed = [high[:, :LANES], high[:, LANES : 2 * LANES] + low, high[:, 2 * LANES :]]
    return jnp.concatenate(packed, axis=1).astype(jnp.bfloat16)


def unpack_small(rows, experts):
    rows = rows.astype(jnp.float32)
    row = lax.broadcasted_iota(jnp.int32, (SMALL, LANES), 0)
    loss_rows = (row == experts + 1) | (row == experts + 2)
    low = rows[:, LANES : 2 * LANES]
    first = rows[:, :LANES] + jnp.where(loss_rows, low, 0.0)
    return jnp.concatenate([first, jnp.where(loss_rows, 0.0, low), rows[:, 2 * LANES :]], axis=1)


def gain_row(param_ref, experts, which):
    return param_ref[experts + which : experts + which + 1, :]


def attention_kernel(
    heads, experts, arrive, pos_ref, tok_ref, param_ref, w_ref, wo_ref, qkv_ref, lse_ref, att_ref,
    *refs,
):
    *parts, flat_ref, image_ref, held_ref = refs
    images, rows, width = qkv_ref.shape[1], qkv_ref.shape[2], heads * HD
    seq_len = tok_ref.shape[1]
    masks = head_masks(rows, heads)
    keys_live = lax.broadcasted_iota(jnp.int32, (rows, rows), 1) < seq_len
    lane = lax.broadcasted_iota(jnp.int32, (rows, LANES), 1)
    flat_ref[images * seq_len :, :] = jnp.zeros(
        (flat_ref.shape[0] - images * seq_len, width), jnp.float32
    )
    arrive(0, 1, 2)

    @pl.loop(0, images)
    def _(i):
        entered = normalize(image_rows(tok_ref, i, image_ref), gain_row(param_ref, experts, 0))[2]
        entered = entered.astype(jnp.bfloat16)
        q, k, v = (
            contract(entered, w_ref[c * width : (c + 1) * width, :], NT).astype(jnp.bfloat16)
            for c in range(3)
        )
        qkv_ref[0, i], qkv_ref[1, i], qkv_ref[2, i] = q, k, v
        attended = jnp.zeros((rows, width), jnp.float32)
        lse_all = jnp.zeros((rows, LANES), jnp.float32)
        for h in range(heads):
            scores = contract(keep_lanes(q, masks[h]), k, NT) * (HD ** (-0.5))
            scores = jnp.where(keys_live, scores, -1e30)
            top = jnp.max(scores, axis=-1, keepdims=True)
            lse = top + jnp.log(jnp.sum(jnp.exp(scores - top), axis=-1, keepdims=True))
            probs = jnp.exp(scores - lse).astype(jnp.bfloat16)
            attended = attended + contract(probs, keep_lanes(v, masks[h]), NN)
            lse_all = jnp.where(lane == h, lse, lse_all)
        lse_ref[i] = lse_all
        held_ref[i] = attended

    for i in range(images):
        flat_ref[pl.ds(i * seq_len, seq_len), :] = held_ref[i, 0:seq_len, :]
    arrive(3)
    att_ref[...] = flat_ref[...].astype(jnp.bfloat16)
    for j, part in enumerate(parts):
        rows_j = flat_ref[chunk_of(pos_ref, j, part.shape[0]), :].astype(jnp.bfloat16)
        part[...] = contract(rows_j, wo_ref[...], NN).astype(jnp.bfloat16)


def route_kernel(experts, pos_ref, *refs):
    *got, x_ref, param_ref, res_ref, routed_ref, prob_ref = refs
    residual = x_ref[...].astype(jnp.float32)
    for part in got:
        residual = residual + part[...].astype(jnp.float32)
    res_ref[...] = residual
    routed = normalize(residual, gain_row(param_ref, experts, 1))[2].astype(jnp.bfloat16)
    routed_ref[...] = routed
    prob_ref[...] = route_probs(routed, router_matrix(param_ref, experts), experts)


def route_probs(rows, router, experts):
    logits = contract(rows, router, NT)
    lane = lax.broadcasted_iota(jnp.int32, logits.shape, 1)
    logits = jnp.where(lane < experts, logits, -1e30)
    weight = jnp.exp(logits - jnp.max(logits, axis=-1, keepdims=True))
    return weight / jnp.sum(weight, axis=-1, keepdims=True)


def gelu_parts(x):
    square = jnp.exp(-0.5 * x * x)
    share = 0.5 * (1.0 + lax.erf(x * (0.5**0.5)))
    return x * share, share + x * square * (0.5 / math.pi) ** 0.5


def expert_halves(x, rg, w_in, w_out, hidden_ref, pre_ref):
    before = contract(x, w_in, NT)
    value, slope = gelu_parts(before)
    hidden = value.astype(jnp.bfloat16)
    hidden_ref[...] = hidden
    part = contract(hidden, w_out, NN)
    pre = (contract(rg, w_out, NT) * slope).astype(jnp.bfloat16)
    pre_ref[...] = pre
    return part, contract(pre, w_in, NN)


def first_expert_kernel(
    experts, pos_ref, x_ref, pay_ref, param_ref, wa_ref, wb_ref, xa_ref, yb_ref, hidden_ref,
    pre_ref, rg_ref,
    gate_ref, part_ref, back_ref,
):
    count, width = x_ref.shape
    prob = route_probs(x_ref[...], router_matrix(param_ref, experts), experts)
    mine = lax.broadcasted_iota(jnp.int32, prob.shape, 1) == lax.axis_index("expert")
    kept = pay_ref[:, width:].astype(jnp.float32)
    kept = jnp.sum(jnp.where(mine, kept, 0.0), axis=-1, keepdims=True)
    gate = jnp.sum(jnp.where(mine, prob, 0.0), axis=-1, keepdims=True) * kept
    gate_ref[:, :LANES] = jnp.broadcast_to(gate, (count, LANES))
    gate_ref[:, LANES:] = jnp.broadcast_to(kept, (count, LANES))
    rg_ref[...] = (gate * pay_ref[:, :width].astype(jnp.float32)).astype(jnp.bfloat16)
    w_in, w_out = (
        jnp.concatenate([ref[s] for ref in (wa_ref, wb_ref, xa_ref, yb_ref)], axis=0)
        for s in range(2)
    )
    part_ref[...], back_ref[...] = expert_halves(
        x_ref[...], rg_ref[...], w_in, w_out, hidden_ref, pre_ref
    )


def second_expert_kernel(
    pos_ref, x_ref, pay_ref, rg_ref, gate_ref, part_in_ref, back_in_ref, pair_y_ref, pair_x_ref,
    hidden_ref, pre_ref, gated_ref, back_ref,
):
    width = x_ref.shape[1]
    w_in, w_out = (
        jnp.concatenate([ref[r, s] for ref in (pair_y_ref, pair_x_ref) for r in range(2)], axis=0)
        for s in range(2)
    )
    part, back = expert_halves(x_ref[...], rg_ref[...], w_in, w_out, hidden_ref, pre_ref)
    back_ref[:, :width] = (back_in_ref[...] + back).astype(back_ref.dtype)
    part = part_in_ref[...] + part
    gated_ref[...] = (gate_ref[:, 0:1] * part).astype(jnp.bfloat16)
    inner = jnp.sum(part * pay_ref[:, :width].astype(jnp.float32), axis=-1, keepdims=True)
    inner = gate_ref[:, LANES:] * inner
    if back_ref.dtype == jnp.bfloat16:
        high, low = split_high_low(inner)
        upper = lax.broadcasted_iota(jnp.int32, inner.shape, 1) < LANES // 2
        inner = jnp.where(upper, high.astype(jnp.float32), low.astype(jnp.float32))
    back_ref[:, width:] = inner.astype(back_ref.dtype)


def first_expert_pass(position, rows, payload, params, weights, experts):
    count, width = rows.shape
    hidden = 4 * weights[0].shape[1]
    return kernel_call(
        functools.partial(first_expert_kernel, experts),
        "experts_first",
        position,
        [rows, payload, params, *weights],
        [
            like((count, hidden), jnp.bfloat16),
            like((count, hidden), jnp.bfloat16),
            like((count, width), jnp.bfloat16),
            like((count, 2 * LANES), jnp.float32),
            like((count, width), jnp.float32),
            like((count, width), jnp.float32),
        ],
        limit=18,
    )


def second_expert_pass(position, rows, payload, first, weights, back_dtype):
    count, width = rows.shape
    hidden = 4 * weights[0].shape[2]
    return kernel_call(
        second_expert_kernel,
        "experts_second",
        position,
        [rows, payload, *first[2:], *weights],
        [
            like((count, hidden), jnp.bfloat16),
            like((count, hidden), jnp.bfloat16),
            like((count, width), jnp.bfloat16),
            like((count, width + LANES), back_dtype),
        ],
        limit=18,
    )


def join_kernel(pos_ref, back_ref, other_ref, gated_ref, gated_other_ref, *outs):
    *backs, own_ref, pair_ref, far_ref = outs
    chunk, width = own_ref.shape
    for k, out in enumerate(backs):
        here = pl.ds(k * chunk, chunk)
        other = other_ref[here, :].astype(jnp.float32)
        out[0:chunk, :] = (back_ref[here, :width] + other[:, :width]).astype(jnp.bfloat16)
        inner = jnp.sum(other[:, width:], axis=-1, keepdims=True) * (2.0 / LANES)
        inner = back_ref[here, width:] + inner
        inner = jnp.concatenate(
            [inner, jnp.zeros((2 * LANES - chunk, LANES), jnp.float32)], axis=0
        ).T
        high, low = split_high_low(inner[0:SMALL, :])
        both = jnp.where(
            live_rows(high.shape, SMALL // 2), high.astype(jnp.float32), low.astype(jnp.float32)
        )
        out[chunk:, : 2 * LANES] = both.astype(jnp.bfloat16)
        out[chunk:, 2 * LANES :] = jnp.zeros((SMALL, width - 2 * LANES), jnp.bfloat16)
        gated = gated_ref[here, :].astype(jnp.float32) + gated_other_ref[here, :].astype(jnp.float32)
        gated = gated.astype(jnp.bfloat16)
        if k % 2:
            pair_ref[k // 2] = gated
        else:
            (own_ref, far_ref)[k // 2][...] = gated


def pair_sum_kernel(pos_ref, base_ref, own_ref, far_ref, got_ref, sum_ref, send_ref):
    total = base_ref[...] + own_ref[...].astype(jnp.float32) + got_ref[0].astype(jnp.float32)
    sum_ref[...] = total
    send_ref[...] = (far_ref[...].astype(jnp.float32) + got_ref[1].astype(jnp.float32)).astype(
        jnp.bfloat16
    )


def expert_grad_kernel(first, pos_ref, *refs):
    outs = refs[8:]
    part_rows = outs[0].shape[2]
    for j, out in enumerate(outs):
        start = 2 * (first + j) * part_rows
        columns = slice(start, start + 2 * part_rows)
        for s in range(2):
            left_a, right_a, left_b, right_b = refs[4 * s : 4 * s + 4]
            grad = contract(left_a[:, columns], right_a[...], TN)
            grad = grad + contract(left_b[:, columns], right_b[...], TN)
            grad = grad.astype(jnp.bfloat16)
            out[0, s] = grad[0:part_rows]
            out[1, s] = grad[part_rows:]


def expert_grads(position, a, b, rows_a, rows_b, first=0, count=2, flops=0):
    width, total = rows_a[0].shape[1], a[0].shape[1]
    return kernel_call(
        functools.partial(expert_grad_kernel, first),
        "expert_grads",
        position,
        [a[1], rows_a[0], b[1], rows_b[0], a[0], rows_a[1], b[0], rows_b[1]],
        [like((2, 2, total // 4, width), jnp.bfloat16)] * count,
        flops=flops,
        limit=10,
    )


def route_back_kernel(
    experts, token_rows, owners, pos_ref, *refs
):
    backs = refs[:owners][::-1]
    prob_ref, res_ref, pay_ref, param_ref = refs[owners : owners + 4]
    grad_ref, up_ref, small_ref = refs[owners + 4 :]
    chunk, width = res_ref.shape
    prob = prob_ref[...]
    lane = lax.broadcasted_iota(jnp.int32, prob.shape, 1)
    route_grad = jnp.zeros_like(prob)
    routed_grad = jnp.zeros((chunk, width), jnp.float32)
    for k, back in enumerate(backs):
        owner = lax.bitwise_xor(lax.axis_index("expert"), k)
        inner = back[chunk:, : 2 * LANES].astype(jnp.float32)
        inner = jnp.concatenate([inner] * (LANES // SMALL), axis=0).T[0:chunk]
        inner = jnp.sum(inner, axis=-1, keepdims=True) * (2.0 / LANES)
        route_grad = jnp.where(lane == owner, inner, route_grad)
        routed_grad = routed_grad + back[0:chunk, :].astype(jnp.float32)
    mean = jnp.sum(route_grad * prob, axis=-1, keepdims=True)
    logit_grad = (prob * (route_grad - mean)).astype(jnp.bfloat16)
    routed_grad = routed_grad + contract(
        logit_grad, router_matrix(param_ref, experts), NN
    )
    normed, inverse, mixed = normalize(res_ref[...], gain_row(param_ref, experts, 1))
    from_norm, gain_grad = normalize_back(
        routed_grad, normed, inverse, gain_row(param_ref, experts, 1)
    )
    total = pay_ref[0:chunk, :].astype(jnp.float32) + from_norm
    grad_ref[...] = total
    up_ref[...] = total.astype(jnp.bfloat16)
    live = live_rows(prob.shape, token_rows, lax.axis_index("tensor") * chunk)
    prob_sum = jnp.sum(jnp.where(live, prob, 0.0), axis=0, keepdims=True)
    grad_router = contract(logit_grad, mixed.astype(jnp.bfloat16), TN)
    small_ref[0:SMALL, :] = grad_router[0:SMALL]
    small_ref[experts : experts + 1, :] = gain_grad[None]
    small_ref[experts + 1 : experts + 2, :] = jnp.zeros((1, width), jnp.float32)
    small_ref[experts + 1 : experts + 2, :LANES] = prob_sum
    small_ref[experts + 2 : experts + 3, :] = param_ref[SMALL - 1 : SMALL, :]


def attention_back_kernel(
    heads, experts, owners, pos_ref, tok_ref, param_ref, w_ref, wo_ref, qkv_ref, lse_ref, att_ref,
    up_ref, small_ref, keep_ref, send_ref, *refs,
):
    *parts, hg_ref, flat_ref, big_ref, image_ref, held_ref, sum_ref, gain_ref = refs
    images, rows, width = qkv_ref.shape[1], qkv_ref.shape[2], heads * HD
    seq_len = tok_ref.shape[1]
    scale = HD ** (-0.5)
    padded, model = up_ref.shape
    chunk = padded // len(parts)
    masks = head_masks(rows, heads)
    keys_live = lax.broadcasted_iota(jnp.int32, (rows, rows), 1) < seq_len
    lane = lax.broadcasted_iota(jnp.int32, (rows, LANES), 1)
    up = up_ref[...]
    hg_ref[0:padded, :] = contract(up, wo_ref[...], NT)
    hg_ref[padded:, :] = jnp.zeros((hg_ref.shape[0] - padded, width), jnp.float32)
    big_ref[3 * width :, :] = contract(att_ref[...], up, TN)
    flat_ref[images * seq_len :, :] = jnp.zeros(
        (flat_ref.shape[0] - images * seq_len, model), jnp.float32
    )
    for i in range(images):
        held_ref[i] = hg_ref[pl.ds(i * seq_len, rows), :]
    big_ref[0 : 3 * width, :] = jnp.zeros((3 * width, model), jnp.float32)

    @pl.loop(0, images, unroll=True)
    def _(i):
        normed, _, mixed = normalize(
            image_rows(tok_ref, i, image_ref), gain_row(param_ref, experts, 0)
        )
        entered = mixed.astype(jnp.bfloat16)
        q, k, v = qkv_ref[0, i], qkv_ref[1, i], qkv_ref[2, i]
        heads_grad = held_ref[i]
        heads_grad = jnp.where(live_rows(heads_grad.shape, seq_len), heads_grad, 0.0)
        heads_grad = heads_grad.astype(jnp.bfloat16)
        dq = jnp.zeros((rows, width), jnp.float32)
        dk, dv = dq, dq
        for h in range(heads):
            q_h, k_h = keep_lanes(q, masks[h]), keep_lanes(k, masks[h])
            up_h = keep_lanes(heads_grad, masks[h])
            scores = contract(q_h, k, NT) * scale
            lse = jnp.sum(jnp.where(lane == h, lse_ref[i], 0.0), axis=-1, keepdims=True)
            probs = jnp.where(keys_live, jnp.exp(scores - lse), 0.0)
            prob_grad = contract(up_h, v, NT)
            total = jnp.sum(prob_grad * probs, axis=-1, keepdims=True)
            score_grad = (probs * (prob_grad - total)).astype(jnp.bfloat16)
            dv = dv + contract(probs.astype(jnp.bfloat16), up_h, TN)
            dq = dq + contract(score_grad, k_h, NN)
            dk = dk + contract(score_grad, q_h, TN)
        grads = [g.astype(jnp.bfloat16) for g in (dq * scale, dk * scale, dv)]
        part = jnp.zeros((rows, model), jnp.float32)
        for c in range(3):
            here = slice(c * width, (c + 1) * width)
            part = part + contract(grads[c], w_ref[here, :], NN)
            big_ref[here, :] += contract(grads[c], entered, TN)
        sum_ref[i] = part
        gain_ref[i] = jnp.broadcast_to(
            jnp.sum(part * normed, axis=0, keepdims=True), gain_ref.shape[1:]
        )

    gain_grad = jnp.zeros((1, model), jnp.float32)
    for i in range(images):
        flat_ref[pl.ds(i * seq_len, seq_len), :] = sum_ref[i, 0:seq_len, :]
        gain_grad = gain_grad + gain_ref[i, 0:1, :]
    small = pack_small(
        jnp.concatenate([small_ref[0 : SMALL - 1, :], gain_grad], axis=0), experts
    )
    for j, part in enumerate(parts):
        part[0:chunk, :] = flat_ref[chunk_of(pos_ref, j, chunk), :].astype(jnp.bfloat16)
        part[chunk:, :] = small
    me, core = lax.axis_index("expert"), lax.axis_index("dp")
    piece = keep_ref.shape[1]
    for k in range(owners):
        place = lax.bitwise_xor(me, k) * piece
        mine = pl.ds(pl.multiple_of(core * owners * piece + place, 8), piece)
        other = pl.ds(pl.multiple_of((1 - core) * owners * piece + place, 8), piece)
        keep_ref[k] = big_ref[mine, :]
        send_ref[k] = big_ref[other, :].astype(jnp.bfloat16)


def norm_back_kernel(experts, tensors, pos_ref, *refs):
    got = refs[:tensors]
    x_ref, res_ref, param_ref, own_ref, *parts, grad_ref, out_ref, small_ref = refs[tensors:]
    chunk, width = x_ref.shape
    upstream = jnp.zeros((chunk, width), jnp.float32)
    for j, part in enumerate(got):
        upstream = upstream + part[0:chunk, :].astype(jnp.float32)
        small_ref[lax.bitwise_xor(lax.axis_index("tensor"), j)] = unpack_small(
            part[chunk:, :], experts
        )
    small = small_ref[0]
    for j in range(1, tensors):
        small = small + small_ref[j]
    gain = gain_row(param_ref, experts, 0)
    normed, inverse, _ = normalize(x_ref[...].astype(jnp.float32), gain)
    from_norm = normalize_back(upstream, normed, inverse, gain)[0]
    grad_ref[...] = (res_ref[...] + from_norm).astype(jnp.bfloat16)
    piece = own_ref.shape[0]
    total = own_ref[...]
    for part in parts:
        total = total + part[...].astype(jnp.float32)
    out_ref[0:piece, :] = total.astype(jnp.bfloat16)
    out_ref[piece:, :] = pack_small(small, experts)


def second_step_kernel(pos_ref, near_ref, from_y, from_x, x_ref, y_ref):
    for target, row, other in ((x_ref, 0, from_y), (y_ref, 1, from_x)):
        total = near_ref[row].astype(jnp.float32) + other[1].astype(jnp.float32)
        target[...] = total.astype(jnp.bfloat16)


def weight_sum_kernel(pos_ref, own_ref, from_y, from_x, last_x, last_y, out_ref):
    part_rows = last_x.shape[1]
    for row, other, last in ((0, from_y, last_x), (1, from_x, last_y)):
        total = own_ref[row].astype(jnp.float32) + other[0].astype(jnp.float32)
        total = total + last[...].astype(jnp.float32)
        out_ref[:, row * part_rows : (row + 1) * part_rows, :] = total.astype(jnp.bfloat16)


def add_core_kernel(pos_ref, keep_ref, other_ref, own_ref, *outs):
    total = keep_ref[...] + other_ref[...].astype(jnp.float32)
    own_ref[...] = total[0]
    for k, out in enumerate(outs):
        out[...] = total[k + 1].astype(jnp.bfloat16)


def spread_kernel(owners, experts, token_total, pos_ref, *refs):
    sides = refs[:2]
    qkv_ref, wo_ref, router_ref, one_ref, two_ref, loss_ref, big_ref, parts_ref = refs[2:]
    span = sides[0].shape[0] // owners
    piece = span - SMALL
    core, me = lax.axis_index("dp"), lax.axis_index("expert")
    for c in range(2):
        side = core if c == 0 else 1 - core
        for k in range(owners):
            block = sides[c].at[k * span : (k + 1) * span]
            place = side * owners + lax.bitwise_xor(me, k)
            here = pl.ds(pl.multiple_of(place * piece, 8), piece)
            big_ref[here, :] = block[0:piece, :].astype(jnp.float32)
            parts_ref[place] = unpack_small(block[piece:, :], experts)
    rows = qkv_ref.shape[0]
    qkv_ref[...] = big_ref[0:rows, :]
    wo_ref[...] = big_ref[rows:, :]
    small = parts_ref[0]
    for p in range(1, 2 * owners):
        small = small + parts_ref[p]
    router_ref[...] = small[0:experts, :]
    one_ref[...] = small[SMALL - 1 : SMALL, :].reshape(small.shape[1])
    two_ref[...] = small[experts : experts + 1, :].reshape(small.shape[1])
    product = small[experts + 1 : experts + 2, :LANES] * small[experts + 2 : experts + 3, :LANES]
    lane = lax.broadcasted_iota(jnp.int32, product.shape, 1)
    product = jnp.where(lane < experts, product, 0.0)
    loss = jnp.sum(product, axis=-1, keepdims=True)
    loss_ref[...] = jnp.broadcast_to(
        loss * (experts / (2.0 * token_total * token_total)), loss_ref.shape
    )


def images_kernel(pos_ref, *refs):
    *chunks, out_ref, flat_ref = refs
    images, seq_len, _ = out_ref.shape
    if len(chunks) == 1:
        flat_ref[...] = chunks[0][...].astype(jnp.float32)
    else:
        for j, part in enumerate(chunks):
            flat_ref[chunk_of(pos_ref, j, part.shape[0]), :] = part[...].astype(jnp.float32)
    for i in range(images):
        out_ref[i] = flat_ref[pl.ds(i * seq_len, seq_len), :].astype(out_ref.dtype)


def weight_out_kernel(pos_ref, mine_ref, other_ref, in_ref, out_ref):
    first_is_mine = lax.axis_index("dp") == 0
    half = mine_ref.shape[1]
    for c in range(2):
        here = slice(c * half, (c + 1) * half)
        take = first_is_mine if c == 0 else jnp.logical_not(first_is_mine)
        grad_in = jnp.where(take, mine_ref[0], other_ref[0]).astype(jnp.float32)
        in_ref[0, :, here] = grad_in.T
        out_ref[0, here, :] = jnp.where(take, mine_ref[1], other_ref[1]).astype(jnp.float32)


def swap_core(value):
    return lax.ppermute(value, "dp", [(0, 1), (1, 0)])


def hop(value, bit):
    size = lax.axis_size("expert")
    return lax.ppermute(value, "expert", [(i, i ^ bit) for i in range(size)])


def cross(value, bit):
    size = lax.axis_size("tensor")
    return lax.ppermute(value, "tensor", [(i, i ^ bit) for i in range(size)])


def after(value, *others):
    return lax.optimization_barrier((value, *others))[0]


def dense_body(
    tokens,
    cotangent,
    expert_ids,
    slot_rank,
    qkv_weight,
    out_weight,
    router_weight,
    expert_in,
    expert_out,
    gain_attention,
    gain_experts,
):
    f32, b16 = jnp.float32, jnp.bfloat16
    images, seq_len, width = tokens.shape
    token_rows = images * seq_len
    local = qkv_weight.shape[2]
    heads = local // HD
    experts = router_weight.shape[1]
    owners = lax.axis_size("expert")
    tensors = lax.axis_size("tensor")
    cores = lax.axis_size("dp")
    chunk = round_up(-(-token_rows // tensors), 8)
    padded = chunk * tensors
    rows = round_up(seq_len, 16)
    flat_rows = padded + 32
    half = expert_in.shape[2] // cores
    quarter = half // 2
    position = jnp.zeros((1,), jnp.int32)
    weight_rows = qkv_weight.transpose(0, 2, 1).reshape(3 * local, width)

    x_chunk, payload, params, first, second = kernel_call(
        functools.partial(chunk_kernel, tensors),
        "chunk",
        position,
        [
            tokens,
            cotangent,
            expert_ids.transpose(0, 2, 1),
            slot_rank.transpose(0, 2, 1),
            router_weight.T,
            gain_attention,
            gain_experts,
            expert_in,
            expert_out,
        ],
        [
            like((chunk, width), b16),
            like((chunk + SMALL, width), b16),
            like((SMALL, width), f32),
            like((2, quarter, width), b16),
            like((2, quarter, width), b16),
        ],
        [
            pltpu.VMEM((flat_rows, width), f32),
            pltpu.VMEM((padded + 2 * LANES, LANES), f32),
        ],
        limit=56,
        loads=tuple(range(9)),
    )
    payload_two = hop(payload, 2)
    first_x = cross(first, 1)
    second_y = cross(second, 2)

    qkv, lse, attended, *parts = kernel_call(
        functools.partial(attention_kernel, heads, experts),
        "attention",
        after(position, first),
        [tokens, params, weight_rows, out_weight],
        [
            like((3, images, rows, local), b16),
            like((images, rows, LANES), f32),
            like((padded, local), b16),
        ]
        + [like((chunk, width), b16)] * tensors,
        [
            pltpu.VMEM((padded, local), f32),
            pltpu.VMEM((rows, width), f32),
            pltpu.VMEM((images, rows, local), f32),
        ],
        flops=40_000_000_000,
        limit=20,
        loads=(0, 1, 2, 3),
    )
    arrived = [parts[0]] + [cross(parts[j], j) for j in range(1, tensors)]
    pair_first, pair_second = stack_pairs(
        after(position, parts[0]), (first, first_x), (second, second_y)
    )
    (payload_near,) = stack_pairs(after(position, pair_first), (payload, payload_two))
    payload_far = hop(payload_near, 1)

    residual, routed, prob = kernel_call(
        functools.partial(route_kernel, experts),
        "route",
        after(position, pair_first, payload_near),
        [*arrived, x_chunk, params],
        [like((chunk, width), f32), like((chunk, width), b16), like((chunk, LANES), f32)],
        limit=8,
    )
    blocks = [routed] + [hop(routed, k) for k in range(1, owners)]
    pair_first, pair_second = after((pair_first, pair_second), routed)
    pair_y = cross(pair_first, 2)
    pair_x = cross(pair_second, 1)
    payload_mine = kernel_call(
        lay_payload_kernel,
        "lay_payload",
        after(position, routed),
        [payload_near, payload_far],
        [like((owners * chunk, width + LANES), b16)],
        limit=6,
    )[0]
    payload_other = swap_core(payload_mine)
    rows_mine = lay_rows(position, "lay_rows", blocks)
    rows_other = swap_core(rows_mine)

    near_weights = (first, second, first_x, second_y)
    far_weights = (pair_y, pair_x)
    first_a = first_expert_pass(position, rows_mine, payload_mine, params, near_weights, experts)
    first_b = first_expert_pass(
        after(position, first_a[2]), rows_other, payload_other, params, near_weights, experts
    )
    second_b = second_expert_pass(
        after(position, first_b[2]), rows_other, payload_other, first_b, far_weights, b16
    )
    back_other, gated_other = swap_core(second_b[3]), swap_core(second_b[2])
    second_a = second_expert_pass(
        after(position, second_b[0]), rows_mine, payload_mine, first_a, far_weights, f32
    )
    *joined, gated_own, gated_pair, gated_far = kernel_call(
        join_kernel,
        "join",
        position,
        [second_a[3], back_other, second_a[2], gated_other],
        [like((chunk + SMALL, width), b16)] * owners
        + [like((chunk, width), b16), like((2, chunk, width), b16), like((chunk, width), b16)],
        limit=8,
    )
    backs = [joined[0]] + [hop(joined[k], k) for k in range(1, owners)]

    grad_pos = after(position, joined)
    far_rows = (rows_mine, first_a[2]), (rows_other, first_b[2])
    (far_y,) = expert_grads(grad_pos, second_a, second_b, *far_rows, first=0, count=1)
    (far_x,) = expert_grads(
        after(grad_pos, far_y), second_a, second_b, *far_rows, first=1, count=1, flops=0
    )
    from_y, from_x = cross(far_y, 2), cross(far_x, 1)
    residual_grad, attn_grad, small = kernel_call(
        functools.partial(route_back_kernel, experts, token_rows, owners),
        "route_back",
        position,
        [*backs[::-1], prob, residual, payload, params],
        [like((chunk, width), f32), like((chunk, width), b16), like((SMALL, width), f32)],
        flops=40_000_000_000,
        limit=8,
    )
    own_grad, near_grad = expert_grads(
        after(position, attn_grad), first_a, first_b, (rows_mine, first_a[2]), (rows_other, first_b[2]),
    )
    gated_near = hop(after(gated_pair, backs[1]), 1)
    block_sum, gated_far = kernel_call(
        pair_sum_kernel,
        "pair_sum",
        after(position, own_grad),
        [residual, gated_own, gated_far, gated_near],
        [like((chunk, width), f32), like((chunk, width), b16)],
        limit=4,
    )
    attn_grad, gated_far = lax.optimization_barrier((attn_grad, gated_far))
    gated_last = hop(gated_far, 2)
    attn_grad = lax.all_gather(attn_grad, "tensor", axis=0, tiled=True)
    piece = 4 * local // (2 * owners)
    keep, send, *parts = kernel_call(
        functools.partial(attention_back_kernel, heads, experts, owners),
        "attention_back",
        after(position, from_y, from_x, gated_last),
        [tokens, params, weight_rows, out_weight, qkv, lse, attended, attn_grad, small],
        [
            like((owners, piece, width), f32),
            like((owners, piece, width), b16),
        ]
        + [like((chunk + SMALL, width), b16)] * tensors,
        [
            pltpu.VMEM((flat_rows, local), f32),
            pltpu.VMEM((flat_rows, width), f32),
            pltpu.VMEM((4 * local, width), f32),
            pltpu.VMEM((rows, width), f32),
            pltpu.VMEM((images, rows, local), f32),
            pltpu.VMEM((images, rows, width), f32),
            pltpu.VMEM((images, SMALL, width), f32),
        ],
        limit=20,
        flops=6_000_000_000,
    )
    own_piece, *pieces = kernel_call(
        add_core_kernel,
        "add_core",
        position,
        [keep, swap_core(send)],
        [like((piece, width), f32)] + [like((piece, width), b16)] * (owners - 1),
        limit=8,
    )
    reduced = [hop(p, k + 1) for k, p in enumerate(pieces)]
    got = [parts[0]] + [cross(parts[j], j) for j in range(1, tensors)]

    up_x, up_y = kernel_call(
        second_step_kernel,
        "second_step",
        after(position, own_piece),
        [near_grad, from_y, from_x],
        [like((2, quarter, width), b16)] * 2,
        limit=8,
    )
    up_x, up_y = after((up_x, up_y), got[1:])
    last_x, last_y = cross(up_x, 1), cross(up_y, 2)

    combined = (block_sum + gated_last.astype(f32)).astype(b16)
    grad_chunk, summed = kernel_call(
        functools.partial(norm_back_kernel, experts, tensors),
        "norm_back",
        after(position, combined),
        [*got, x_chunk, residual_grad, params, own_piece, *reduced],
        [like((chunk, width), b16), like((piece + SMALL, width), b16)],
        [pltpu.VMEM((tensors, SMALL, width), f32)],
        flops=40_000_000_000,
        limit=8,
    )
    around = [summed] + [hop(summed, k) for k in range(1, owners)]
    grad_rows = lax.all_gather(grad_chunk, "tensor", axis=0, tiled=True)
    combined = after(combined, grad_rows)
    block_parts = [combined] + [cross(combined, j) for j in range(1, tensors)]

    grad_tokens = kernel_call(
        images_kernel,
        "grad_tokens",
        position,
        [grad_rows],
        [like(tokens.shape, f32)],
        [pltpu.VMEM((padded, width), f32)],
        limit=8,
    )[0]
    grad_half = kernel_call(
        weight_sum_kernel,
        "weight_sum",
        after(position, grad_rows, around),
        [own_grad, from_y, from_x, last_x, last_y],
        [like((2, half, width), b16)],
        limit=8,
    )[0]
    grad_expert_in, grad_expert_out = kernel_call(
        weight_out_kernel,
        "weight_out",
        position,
        [grad_half, swap_core(grad_half)],
        [like((1, width, 2 * half), f32), like((1, 2 * half, width), f32)],
        limit=10,
    )
    around_rows = lay_rows(position, "lay_grads", around)
    token_total = token_rows * cores * owners
    grad_qkv, grad_out, grad_router, gain_one, gain_two, loss = kernel_call(
        functools.partial(spread_kernel, owners, experts, token_total),
        "spread",
        position,
        [around_rows, swap_core(around_rows)],
        [
            like((3 * local, width), f32),
            like((local, width), f32),
            like((experts, width), f32),
            like((width,), f32),
            like((width,), f32),
            like((1, LANES), f32),
        ],
        [
            pltpu.VMEM((4 * local, width), f32),
            pltpu.VMEM((2 * owners, SMALL, width), f32),
        ],
        limit=8,
    )
    block_out = kernel_call(
        images_kernel,
        "block_out",
        after(position, grad_tokens, grad_expert_in, grad_qkv),
        block_parts,
        [like(tokens.shape, b16)],
        [pltpu.VMEM((padded, width), f32)],
        limit=8,
    )[0]
    return (
        block_out,
        grad_tokens,
        grad_qkv.reshape(3, local, width).transpose(0, 2, 1),
        grad_out,
        grad_router.T,
        grad_expert_in,
        grad_expert_out,
        gain_one,
        gain_two,
        loss[0, 0],
    )


def solution(mesh):
    placed = (
        P(("dp", "expert"), None, None),
        P(("dp", "expert"), None, None),
        P(("dp", "expert"), None, None),
        P(("dp", "expert"), None, None),
        P(None, None, "tensor"),
        P("tensor", None),
        P(),
        P("expert", None, "tensor"),
        P("expert", "tensor", None),
        P(),
        P(),
    )
    shape = mesh.shape
    dense = shape["dp"] == 2 and shape["expert"] == 4 and shape["tensor"] == 4
    return jax.shard_map(
        dense_body if dense else body,
        mesh=mesh,
        in_specs=placed,
        out_specs=(
            P(("dp", "expert"), None, None),
            P(("dp", "expert"), None, None),
            P(None, None, "tensor"),
            P("tensor", None),
            P(),
            P("expert", None, "tensor"),
            P("expert", "tensor", None),
            P(),
            P(),
            P(),
        ),
        check_vma=False,
    )
```
